32 devices in a mesh: fsdp: 8 (over y, x, core), tp: 4 (over z).
Axes of the slice: x: 2, y: 2, z: 4, core: 2. Of those that a mesh axis runs over, the one named last changes fastest.
Arguments:
- hidden: bfloat16 [8192, 2048], P(('fsdp', 'tp')), may hold values from -6 to 6
- embed: bfloat16 [8192, 2048], P(('fsdp', 'tp')), may hold values from -6 to 6
- lengths: int32 [8, 3], P('fsdp'), may hold values from 1 to 768, 1024 in all within a row
- attention_norm_gain: bfloat16 [4096], P('fsdp'), may hold values from 0.5 to 1.5
- query_key_value_weight: bfloat16 [4096, 3, 4096], P('fsdp', None, 'tp'), may hold values from -0.09375 to 0.09375
- attention_adapter_down: bfloat16 [4096, 3, 128], P('fsdp'), may hold values from -0.09375 to 0.09375
- attention_adapter_up: bfloat16 [128, 3, 4096], P('fsdp', None, 'tp'), may hold values from -0.25 to 0.25
- attention_output_weight: bfloat16 [4096, 2048], P('tp', 'fsdp'), may hold values from -0.25 to 0.25
- feedforward_norm_gain: bfloat16 [2048], P('fsdp'), may hold values from 0.5 to 1.5
- gate_up_weight: bfloat16 [2048, 2, 8192], P('fsdp', None, 'tp'), may hold values from -0.125 to 0.125
- feedforward_adapter_down: bfloat16 [2048, 128], P('fsdp'), may hold values from -0.125 to 0.125
- feedforward_adapter_up: bfloat16 [128, 2, 8192], P('fsdp', None, 'tp'), may hold values from -0.25 to 0.25
- down_weight: bfloat16 [8192, 2048], P('tp', 'fsdp'), may hold values from -0.0625 to 0.0625
- mixer_norm_gain: bfloat16 [2048], P('fsdp'), may hold values from 0.5 to 1.5
- gate_inner_weight: bfloat16 [2048, 2, 4096], P('fsdp', None, 'tp'), may hold values from -0.125 to 0.125
- state_input_weight: bfloat16 [2048, 2, 64], P('fsdp'), may hold values from -0.125 to 0.125
- step_projection: bfloat16 [2048, 64], P('fsdp', 'tp'), may hold values from -0.125 to 0.125
- inner_conv_taps: bfloat16 [4, 64, 64], P(None, 'tp', 'fsdp'), may hold values from -2 to 2
- state_conv_taps: bfloat16 [4, 2, 64], P(None, None, 'fsdp'), may hold values from -2 to 2
- head_step_bias: float32 [64], P('tp'), may hold values from -6 to -3.5
- decay_log_rate: float32 [64], P('tp'), may hold values from -0.5 to 1
- inner_skip_gains: bfloat16 [64, 64], P('tp', 'fsdp'), may hold values from 0.5 to 1.5
- gated_norm_gain: bfloat16 [64, 64], P('tp', 'fsdp'), may hold values from 0.5 to 1.5
- mixer_output_weight: bfloat16 [4096, 2048], P('tp', 'fsdp'), may hold values from -0.09375 to 0.09375
- output_cotangent: bfloat16 [8192, 2048], P(('fsdp', 'tp')), may hold values from -6 to 6
Outputs:
- out: float32 [8192, 2048], P(('fsdp', 'tp'))
- grad_hidden: float32 [8192, 2048], P(('fsdp', 'tp'))
- grad_embed: float32 [8192, 2048], P(('fsdp', 'tp'))
- attention_gain_gradient: float32 [4096], P(('fsdp', 'tp'))
- grad_w_qkv: float32 [4096, 3, 4096], P('fsdp', None, 'tp')
- attention_down_gradient: float32 [4096, 3, 128], P(('fsdp', 'tp'))
- attention_up_gradient: float32 [128, 3, 4096], P('fsdp', None, 'tp')
- grad_w_o: float32 [4096, 2048], P('tp', 'fsdp')
- grad_mlp_gain: float32 [2048], P('fsdp')
- grad_w_fc1: float32 [2048, 2, 8192], P('fsdp', None, 'tp')
- feedforward_down_gradient: float32 [2048, 128], P('fsdp')
- feedforward_up_gradient: float32 [128, 2, 8192], P('fsdp', None, 'tp')
- grad_w_fc2: float32 [8192, 2048], P('tp', 'fsdp')
- grad_mixer_gain: float32 [2048], P('fsdp')
- grad_w_in_zx: float32 [2048, 2, 4096], P('fsdp', None, 'tp')
- grad_w_in_bc: float32 [2048, 2, 64], P('fsdp')
- grad_w_dt: float32 [2048, 64], P('fsdp', 'tp')
- grad_conv_x: float32 [4, 64, 64], P(None, 'tp', 'fsdp')
- grad_conv_bc: float32 [4, 2, 64], P(None, None, 'fsdp')
- grad_dt_bias: float32 [64], P('tp')
- grad_a_log: float32 [64], P('tp')
- grad_d_skip: float32 [64, 64], P('tp', 'fsdp')
- grad_gate_gain: float32 [64, 64], P('tp', 'fsdp')
- grad_w_out: float32 [4096, 2048], P('tp', 'fsdp')
The draws below stay inside these ranges and needn't reach their ends.
Inputs may be any that keep to these rules, and one draw needn't show every extreme that they name: Each row holds the lengths of the 3 sequences of one group; a row sums to 1024 and its longest is exactly 768.
All inputs are finite; a program needn't handle non-finite values.
Results may differ from the reference program's by a relative error of at most 0.025.
Values may be sent and summed in bfloat16 or wider, within the bound.
No kernel may reach another device: no remote copies, remote signals or barrier semaphores. Data moves between devices by JAX's collectives and lax.ppermute only.
A program may use at most 320 MiB of HBM per device.

```python
import math
import jax
import jax.numpy as jnp
import numpy as np
from jax import lax

MODEL_WIDTH = 2048
BLOCK_INPUT_WIDTH = 4096
HDA = 128
NHA = 32
ADAPTER_RANK = 128
FEEDFORWARD_UNITS = 8192
DI = 4096
HD = 64
NH = 64
NS = 64
KC = 4
SEQS = 3
MAXLEN = 768
TOK_GROUP = 1024
TOKENS = 8192
N_FSDP = 8


def steps_of(own_key, dims, split, low, largest):
    def one(axis_at, blocks):
        draws = jax.random.uniform(jax.random.fold_in(jax.random.fold_in(own_key, 6), axis_at), (blocks,), jnp.float32, low / len(split), largest / len(split))
        return jnp.repeat(jnp.exp(draws), dims[axis_at] // blocks).reshape((-1,) + (1,) * (len(dims) - axis_at - 1))

    factor_of = one(*split[0])
    for cut in split[1:]:
        factor_of = factor_of * one(*cut)
    return factor_of


def profile(number_of, total, most, skew):
    portions = [(1 << 20) // math.isqrt(standing ** skew) + 1 for standing in range(2, number_of + 1)]
    surplus, given = total - most - (number_of - 1), [1] * (number_of - 1)
    while surplus > 0:
        candidates = [i for i in range(number_of - 1) if given[i] < most]
        whole, left = sum([portions[i] for i in candidates]), surplus
        for i in candidates:
            extra = min(most - given[i], max(1, left * portions[i] // whole), surplus)
            given[i] = given[i] + extra
            surplus = surplus - extra
    return np.array([most] + given)


def uneven_parts(own_key, number_of, total, limit, skew):
    if number_of == 2:
        one = jax.random.randint(own_key, (), max(1, total - limit), min(limit, total - 1) + 1)
        return jnp.stack([one, total - one])
    sizes = jnp.asarray(profile(number_of, total, limit, skew), jnp.int32)
    couples = (number_of - 1) // 2
    donor, taker = sizes[1:1 + 2 * couples:2], sizes[2:2 + 2 * couples:2]
    margin = jnp.minimum(donor - 1, limit - taker)
    moved = jax.random.randint(jax.random.fold_in(own_key, 1), (couples,), 0, 1 << 20) % (margin + 1)
    sizes = sizes.at[1:1 + 2 * couples:2].set(donor - moved).at[2:2 + 2 * couples:2].set(taker + moved)
    return sizes[jax.random.permutation(jax.random.fold_in(own_key, 2), number_of)]


def centred(own_key, extent, scale, most, split=(), held_as=jnp.bfloat16):
    entries = scale * jax.random.normal(own_key, extent, jnp.float32)
    if split:
        entries = entries * steps_of(own_key, extent, split, -0.22, 0.18)
    return jnp.clip(entries, -most, most).astype(held_as)


def setup_inputs(seed: int = 0) -> dict:
    seeds = jax.random.split(jax.random.key(seed), 26)
    hidden = centred(seeds[0], (TOKENS, MODEL_WIDTH), 1.0, 6.0, ((0, 32),))
    embed = centred(seeds[1], (TOKENS, MODEL_WIDTH), 1.0, 6.0, ((0, 32),))
    lengths = jax.vmap(lambda own: uneven_parts(own, SEQS, TOK_GROUP, MAXLEN, 2))(jax.random.split(seeds[2], N_FSDP)).reshape((N_FSDP, SEQS)).astype(jnp.int32)
    attention_norm_gain = jnp.clip(1.0 + 0.1 * jax.random.normal(seeds[3], (BLOCK_INPUT_WIDTH,), jnp.float32), 0.5, 1.5).astype(jnp.bfloat16)
    query_key_value_weight = centred(seeds[4], (BLOCK_INPUT_WIDTH, 3, BLOCK_INPUT_WIDTH), BLOCK_INPUT_WIDTH ** -0.5, 0.09375, ((0, 8), (2, 4)))
    attention_adapter_down = centred(seeds[5], (BLOCK_INPUT_WIDTH, 3, ADAPTER_RANK), BLOCK_INPUT_WIDTH ** -0.5, 0.09375, ((0, 8),))
    attention_adapter_up = centred(seeds[6], (ADAPTER_RANK, 3, BLOCK_INPUT_WIDTH), (4 * ADAPTER_RANK) ** -0.5, 0.25, ((0, 8), (2, 4)))
    attention_output_weight = centred(seeds[7], (BLOCK_INPUT_WIDTH, MODEL_WIDTH), (BLOCK_INPUT_WIDTH // 8) ** -0.5, 0.25, ((0, 4), (1, 8)))
    feedforward_norm_gain = jnp.clip(1.0 + 0.1 * jax.random.normal(seeds[8], (MODEL_WIDTH,), jnp.float32), 0.5, 1.5).astype(jnp.bfloat16)
    gate_up_weight = centred(seeds[9], (MODEL_WIDTH, 2, FEEDFORWARD_UNITS), MODEL_WIDTH ** -0.5, 0.125, ((0, 8), (2, 4)))
    feedforward_adapter_down = centred(seeds[10], (MODEL_WIDTH, ADAPTER_RANK), MODEL_WIDTH ** -0.5, 0.125, ((0, 8),))
    feedforward_adapter_up = centred(seeds[11], (ADAPTER_RANK, 2, FEEDFORWARD_UNITS), (4 * ADAPTER_RANK) ** -0.5, 0.25, ((0, 8), (2, 4)))
    down_weight = centred(seeds[12], (FEEDFORWARD_UNITS, MODEL_WIDTH), FEEDFORWARD_UNITS ** -0.5, 0.0625, ((0, 4), (1, 8)))
    mixer_norm_gain = jnp.clip(1.0 + 0.1 * jax.random.normal(seeds[13], (MODEL_WIDTH,), jnp.float32), 0.5, 1.5).astype(jnp.bfloat16)
    gate_inner_weight = centred(seeds[14], (MODEL_WIDTH, 2, DI), MODEL_WIDTH ** -0.5, 0.125, ((0, 8), (2, 4)))
    state_input_weight = centred(seeds[15], (MODEL_WIDTH, 2, NS), MODEL_WIDTH ** -0.5, 0.125, ((0, 8),))
    step_projection = centred(seeds[16], (MODEL_WIDTH, NH), MODEL_WIDTH ** -0.5, 0.125, ((0, 8), (1, 4)))
    inner_conv_taps = centred(seeds[17], (KC, NH, HD), 0.5, 2.0, ((1, 4), (2, 8)))
    state_conv_taps = centred(seeds[18], (KC, 2, NS), 0.5, 2.0, ((2, 8),))
    head_step_bias = jnp.clip(-6.0 + 2.5 * jax.random.uniform(seeds[19], (NH,), jnp.float32) ** steps_of(seeds[19], (NH,), ((0, 4),), -0.2, 0.2), -6.0, -3.5)
    decay_log_rate = jnp.clip(-0.5 + 1.5 * jax.random.uniform(seeds[20], (NH,), jnp.float32) ** steps_of(seeds[20], (NH,), ((0, 4),), -0.2, 0.2), -0.5, 1.0)
    inner_skip_gains = jnp.clip(0.5 + 1.0 * jax.random.uniform(seeds[21], (NH, HD), jnp.float32) ** steps_of(seeds[21], (NH, HD), ((0, 4), (1, 8)), -0.2, 0.2), 0.5, 1.5).astype(jnp.bfloat16)
    gated_norm_gain = jnp.clip(1.0 + 0.1 * jax.random.normal(seeds[22], (NH, HD), jnp.float32), 0.5, 1.5).astype(jnp.bfloat16)
    mixer_output_weight = centred(seeds[23], (DI, MODEL_WIDTH), DI ** -0.5, 0.09375, ((0, 4), (1, 8)))
    output_cotangent = centred(seeds[24], (TOKENS, MODEL_WIDTH), 1.0, 6.0, ((0, 32),))
    return {"hidden": hidden, "embed": embed, "lengths": lengths, "attention_norm_gain": attention_norm_gain, "query_key_value_weight": query_key_value_weight, "attention_adapter_down": attention_adapter_down, "attention_adapter_up": attention_adapter_up, "attention_output_weight": attention_output_weight, "feedforward_norm_gain": feedforward_norm_gain, "gate_up_weight": gate_up_weight, "feedforward_adapter_down": feedforward_adapter_down, "feedforward_adapter_up": feedforward_adapter_up, "down_weight": down_weight, "mixer_norm_gain": mixer_norm_gain, "gate_inner_weight": gate_inner_weight, "state_input_weight": state_input_weight, "step_projection": step_projection, "inner_conv_taps": inner_conv_taps, "state_conv_taps": state_conv_taps, "head_step_bias": head_step_bias, "decay_log_rate": decay_log_rate, "inner_skip_gains": inner_skip_gains, "gated_norm_gain": gated_norm_gain, "mixer_output_weight": mixer_output_weight, "output_cotangent": output_cotangent}


PRECISE_MODE = lax.Precision.HIGHEST
norm_eps = 1e-05

@jax.custom_vjp
def low(v):
    return lax.optimization_barrier(v.astype(jnp.bfloat16)).astype(jnp.float32)

@jax.custom_vjp
def low_back(v):
    return v

def low_keep(v):
    return (low(v), None)

def low_pass(kept, grad):
    return (grad,)

def back_keep(v):
    return (v, None)

def back_low(kept, grad):
    return (low(grad),)
low.defvjp(low_keep, low_pass)
low_back.defvjp(back_keep, back_low)

def matrix_product(left, right):
    return jnp.dot(left, right, precision=PRECISE_MODE)

def root_mean(values):
    return lax.rsqrt(lax.optimization_barrier(jnp.mean(values * values, axis=-1, keepdims=True)) + norm_eps)

def segments_of(lengths_row, count):
    ends = jnp.cumsum(lengths_row).astype(jnp.int32)
    starts = (ends - lengths_row).astype(jnp.int32)
    places = jnp.arange(count, dtype=jnp.int32)
    segment = lax.optimization_barrier(jnp.sum((places[:, None] >= ends[None, :]).astype(jnp.int32), axis=1)).astype(jnp.int32)
    owners = segment[:, None] == jnp.arange(ends.shape[0], dtype=jnp.int32)[None, :]
    offsets = lax.optimization_barrier(jnp.sum(jnp.where(owners, starts[None, :], 0), axis=1)).astype(jnp.int32)
    return (segment, (places - offsets).astype(jnp.int32))

def rotate(values, position, direction):
    half = values.shape[-1] // 2
    freqs = jnp.exp(jnp.arange(half, dtype=jnp.float32) * (-2.0 * math.log(10000.0) / values.shape[-1]))
    angles = position.astype(jnp.float32)[:, None] * freqs[None, :]
    cosine = jnp.cos(angles)[:, None, :]
    sine_part = direction * jnp.sin(angles)[:, None, :]
    front = values[..., :half]
    behind = values[..., half:]
    return jnp.concatenate([front * cosine - behind * sine_part, behind * cosine + front * sine_part], axis=-1)

def causal_conv(values, taps, segment):
    count = taps.shape[0]
    sequence_length = values.shape[0]
    total = jnp.zeros_like(values)
    for shift_by in range(count):
        moved = jnp.concatenate([jnp.zeros((shift_by,) + values.shape[1:], values.dtype), values[:sequence_length - shift_by]], 0)
        moved_seg = jnp.concatenate([jnp.full((shift_by,), -1, jnp.int32), segment[:sequence_length - shift_by]], 0)
        keeper = (moved_seg == segment).astype(values.dtype).reshape((sequence_length,) + (1,) * (values.ndim - 1))
        total = total + taps[count - 1 - shift_by] * moved * keeper
    return total

def mixer_core(x_heads, state_in, step_raw, taps_x, taps_state, bias_step, log_rate, skip_gain, segment):
    x_conv = jax.nn.silu(causal_conv(x_heads, taps_x, segment))
    state_conv = jax.nn.silu(causal_conv(state_in, taps_state, segment))
    step = jax.nn.softplus(step_raw + bias_step)
    cumul = jnp.cumsum(-step * jnp.exp(log_rate), axis=0)
    sequence_length = x_heads.shape[0]
    places = jnp.arange(sequence_length, dtype=jnp.int32)
    allowed = (segment[:, None] == segment[None, :]) & (places[None, :] <= places[:, None])
    inner = jnp.dot(state_conv[:, 1], state_conv[:, 0].T, precision=PRECISE_MODE)

    def one_head(pieces):
        cum_head, step_head, x_head = pieces
        spread = jnp.where(allowed, cum_head[:, None] - cum_head[None, :], -1e+30)
        mixing = jnp.exp(spread) * inner
        return jnp.dot(mixing, step_head[:, None] * x_head, precision=PRECISE_MODE)
    heads_out = lax.map(jax.checkpoint(one_head), (cumul.T, step.T, jnp.transpose(x_conv, (1, 0, 2))))
    return jnp.transpose(heads_out, (1, 0, 2)) + skip_gain * x_conv

def attention(queries, keys, values, segment):
    sequence_length = queries.shape[0]
    places = jnp.arange(sequence_length, dtype=jnp.int32)
    allowed = (segment[:, None] == segment[None, :]) & (places[None, :] <= places[:, None])

    def one_head(pieces):
        query_head, key_head, value_head = pieces
        scores = low_back(matrix_product(query_head, key_head.T) * HDA ** (-0.5))
        scores = jnp.where(allowed, scores, -1e+30)
        probs = low(jax.nn.softmax(scores, axis=-1))
        return matrix_product(probs, value_head)
    heads_out = lax.map(jax.checkpoint(one_head), (jnp.transpose(queries, (1, 0, 2)), jnp.transpose(keys, (1, 0, 2)), jnp.transpose(values, (1, 0, 2))))
    return jnp.transpose(heads_out, (1, 0, 2))

def group_layer(weight_collection, hidden, embed, lengths_row):
    attention_norm_gain, query_key_value_weight, attention_adapter_down, attention_adapter_up, attention_output_weight, feedforward_norm_gain, gate_up_weight, feedforward_adapter_down, feedforward_adapter_up, down_weight, mixer_norm_gain, gate_inner_weight, state_input_weight, step_projection, inner_conv_taps, state_conv_taps, head_step_bias, decay_log_rate, inner_skip_gains, gated_norm_gain, mixer_output_weight = weight_collection
    sequence_length = hidden.shape[0]
    segment, position = segments_of(lengths_row, sequence_length)
    joined = jnp.concatenate([hidden, embed], axis=1)
    normalized = low(joined * root_mean(joined) * attention_norm_gain)
    adapter_middle = low(matrix_product(normalized, attention_adapter_down.reshape(BLOCK_INPUT_WIDTH, 3 * ADAPTER_RANK)))
    adapter_contribution = jnp.einsum('kdp,pdw->kdw', adapter_middle.reshape(sequence_length, 3, ADAPTER_RANK), attention_adapter_up, precision=PRECISE_MODE)
    projected_rows = matrix_product(normalized, query_key_value_weight.reshape(BLOCK_INPUT_WIDTH, 3 * BLOCK_INPUT_WIDTH)).reshape(sequence_length, 3, BLOCK_INPUT_WIDTH) + adapter_contribution
    projected_rows = low_back(projected_rows).reshape(sequence_length, 3, NHA, HDA)
    queries = low(rotate(projected_rows[:, 0], position, 1.0))
    keys = low(rotate(projected_rows[:, 1], position, 1.0))
    values = low(projected_rows[:, 2])
    attended = low_back(low(attention(queries, keys, values, segment).reshape(sequence_length, BLOCK_INPUT_WIDTH)))
    mixed = low_back(matrix_product(attended, attention_output_weight))
    feedforward_input = low(mixed * root_mean(mixed) * feedforward_norm_gain)
    feedforward_middle = low(matrix_product(feedforward_input, feedforward_adapter_down))
    gate_up_product = matrix_product(feedforward_input, gate_up_weight.reshape(MODEL_WIDTH, 2 * FEEDFORWARD_UNITS)) + matrix_product(feedforward_middle, feedforward_adapter_up.reshape(ADAPTER_RANK, 2 * FEEDFORWARD_UNITS))
    gate_up_product = low_back(gate_up_product).reshape(sequence_length, 2, FEEDFORWARD_UNITS)
    units = low(jax.nn.gelu(gate_up_product[:, 0]) * gate_up_product[:, 1])
    residual = hidden + mixed + low_back(matrix_product(units, down_weight))
    mixer_in = low(residual * root_mean(residual) * mixer_norm_gain)
    gate_inner = low_back(matrix_product(mixer_in, gate_inner_weight.reshape(MODEL_WIDTH, 2 * DI))).reshape(sequence_length, 2, DI)
    state_in = matrix_product(mixer_in, state_input_weight.reshape(MODEL_WIDTH, 2 * NS)).reshape(sequence_length, 2, NS)
    step_raw = matrix_product(mixer_in, step_projection)
    scan_y = mixer_core(gate_inner[:, 1].reshape(sequence_length, NH, HD), state_in, step_raw, inner_conv_taps, state_conv_taps, head_step_bias, decay_log_rate, inner_skip_gains, segment).reshape(sequence_length, DI)
    gated = scan_y * jax.nn.silu(gate_inner[:, 0])
    scaled = low(gated * root_mean(gated) * gated_norm_gain.reshape(DI))
    return residual + low_back(matrix_product(scaled, mixer_output_weight))

def reference(hidden, embed, lengths, attention_norm_gain, query_key_value_weight, attention_adapter_down, attention_adapter_up, attention_output_weight, feedforward_norm_gain, gate_up_weight, feedforward_adapter_down, feedforward_adapter_up, down_weight, mixer_norm_gain, gate_inner_weight, state_input_weight, step_projection, inner_conv_taps, state_conv_taps, head_step_bias, decay_log_rate, inner_skip_gains, gated_norm_gain, mixer_output_weight, output_cotangent):
    weight_collection = tuple((weight_argument.astype(jnp.float32) for weight_argument in (attention_norm_gain, query_key_value_weight, attention_adapter_down, attention_adapter_up, attention_output_weight, feedforward_norm_gain, gate_up_weight, feedforward_adapter_down, feedforward_adapter_up, down_weight, mixer_norm_gain, gate_inner_weight, state_input_weight, step_projection, inner_conv_taps, state_conv_taps, head_step_bias, decay_log_rate, inner_skip_gains, gated_norm_gain, mixer_output_weight)))
    hidden_groups = hidden.astype(jnp.float32).reshape(N_FSDP, TOK_GROUP, MODEL_WIDTH)
    embed_groups = embed.astype(jnp.float32).reshape(N_FSDP, TOK_GROUP, MODEL_WIDTH)
    grad_groups = output_cotangent.astype(jnp.float32).reshape(N_FSDP, TOK_GROUP, MODEL_WIDTH)

    def forward(weights_now, hidden_now, embed_now):

        def one_group(carry, pieces):
            return (carry, jax.checkpoint(group_layer)(weights_now, pieces[0], pieces[1], pieces[2]))
        unused, results = lax.scan(one_group, jnp.zeros((), jnp.float32), (hidden_now, embed_now, lengths))
        return results
    result, backward = jax.vjp(forward, weight_collection, hidden_groups, embed_groups)
    weight_grads, hidden_grad, embed_grad = backward(grad_groups)
    return (result.reshape(TOKENS, MODEL_WIDTH), hidden_grad.reshape(TOKENS, MODEL_WIDTH), embed_grad.reshape(TOKENS, MODEL_WIDTH), weight_grads[0], weight_grads[1], weight_grads[2], weight_grads[3], weight_grads[4], weight_grads[5], weight_grads[6], weight_grads[7], weight_grads[8], weight_grads[9], weight_grads[10], weight_grads[11], weight_grads[12], weight_grads[13], weight_grads[14], weight_grads[15], weight_grads[16], weight_grads[17], weight_grads[18], weight_grads[19], weight_grads[20])
```

```python
import functools
import math

import jax
import jax.numpy as jnp
from jax import lax
from jax.experimental import pallas as pl
from jax.experimental.pallas import tpu as pltpu
from jax.sharding import PartitionSpec as P

HDA = 128
HD = 64
LANES = 128
CHUNK = 128

norm_eps = 1e-05
f32 = jnp.float32
bf16 = jnp.bfloat16
HIGHEST = lax.Precision.HIGHEST
VMEM_LIMIT = 56 * 1024 * 1024


def mm(left, right):
    return jnp.dot(left, right, preferred_element_type=f32)


def mm_nt(left, right):
    return lax.dot_general(left, right, (((1,), (1,)), ((), ())), preferred_element_type=f32)


def mm_tn(left, right):
    return lax.dot_general(left, right, (((0,), (0,)), ((), ())), preferred_element_type=f32)


def starts_of(index, ends):
    start = jnp.zeros_like(index)
    for end in ends:
        start = jnp.where(index >= end, end, start)
    return start


def ends_of(lengths_ref):
    ends = []
    end = jnp.int32(0)
    for i in range(lengths_ref.shape[0] - 1):
        end = end + lengths_ref[i]
        ends.append(end)
    return ends


def iota(shape, axis):
    return lax.broadcasted_iota(jnp.int32, shape, axis)


def attention_forward_kernel(tp, place_ref, lengths_ref, cosine_ref, sine_ref, *refs):
    q_in, k_in, v_in = refs[:tp], refs[tp : 2 * tp], refs[2 * tp : 3 * tp]
    attended_ref, q_ref, k_ref, v_ref, held = refs[3 * tp :]
    rows = q_ref.shape[0]
    share = rows // tp
    here = place_ref[0]
    ends = ends_of(lengths_ref)
    for p in range(tp):
        owner = lax.rem(here - p + tp, tp)
        part = pl.ds(pl.multiple_of(owner * share, share), share)
        cosine, sine = cosine_ref[part, :], sine_ref[part, :]
        for source, target in ((q_in[p], q_ref), (k_in[p], k_ref)):
            value = source[...]
            turned = value * cosine + pltpu.roll(value, HDA // 2, 1) * sine
            target[part, :] = turned.astype(bf16)
        v_ref[part, :] = v_in[p][...].astype(bf16)
    block = min(256, rows)
    scale = HDA ** (-0.5)
    for at in range(0, rows, block):
        upto = at + block
        scores = mm_nt(q_ref[at:upto, :], k_ref[:upto, :]) * scale
        query = at + iota((block, 1), 0)
        key = iota((1, upto), 1)
        seen = (key <= query) & (key >= starts_of(query, ends))
        scores = jnp.where(seen, scores, -1e30)
        raised = jnp.exp(scores - jnp.max(scores, axis=1, keepdims=True))
        probs = (raised * (1.0 / jnp.sum(raised, axis=1, keepdims=True))).astype(bf16)
        held[at:upto, :] = mm(probs, v_ref[:upto, :]).astype(bf16)
    for p in range(tp):
        owner = lax.rem(here - p + tp, tp)
        part = pl.ds(pl.multiple_of(owner * share, share), share)
        attended_ref[p * share : (p + 1) * share, :] = held[part, :]


def attention_forward(place, lengths, pieces, cosine, sine):
    tp = len(pieces)
    share, columns = pieces[0][0].shape
    rows = share * tp
    heads = columns // HDA
    piece_spec = pl.BlockSpec((share, HDA), lambda h, *_: (0, h))
    table_spec = pl.BlockSpec((rows, HDA), lambda h, *_: (0, 0))
    head_spec = pl.BlockSpec((rows, HDA), lambda h, *_: (0, h))
    flat = [pieces[p][j] for j in range(3) for p in range(tp)]
    work = heads * rows * rows * HDA
    return pl.pallas_call(
        functools.partial(attention_forward_kernel, tp),
        out_shape=[jax.ShapeDtypeStruct((rows, columns), bf16)] * 4,
        grid_spec=pltpu.PrefetchScalarGridSpec(
            num_scalar_prefetch=2,
            grid=(heads,),
            in_specs=[table_spec, table_spec] + [piece_spec] * (3 * tp),
            out_specs=[head_spec] * 4,
            scratch_shapes=[pltpu.VMEM((rows, HDA), bf16)],
        ),
        compiler_params=pltpu.CompilerParams(vmem_limit_bytes=VMEM_LIMIT),
        cost_estimate=pl.CostEstimate(
            flops=4 * work, bytes_accessed=20 * rows * columns, transcendentals=heads * rows * rows
        ),
        name="attention_forward",
    )(place, lengths, cosine, sine, *flat)


def attention_backward_kernel(tp, place_ref, lengths_ref, cosine_ref, sine_ref, *refs):
    q_ref, k_ref, v_ref = refs[:3]
    grad_in = refs[3 : 3 + tp]
    out_refs = refs[3 + tp : 6 + tp]
    held, dq, dk, dv = refs[6 + tp :]
    rows = q_ref.shape[0]
    share = rows // tp
    here = place_ref[0]
    ends = ends_of(lengths_ref)
    for p in range(tp):
        owner = lax.rem(here - p + tp, tp)
        part = pl.ds(pl.multiple_of(owner * share, share), share)
        held[part, :] = grad_in[p][...]
    dk[...] = jnp.zeros_like(dk)
    dv[...] = jnp.zeros_like(dv)
    block = min(256, rows)
    scale = HDA ** (-0.5)
    for at in range(0, rows, block):
        upto = at + block
        query_rows = q_ref[at:upto, :]
        grad_rows = held[at:upto, :]
        scores = mm_nt(k_ref[:upto, :], query_rows) * scale
        query = at + iota((1, block), 1)
        key = iota((upto, 1), 0)
        seen = (key <= query) & (key >= starts_of(query, ends))
        scores = jnp.where(seen, scores, -1e30)
        raised = jnp.exp(scores - jnp.max(scores, axis=0, keepdims=True))
        probs = raised * (1.0 / jnp.sum(raised, axis=0, keepdims=True))
        grad_probs = mm_nt(v_ref[:upto, :], grad_rows)
        cross = jnp.sum(probs * grad_probs, axis=0, keepdims=True)
        grad_scores = (probs * (grad_probs - cross)).astype(bf16)
        dv[:upto, :] += mm(probs.astype(bf16), grad_rows)
        dk[:upto, :] += mm(grad_scores, query_rows)
        dq[at:upto, :] = mm_tn(grad_scores, k_ref[:upto, :])
    for p in range(tp):
        owner = lax.rem(here - p + tp, tp)
        part = pl.ds(pl.multiple_of(owner * share, share), share)
        cosine, sine = cosine_ref[part, :], sine_ref[part, :]
        mine = slice(p * share, (p + 1) * share)
        for source, target in ((dq, out_refs[0]), (dk, out_refs[1])):
            value = source[part, :] * scale
            turned = value * cosine - pltpu.roll(value, HDA // 2, 1) * sine
            target[mine, :] = turned.astype(bf16)
        out_refs[2][mine, :] = dv[part, :].astype(bf16)


def attention_backward(place, lengths, queries, keys, values, pieces, cosine, sine):
    tp = len(pieces)
    share, columns = pieces[0].shape
    rows = share * tp
    heads = columns // HDA
    piece_spec = pl.BlockSpec((share, HDA), lambda h, *_: (0, h))
    table_spec = pl.BlockSpec((rows, HDA), lambda h, *_: (0, 0))
    head_spec = pl.BlockSpec((rows, HDA), lambda h, *_: (0, h))
    work = heads * rows * rows * HDA
    return pl.pallas_call(
        functools.partial(attention_backward_kernel, tp),
        out_shape=[jax.ShapeDtypeStruct((rows, columns), bf16)] * 3,
        grid_spec=pltpu.PrefetchScalarGridSpec(
            num_scalar_prefetch=2,
            grid=(heads,),
            in_specs=[table_spec, table_spec] + [head_spec] * 3 + [piece_spec] * tp,
            out_specs=[head_spec] * 3,
            scratch_shapes=[pltpu.VMEM((rows, HDA), bf16)] + [pltpu.VMEM((rows, HDA), f32)] * 3,
        ),
        compiler_params=pltpu.CompilerParams(vmem_limit_bytes=VMEM_LIMIT),
        cost_estimate=pl.CostEstimate(
            flops=10 * work, bytes_accessed=14 * rows * columns, transcendentals=heads * rows * rows
        ),
        name="attention_backward",
    )(place, lengths, cosine, sine, queries, keys, values, *pieces)


def conv_rows(extended, taps, position):
    count = 4
    rows = extended.shape[0] - 8
    total = None
    for k in range(count):
        moved = extended[8 - k : 8 - k + rows, :]
        if k:
            moved = jnp.where(position >= k, moved, 0.0)
        term = taps[count - 1 - k : count - k, :] * moved
        total = term if total is None else total + term
    return total


def conv_back(extended, taps, position):
    count = 4
    rows = extended.shape[0] - 8
    total = None
    for k in range(count):
        kept = jnp.where(position >= k, extended, 0.0) if k else extended
        term = taps[count - 1 - k : count - k, :] * kept[k : k + rows, :]
        total = term if total is None else total + term
    return total


def taps_back(extended, grad, position, target):
    count = 4
    rows = extended.shape[0] - 8
    for k in range(count):
        moved = extended[8 - k : 8 - k + rows, :]
        if k:
            moved = jnp.where(position >= k, moved, 0.0)
        at = count - 1 - k
        target[at : at + 1, :] += jnp.sum(grad * moved, axis=0, keepdims=True)


def silu_grad(value, gate):
    return gate * (1.0 + value * (1.0 - gate))


class Chunk:
    def __init__(self, c0, ends, zx, before, sd, sd_before, wide, narrow, rates):
        rows = zx.shape[0]
        width = zx.shape[1] // 2
        self.rows, self.width = rows, width
        index = c0 + iota((rows, 1), 0)
        start = starts_of(index, ends)
        self.index, self.start = index, start
        self.position = index - start
        last_start = starts_of(c0 + rows - 1, ends)
        self.z = zx[:, :width].astype(f32)
        self.x_ext = jnp.concatenate(
            [before[...].astype(f32)[8:16, :], zx[:, width:].astype(f32)], axis=0
        )
        self.s_ext = jnp.concatenate([sd_before[:, : 2 * LANES], sd[:, : 2 * LANES]], axis=0)
        self.pre = conv_rows(self.x_ext, wide, self.position)
        self.gate_x = jax.nn.sigmoid(self.pre)
        self.xc = self.pre * self.gate_x
        self.pre_s = conv_rows(self.s_ext, narrow, self.position)
        self.gate_s = jax.nn.sigmoid(self.pre_s)
        sc = self.pre_s * self.gate_s
        self.b_low = sc[:, :HD].astype(bf16)
        self.c_low = sc[:, LANES : LANES + HD].astype(bf16)
        self.raw = sd[:, 2 * LANES : 3 * LANES] + rates[0:1, :]
        self.step = jnp.maximum(self.raw, 0.0) + jnp.log1p(jnp.exp(-jnp.abs(self.raw)))
        self.rate = jnp.exp(rates[1:2, :])
        row, col = iota((rows, rows), 0), iota((rows, rows), 1)
        below = (col <= row).astype(f32)
        self.cum = jnp.dot(below, -self.step * self.rate, precision=HIGHEST, preferred_element_type=f32)
        self.cum_t = self.cum.T
        self.allowed = (col <= row) & ((c0 + col) >= start)
        self.inner = jnp.where(self.allowed, mm_nt(self.c_low, self.b_low), 0.0)
        last = self.cum[rows - 1 : rows, :]
        self.into = jnp.exp(self.cum) * (start < c0).astype(f32)
        self.onto = jnp.exp(last - self.cum) * (index >= last_start).astype(f32)
        self.decay = jnp.exp(last) * (last_start < c0).astype(f32)
        self.low_half = iota((1, LANES), 1) < HD

    def pair(self, table, i):
        return jnp.where(self.low_half, table[:, 2 * i : 2 * i + 1], table[:, 2 * i + 1 : 2 * i + 2])

    def spread(self, h):
        return jnp.exp(jnp.minimum(self.cum[:, h : h + 1] - self.cum_t[h : h + 1, :], 0.0))


def mixer_forward_kernel(
    place_ref, lengths_ref, zx, before, sd, sd_before, wide, narrow, rates, gated, states, state
):
    rows = zx.shape[0]
    c0 = pl.program_id(0) * rows
    ends = ends_of(lengths_ref)

    @pl.when(pl.program_id(0) == 0)
    def _():
        state[...] = jnp.zeros_like(state)

    v = Chunk(c0, ends, zx, before, sd, sd_before, wide, narrow, rates)
    state_low = state[...].astype(bf16)
    states[...] = state_low
    for i in range(v.width // LANES):
        cols = slice(i * LANES, (i + 1) * LANES)
        xc = v.xc[:, cols]
        xs = v.pair(v.step, i) * xc
        xs_low = xs.astype(bf16)
        first = (v.spread(2 * i) * v.inner).astype(bf16)
        second = (v.spread(2 * i + 1) * v.inner).astype(bf16)
        y = jnp.where(v.low_half, mm(first, xs_low), mm(second, xs_low))
        y = y + v.pair(v.into, i) * mm(v.c_low, state_low[:, cols])
        y = y + wide[4:5, cols] * xc
        z = v.z[:, cols]
        gated[:, cols] = (y * z * jax.nn.sigmoid(z)).astype(bf16)
        state[:, cols] = v.pair(v.decay, i) * state[:, cols] + mm_tn(
            v.b_low, (v.pair(v.onto, i) * xs).astype(bf16)
        )


def split_sum(values, ones):
    high = values.astype(bf16)
    low = (values - high.astype(f32)).astype(bf16)
    return mm(high, ones) + mm(low, ones)


def mixer_backward_kernel(
    chunks,
    place_ref,
    lengths_ref,
    zx,
    before,
    sd,
    sd_before,
    grad_scaled,
    stats,
    states,
    wide,
    narrow,
    rates,
    grad_zx,
    grad_sd,
    grad_wide,
    grad_narrow,
    grad_rates,
    grad_state,
    next_pre,
    next_pre_s,
    carry,
    products,
    directs,
    grad_pre,
):
    rows = zx.shape[0]
    turn = pl.program_id(0)
    c0 = (chunks - 1 - turn) * rows
    ends = ends_of(lengths_ref)

    @pl.when(turn == 0)
    def _():
        for ref in (grad_state, next_pre, next_pre_s, carry, grad_wide, grad_narrow, grad_rates):
            ref[...] = jnp.zeros_like(ref)

    v = Chunk(c0, ends, zx, before, sd, sd_before, wide, narrow, rates)
    width = v.width
    root, pull = stats[:, 0:1], stats[:, 1:2]
    grad_inner = jnp.zeros((rows, rows), f32)
    grad_b = jnp.zeros((rows, HD), f32)
    grad_c = jnp.zeros((rows, HD), f32)
    for i in range(width // LANES):
        cols = slice(i * LANES, (i + 1) * LANES)
        xc = v.xc[:, cols]
        step = v.pair(v.step, i)
        xs = step * xc
        xs_low = xs.astype(bf16)
        spread_a, spread_b = v.spread(2 * i), v.spread(2 * i + 1)
        first = (spread_a * v.inner).astype(bf16)
        second = (spread_b * v.inner).astype(bf16)
        state_low = states[:, cols]
        into, onto = v.pair(v.into, i), v.pair(v.onto, i)
        y = jnp.where(v.low_half, mm(first, xs_low), mm(second, xs_low))
        y = y + into * mm(v.c_low, state_low)
        skip, gain = wide[4:5, cols], wide[5:6, cols]
        whole = y + skip * xc
        z = v.z[:, cols]
        gate = jax.nn.sigmoid(z)
        gated = whole * z * gate
        incoming = grad_scaled[:, cols].astype(f32)
        rooted = incoming * root
        grad_wide[5:6, cols] += jnp.sum(rooted * gated, axis=0, keepdims=True)
        grad_gated = rooted * gain - gated * pull
        grad_y = grad_gated * z * gate
        grad_zx[:, cols] = (grad_gated * whole * silu_grad(z, gate)).astype(bf16)
        grad_wide[4:5, cols] += jnp.sum(grad_y * xc, axis=0, keepdims=True)
        low = grad_y.astype(bf16)
        low_a = jnp.where(v.low_half, grad_y, 0.0).astype(bf16)
        low_b = jnp.where(v.low_half, 0.0, grad_y).astype(bf16)
        grad_inner = grad_inner + spread_a * mm_nt(low_a, xs_low) + spread_b * mm_nt(low_b, xs_low)
        grad_end = grad_state[:, cols]
        grad_end_low = grad_end.astype(bf16)
        grad_xs = jnp.where(v.low_half, mm_tn(first, low), mm_tn(second, low))
        grad_xs = grad_xs + onto * mm(v.b_low, grad_end_low)
        into_y = (into * grad_y).astype(bf16)
        onto_x = (onto * xs).astype(bf16)
        grad_b = grad_b + mm_nt(onto_x, grad_end_low)
        grad_c = grad_c + mm_nt(into_y, state_low)
        grad_state[:, cols] = v.pair(v.decay, i) * grad_end + mm_tn(v.c_low, into_y)
        products[:, cols] = low.astype(f32) * y - xs_low.astype(f32) * grad_xs
        directs[:, cols] = xc * grad_xs
        grad_xc = step * grad_xs + skip * grad_y
        grad_pre[:, cols] = grad_xc * silu_grad(v.pre[:, cols], v.gate_x[:, cols])
    grad_inner = jnp.where(v.allowed, grad_inner, 0.0).astype(bf16)
    grad_b = grad_b + mm_tn(grad_inner, v.c_low)
    grad_c = grad_c + mm(grad_inner, v.b_low)

    lane, head = iota((width, LANES), 0), iota((width, LANES), 1)
    ones = ((lane >= head * HD) & (lane < head * HD + HD)).astype(bf16)
    grad_cum = split_sum(products[...], ones)
    direct = split_sum(directs[...], ones)
    row, col = iota((rows, rows), 0), iota((rows, rows), 1)
    col_start = starts_of(c0 + iota((1, rows), 1), ends)
    above = ((col >= row) & (col_start <= c0 + row)).astype(f32)
    next_start = starts_of(c0 + rows, ends)
    reaches = (v.index >= next_start).astype(f32)
    after = jnp.dot(above, grad_cum, precision=HIGHEST, preferred_element_type=f32) + reaches * carry[0:1, :]
    flux = jnp.sum(grad_state[...] * states[...].astype(f32), axis=0, keepdims=True)
    carry[...] = split_sum(jnp.broadcast_to(flux, (8, width)), ones)
    grad_log = -v.step * v.rate * after
    grad_raw = (direct - v.rate * after) * jax.nn.sigmoid(v.raw)
    grad_rates[0:1, :] += jnp.sum(grad_raw, axis=0, keepdims=True)
    grad_rates[1:2, :] += jnp.sum(grad_log, axis=0, keepdims=True)

    index_ext = c0 + iota((rows + 8, 1), 0)
    position_ext = index_ext - starts_of(index_ext, ends)
    taps_back(v.x_ext, grad_pre[...], v.position, grad_wide)
    extended = jnp.concatenate([grad_pre[...], next_pre[...]], axis=0)
    grad_zx[:, width:] = conv_back(extended, wide, position_ext).astype(bf16)
    next_pre[...] = grad_pre[0:8, :]

    blank = jnp.zeros((rows, LANES - HD), f32)
    grad_sc = jnp.concatenate([grad_b, blank, grad_c, blank], axis=1)
    grad_pre_s = grad_sc * silu_grad(v.pre_s, v.gate_s)
    taps_back(v.s_ext, grad_pre_s, v.position, grad_narrow)
    extended_s = jnp.concatenate([grad_pre_s, next_pre_s[...]], axis=0)
    grad_sd[:, : 2 * LANES] = conv_back(extended_s, narrow, position_ext).astype(bf16)
    next_pre_s[...] = grad_pre_s[0:8, :]
    grad_sd[:, 2 * LANES :] = grad_raw.astype(bf16)


def mixer_specs(tp, rows, width, order):
    share = rows // tp
    per_share = share // CHUNK

    def here(place, c):
        owner = lax.div(c, per_share)
        piece = lax.rem(place[0] - owner + tp, tp)
        return piece * per_share + lax.rem(c, per_share)

    def chunk_map(i, place, lengths):
        return (here(place, order(i)), 0)

    def before_map(unit, column):
        def index(i, place, lengths):
            c = order(i)
            previous = jnp.maximum(c - 1, 0)
            return (here(place, previous) * (CHUNK // unit) + CHUNK // unit - 1, column)

        return index

    def fixed(i, place, lengths):
        return (0, 0)

    return chunk_map, before_map, fixed


def mixer_forward(place, lengths, tp, zx, sd, wide, narrow, rates):
    rows, width = zx.shape[0], zx.shape[1] // 2
    chunks = rows // CHUNK
    chunk_map, before_map, fixed = mixer_specs(tp, rows, width, lambda i: i)
    work = rows * width * CHUNK
    return pl.pallas_call(
        mixer_forward_kernel,
        out_shape=[
            jax.ShapeDtypeStruct((rows, width), bf16),
            jax.ShapeDtypeStruct((chunks, HD, width), bf16),
        ],
        grid_spec=pltpu.PrefetchScalarGridSpec(
            num_scalar_prefetch=2,
            grid=(chunks,),
            in_specs=[
                pl.BlockSpec((CHUNK, 2 * width), chunk_map),
                pl.BlockSpec((16, width), before_map(16, 1)),
                pl.BlockSpec((CHUNK, 3 * LANES), chunk_map),
                pl.BlockSpec((8, 3 * LANES), before_map(8, 0)),
                pl.BlockSpec((8, width), fixed),
                pl.BlockSpec((8, 2 * LANES), fixed),
                pl.BlockSpec((8, LANES), fixed),
            ],
            out_specs=[
                pl.BlockSpec((CHUNK, width), chunk_map),
                pl.BlockSpec((None, HD, width), lambda i, *_: (i, 0, 0)),
            ],
            scratch_shapes=[pltpu.VMEM((HD, width), f32)],
        ),
        compiler_params=pltpu.CompilerParams(vmem_limit_bytes=VMEM_LIMIT),
        cost_estimate=pl.CostEstimate(
            flops=8 * work, bytes_accessed=8 * rows * width, transcendentals=4 * rows * width
        ),
        name="mixer_forward",
    )(place, lengths, zx, zx, sd, sd, wide, narrow, rates)


def mixer_backward(place, lengths, tp, zx, sd, grad_scaled, stats, states, wide, narrow, rates):
    rows, width = zx.shape[0], zx.shape[1] // 2
    chunks = rows // CHUNK
    chunk_map, before_map, fixed = mixer_specs(tp, rows, width, lambda i: chunks - 1 - i)
    work = rows * width * CHUNK
    return pl.pallas_call(
        functools.partial(mixer_backward_kernel, chunks),
        out_shape=[
            jax.ShapeDtypeStruct((rows, 2 * width), bf16),
            jax.ShapeDtypeStruct((rows, 3 * LANES), bf16),
            jax.ShapeDtypeStruct((8, width), f32),
            jax.ShapeDtypeStruct((8, 2 * LANES), f32),
            jax.ShapeDtypeStruct((8, LANES), f32),
        ],
        grid_spec=pltpu.PrefetchScalarGridSpec(
            num_scalar_prefetch=2,
            grid=(chunks,),
            in_specs=[
                pl.BlockSpec((CHUNK, 2 * width), chunk_map),
                pl.BlockSpec((16, width), before_map(16, 1)),
                pl.BlockSpec((CHUNK, 3 * LANES), chunk_map),
                pl.BlockSpec((8, 3 * LANES), before_map(8, 0)),
                pl.BlockSpec((CHUNK, width), chunk_map),
                pl.BlockSpec((CHUNK, 2), chunk_map),
                pl.BlockSpec((None, HD, width), lambda i, *_: (chunks - 1 - i, 0, 0)),
                pl.BlockSpec((8, width), fixed),
                pl.BlockSpec((8, 2 * LANES), fixed),
                pl.BlockSpec((8, LANES), fixed),
            ],
            out_specs=[
                pl.BlockSpec((CHUNK, 2 * width), chunk_map),
                pl.BlockSpec((CHUNK, 3 * LANES), chunk_map),
                pl.BlockSpec((8, width), fixed),
                pl.BlockSpec((8, 2 * LANES), fixed),
                pl.BlockSpec((8, LANES), fixed),
            ],
            scratch_shapes=[
                pltpu.VMEM((HD, width), f32),
                pltpu.VMEM((8, width), f32),
                pltpu.VMEM((8, 2 * LANES), f32),
                pltpu.VMEM((8, LANES), f32),
                pltpu.VMEM((CHUNK, width), f32),
                pltpu.VMEM((CHUNK, width), f32),
                pltpu.VMEM((CHUNK, width), f32),
            ],
        ),
        compiler_params=pltpu.CompilerParams(vmem_limit_bytes=VMEM_LIMIT),
        cost_estimate=pl.CostEstimate(
            flops=24 * work, bytes_accessed=12 * rows * width, transcendentals=5 * rows * width
        ),
        name="mixer_backward",
    )(place, lengths, zx, zx, sd, sd, grad_scaled, stats, states, wide, narrow, rates)


def ring_gather(own):
    tp = lax.axis_size("tp")
    pairs = [(i, (i + 1) % tp) for i in range(tp)]
    pieces = [own]
    for _ in range(tp - 1):
        pieces.append(lax.ppermute(pieces[-1], "tp", pairs))
    return pieces


def ring_scatter(part):
    tp = lax.axis_size("tp")
    pairs = [(i, (i + 1) % tp) for i in range(tp)]
    total = part(1 % tp)
    for p in range(2, tp + 1):
        moved = lax.ppermute(total.astype(bf16), "tp", pairs)
        total = moved.astype(f32) + part(p % tp)
    return total


def inverse_root(values):
    return lax.rsqrt(jnp.mean(values * values, axis=1, keepdims=True) + norm_eps)


def rms_backward(values, inv_root, gain, grad_out):
    unit_rows = values * inv_root
    grad_gain = jnp.sum(grad_out * unit_rows, axis=0)
    grad_unit = grad_out * gain
    grad_values = inv_root * (
        grad_unit - unit_rows * jnp.mean(grad_unit * unit_rows, axis=-1, keepdims=True)
    )
    return (grad_values, grad_gain)


def gather(values, axis=0):
    return lax.all_gather(values, "fsdp", axis=axis, tiled=True)


def scatter(values, axis=0):
    return lax.psum_scatter(values, "fsdp", scatter_dimension=axis, tiled=True)


def local(
    hidden,
    embed,
    lengths,
    attention_norm_gain,
    query_key_value_weight,
    attention_adapter_down,
    attention_adapter_up,
    attention_output_weight,
    feedforward_norm_gain,
    gate_up_weight,
    feedforward_adapter_down,
    feedforward_adapter_up,
    down_weight,
    mixer_norm_gain,
    gate_inner_weight,
    state_input_weight,
    step_projection,
    inner_conv_taps,
    state_conv_taps,
    head_step_bias,
    decay_log_rate,
    inner_skip_gains,
    gated_norm_gain,
    mixer_output_weight,
    output_cotangent,
):
    tp = lax.axis_size("tp")
    fsdp = lax.axis_size("fsdp")
    share, width = hidden.shape
    rows = share * tp
    here = lax.axis_index("tp").astype(jnp.int32)
    place = here.reshape(1)
    lengths = lengths.reshape(-1)
    rank = attention_adapter_down.shape[2]
    head_cols = query_key_value_weight.shape[2]
    units_here = gate_up_weight.shape[2]
    inner_cols = gate_inner_weight.shape[2]
    mixer_heads = inner_cols // HD
    states = state_input_weight.shape[2]
    count = inner_conv_taps.shape[0]
    inner_total = inner_cols * tp

    small = [
        attention_norm_gain,
        feedforward_norm_gain,
        mixer_norm_gain,
        inner_conv_taps.reshape(-1),
        state_conv_taps.reshape(-1),
        inner_skip_gains.reshape(-1),
        gated_norm_gain.reshape(-1),
    ]
    sizes = [v.shape[0] for v in small]
    padding = -sum(sizes) % LANES
    packed = jnp.concatenate(small + [jnp.zeros((padding,), bf16)]).reshape(1, -1)
    spread = gather(packed).astype(f32)
    cuts = [sum(sizes[:i]) for i in range(len(sizes) + 1)]
    parts = [spread[:, cuts[i] : cuts[i + 1]] for i in range(len(sizes))]
    gain_attn, gain_mlp, gain_mixer = (parts[i].reshape(1, -1) for i in range(3))
    taps_x = parts[3].reshape(fsdp, count, mixer_heads, -1)
    taps_x = jnp.transpose(taps_x, (1, 2, 0, 3)).reshape(count, inner_cols)
    taps_s = parts[4].reshape(fsdp, count, 2, -1)
    taps_s = jnp.transpose(taps_s, (1, 2, 0, 3)).reshape(count, 2, states)
    skip = jnp.transpose(parts[5].reshape(fsdp, mixer_heads, -1), (1, 0, 2)).reshape(1, inner_cols)
    gain_gate = jnp.transpose(parts[6].reshape(fsdp, mixer_heads, -1), (1, 0, 2)).reshape(1, inner_cols)
    wide = jnp.concatenate([taps_x, skip, gain_gate, jnp.zeros((2, inner_cols), f32)], axis=0)
    narrow = jnp.pad(taps_s, ((0, 8 - count), (0, 0), (0, LANES - states))).reshape(8, 2 * LANES)
    rates = jnp.pad(
        jnp.stack([head_step_bias, decay_log_rate]), ((0, 6), (0, LANES - mixer_heads))
    )

    weights_qkv = [gather(query_key_value_weight[:, j, :]) for j in range(3)]
    adapter_down = gather(attention_adapter_down.reshape(-1, 3 * rank))
    ups = jnp.concatenate(
        [attention_adapter_up.reshape(-1, 3 * head_cols), feedforward_adapter_up.reshape(-1, 2 * units_here)],
        axis=1,
    )
    ups = gather(ups)
    adapter_up = [ups[:, j * head_cols : (j + 1) * head_cols] for j in range(3)]
    fc_up = ups[:, 3 * head_cols :]
    weight_o = gather(attention_output_weight, 1)
    lanes_s = jnp.pad(state_input_weight, ((0, 0), (0, 0), (0, LANES - states))).reshape(-1, 2 * LANES)
    lanes_t = jnp.pad(step_projection, ((0, 0), (0, LANES - mixer_heads)))
    downs = gather(jnp.concatenate([lanes_s, lanes_t, feedforward_adapter_down], axis=1))
    weight_sd, fc_down = downs[:, : 3 * LANES], downs[:, 3 * LANES :]
    weight_fc1 = gather(gate_up_weight.reshape(-1, 2 * units_here))
    weight_fc2 = gather(down_weight, 1)
    weight_zx = gather(gate_inner_weight.reshape(-1, 2 * inner_cols))
    weight_out = gather(mixer_output_weight, 1)

    places = jnp.arange(rows, dtype=jnp.int32)
    ends = [jnp.sum(lengths[: i + 1]) for i in range(lengths.shape[0] - 1)]
    position = places - starts_of(places, ends)
    freqs = jnp.exp(jnp.arange(HDA // 2, dtype=f32) * (-2.0 * math.log(10000.0) / HDA))
    angles = position.astype(f32)[:, None] * freqs[None, :]
    cosine = jnp.cos(angles)
    sine = jnp.sin(angles)
    cosine = jnp.concatenate([cosine, cosine], axis=1)
    sine = jnp.concatenate([-sine, sine], axis=1)

    joined = jnp.concatenate([hidden.astype(f32), embed.astype(f32)], axis=1)
    attn_root = inverse_root(joined)
    normed = ring_gather((joined * attn_root * gain_attn).astype(bf16))
    lora_mid = [mm(piece, adapter_down).astype(bf16) for piece in normed]

    def project(p, j):
        middle = lora_mid[p][:, j * rank : (j + 1) * rank]
        return mm(normed[p], weights_qkv[j]) + mm(middle, adapter_up[j])

    projected = [[project(p, j) for j in range(3)] for p in range(tp)]
    attended, queries, keys, values = attention_forward(place, lengths, projected, cosine, sine)

    def piece(values, p):
        return values[p * share : (p + 1) * share]

    mixed = ring_scatter(lambda p: mm(piece(attended, p), weight_o))

    mlp_root = inverse_root(mixed)
    mlp_in = ring_gather((mixed * mlp_root * gain_mlp).astype(bf16))
    fc_mid = [mm(v, fc_down).astype(bf16) for v in mlp_in]
    gate_up = [(mm(mlp_in[p], weight_fc1) + mm(fc_mid[p], fc_up)).astype(bf16) for p in range(tp)]

    def unit_rows(p):
        gate = gate_up[p][:, :units_here].astype(f32)
        up = gate_up[p][:, units_here:].astype(f32)
        return (jax.nn.gelu(gate) * up).astype(bf16)

    units = [unit_rows(p) for p in range(tp)]
    branch = ring_scatter(lambda p: mm(units[p], weight_fc2))
    residual = hidden.astype(f32) + mixed + branch

    mixer_root = inverse_root(residual)
    mixer_in = ring_gather((residual * mixer_root * gain_mixer).astype(bf16))
    out_grad = ring_gather(output_cotangent)
    mixer_rows = jnp.concatenate(mixer_in, axis=0)
    zx = jnp.concatenate([mm(v, weight_zx).astype(bf16) for v in mixer_in], axis=0)
    sd = mm(mixer_rows, weight_sd)
    gated, chunk_states = mixer_forward(place, lengths, tp, zx, sd, wide, narrow, rates)
    out_grad_rows = jnp.concatenate(out_grad, axis=0)
    grad_scaled = mm_nt(out_grad_rows, weight_out).astype(bf16)
    gated_wide = gated.astype(f32)
    sums = jnp.stack(
        [
            jnp.sum(gated_wide * gated_wide, axis=1),
            jnp.sum(grad_scaled.astype(f32) * gain_gate * gated_wide, axis=1),
        ],
        axis=0,
    )
    sums = jnp.roll(jnp.flip(sums.reshape(2, tp, share), axis=1), here + 1, axis=1)
    sums = lax.psum(sums, "tp")
    sums = jnp.flip(jnp.roll(sums, -(here + 1), axis=1), axis=1).reshape(2, rows)
    gate_root = lax.rsqrt(sums[0] / inner_total + norm_eps)
    stats = jnp.stack([gate_root, gate_root**3 * sums[1] / inner_total], axis=1)
    scaled = (gated_wide * gate_root[:, None] * gain_gate).astype(bf16)
    out = residual + ring_scatter(lambda p: mm(piece(scaled, p), weight_out))
    grad_w_out = scatter(mm_tn(scaled, out_grad_rows).astype(bf16), 1).astype(f32)

    grad_zx, grad_sd, grad_wide, grad_narrow, grad_rates = mixer_backward(
        place, lengths, tp, zx, sd, grad_scaled, stats, chunk_states, wide, narrow, rates
    )
    grad_mixer_in = ring_scatter(
        lambda p: mm_nt(piece(grad_zx, p), weight_zx) + mm_nt(piece(grad_sd, p), weight_sd)
    )
    grad_w_zx = scatter(mm_tn(mixer_rows, grad_zx).astype(bf16)).astype(f32)
    grad_w_sd = mm_tn(mixer_rows, grad_sd)
    grad_resid_norm, grad_gain_mixer = rms_backward(residual, mixer_root, gain_mixer, grad_mixer_in)
    grad_residual = output_cotangent.astype(f32) + grad_resid_norm

    grad_branch = ring_gather(grad_residual.astype(bf16))

    def gate_up_back(p):
        grad_units = mm_nt(grad_branch[p], weight_fc2)
        gate = gate_up[p][:, :units_here].astype(f32)
        up = gate_up[p][:, units_here:].astype(f32)
        raised, back = jax.vjp(jax.nn.gelu, gate)
        return jnp.concatenate(
            [back(grad_units * up)[0].astype(bf16), (grad_units * raised).astype(bf16)], axis=1
        )

    grad_gate_up = [gate_up_back(p) for p in range(tp)]
    grad_fc_mid = [mm_nt(v, fc_up).astype(bf16) for v in grad_gate_up]
    grad_mlp_in = ring_scatter(
        lambda p: mm_nt(grad_gate_up[p], weight_fc1) + mm_nt(grad_fc_mid[p], fc_down)
    )
    mlp_rows = jnp.concatenate(mlp_in, axis=0)
    grad_gate_up_rows = jnp.concatenate(grad_gate_up, axis=0)
    grad_w_fc2 = scatter(
        mm_tn(jnp.concatenate(units, axis=0), jnp.concatenate(grad_branch, axis=0)).astype(bf16), 1
    ).astype(f32)
    grad_w_fc1 = scatter(mm_tn(mlp_rows, grad_gate_up_rows).astype(bf16)).astype(f32)
    grad_fc_up = mm_tn(jnp.concatenate(fc_mid, axis=0), grad_gate_up_rows)
    grad_fc_down = mm_tn(mlp_rows, jnp.concatenate(grad_fc_mid, axis=0))
    grad_mixed_norm, grad_gain_mlp = rms_backward(mixed, mlp_root, gain_mlp, grad_mlp_in)

    grad_mixed = ring_gather((grad_residual + grad_mixed_norm).astype(bf16))
    grad_attended = [mm_nt(v, weight_o).astype(bf16) for v in grad_mixed]
    grad_w_o = scatter(mm_tn(attended, jnp.concatenate(grad_mixed, axis=0)).astype(bf16), 1).astype(f32)
    grad_projected = attention_backward(
        place, lengths, queries, keys, values, grad_attended, cosine, sine
    )
    normed_rows = jnp.concatenate(normed, axis=0)
    lora_rows = jnp.concatenate(lora_mid, axis=0)
    grad_lora = jnp.concatenate(
        [mm_nt(grad_projected[j], adapter_up[j]).astype(bf16) for j in range(3)], axis=1
    )

    def normed_back(p):
        total = mm_nt(piece(grad_lora, p), adapter_down)
        for j in range(3):
            total = total + mm_nt(piece(grad_projected[j], p), weights_qkv[j])
        return total

    grad_normed = ring_scatter(normed_back)
    grad_w_qkv = [
        scatter(mm_tn(normed_rows, grad_projected[j]).astype(bf16)).astype(f32) for j in range(3)
    ]
    grad_up = [
        mm_tn(lora_rows[:, j * rank : (j + 1) * rank], grad_projected[j]) for j in range(3)
    ]
    grad_down = scatter(mm_tn(normed_rows, grad_lora).astype(bf16))
    grad_down = lax.psum_scatter(grad_down, "tp", scatter_dimension=0, tiled=True).astype(f32)
    grad_joined, grad_gain_attn = rms_backward(joined, attn_root, gain_attn, grad_normed)
    grad_hidden = grad_residual + grad_joined[:, :width]
    grad_embed = grad_joined[:, width:]

    grad_ups = scatter(jnp.concatenate(grad_up + [grad_fc_up], axis=1).astype(bf16)).astype(f32)
    grad_downs = scatter(jnp.concatenate([grad_w_sd, grad_fc_down], axis=1).astype(bf16)).astype(f32)
    grad_w_dt = grad_downs[:, 2 * LANES : 2 * LANES + mixer_heads]
    shared = jnp.concatenate([grad_downs[:, : 2 * LANES], grad_downs[:, 3 * LANES :]], axis=1)

    def by_fsdp(values):
        lead = values.shape[:-1]
        cut = values.reshape(lead + (fsdp, values.shape[-1] // fsdp))
        return jnp.moveaxis(cut, -2, 0).reshape(fsdp, -1)

    grad_taps_x = grad_wide[:count].reshape(count, mixer_heads, HD)
    grad_taps_s = grad_narrow[:count].reshape(count, 2, LANES)[:, :, :states]
    local_small = [
        by_fsdp(grad_taps_x),
        by_fsdp(grad_wide[4].reshape(mixer_heads, HD)),
        by_fsdp(grad_wide[5].reshape(mixer_heads, HD)),
        jnp.broadcast_to(grad_rates[:2, :mixer_heads].reshape(1, -1), (fsdp, 2 * mixer_heads)),
    ]
    shared_small = [by_fsdp(grad_taps_s), by_fsdp(grad_gain_mixer), by_fsdp(grad_gain_mlp)]
    small_sizes = [v.shape[1] for v in local_small + shared_small]
    small_cuts = [sum(small_sizes[:i]) for i in range(len(small_sizes) + 1)]
    small_sum = lax.psum_scatter(
        jnp.concatenate(local_small + shared_small, axis=1), "fsdp", scatter_dimension=0, tiled=True
    ).reshape(-1)
    small_parts = [small_sum[small_cuts[i] : small_cuts[i + 1]] for i in range(len(small_sizes))]
    shared, tail = lax.psum((shared, small_sum[small_cuts[4] :]), "tp")
    tail_cuts = [v - small_cuts[4] for v in small_cuts[4:]]
    grad_conv_bc, sum_gain_mixer, sum_gain_mlp = (
        tail[tail_cuts[i] : tail_cuts[i + 1]] for i in range(3)
    )
    grad_gain_attn = lax.psum_scatter(grad_gain_attn, ("fsdp", "tp"), scatter_dimension=0, tiled=True)
    sum_rates = small_parts[3].reshape(2, mixer_heads)
    return (
        out,
        grad_hidden,
        grad_embed,
        grad_gain_attn,
        jnp.stack(grad_w_qkv, axis=1),
        grad_down.reshape(-1, 3, rank),
        grad_ups[:, : 3 * head_cols].reshape(-1, 3, head_cols),
        grad_w_o,
        sum_gain_mlp,
        grad_w_fc1.reshape(-1, 2, units_here),
        shared[:, 2 * LANES :],
        grad_ups[:, 3 * head_cols :].reshape(-1, 2, units_here),
        grad_w_fc2,
        sum_gain_mixer,
        grad_w_zx.reshape(-1, 2, inner_cols),
        shared[:, : 2 * LANES].reshape(-1, 2, LANES)[:, :, :states],
        grad_w_dt,
        small_parts[0].reshape(count, mixer_heads, -1),
        grad_conv_bc.reshape(count, 2, -1),
        sum_rates[0],
        sum_rates[1],
        small_parts[1].reshape(mixer_heads, -1),
        small_parts[2].reshape(mixer_heads, -1),
        grad_w_out,
    )


def solution(mesh):
    placed = (
        P(("fsdp", "tp"), None),
        P(("fsdp", "tp"), None),
        P("fsdp", None),
        P("fsdp"),
        P("fsdp", None, "tp"),
        P("fsdp", None, None),
        P("fsdp", None, "tp"),
        P("tp", "fsdp"),
        P("fsdp"),
        P("fsdp", None, "tp"),
        P("fsdp", None),
        P("fsdp", None, "tp"),
        P("tp", "fsdp"),
        P("fsdp"),
        P("fsdp", None, "tp"),
        P("fsdp", None, None),
        P("fsdp", "tp"),
        P(None, "tp", "fsdp"),
        P(None, None, "fsdp"),
        P("tp"),
        P("tp"),
        P("tp", "fsdp"),
        P("tp", "fsdp"),
        P("tp", "fsdp"),
        P(("fsdp", "tp"), None),
    )
    return jax.shard_map(
        local,
        mesh=mesh,
        in_specs=placed,
        out_specs=(
            P(("fsdp", "tp"), None),
            P(("fsdp", "tp"), None),
            P(("fsdp", "tp"), None),
            P(("fsdp", "tp")),
            P("fsdp", None, "tp"),
            P(("fsdp", "tp"), None, None),
            P("fsdp", None, "tp"),
            P("tp", "fsdp"),
            P("fsdp"),
            P("fsdp", None, "tp"),
            P("fsdp", None),
            P("fsdp", None, "tp"),
            P("tp", "fsdp"),
            P("fsdp"),
            P("fsdp", None, "tp"),
            P("fsdp", None, None),
            P("fsdp", "tp"),
            P(None, "tp", "fsdp"),
            P(None, None, "fsdp"),
            P("tp"),
            P("tp"),
            P("tp", "fsdp"),
            P("tp", "fsdp"),
            P("tp", "fsdp"),
        ),
        check_vma=False,
    )
```

```python
import functools
import math

import jax
import jax.numpy as jnp
from jax import lax
from jax.experimental import pallas as pl
from jax.experimental.pallas import tpu as pltpu
from jax.sharding import PartitionSpec as P

HDA = 128
HD = 64
LANES = 128
CHUNK = 128

norm_eps = 1e-05
f32 = jnp.float32
bf16 = jnp.bfloat16
HIGHEST = lax.Precision.HIGHEST
VMEM_LIMIT = 56 * 1024 * 1024


def mm(left, right):
    return jnp.dot(left, right, preferred_element_type=f32)


def mm_nt(left, right):
    return lax.dot_general(left, right, (((1,), (1,)), ((), ())), preferred_element_type=f32)


def mm_tn(left, right):
    return lax.dot_general(left, right, (((0,), (0,)), ((), ())), preferred_element_type=f32)


def starts_of(index, ends):
    start = jnp.zeros_like(index)
    for end in ends:
        start = jnp.where(index >= end, end, start)
    return start


def ends_of(lengths_ref):
    ends = []
    end = jnp.int32(0)
    for i in range(lengths_ref.shape[0] - 1):
        end = end + lengths_ref[i]
        ends.append(end)
    return ends


def iota(shape, axis):
    return lax.broadcasted_iota(jnp.int32, shape, axis)


def attention_forward_kernel(
    tp,
    place_ref,
    lengths_ref,
    cosine_ref,
    sine_ref,
    q_up,
    k_up,
    v_up,
    *refs,
):
    pieces = refs[: 4 * tp]
    attended_ref, q_ref, k_ref, v_ref, held = refs[4 * tp :]
    rows = q_ref.shape[0]
    share = rows // tp
    rank = q_up.shape[0]
    here = place_ref[0]
    ends = ends_of(lengths_ref)
    for p in range(tp):
        owner = lax.rem(here - p + tp, tp)
        part = pl.ds(pl.multiple_of(owner * share, share), share)
        cosine, sine = cosine_ref[part, :], sine_ref[part, :]
        middle = pieces[4 * p + 3]
        for j, (up, target) in enumerate(((q_up, q_ref), (k_up, k_ref), (v_up, v_ref))):
            low = middle[:, j * rank : (j + 1) * rank].astype(bf16)
            value = pieces[4 * p + j][...] + mm(low, up[...])
            if j < 2:
                value = value * cosine + pltpu.roll(value, HDA // 2, 1) * sine
            target[part, :] = value.astype(bf16)
    block = min(256, rows)
    scale = HDA ** (-0.5)
    for at in range(0, rows, block):
        upto = at + block
        scores = mm_nt(q_ref[at:upto, :], k_ref[:upto, :]) * scale
        query = at + iota((block, 1), 0)
        key = iota((1, upto), 1)
        seen = (key <= query) & (key >= starts_of(query, ends))
        scores = jnp.where(seen, scores, -1e30)
        raised = jnp.exp(scores - jnp.max(scores, axis=1, keepdims=True))
        probs = (raised * (1.0 / jnp.sum(raised, axis=1, keepdims=True))).astype(bf16)
        held[at:upto, :] = mm(probs, v_ref[:upto, :]).astype(bf16)
    for p in range(tp):
        owner = lax.rem(here - p + tp, tp)
        part = pl.ds(pl.multiple_of(owner * share, share), share)
        attended_ref[p * share : (p + 1) * share, :] = held[part, :]


def attention_forward(place, lengths, projected, ups, columns, cosine, sine):
    tp = len(projected)
    share = projected[0].shape[0]
    rows = share * tp
    heads = columns // HDA
    rank = ups.shape[0]
    table_spec = pl.BlockSpec((rows, HDA), lambda h, *_: (0, 0))

    def head_spec(j, height=rows):
        return pl.BlockSpec((height, HDA), lambda h, *_: (0, j * heads + h))

    work = heads * rows * rows * HDA
    return pl.pallas_call(
        functools.partial(attention_forward_kernel, tp),
        out_shape=[jax.ShapeDtypeStruct((rows, columns), bf16)] * 4,
        grid_spec=pltpu.PrefetchScalarGridSpec(
            num_scalar_prefetch=2,
            grid=(heads,),
            in_specs=[table_spec, table_spec]
            + [head_spec(j, rank) for j in range(3)]
            + (
                [head_spec(j, share) for j in range(3)]
                + [pl.BlockSpec((share, 3 * rank), lambda h, *_: (0, columns // rank))]
            )
            * tp,
            out_specs=[head_spec(0)] * 4,
            scratch_shapes=[pltpu.VMEM((rows, HDA), bf16)],
        ),
        compiler_params=pltpu.CompilerParams(vmem_limit_bytes=VMEM_LIMIT),
        cost_estimate=pl.CostEstimate(
            flops=4 * work, bytes_accessed=20 * rows * columns, transcendentals=heads * rows * rows
        ),
        name="attention_forward",
    )(place, lengths, cosine, sine, ups, ups, ups, *[v for v in projected for _ in range(4)])


def attention_backward_kernel(
    tp,
    heads,
    place_ref,
    lengths_ref,
    cosine_ref,
    sine_ref,
    q_ref,
    k_ref,
    v_ref,
    q_up,
    k_up,
    v_up,
    *refs,
):
    grad_in = refs[:tp]
    out_ref, held, dq, dk, dv, lora = refs[tp:]
    rows = q_ref.shape[0]
    share = rows // tp
    rank = q_up.shape[0]
    here = place_ref[0]
    head = pl.program_id(0)
    ends = ends_of(lengths_ref)
    for p in range(tp):
        owner = lax.rem(here - p + tp, tp)
        part = pl.ds(pl.multiple_of(owner * share, share), share)
        held[part, :] = grad_in[p][...]
    dk[...] = jnp.zeros_like(dk)
    dv[...] = jnp.zeros_like(dv)

    @pl.when(head == 0)
    def _():
        lora[...] = jnp.zeros_like(lora)

    block = min(256, rows)
    scale = HDA ** (-0.5)
    for at in range(0, rows, block):
        upto = at + block
        query_rows = q_ref[at:upto, :]
        grad_rows = held[at:upto, :]
        scores = mm_nt(k_ref[:upto, :], query_rows) * scale
        query = at + iota((1, block), 1)
        key = iota((upto, 1), 0)
        seen = (key <= query) & (key >= starts_of(query, ends))
        scores = jnp.where(seen, scores, -1e30)
        raised = jnp.exp(scores - jnp.max(scores, axis=0, keepdims=True))
        probs = raised * (1.0 / jnp.sum(raised, axis=0, keepdims=True))
        grad_probs = mm_nt(v_ref[:upto, :], grad_rows)
        cross = jnp.sum(probs * grad_probs, axis=0, keepdims=True)
        grad_scores = (probs * (grad_probs - cross)).astype(bf16)
        dv[:upto, :] += mm(probs.astype(bf16), grad_rows)
        dk[:upto, :] += mm(grad_scores, query_rows)
        dq[at:upto, :] = mm_tn(grad_scores, k_ref[:upto, :])
    for p in range(tp):
        owner = lax.rem(here - p + tp, tp)
        part = pl.ds(pl.multiple_of(owner * share, share), share)
        cosine, sine = cosine_ref[part, :], sine_ref[part, :]
        mine = slice(p * share, (p + 1) * share)
        for j, (source, up) in enumerate(((dq, q_up), (dk, k_up), (dv, v_up))):
            value = source[part, :]
            if j < 2:
                value = value * scale
                value = value * cosine - pltpu.roll(value, HDA // 2, 1) * sine
            low = value.astype(bf16)
            at = pl.multiple_of((j * heads + head) * HDA, HDA)
            out_ref[mine, pl.ds(at, HDA)] = low
            lora[mine, j * rank : (j + 1) * rank] += mm_nt(low, up[...])

    @pl.when(head == heads - 1)
    def _():
        out_ref[:, 3 * heads * HDA :] = lora[...].astype(bf16)


def attention_backward(place, lengths, queries, keys, values, ups, pieces, cosine, sine):
    tp = len(pieces)
    share, columns = pieces[0].shape
    rows = share * tp
    heads = columns // HDA
    rank = ups.shape[0]
    piece_spec = pl.BlockSpec((share, HDA), lambda h, *_: (0, h))
    table_spec = pl.BlockSpec((rows, HDA), lambda h, *_: (0, 0))
    head_spec = pl.BlockSpec((rows, HDA), lambda h, *_: (0, h))

    def up_spec(j):
        return pl.BlockSpec((rank, HDA), lambda h, *_: (0, j * heads + h))

    total = 3 * columns + 3 * rank
    work = heads * rows * rows * HDA
    return pl.pallas_call(
        functools.partial(attention_backward_kernel, tp, heads),
        out_shape=jax.ShapeDtypeStruct((rows, total), bf16),
        grid_spec=pltpu.PrefetchScalarGridSpec(
            num_scalar_prefetch=2,
            grid=(heads,),
            in_specs=[table_spec, table_spec]
            + [head_spec] * 3
            + [up_spec(j) for j in range(3)]
            + [piece_spec] * tp,
            out_specs=pl.BlockSpec((rows, total), lambda h, *_: (0, 0)),
            scratch_shapes=[pltpu.VMEM((rows, HDA), bf16)]
            + [pltpu.VMEM((rows, HDA), f32)] * 3
            + [pltpu.VMEM((rows, 3 * rank), f32)],
        ),
        compiler_params=pltpu.CompilerParams(vmem_limit_bytes=VMEM_LIMIT),
        cost_estimate=pl.CostEstimate(
            flops=10 * work, bytes_accessed=14 * rows * columns, transcendentals=heads * rows * rows
        ),
        name="attention_backward",
    )(place, lengths, cosine, sine, queries, keys, values, ups, ups, ups, *pieces)


def conv_rows(extended, taps, position):
    count = 4
    rows = extended.shape[0] - 8
    total = None
    for k in range(count):
        moved = extended[8 - k : 8 - k + rows, :]
        if k:
            moved = jnp.where(position >= k, moved, 0.0)
        term = taps[count - 1 - k : count - k, :] * moved
        total = term if total is None else total + term
    return total


def conv_back(extended, taps, position):
    count = 4
    rows = extended.shape[0] - 8
    total = None
    for k in range(count):
        kept = jnp.where(position >= k, extended, 0.0) if k else extended
        term = taps[count - 1 - k : count - k, :] * kept[k : k + rows, :]
        total = term if total is None else total + term
    return total


def taps_back(extended, grad, position, target):
    count = 4
    rows = extended.shape[0] - 8
    for k in range(count):
        moved = extended[8 - k : 8 - k + rows, :]
        if k:
            moved = jnp.where(position >= k, moved, 0.0)
        at = count - 1 - k
        target[at : at + 1, :] += jnp.sum(grad * moved, axis=0, keepdims=True)


def silu_grad(value, gate):
    return gate * (1.0 + value * (1.0 - gate))


class Chunk:
    def __init__(self, c0, ends, zx, before, sd, sd_before, wide, narrow, rates):
        rows = zx.shape[0]
        width = zx.shape[1] // 2
        self.rows, self.width = rows, width
        index = c0 + iota((rows, 1), 0)
        start = starts_of(index, ends)
        self.index, self.start = index, start
        self.position = index - start
        last_start = starts_of(c0 + rows - 1, ends)
        self.z = zx[:, :width].astype(f32)
        self.x_ext = jnp.concatenate(
            [before[...].astype(f32)[8:16, :], zx[:, width:].astype(f32)], axis=0
        )
        self.s_ext = jnp.concatenate([sd_before[:, : 2 * LANES], sd[:, : 2 * LANES]], axis=0)
        self.pre = conv_rows(self.x_ext, wide, self.position)
        self.gate_x = jax.nn.sigmoid(self.pre)
        self.xc = self.pre * self.gate_x
        self.pre_s = conv_rows(self.s_ext, narrow, self.position)
        self.gate_s = jax.nn.sigmoid(self.pre_s)
        sc = self.pre_s * self.gate_s
        self.b_low = sc[:, :HD].astype(bf16)
        self.c_low = sc[:, LANES : LANES + HD].astype(bf16)
        self.raw = sd[:, 2 * LANES : 3 * LANES] + rates[0:1, :]
        self.step = jnp.maximum(self.raw, 0.0) + jnp.log1p(jnp.exp(-jnp.abs(self.raw)))
        self.rate = jnp.exp(rates[1:2, :])
        row, col = iota((rows, rows), 0), iota((rows, rows), 1)
        below = (col <= row).astype(f32)
        self.cum = jnp.dot(below, -self.step * self.rate, precision=HIGHEST, preferred_element_type=f32)
        self.cum_t = self.cum.T
        self.allowed = (col <= row) & ((c0 + col) >= start)
        self.inner = jnp.where(self.allowed, mm_nt(self.c_low, self.b_low), 0.0)
        last = self.cum[rows - 1 : rows, :]
        self.into = jnp.exp(self.cum) * (start < c0).astype(f32)
        self.onto = jnp.exp(last - self.cum) * (index >= last_start).astype(f32)
        self.decay = jnp.exp(last) * (last_start < c0).astype(f32)
        self.low_half = iota((1, LANES), 1) < HD

    def pair(self, table, i):
        return jnp.where(self.low_half, table[:, 2 * i : 2 * i + 1], table[:, 2 * i + 1 : 2 * i + 2])

    def spread(self, h):
        return jnp.exp(jnp.minimum(self.cum[:, h : h + 1] - self.cum_t[h : h + 1, :], 0.0))


def mixer_forward_kernel(
    place_ref, lengths_ref, zx, before, sd, sd_before, wide, narrow, rates, gated, states, state
):
    rows = zx.shape[0]
    c0 = pl.program_id(0) * rows
    ends = ends_of(lengths_ref)

    @pl.when(pl.program_id(0) == 0)
    def _():
        state[...] = jnp.zeros_like(state)

    v = Chunk(c0, ends, zx, before, sd, sd_before, wide, narrow, rates)
    state_low = state[...].astype(bf16)
    states[...] = state_low
    for i in range(v.width // LANES):
        cols = slice(i * LANES, (i + 1) * LANES)
        xc = v.xc[:, cols]
        xs = v.pair(v.step, i) * xc
        xs_low = xs.astype(bf16)
        first = (v.spread(2 * i) * v.inner).astype(bf16)
        second = (v.spread(2 * i + 1) * v.inner).astype(bf16)
        y = jnp.where(v.low_half, mm(first, xs_low), mm(second, xs_low))
        y = y + v.pair(v.into, i) * mm(v.c_low, state_low[:, cols])
        y = y + wide[4:5, cols] * xc
        z = v.z[:, cols]
        gated[:, cols] = (y * z * jax.nn.sigmoid(z)).astype(bf16)
        state[:, cols] = v.pair(v.decay, i) * state[:, cols] + mm_tn(
            v.b_low, (v.pair(v.onto, i) * xs).astype(bf16)
        )


def split_sum(values, ones):
    high = values.astype(bf16)
    low = (values - high.astype(f32)).astype(bf16)
    return mm(high, ones) + mm(low, ones)


def mixer_backward_kernel(
    chunks,
    place_ref,
    lengths_ref,
    zx,
    before,
    sd,
    sd_before,
    grad_scaled,
    stats,
    states,
    wide,
    narrow,
    rates,
    grad_all,
    grad_wide,
    grad_narrow,
    grad_rates,
    grad_state,
    next_pre,
    next_pre_s,
    carry,
    products,
    directs,
    grad_pre,
):
    rows = zx.shape[0]
    turn = pl.program_id(0)
    c0 = (chunks - 1 - turn) * rows
    ends = ends_of(lengths_ref)

    @pl.when(turn == 0)
    def _():
        for ref in (grad_state, next_pre, next_pre_s, carry, grad_wide, grad_narrow, grad_rates):
            ref[...] = jnp.zeros_like(ref)

    v = Chunk(c0, ends, zx, before, sd, sd_before, wide, narrow, rates)
    width = v.width
    root, pull = stats[:, 0:1], stats[:, 1:2]
    grad_inner = jnp.zeros((rows, rows), f32)
    grad_b = jnp.zeros((rows, HD), f32)
    grad_c = jnp.zeros((rows, HD), f32)
    for i in range(width // LANES):
        cols = slice(i * LANES, (i + 1) * LANES)
        xc = v.xc[:, cols]
        step = v.pair(v.step, i)
        xs = step * xc
        xs_low = xs.astype(bf16)
        spread_a, spread_b = v.spread(2 * i), v.spread(2 * i + 1)
        first = (spread_a * v.inner).astype(bf16)
        second = (spread_b * v.inner).astype(bf16)
        state_low = states[:, cols]
        into, onto = v.pair(v.into, i), v.pair(v.onto, i)
        y = jnp.where(v.low_half, mm(first, xs_low), mm(second, xs_low))
        y = y + into * mm(v.c_low, state_low)
        skip, gain = wide[4:5, cols], wide[5:6, cols]
        whole = y + skip * xc
        z = v.z[:, cols]
        gate = jax.nn.sigmoid(z)
        gated = whole * z * gate
        incoming = grad_scaled[:, cols].astype(f32)
        rooted = incoming * root
        grad_wide[5:6, cols] += jnp.sum(rooted * gated, axis=0, keepdims=True)
        grad_gated = rooted * gain - gated * pull
        grad_y = grad_gated * z * gate
        grad_all[:, cols] = (grad_gated * whole * silu_grad(z, gate)).astype(bf16)
        grad_wide[4:5, cols] += jnp.sum(grad_y * xc, axis=0, keepdims=True)
        low = grad_y.astype(bf16)
        low_a = jnp.where(v.low_half, grad_y, 0.0).astype(bf16)
        low_b = jnp.where(v.low_half, 0.0, grad_y).astype(bf16)
        grad_inner = grad_inner + spread_a * mm_nt(low_a, xs_low) + spread_b * mm_nt(low_b, xs_low)
        grad_end = grad_state[:, cols]
        grad_end_low = grad_end.astype(bf16)
        grad_xs = jnp.where(v.low_half, mm_tn(first, low), mm_tn(second, low))
        grad_xs = grad_xs + onto * mm(v.b_low, grad_end_low)
        into_y = (into * grad_y).astype(bf16)
        onto_x = (onto * xs).astype(bf16)
        grad_b = grad_b + mm_nt(onto_x, grad_end_low)
        grad_c = grad_c + mm_nt(into_y, state_low)
        grad_state[:, cols] = v.pair(v.decay, i) * grad_end + mm_tn(v.c_low, into_y)
        products[:, cols] = low.astype(f32) * y - xs_low.astype(f32) * grad_xs
        directs[:, cols] = xc * grad_xs
        grad_xc = step * grad_xs + skip * grad_y
        grad_pre[:, cols] = grad_xc * silu_grad(v.pre[:, cols], v.gate_x[:, cols])
    grad_inner = jnp.where(v.allowed, grad_inner, 0.0).astype(bf16)
    grad_b = grad_b + mm_tn(grad_inner, v.c_low)
    grad_c = grad_c + mm(grad_inner, v.b_low)

    lane, head = iota((width, LANES), 0), iota((width, LANES), 1)
    ones = ((lane >= head * HD) & (lane < head * HD + HD)).astype(bf16)
    grad_cum = split_sum(products[...], ones)
    direct = split_sum(directs[...], ones)
    row, col = iota((rows, rows), 0), iota((rows, rows), 1)
    col_start = starts_of(c0 + iota((1, rows), 1), ends)
    above = ((col >= row) & (col_start <= c0 + row)).astype(f32)
    next_start = starts_of(c0 + rows, ends)
    reaches = (v.index >= next_start).astype(f32)
    after = jnp.dot(above, grad_cum, precision=HIGHEST, preferred_element_type=f32) + reaches * carry[0:1, :]
    flux = jnp.sum(grad_state[...] * states[...].astype(f32), axis=0, keepdims=True)
    carry[...] = split_sum(jnp.broadcast_to(flux, (8, width)), ones)
    grad_log = -v.step * v.rate * after
    grad_raw = (direct - v.rate * after) * jax.nn.sigmoid(v.raw)
    grad_rates[0:1, :] += jnp.sum(grad_raw, axis=0, keepdims=True)
    grad_rates[1:2, :] += jnp.sum(grad_log, axis=0, keepdims=True)

    index_ext = c0 + iota((rows + 8, 1), 0)
    position_ext = index_ext - starts_of(index_ext, ends)
    taps_back(v.x_ext, grad_pre[...], v.position, grad_wide)
    extended = jnp.concatenate([grad_pre[...], next_pre[...]], axis=0)
    grad_all[:, width : 2 * width] = conv_back(extended, wide, position_ext).astype(bf16)
    next_pre[...] = grad_pre[0:8, :]

    blank = jnp.zeros((rows, LANES - HD), f32)
    grad_sc = jnp.concatenate([grad_b, blank, grad_c, blank], axis=1)
    grad_pre_s = grad_sc * silu_grad(v.pre_s, v.gate_s)
    taps_back(v.s_ext, grad_pre_s, v.position, grad_narrow)
    extended_s = jnp.concatenate([grad_pre_s, next_pre_s[...]], axis=0)
    grad_all[:, 2 * width : 2 * width + 2 * LANES] = conv_back(extended_s, narrow, position_ext).astype(bf16)
    next_pre_s[...] = grad_pre_s[0:8, :]
    grad_all[:, 2 * width + 2 * LANES :] = grad_raw.astype(bf16)


def mixer_specs(tp, rows, width, order):
    share = rows // tp
    per_share = share // CHUNK

    def here(place, c):
        owner = lax.div(c, per_share)
        piece = lax.rem(place[0] - owner + tp, tp)
        return piece * per_share + lax.rem(c, per_share)

    def chunk_map(i, place, lengths):
        return (here(place, order(i)), 0)

    def before_map(unit, column):
        def index(i, place, lengths):
            c = order(i)
            previous = jnp.maximum(c - 1, 0)
            return (here(place, previous) * (CHUNK // unit) + CHUNK // unit - 1, column)

        return index

    def fixed(i, place, lengths):
        return (0, 0)

    return chunk_map, before_map, fixed


def mixer_forward(place, lengths, tp, zx, sd, wide, narrow, rates):
    rows, width = zx.shape[0], zx.shape[1] // 2
    chunks = rows // CHUNK
    chunk_map, before_map, fixed = mixer_specs(tp, rows, width, lambda i: i)
    work = rows * width * CHUNK
    return pl.pallas_call(
        mixer_forward_kernel,
        out_shape=[
            jax.ShapeDtypeStruct((rows, width), bf16),
            jax.ShapeDtypeStruct((chunks, HD, width), bf16),
        ],
        grid_spec=pltpu.PrefetchScalarGridSpec(
            num_scalar_prefetch=2,
            grid=(chunks,),
            in_specs=[
                pl.BlockSpec((CHUNK, 2 * width), chunk_map),
                pl.BlockSpec((16, width), before_map(16, 1)),
                pl.BlockSpec((CHUNK, 3 * LANES), chunk_map),
                pl.BlockSpec((8, 3 * LANES), before_map(8, 0)),
                pl.BlockSpec((8, width), fixed),
                pl.BlockSpec((8, 2 * LANES), fixed),
                pl.BlockSpec((8, LANES), fixed),
            ],
            out_specs=[
                pl.BlockSpec((CHUNK, width), chunk_map),
                pl.BlockSpec((None, HD, width), lambda i, *_: (i, 0, 0)),
            ],
            scratch_shapes=[pltpu.VMEM((HD, width), f32)],
        ),
        compiler_params=pltpu.CompilerParams(vmem_limit_bytes=VMEM_LIMIT),
        cost_estimate=pl.CostEstimate(
            flops=8 * work, bytes_accessed=8 * rows * width, transcendentals=4 * rows * width
        ),
        name="mixer_forward",
    )(place, lengths, zx, zx, sd, sd, wide, narrow, rates)


def mixer_backward(place, lengths, tp, zx, sd, grad_scaled, stats, states, wide, narrow, rates):
    rows, width = zx.shape[0], zx.shape[1] // 2
    chunks = rows // CHUNK
    chunk_map, before_map, fixed = mixer_specs(tp, rows, width, lambda i: chunks - 1 - i)
    work = rows * width * CHUNK
    return pl.pallas_call(
        functools.partial(mixer_backward_kernel, chunks),
        out_shape=[
            jax.ShapeDtypeStruct((rows, 2 * width + 3 * LANES), bf16),
            jax.ShapeDtypeStruct((8, width), f32),
            jax.ShapeDtypeStruct((8, 2 * LANES), f32),
            jax.ShapeDtypeStruct((8, LANES), f32),
        ],
        grid_spec=pltpu.PrefetchScalarGridSpec(
            num_scalar_prefetch=2,
            grid=(chunks,),
            in_specs=[
                pl.BlockSpec((CHUNK, 2 * width), chunk_map),
                pl.BlockSpec((16, width), before_map(16, 1)),
                pl.BlockSpec((CHUNK, 3 * LANES), chunk_map),
                pl.BlockSpec((8, 3 * LANES), before_map(8, 0)),
                pl.BlockSpec((CHUNK, width), chunk_map),
                pl.BlockSpec((CHUNK, 2), chunk_map),
                pl.BlockSpec((None, HD, width), lambda i, *_: (chunks - 1 - i, 0, 0)),
                pl.BlockSpec((8, width), fixed),
                pl.BlockSpec((8, 2 * LANES), fixed),
                pl.BlockSpec((8, LANES), fixed),
            ],
            out_specs=[
                pl.BlockSpec((CHUNK, 2 * width + 3 * LANES), chunk_map),
                pl.BlockSpec((8, width), fixed),
                pl.BlockSpec((8, 2 * LANES), fixed),
                pl.BlockSpec((8, LANES), fixed),
            ],
            scratch_shapes=[
                pltpu.VMEM((HD, width), f32),
                pltpu.VMEM((8, width), f32),
                pltpu.VMEM((8, 2 * LANES), f32),
                pltpu.VMEM((8, LANES), f32),
                pltpu.VMEM((CHUNK, width), f32),
                pltpu.VMEM((CHUNK, width), f32),
                pltpu.VMEM((CHUNK, width), f32),
            ],
        ),
        compiler_params=pltpu.CompilerParams(vmem_limit_bytes=VMEM_LIMIT),
        cost_estimate=pl.CostEstimate(
            flops=24 * work, bytes_accessed=12 * rows * width, transcendentals=5 * rows * width
        ),
        name="mixer_backward",
    )(place, lengths, zx, zx, sd, sd, grad_scaled, stats, states, wide, narrow, rates)


def tie(value, others):
    return lax.optimization_barrier((value, others))[0]


def ring_pairs():
    tp = lax.axis_size("tp")
    return [(i, (i + 1) % tp) for i in range(tp)]


def hop(values):
    return lax.ppermute(values, "tp", ring_pairs())


def ring_gather(own, use=None):
    tp = lax.axis_size("tp")
    pieces, results = [own], []
    for p in range(tp):
        moved = hop(pieces[p]) if p < tp - 1 else None
        if use is not None:
            results.append(use(p, pieces[p]))
            if moved is not None:
                moved = tie(moved, results[-1])
        if moved is not None:
            pieces.append(moved)
    return pieces, results


def ring_scatter(part, fill=()):
    tp = lax.axis_size("tp")
    fill = list(fill)
    filled = []
    total = part(1 % tp)
    for p in range(2, tp + 1):
        low = total.astype(bf16)
        moved = hop(low)
        term = part(p % tp)
        if fill:
            filled.append(fill.pop(0)(low))
            moved = tie(moved, filled[-1])
        total = moved.astype(f32) + term
    for thunk in fill:
        filled.append(thunk(low))
    return total, filled


def ring_both(own, work, last=None, fill=()):
    tp = lax.axis_size("tp")
    fill = list(fill)
    filled = []
    pieces = [own]
    moved = hop(own)
    first = work(0, own)
    moved = tie(moved, first)
    total, ahead = None, None
    for p in range(1, tp):
        pieces.append(moved)
        if p < tp - 1:
            moved = hop(pieces[p])
        elif last is not None:
            filled.append(last(pieces))
            pieces[p] = tie(pieces[p], filled[-1])
        term = work(p, pieces[p])
        total = term if total is None else ahead.astype(f32) + term
        ahead = hop(total.astype(bf16))
        if p < tp - 1:
            moved = tie(moved, total)
    if fill:
        filled.extend(thunk() for thunk in fill)
        ahead = tie(ahead, filled[-1])
    return pieces, ahead.astype(f32) + first, filled


def halving(values, name, sent_as=f32):
    count = lax.axis_size(name)
    here = lax.axis_index(name)
    half = count // 2
    while half:
        upper = (here & half) != 0
        low, high = values[:half], values[half:]
        sent = jnp.where(upper, low, high)
        kept = jnp.where(upper, high, low)
        moved = lax.ppermute(sent.astype(sent_as), name, [(i, i ^ half) for i in range(count)])
        values = kept + moved.astype(f32)
        half //= 2
    return values[0]


def doubling_gather(values, name):
    count = lax.axis_size(name)
    here = lax.axis_index(name)
    step = 1
    while step < count:
        moved = lax.ppermute(values, name, [(i, i ^ step) for i in range(count)])
        upper = (here & step) != 0
        values = jnp.concatenate(
            [jnp.where(upper, moved, values), jnp.where(upper, values, moved)], axis=0
        )
        step *= 2
    return values


def doubling(values, name):
    count = lax.axis_size(name)
    step = 1
    while step < count:
        values = values + lax.ppermute(values, name, [(i, i ^ step) for i in range(count)])
        step *= 2
    return values


def inverse_root(values):
    return lax.rsqrt(jnp.mean(values * values, axis=1, keepdims=True) + norm_eps)


def rms_backward(values, inv_root, gain, grad_out):
    unit_rows = values * inv_root
    grad_gain = jnp.sum(grad_out * unit_rows, axis=0)
    grad_unit = grad_out * gain
    grad_values = inv_root * (
        grad_unit - unit_rows * jnp.mean(grad_unit * unit_rows, axis=-1, keepdims=True)
    )
    return (grad_values, grad_gain)


def gather(values, axis=0):
    return lax.all_gather(values, "fsdp", axis=axis, tiled=True)


def scatter(values, axis=0):
    return lax.psum_scatter(values, "fsdp", scatter_dimension=axis, tiled=True)


def local(
    hidden,
    embed,
    lengths,
    attention_norm_gain,
    query_key_value_weight,
    attention_adapter_down,
    attention_adapter_up,
    attention_output_weight,
    feedforward_norm_gain,
    gate_up_weight,
    feedforward_adapter_down,
    feedforward_adapter_up,
    down_weight,
    mixer_norm_gain,
    gate_inner_weight,
    state_input_weight,
    step_projection,
    inner_conv_taps,
    state_conv_taps,
    head_step_bias,
    decay_log_rate,
    inner_skip_gains,
    gated_norm_gain,
    mixer_output_weight,
    output_cotangent,
):
    tp = lax.axis_size("tp")
    fsdp = lax.axis_size("fsdp")
    share, width = hidden.shape
    rows = share * tp
    here = lax.axis_index("tp").astype(jnp.int32)
    place = here.reshape(1)
    lengths = lengths.reshape(-1)
    rank = attention_adapter_down.shape[2]
    head_cols = query_key_value_weight.shape[2]
    units_here = gate_up_weight.shape[2]
    inner_cols = gate_inner_weight.shape[2]
    mixer_heads = inner_cols // HD
    states = state_input_weight.shape[2]
    count = inner_conv_taps.shape[0]
    inner_total = inner_cols * tp

    def piece(values, p):
        return values[p * share : (p + 1) * share]

    joined_low = jnp.concatenate([hidden, embed], axis=1)
    query_key_value_weight = tie(query_key_value_weight, joined_low)
    weight_qkv = gather(
        jnp.concatenate(
            [query_key_value_weight[:, j, :] for j in range(3)]
            + [attention_adapter_down[:, j, :] for j in range(3)],
            axis=1,
        )
    )
    ups = doubling_gather(
        jnp.concatenate(
            [attention_adapter_up[:, j, :] for j in range(3)]
            + [feedforward_adapter_up[:, j, :] for j in range(2)],
            axis=1,
        ),
        "fsdp",
    )
    fc_up = ups[:, 3 * head_cols :]
    weight_o = gather(attention_output_weight, 1)
    weight_fc1 = gather(
        jnp.concatenate(
            [gate_up_weight[:, j, :] for j in range(2)] + [feedforward_adapter_down], axis=1
        )
    )
    weight_down = gather(jnp.concatenate([down_weight, mixer_output_weight], axis=0), 1)
    weight_fc2, weight_out = weight_down[:units_here], weight_down[units_here:]
    weight_zx = gather(
        jnp.concatenate(
            [gate_inner_weight[:, j, :] for j in range(2)]
            + [jnp.pad(state_input_weight[:, j, :], ((0, 0), (0, LANES - states))) for j in range(2)]
            + [jnp.pad(step_projection, ((0, 0), (0, LANES - mixer_heads)))],
            axis=1,
        )
    )

    small = [
        attention_norm_gain,
        feedforward_norm_gain,
        mixer_norm_gain,
        inner_conv_taps.reshape(-1),
        state_conv_taps.reshape(-1),
        inner_skip_gains.reshape(-1),
        gated_norm_gain.reshape(-1),
    ]
    sizes = [v.shape[0] for v in small]
    padding = -sum(sizes) % LANES
    packed = jnp.concatenate(small + [jnp.zeros((padding,), bf16)]).reshape(1, -1)
    spread = gather(packed).astype(f32)
    cuts = [sum(sizes[:i]) for i in range(len(sizes) + 1)]
    parts = [spread[:, cuts[i] : cuts[i + 1]] for i in range(len(sizes))]
    gain_attn, gain_mlp, gain_mixer = (parts[i].reshape(1, -1) for i in range(3))
    taps_x = parts[3].reshape(fsdp, count, mixer_heads, -1)
    taps_x = jnp.transpose(taps_x, (1, 2, 0, 3)).reshape(count, inner_cols)
    taps_s = parts[4].reshape(fsdp, count, 2, -1)
    taps_s = jnp.transpose(taps_s, (1, 2, 0, 3)).reshape(count, 2, states)
    skip = jnp.transpose(parts[5].reshape(fsdp, mixer_heads, -1), (1, 0, 2)).reshape(1, inner_cols)
    gain_gate = jnp.transpose(parts[6].reshape(fsdp, mixer_heads, -1), (1, 0, 2)).reshape(1, inner_cols)
    wide = jnp.concatenate([taps_x, skip, gain_gate, jnp.zeros((2, inner_cols), f32)], axis=0)
    narrow = jnp.pad(taps_s, ((0, 8 - count), (0, 0), (0, LANES - states))).reshape(8, 2 * LANES)
    rates = jnp.pad(
        jnp.stack([head_step_bias, decay_log_rate]), ((0, 6), (0, LANES - mixer_heads))
    )

    places = jnp.arange(rows, dtype=jnp.int32)
    ends = [jnp.sum(lengths[: i + 1]) for i in range(lengths.shape[0] - 1)]
    position = places - starts_of(places, ends)
    freqs = jnp.exp(jnp.arange(HDA // 2, dtype=f32) * (-2.0 * math.log(10000.0) / HDA))
    angles = position.astype(f32)[:, None] * freqs[None, :]
    cosine = jnp.cos(angles)
    sine = jnp.sin(angles)
    cosine = jnp.concatenate([cosine, cosine], axis=1)
    sine = jnp.concatenate([-sine, sine], axis=1)

    joined = joined_low.astype(f32)
    attn_root = inverse_root(joined)

    def norm_rows(values):
        values = values.astype(f32)
        return (values * inverse_root(values) * gain_attn).astype(bf16)

    raw, normed = [joined_low], []
    for p in range(1, tp):
        moved = hop(raw[-1])
        if p > 1:
            normed.append(norm_rows(raw[p - 2]))
            moved = tie(moved, normed[-1])
        raw.append(moved)
    normed += [norm_rows(v) for v in raw[len(normed) :]]

    out_grad = [tie(output_cotangent, raw[-1])]
    projected = []
    for i in range(tp - 1):
        moved = hop(out_grad[-1])
        if i < tp - 2:
            low, high = (tp * i) // (tp - 2), (tp * (i + 1)) // (tp - 2)
            projected += [mm(normed[p], weight_qkv) for p in range(low, high)]
            moved = tie(moved, projected)
        else:
            attended, queries, keys, values = attention_forward(
                place, lengths, projected, ups, head_cols, cosine, sine
            )
            moved = tie(moved, attended)
        out_grad.append(moved)
    attended = tie(attended, moved)
    out_grad_rows = jnp.concatenate(out_grad, axis=0)
    mixed, _ = ring_scatter(lambda p: mm(piece(attended, p), weight_o))

    mlp_root = inverse_root(mixed)
    gate_up, fc_mid, units = [], [], []

    def feed(p, rows_in):
        wide_rows = mm(rows_in, weight_fc1)
        middle = wide_rows[:, 2 * units_here :].astype(bf16)
        both = (wide_rows[:, : 2 * units_here] + mm(middle, fc_up)).astype(bf16)
        gate, up = both[:, :units_here].astype(f32), both[:, units_here:].astype(f32)
        unit = (jax.nn.gelu(gate) * up).astype(bf16)
        fc_mid.append(middle)
        gate_up.append(both)
        units.append(unit)
        return mm(unit, weight_fc2)

    mlp_in, branch, _ = ring_both((mixed * mlp_root * gain_mlp).astype(bf16), feed)
    residual = hidden.astype(f32) + mixed + branch

    mixer_root = inverse_root(residual)
    scaled_grads = []

    def mix(p, rows_in):
        result = mm(rows_in, weight_zx)
        if p == 0:
            scaled_grads.append(mm_nt(tie(out_grad_rows, result), weight_out).astype(bf16))
            result = tie(result, scaled_grads[0])
        return result

    mixer_in, zxs = ring_gather((residual * mixer_root * gain_mixer).astype(bf16), mix)
    grad_scaled = scaled_grads[0]
    mixer_rows = jnp.concatenate(mixer_in, axis=0)
    zx = jnp.concatenate([v[:, : 2 * inner_cols].astype(bf16) for v in zxs], axis=0)
    sd = jnp.concatenate([v[:, 2 * inner_cols :] for v in zxs], axis=0)
    gated, chunk_states = mixer_forward(place, lengths, tp, zx, sd, wide, narrow, rates)
    gated_wide = gated.astype(f32)
    sums = jnp.stack(
        [
            jnp.sum(gated_wide * gated_wide, axis=1),
            jnp.sum(grad_scaled.astype(f32) * gain_gate * gated_wide, axis=1),
        ],
        axis=0,
    )
    sums = jnp.roll(jnp.flip(sums.reshape(2, tp, share), axis=1), here + 1, axis=1)
    sums = lax.psum(sums, "tp")
    sums = jnp.flip(jnp.roll(sums, -(here + 1), axis=1), axis=1).reshape(2, rows)
    gate_root = lax.rsqrt(sums[0] / inner_total + norm_eps)
    stats = jnp.stack([gate_root, gate_root**3 * sums[1] / inner_total], axis=1)
    scaled = (gated_wide * gate_root[:, None] * gain_gate).astype(bf16)
    out_terms = [mm(piece(scaled, p), weight_out) for p in range(tp)]
    out = hop(out_terms[1 % tp].astype(bf16))

    grad_all, grad_wide, grad_narrow, grad_rates = mixer_backward(
        place, lengths, tp, zx, sd, grad_scaled, stats, chunk_states, wide, narrow, rates
    )
    out = tie(out, grad_all).astype(f32) + out_terms[2 % tp]
    grad_mixer_in, (sum_w_out, sum_w_zx) = ring_scatter(
        lambda p: mm_nt(piece(grad_all, p), weight_zx),
        [
            lambda t: mm_tn(tie(scaled, t), out_grad_rows).astype(bf16),
            lambda t: mm_tn(tie(mixer_rows, t), grad_all).astype(bf16),
        ],
    )
    sum_w_out = scatter(sum_w_out, 1)
    sum_w_zx = scatter(sum_w_zx)
    grad_resid_norm, grad_gain_mixer = rms_backward(residual, mixer_root, gain_mixer, grad_mixer_in)
    grad_residual = output_cotangent.astype(f32) + grad_resid_norm

    grad_gate_up = []

    def feed_back(p, grad_rows):
        grad_units = mm_nt(grad_rows, weight_fc2)
        gate = gate_up[p][:, :units_here].astype(f32)
        up = gate_up[p][:, units_here:].astype(f32)
        raised, back = jax.vjp(jax.nn.gelu, gate)
        both = jnp.concatenate(
            [back(grad_units * up)[0].astype(bf16), (grad_units * raised).astype(bf16)], axis=1
        )
        both = jnp.concatenate([both, mm_nt(both, fc_up).astype(bf16)], axis=1)
        grad_gate_up.append(both)
        return mm_nt(both, weight_fc1)

    units_rows = jnp.concatenate(units, axis=0)
    mlp_rows = jnp.concatenate(mlp_in, axis=0)
    grad_branch, grad_mlp_in, (sum_w_fc2, sum_w_fc1) = ring_both(
        grad_residual.astype(bf16),
        feed_back,
        lambda pieces: mm_tn(tie(units_rows, sum_w_out), jnp.concatenate(pieces, axis=0)).astype(bf16),
        [lambda: mm_tn(mlp_rows, jnp.concatenate(grad_gate_up, axis=0)).astype(bf16)],
    )
    sum_w_fc2 = scatter(sum_w_fc2, 1)
    sum_w_fc1 = scatter(sum_w_fc1)
    grad_gate_up_rows = jnp.concatenate(grad_gate_up, axis=0)
    grad_mixed_norm, grad_gain_mlp = rms_backward(mixed, mlp_root, gain_mlp, grad_mlp_in)

    grad_mixed, grad_attended = ring_gather(
        tie((grad_residual + grad_mixed_norm).astype(bf16), sum_w_zx),
        lambda p, v: mm_nt(v, weight_o).astype(bf16),
    )
    sum_w_o = mm_tn(tie(attended, sum_w_fc2), jnp.concatenate(grad_mixed, axis=0)).astype(bf16)
    grad_attended[-1] = tie(grad_attended[-1], sum_w_o)
    sum_w_o = scatter(sum_w_o, 1)
    out = hop(out.astype(bf16))
    grad_projected = attention_backward(
        place, lengths, queries, keys, values, ups, grad_attended, cosine, sine
    )
    out = tie(out, grad_projected).astype(f32) + out_terms[3 % tp]
    normed_rows = jnp.concatenate(normed, axis=0)
    lora_rows = jnp.concatenate([v[:, 3 * head_cols :].astype(bf16) for v in projected], axis=0)

    def finish(total):
        for p in range(4, tp + 1):
            total = hop(total.astype(bf16)).astype(f32) + out_terms[p % tp]
        return residual + total

    grad_normed, (sum_w_qkv, (grad_up, grad_fc_up), (out, late)) = ring_scatter(
        lambda p: mm_nt(piece(grad_projected, p), weight_qkv),
        [
            lambda t: mm_tn(tie(normed_rows, t), grad_projected).astype(bf16),
            lambda t: (
                [
                    mm_tn(
                        tie(lora_rows, t)[:, j * rank : (j + 1) * rank],
                        grad_projected[:, j * head_cols : (j + 1) * head_cols],
                    )
                    for j in range(3)
                ],
                mm_tn(tie(jnp.concatenate(fc_mid, axis=0), t), grad_gate_up_rows[:, : 2 * units_here]),
            ),
            lambda t: lax.optimization_barrier(
                (finish(tie(out, t)), tie((grad_wide, grad_narrow, grad_rates), t))
            ),
        ],
    )
    sum_w_qkv = scatter(sum_w_qkv)
    grad_wide, grad_narrow, grad_rates = late
    grad_joined, grad_gain_attn = rms_backward(joined, attn_root, gain_attn, grad_normed)
    grad_hidden = grad_residual + grad_joined[:, :width]
    grad_embed = grad_joined[:, width:]
    grad_down = halving(sum_w_qkv[:, 3 * head_cols :].astype(f32).reshape(tp, -1, 3 * rank), "tp")

    grad_ups = jnp.concatenate(grad_up + [grad_fc_up], axis=1)
    grad_ups = halving(grad_ups.reshape(fsdp, -1, grad_ups.shape[1]), "fsdp", bf16)
    sum_w_zx = sum_w_zx.astype(f32)
    sum_w_fc1 = sum_w_fc1.astype(f32)
    at_t = 2 * inner_cols + 2 * LANES
    grad_w_dt = sum_w_zx[:, at_t : at_t + mixer_heads]
    shared = jnp.concatenate([sum_w_zx[:, 2 * inner_cols : at_t], sum_w_fc1[:, 2 * units_here :]], axis=1)
    shared = doubling(shared, "tp")

    def by_fsdp(values):
        lead = values.shape[:-1]
        cut = values.reshape(lead + (fsdp, values.shape[-1] // fsdp))
        return jnp.moveaxis(cut, -2, 0).reshape(fsdp, -1)

    grad_taps_x = grad_wide[:count].reshape(count, mixer_heads, HD)
    grad_taps_s = grad_narrow[:count].reshape(count, 2, LANES)[:, :, :states]
    local_small = [
        by_fsdp(grad_taps_x),
        by_fsdp(grad_wide[4].reshape(mixer_heads, HD)),
        by_fsdp(grad_wide[5].reshape(mixer_heads, HD)),
        jnp.broadcast_to(grad_rates[:2, :mixer_heads].reshape(1, -1), (fsdp, 2 * mixer_heads)),
    ]
    shared_small = [by_fsdp(grad_taps_s), by_fsdp(grad_gain_mixer), by_fsdp(grad_gain_mlp)]
    small_sizes = [v.shape[1] for v in local_small + shared_small]
    small_cuts = [sum(small_sizes[:i]) for i in range(len(small_sizes) + 1)]
    small_sum = halving(jnp.concatenate(local_small + shared_small, axis=1), "fsdp")
    small_parts = [small_sum[small_cuts[i] : small_cuts[i + 1]] for i in range(len(small_sizes))]
    tail = doubling(small_sum[small_cuts[4] :], "tp")
    tail_cuts = [v - small_cuts[4] for v in small_cuts[4:]]
    grad_conv_bc, sum_gain_mixer, sum_gain_mlp = (
        tail[tail_cuts[i] : tail_cuts[i + 1]] for i in range(3)
    )
    grad_gain_attn = halving(halving(grad_gain_attn.reshape(fsdp, -1), "fsdp").reshape(tp, -1), "tp")
    sum_rates = small_parts[3].reshape(2, mixer_heads)
    return (
        out,
        grad_hidden,
        grad_embed,
        grad_gain_attn,
        jnp.stack(
            [sum_w_qkv[:, j * head_cols : (j + 1) * head_cols].astype(f32) for j in range(3)], axis=1
        ),
        grad_down.reshape(-1, 3, rank),
        grad_ups[:, : 3 * head_cols].reshape(-1, 3, head_cols),
        sum_w_o.astype(f32),
        sum_gain_mlp,
        sum_w_fc1[:, : 2 * units_here].reshape(-1, 2, units_here),
        shared[:, 2 * LANES :],
        grad_ups[:, 3 * head_cols :].reshape(-1, 2, units_here),
        sum_w_fc2.astype(f32),
        sum_gain_mixer,
        sum_w_zx[:, : 2 * inner_cols].reshape(-1, 2, inner_cols),
        shared[:, : 2 * LANES].reshape(-1, 2, LANES)[:, :, :states],
        grad_w_dt,
        small_parts[0].reshape(count, mixer_heads, -1),
        grad_conv_bc.reshape(count, 2, -1),
        sum_rates[0],
        sum_rates[1],
        small_parts[1].reshape(mixer_heads, -1),
        small_parts[2].reshape(mixer_heads, -1),
        sum_w_out.astype(f32),
    )


def solution(mesh):
    placed = (
        P(("fsdp", "tp"), None),
        P(("fsdp", "tp"), None),
        P("fsdp", None),
        P("fsdp"),
        P("fsdp", None, "tp"),
        P("fsdp", None, None),
        P("fsdp", None, "tp"),
        P("tp", "fsdp"),
        P("fsdp"),
        P("fsdp", None, "tp"),
        P("fsdp", None),
        P("fsdp", None, "tp"),
        P("tp", "fsdp"),
        P("fsdp"),
        P("fsdp", None, "tp"),
        P("fsdp", None, None),
        P("fsdp", "tp"),
        P(None, "tp", "fsdp"),
        P(None, None, "fsdp"),
        P("tp"),
        P("tp"),
        P("tp", "fsdp"),
        P("tp", "fsdp"),
        P("tp", "fsdp"),
        P(("fsdp", "tp"), None),
    )
    return jax.shard_map(
        local,
        mesh=mesh,
        in_specs=placed,
        out_specs=(
            P(("fsdp", "tp"), None),
            P(("fsdp", "tp"), None),
            P(("fsdp", "tp"), None),
            P(("fsdp", "tp")),
            P("fsdp", None, "tp"),
            P(("fsdp", "tp"), None, None),
            P("fsdp", None, "tp"),
            P("tp", "fsdp"),
            P("fsdp"),
            P("fsdp", None, "tp"),
            P("fsdp", None),
            P("fsdp", None, "tp"),
            P("tp", "fsdp"),
            P("fsdp"),
            P("fsdp", None, "tp"),
            P("fsdp", None, None),
            P("fsdp", "tp"),
            P(None, "tp", "fsdp"),
            P(None, None, "fsdp"),
            P("tp"),
            P("tp"),
            P("tp", "fsdp"),
            P("tp", "fsdp"),
            P("tp", "fsdp"),
        ),
        check_vma=False,
    )
```

```python
import functools
import math

import jax
import jax.numpy as jnp
from jax import lax
from jax.experimental import pallas as pl
from jax.experimental.layout import Layout, with_layout_constraint
from jax.experimental.pallas import tpu as pltpu
from jax.sharding import PartitionSpec as P

HDA = 128
HD = 64
LANES = 128
CHUNK = 128

norm_eps = 1e-05
f32 = jnp.float32
bf16 = jnp.bfloat16
HIGHEST = lax.Precision.HIGHEST
VMEM_LIMIT = 56 * 1024 * 1024


def mm(left, right):
    return jnp.dot(left, right, preferred_element_type=f32)


def mm_nt(left, right):
    return lax.dot_general(left, right, (((1,), (1,)), ((), ())), preferred_element_type=f32)


def mm_tn(left, right):
    return lax.dot_general(left, right, (((0,), (0,)), ((), ())), preferred_element_type=f32)


def starts_of(index, ends):
    start = jnp.zeros_like(index)
    for end in ends:
        start = jnp.where(index >= end, end, start)
    return start


def ends_of(lengths_ref):
    ends = []
    end = jnp.int32(0)
    for i in range(lengths_ref.shape[0] - 1):
        end = end + lengths_ref[i]
        ends.append(end)
    return ends


def iota(shape, axis):
    return lax.broadcasted_iota(jnp.int32, shape, axis)


def attention_forward_kernel(
    tp,
    parts,
    place_ref,
    lengths_ref,
    cosine_ref,
    sine_ref,
    q_up,
    k_up,
    v_up,
    *refs,
):
    pieces = refs[: 4 * parts]
    attended_ref, q_ref, k_ref, v_ref, held = refs[4 * parts :]
    rows = q_ref.shape[0]
    share = rows // tp
    rank = q_up.shape[0]
    here = place_ref[0]
    ends = ends_of(lengths_ref)
    for p in range(tp):
        owner = lax.rem(here - p + tp, tp)
        part = pl.ds(pl.multiple_of(owner * share, share), share)
        cosine, sine = cosine_ref[part, :], sine_ref[part, :]
        at = p * share
        source = 0
        while at >= pieces[4 * source].shape[0]:
            at -= pieces[4 * source].shape[0]
            source += 1
        mine = slice(at, at + share)
        for j, (up, target) in enumerate(((q_up, q_ref), (k_up, k_ref), (v_up, v_ref))):
            low = pieces[4 * source + 3][mine, j * rank : (j + 1) * rank].astype(bf16)
            value = pieces[4 * source + j][mine, :] + mm(low, up[...])
            if j < 2:
                value = value * cosine + pltpu.roll(value, HDA // 2, 1) * sine
            target[part, :] = value.astype(bf16)
    block = min(256, rows)
    scale = HDA ** (-0.5)
    for at in range(0, rows, block):
        upto = at + block
        scores = mm_nt(q_ref[at:upto, :], k_ref[:upto, :]) * scale
        query = at + iota((block, 1), 0)
        key = iota((1, upto), 1)
        seen = (key <= query) & (key >= starts_of(query, ends))
        scores = jnp.where(seen, scores, -1e30)
        raised = jnp.exp(scores - jnp.max(scores, axis=1, keepdims=True))
        probs = (raised * (1.0 / jnp.sum(raised, axis=1, keepdims=True))).astype(bf16)
        held[at:upto, :] = mm(probs, v_ref[:upto, :]).astype(bf16)
    for p in range(tp):
        owner = lax.rem(here - p + tp, tp)
        part = pl.ds(pl.multiple_of(owner * share, share), share)
        attended_ref[p * share : (p + 1) * share, :] = held[part, :]


def attention_forward(place, lengths, tp, projected, ups, columns, cosine, sine):
    rows = sum(v.shape[0] for v in projected)
    heads = columns // HDA
    rank = ups.shape[0]
    table_spec = pl.BlockSpec((rows, HDA), lambda h, *_: (0, 0))

    def head_spec(j, height=rows):
        return pl.BlockSpec((height, HDA), lambda h, *_: (0, j * heads + h))

    work = heads * rows * rows * HDA
    return pl.pallas_call(
        functools.partial(attention_forward_kernel, tp, len(projected)),
        out_shape=[jax.ShapeDtypeStruct((rows, columns), bf16)] * 4,
        grid_spec=pltpu.PrefetchScalarGridSpec(
            num_scalar_prefetch=2,
            grid=(heads,),
            in_specs=[table_spec, table_spec]
            + [head_spec(j, rank) for j in range(3)]
            + [
                pl.BlockSpec((v.shape[0], 3 * rank), lambda h, *_: (0, columns // rank))
                if j == 3
                else head_spec(j, v.shape[0])
                for v in projected
                for j in range(4)
            ],
            out_specs=[head_spec(0)] * 4,
            scratch_shapes=[pltpu.VMEM((rows, HDA), bf16)],
        ),
        compiler_params=pltpu.CompilerParams(vmem_limit_bytes=VMEM_LIMIT),
        cost_estimate=pl.CostEstimate(
            flops=4 * work, bytes_accessed=20 * rows * columns, transcendentals=heads * rows * rows
        ),
        name="attention_forward",
    )(place, lengths, cosine, sine, ups, ups, ups, *[v for v in projected for _ in range(4)])


def attention_backward_kernel(
    tp,
    heads,
    place_ref,
    lengths_ref,
    cosine_ref,
    sine_ref,
    q_ref,
    k_ref,
    v_ref,
    q_up,
    k_up,
    v_up,
    *refs,
):
    grad_in = refs[:tp]
    out_ref, held, dq, dk, dv, lora = refs[tp:]
    rows = q_ref.shape[0]
    share = rows // tp
    rank = q_up.shape[0]
    here = place_ref[0]
    head = pl.program_id(0)
    ends = ends_of(lengths_ref)
    for p in range(tp):
        owner = lax.rem(here - p + tp, tp)
        part = pl.ds(pl.multiple_of(owner * share, share), share)
        held[part, :] = grad_in[p][...]
    dk[...] = jnp.zeros_like(dk)
    dv[...] = jnp.zeros_like(dv)

    @pl.when(head == 0)
    def _():
        lora[...] = jnp.zeros_like(lora)

    block = min(256, rows)
    scale = HDA ** (-0.5)
    for at in range(0, rows, block):
        upto = at + block
        query_rows = q_ref[at:upto, :]
        grad_rows = held[at:upto, :]
        scores = mm_nt(k_ref[:upto, :], query_rows) * scale
        query = at + iota((1, block), 1)
        key = iota((upto, 1), 0)
        seen = (key <= query) & (key >= starts_of(query, ends))
        scores = jnp.where(seen, scores, -1e30)
        raised = jnp.exp(scores - jnp.max(scores, axis=0, keepdims=True))
        probs = raised * (1.0 / jnp.sum(raised, axis=0, keepdims=True))
        grad_probs = mm_nt(v_ref[:upto, :], grad_rows)
        cross = jnp.sum(probs * grad_probs, axis=0, keepdims=True)
        grad_scores = (probs * (grad_probs - cross)).astype(bf16)
        dv[:upto, :] += mm(probs.astype(bf16), grad_rows)
        dk[:upto, :] += mm(grad_scores, query_rows)
        dq[at:upto, :] = mm_tn(grad_scores, k_ref[:upto, :])
    for p in range(tp):
        owner = lax.rem(here - p + tp, tp)
        part = pl.ds(pl.multiple_of(owner * share, share), share)
        cosine, sine = cosine_ref[part, :], sine_ref[part, :]
        mine = slice(p * share, (p + 1) * share)
        for j, (source, up) in enumerate(((dq, q_up), (dk, k_up), (dv, v_up))):
            value = source[part, :]
            if j < 2:
                value = value * scale
                value = value * cosine - pltpu.roll(value, HDA // 2, 1) * sine
            low = value.astype(bf16)
            at = pl.multiple_of((j * heads + head) * HDA, HDA)
            out_ref[mine, pl.ds(at, HDA)] = low
            lora[mine, j * rank : (j + 1) * rank] += mm_nt(low, up[...])

    @pl.when(head == heads - 1)
    def _():
        out_ref[:, 3 * heads * HDA :] = lora[...].astype(bf16)


def attention_backward(place, lengths, queries, keys, values, ups, pieces, cosine, sine):
    tp = len(pieces)
    share, columns = pieces[0].shape
    rows = share * tp
    heads = columns // HDA
    rank = ups.shape[0]
    piece_spec = pl.BlockSpec((share, HDA), lambda h, *_: (0, h))
    table_spec = pl.BlockSpec((rows, HDA), lambda h, *_: (0, 0))
    head_spec = pl.BlockSpec((rows, HDA), lambda h, *_: (0, h))

    def up_spec(j):
        return pl.BlockSpec((rank, HDA), lambda h, *_: (0, j * heads + h))

    total = 3 * columns + 3 * rank
    work = heads * rows * rows * HDA
    return pl.pallas_call(
        functools.partial(attention_backward_kernel, tp, heads),
        out_shape=jax.ShapeDtypeStruct((rows, total), bf16),
        grid_spec=pltpu.PrefetchScalarGridSpec(
            num_scalar_prefetch=2,
            grid=(heads,),
            in_specs=[table_spec, table_spec]
            + [head_spec] * 3
            + [up_spec(j) for j in range(3)]
            + [piece_spec] * tp,
            out_specs=pl.BlockSpec((rows, total), lambda h, *_: (0, 0)),
            scratch_shapes=[pltpu.VMEM((rows, HDA), bf16)]
            + [pltpu.VMEM((rows, HDA), f32)] * 3
            + [pltpu.VMEM((rows, 3 * rank), f32)],
        ),
        compiler_params=pltpu.CompilerParams(vmem_limit_bytes=VMEM_LIMIT),
        cost_estimate=pl.CostEstimate(
            flops=10 * work, bytes_accessed=14 * rows * columns, transcendentals=heads * rows * rows
        ),
        name="attention_backward",
    )(place, lengths, cosine, sine, queries, keys, values, ups, ups, ups, *pieces)


def conv_rows(extended, taps, position):
    count = 4
    rows = extended.shape[0] - 8
    total = None
    for k in range(count):
        moved = extended[8 - k : 8 - k + rows, :]
        if k:
            moved = jnp.where(position >= k, moved, 0.0)
        term = taps[count - 1 - k : count - k, :] * moved
        total = term if total is None else total + term
    return total


def conv_back(extended, taps, position):
    count = 4
    rows = extended.shape[0] - 8
    total = None
    for k in range(count):
        kept = jnp.where(position >= k, extended, 0.0) if k else extended
        term = taps[count - 1 - k : count - k, :] * kept[k : k + rows, :]
        total = term if total is None else total + term
    return total


def taps_back(extended, grad, position, target):
    count = 4
    rows = extended.shape[0] - 8
    for k in range(count):
        moved = extended[8 - k : 8 - k + rows, :]
        if k:
            moved = jnp.where(position >= k, moved, 0.0)
        at = count - 1 - k
        target[at : at + 1, :] += jnp.sum(grad * moved, axis=0, keepdims=True)


def silu_grad(value, gate):
    return gate * (1.0 + value * (1.0 - gate))


class Chunk:
    def __init__(self, c0, ends, zx, before, sd, sd_before, wide, narrow, rates):
        rows = zx.shape[0]
        width = zx.shape[1] // 2
        self.rows, self.width = rows, width
        index = c0 + iota((rows, 1), 0)
        start = starts_of(index, ends)
        self.index, self.start = index, start
        self.position = index - start
        last_start = starts_of(c0 + rows - 1, ends)
        self.z = zx[:, :width].astype(f32)
        self.x_ext = jnp.concatenate(
            [before[...].astype(f32)[8:16, :], zx[:, width:].astype(f32)], axis=0
        )
        self.s_ext = jnp.concatenate([sd_before[:, : 2 * LANES], sd[:, : 2 * LANES]], axis=0)
        self.pre = conv_rows(self.x_ext, wide, self.position)
        self.gate_x = jax.nn.sigmoid(self.pre)
        self.xc = self.pre * self.gate_x
        self.pre_s = conv_rows(self.s_ext, narrow, self.position)
        self.gate_s = jax.nn.sigmoid(self.pre_s)
        sc = self.pre_s * self.gate_s
        self.b_low = sc[:, :HD].astype(bf16)
        self.c_low = sc[:, LANES : LANES + HD].astype(bf16)
        self.raw = sd[:, 2 * LANES : 3 * LANES] + rates[0:1, :]
        self.step = jnp.maximum(self.raw, 0.0) + jnp.log1p(jnp.exp(-jnp.abs(self.raw)))
        self.rate = jnp.exp(rates[1:2, :])
        row, col = iota((rows, rows), 0), iota((rows, rows), 1)
        below = (col <= row).astype(f32)
        self.cum = jnp.dot(below, -self.step * self.rate, precision=HIGHEST, preferred_element_type=f32)
        self.cum_t = self.cum.T
        self.allowed = (col <= row) & ((c0 + col) >= start)
        self.inner = jnp.where(self.allowed, mm_nt(self.c_low, self.b_low), 0.0)
        last = self.cum[rows - 1 : rows, :]
        self.into = jnp.exp(self.cum) * (start < c0).astype(f32)
        self.onto = jnp.exp(last - self.cum) * (index >= last_start).astype(f32)
        self.decay = jnp.exp(last) * (last_start < c0).astype(f32)
        self.low_half = iota((1, LANES), 1) < HD

    def pair(self, table, i):
        return jnp.where(self.low_half, table[:, 2 * i : 2 * i + 1], table[:, 2 * i + 1 : 2 * i + 2])

    def spread(self, h):
        return jnp.exp(jnp.minimum(self.cum[:, h : h + 1] - self.cum_t[h : h + 1, :], 0.0))


def mixer_forward_kernel(
    place_ref, lengths_ref, zx, before, sd, sd_before, wide, narrow, rates, gated, states, state
):
    rows = zx.shape[0]
    c0 = pl.program_id(0) * rows
    ends = ends_of(lengths_ref)

    @pl.when(pl.program_id(0) == 0)
    def _():
        state[...] = jnp.zeros_like(state)

    v = Chunk(c0, ends, zx, before, sd, sd_before, wide, narrow, rates)
    state_low = state[...].astype(bf16)
    states[...] = state_low
    for i in range(v.width // LANES):
        cols = slice(i * LANES, (i + 1) * LANES)
        xc = v.xc[:, cols]
        xs = v.pair(v.step, i) * xc
        xs_low = xs.astype(bf16)
        first = (v.spread(2 * i) * v.inner).astype(bf16)
        second = (v.spread(2 * i + 1) * v.inner).astype(bf16)
        y = jnp.where(v.low_half, mm(first, xs_low), mm(second, xs_low))
        y = y + v.pair(v.into, i) * mm(v.c_low, state_low[:, cols])
        y = y + wide[4:5, cols] * xc
        z = v.z[:, cols]
        gated[:, cols] = (y * z * jax.nn.sigmoid(z)).astype(bf16)
        state[:, cols] = v.pair(v.decay, i) * state[:, cols] + mm_tn(
            v.b_low, (v.pair(v.onto, i) * xs).astype(bf16)
        )


def split_sum(values, ones):
    high = values.astype(bf16)
    low = (values - high.astype(f32)).astype(bf16)
    return mm(high, ones) + mm(low, ones)


def mixer_backward_kernel(
    chunks,
    place_ref,
    lengths_ref,
    zx,
    before,
    sd,
    sd_before,
    grad_scaled,
    stats,
    states,
    wide,
    narrow,
    rates,
    grad_all,
    grad_wide,
    grad_narrow,
    grad_rates,
    grad_state,
    next_pre,
    next_pre_s,
    carry,
    products,
    directs,
    grad_pre,
):
    rows = zx.shape[0]
    turn = pl.program_id(0)
    c0 = (chunks - 1 - turn) * rows
    ends = ends_of(lengths_ref)

    @pl.when(turn == 0)
    def _():
        for ref in (grad_state, next_pre, next_pre_s, carry, grad_wide, grad_narrow, grad_rates):
            ref[...] = jnp.zeros_like(ref)

    v = Chunk(c0, ends, zx, before, sd, sd_before, wide, narrow, rates)
    width = v.width
    root, pull = stats[:, 0:1], stats[:, 1:2]
    grad_inner = jnp.zeros((rows, rows), f32)
    grad_b = jnp.zeros((rows, HD), f32)
    grad_c = jnp.zeros((rows, HD), f32)
    for i in range(width // LANES):
        cols = slice(i * LANES, (i + 1) * LANES)
        xc = v.xc[:, cols]
        step = v.pair(v.step, i)
        xs = step * xc
        xs_low = xs.astype(bf16)
        spread_a, spread_b = v.spread(2 * i), v.spread(2 * i + 1)
        first = (spread_a * v.inner).astype(bf16)
        second = (spread_b * v.inner).astype(bf16)
        state_low = states[:, cols]
        into, onto = v.pair(v.into, i), v.pair(v.onto, i)
        y = jnp.where(v.low_half, mm(first, xs_low), mm(second, xs_low))
        y = y + into * mm(v.c_low, state_low)
        skip, gain = wide[4:5, cols], wide[5:6, cols]
        whole = y + skip * xc
        z = v.z[:, cols]
        gate = jax.nn.sigmoid(z)
        gated = whole * z * gate
        incoming = grad_scaled[:, cols].astype(f32)
        rooted = incoming * root
        grad_wide[5:6, cols] += jnp.sum(rooted * gated, axis=0, keepdims=True)
        grad_gated = rooted * gain - gated * pull
        grad_y = grad_gated * z * gate
        grad_all[:, cols] = (grad_gated * whole * silu_grad(z, gate)).astype(bf16)
        grad_wide[4:5, cols] += jnp.sum(grad_y * xc, axis=0, keepdims=True)
        low = grad_y.astype(bf16)
        low_a = jnp.where(v.low_half, grad_y, 0.0).astype(bf16)
        low_b = jnp.where(v.low_half, 0.0, grad_y).astype(bf16)
        grad_inner = grad_inner + spread_a * mm_nt(low_a, xs_low) + spread_b * mm_nt(low_b, xs_low)
        grad_end = grad_state[:, cols]
        grad_end_low = grad_end.astype(bf16)
        grad_xs = jnp.where(v.low_half, mm_tn(first, low), mm_tn(second, low))
        grad_xs = grad_xs + onto * mm(v.b_low, grad_end_low)
        into_y = (into * grad_y).astype(bf16)
        onto_x = (onto * xs).astype(bf16)
        grad_b = grad_b + mm_nt(onto_x, grad_end_low)
        grad_c = grad_c + mm_nt(into_y, state_low)
        grad_state[:, cols] = v.pair(v.decay, i) * grad_end + mm_tn(v.c_low, into_y)
        products[:, cols] = low.astype(f32) * y - xs_low.astype(f32) * grad_xs
        directs[:, cols] = xc * grad_xs
        grad_xc = step * grad_xs + skip * grad_y
        grad_pre[:, cols] = grad_xc * silu_grad(v.pre[:, cols], v.gate_x[:, cols])
    grad_inner = jnp.where(v.allowed, grad_inner, 0.0).astype(bf16)
    grad_b = grad_b + mm_tn(grad_inner, v.c_low)
    grad_c = grad_c + mm(grad_inner, v.b_low)

    lane, head = iota((width, LANES), 0), iota((width, LANES), 1)
    ones = ((lane >= head * HD) & (lane < head * HD + HD)).astype(bf16)
    grad_cum = split_sum(products[...], ones)
    direct = split_sum(directs[...], ones)
    row, col = iota((rows, rows), 0), iota((rows, rows), 1)
    col_start = starts_of(c0 + iota((1, rows), 1), ends)
    above = ((col >= row) & (col_start <= c0 + row)).astype(f32)
    next_start = starts_of(c0 + rows, ends)
    reaches = (v.index >= next_start).astype(f32)
    after = jnp.dot(above, grad_cum, precision=HIGHEST, preferred_element_type=f32) + reaches * carry[0:1, :]
    flux = jnp.sum(grad_state[...] * states[...].astype(f32), axis=0, keepdims=True)
    carry[...] = split_sum(jnp.broadcast_to(flux, (8, width)), ones)
    grad_log = -v.step * v.rate * after
    grad_raw = (direct - v.rate * after) * jax.nn.sigmoid(v.raw)
    grad_rates[0:1, :] += jnp.sum(grad_raw, axis=0, keepdims=True)
    grad_rates[1:2, :] += jnp.sum(grad_log, axis=0, keepdims=True)

    index_ext = c0 + iota((rows + 8, 1), 0)
    position_ext = index_ext - starts_of(index_ext, ends)
    taps_back(v.x_ext, grad_pre[...], v.position, grad_wide)
    extended = jnp.concatenate([grad_pre[...], next_pre[...]], axis=0)
    grad_all[:, width : 2 * width] = conv_back(extended, wide, position_ext).astype(bf16)
    next_pre[...] = grad_pre[0:8, :]

    blank = jnp.zeros((rows, LANES - HD), f32)
    grad_sc = jnp.concatenate([grad_b, blank, grad_c, blank], axis=1)
    grad_pre_s = grad_sc * silu_grad(v.pre_s, v.gate_s)
    taps_back(v.s_ext, grad_pre_s, v.position, grad_narrow)
    extended_s = jnp.concatenate([grad_pre_s, next_pre_s[...]], axis=0)
    grad_all[:, 2 * width : 2 * width + 2 * LANES] = conv_back(extended_s, narrow, position_ext).astype(bf16)
    next_pre_s[...] = grad_pre_s[0:8, :]
    grad_all[:, 2 * width + 2 * LANES :] = grad_raw.astype(bf16)


def mixer_specs(tp, rows, width, order):
    share = rows // tp
    per_share = share // CHUNK

    def here(place, c):
        owner = lax.div(c, per_share)
        piece = lax.rem(place[0] - owner + tp, tp)
        return piece * per_share + lax.rem(c, per_share)

    def chunk_map(i, place, lengths):
        return (here(place, order(i)), 0)

    def before_map(unit, column):
        def index(i, place, lengths):
            c = order(i)
            previous = jnp.maximum(c - 1, 0)
            return (here(place, previous) * (CHUNK // unit) + CHUNK // unit - 1, column)

        return index

    def fixed(i, place, lengths):
        return (0, 0)

    return chunk_map, before_map, fixed


def mixer_forward(place, lengths, tp, zx, sd, wide, narrow, rates):
    rows, width = zx.shape[0], zx.shape[1] // 2
    chunks = rows // CHUNK
    chunk_map, before_map, fixed = mixer_specs(tp, rows, width, lambda i: i)
    work = rows * width * CHUNK
    return pl.pallas_call(
        mixer_forward_kernel,
        out_shape=[
            jax.ShapeDtypeStruct((rows, width), bf16),
            jax.ShapeDtypeStruct((chunks, HD, width), bf16),
        ],
        grid_spec=pltpu.PrefetchScalarGridSpec(
            num_scalar_prefetch=2,
            grid=(chunks,),
            in_specs=[
                pl.BlockSpec((CHUNK, 2 * width), chunk_map),
                pl.BlockSpec((16, width), before_map(16, 1)),
                pl.BlockSpec((CHUNK, 3 * LANES), chunk_map),
                pl.BlockSpec((8, 3 * LANES), before_map(8, 0)),
                pl.BlockSpec((8, width), fixed),
                pl.BlockSpec((8, 2 * LANES), fixed),
                pl.BlockSpec((8, LANES), fixed),
            ],
            out_specs=[
                pl.BlockSpec((CHUNK, width), chunk_map),
                pl.BlockSpec((None, HD, width), lambda i, *_: (i, 0, 0)),
            ],
            scratch_shapes=[pltpu.VMEM((HD, width), f32)],
        ),
        compiler_params=pltpu.CompilerParams(vmem_limit_bytes=VMEM_LIMIT),
        cost_estimate=pl.CostEstimate(
            flops=8 * work, bytes_accessed=8 * rows * width, transcendentals=4 * rows * width
        ),
        name="mixer_forward",
    )(place, lengths, zx, zx, sd, sd, wide, narrow, rates)


def mixer_backward(place, lengths, tp, zx, sd, grad_scaled, stats, states, wide, narrow, rates):
    rows, width = zx.shape[0], zx.shape[1] // 2
    chunks = rows // CHUNK
    chunk_map, before_map, fixed = mixer_specs(tp, rows, width, lambda i: chunks - 1 - i)
    work = rows * width * CHUNK
    return pl.pallas_call(
        functools.partial(mixer_backward_kernel, chunks),
        out_shape=[
            jax.ShapeDtypeStruct((rows, 2 * width + 3 * LANES), bf16),
            jax.ShapeDtypeStruct((8, width), f32),
            jax.ShapeDtypeStruct((8, 2 * LANES), f32),
            jax.ShapeDtypeStruct((8, LANES), f32),
        ],
        grid_spec=pltpu.PrefetchScalarGridSpec(
            num_scalar_prefetch=2,
            grid=(chunks,),
            in_specs=[
                pl.BlockSpec((CHUNK, 2 * width), chunk_map),
                pl.BlockSpec((16, width), before_map(16, 1)),
                pl.BlockSpec((CHUNK, 3 * LANES), chunk_map),
                pl.BlockSpec((8, 3 * LANES), before_map(8, 0)),
                pl.BlockSpec((CHUNK, width), chunk_map),
                pl.BlockSpec((CHUNK, 2), chunk_map),
                pl.BlockSpec((None, HD, width), lambda i, *_: (chunks - 1 - i, 0, 0)),
                pl.BlockSpec((8, width), fixed),
                pl.BlockSpec((8, 2 * LANES), fixed),
                pl.BlockSpec((8, LANES), fixed),
            ],
            out_specs=[
                pl.BlockSpec((CHUNK, 2 * width + 3 * LANES), chunk_map),
                pl.BlockSpec((8, width), fixed),
                pl.BlockSpec((8, 2 * LANES), fixed),
                pl.BlockSpec((8, LANES), fixed),
            ],
            scratch_shapes=[
                pltpu.VMEM((HD, width), f32),
                pltpu.VMEM((8, width), f32),
                pltpu.VMEM((8, 2 * LANES), f32),
                pltpu.VMEM((8, LANES), f32),
                pltpu.VMEM((CHUNK, width), f32),
                pltpu.VMEM((CHUNK, width), f32),
                pltpu.VMEM((CHUNK, width), f32),
            ],
        ),
        compiler_params=pltpu.CompilerParams(vmem_limit_bytes=VMEM_LIMIT),
        cost_estimate=pl.CostEstimate(
            flops=24 * work, bytes_accessed=12 * rows * width, transcendentals=5 * rows * width
        ),
        name="mixer_backward",
    )(place, lengths, zx, zx, sd, sd, grad_scaled, stats, states, wide, narrow, rates)


def norm_back_kernel(parts, with_base, with_low, *refs):
    values, refs = refs[:parts], refs[parts:]
    grad, gain, refs = refs[0], refs[1], refs[2:]
    base, refs = (refs[0], refs[1:]) if with_base else (None, refs)
    outs, refs = refs[:parts], refs[parts:]
    low, refs = (refs[0], refs[1:]) if with_low else (None, refs)
    grad_gain = refs[0]

    @pl.when(pl.program_id(0) == 0)
    def _():
        grad_gain[...] = jnp.zeros_like(grad_gain)

    width = grad.shape[1]
    each = width // parts
    wide = [v[...].astype(f32) for v in values]
    squares = sum(jnp.sum(v * v, axis=1, keepdims=True) for v in wide)
    inv_root = lax.rsqrt(squares / width + norm_eps)
    units = [v * inv_root for v in wide]
    grads = [grad[:, i * each : (i + 1) * each] for i in range(parts)]
    grad_units = [g * gain[:, i * each : (i + 1) * each] for i, g in enumerate(grads)]
    cross = sum(jnp.sum(g * u, axis=1, keepdims=True) for g, u in zip(grad_units, units)) / width
    for i in range(parts):
        cols = slice(i * each, (i + 1) * each)
        grad_gain[0:1, cols] += jnp.sum(grads[i] * units[i], axis=0, keepdims=True)
        result = inv_root * (grad_units[i] - units[i] * cross)
        if with_base and i == 0:
            result = result + base[...].astype(f32)
        outs[i][...] = result
        if with_low and i == 0:
            low[...] = result.astype(bf16)


def norm_back(values, grad, gain, base=None, with_low=False):
    rows, width = grad.shape
    parts = len(values)
    block = math.gcd(rows, 64)
    row_spec = pl.BlockSpec((block, width // parts), lambda i: (i, 0))
    full_spec = pl.BlockSpec((block, width), lambda i: (i, 0))
    operands = list(values) + [grad, gain] + ([base] if base is not None else [])
    shapes = [jax.ShapeDtypeStruct((rows, width // parts), f32)] * parts
    shapes += [jax.ShapeDtypeStruct((rows, width // parts), bf16)] if with_low else []
    results = pl.pallas_call(
        functools.partial(norm_back_kernel, parts, base is not None, with_low),
        out_shape=shapes + [jax.ShapeDtypeStruct((8, width), f32)],
        grid=(rows // block,),
        in_specs=[row_spec] * parts
        + [full_spec, pl.BlockSpec((1, width), lambda i: (0, 0))]
        + ([row_spec] if base is not None else []),
        out_specs=[row_spec] * (parts + int(with_low)) + [pl.BlockSpec((8, width), lambda i: (0, 0))],
        compiler_params=pltpu.CompilerParams(vmem_limit_bytes=VMEM_LIMIT),
        cost_estimate=pl.CostEstimate(
            flops=20 * rows * width, bytes_accessed=14 * rows * width, transcendentals=rows
        ),
        name="norm_back",
    )(*operands)
    return list(results[:-1]) + [results[-1][0]]


def tie(value, others):
    return lax.optimization_barrier((value, others))[0]


def ring_pairs():
    tp = lax.axis_size("tp")
    return [(i, (i + 1) % tp) for i in range(tp)]


def hop(values):
    return lax.ppermute(values, "tp", ring_pairs())


class Halving:
    def __init__(self, values, name, sent_as=f32):
        self.values, self.name, self.sent_as = values, name, sent_as
        self.half = lax.axis_size(name) // 2

    def live(self):
        return self.half > 0

    def start(self):
        count, half = lax.axis_size(self.name), self.half
        upper = (lax.axis_index(self.name) & half) != 0
        low, high = self.values[:half], self.values[half:]
        self.kept = jnp.where(upper, high, low)
        sent = jnp.where(upper, low, high).astype(self.sent_as)
        self.moved = lax.ppermute(sent, self.name, [(i, i ^ half) for i in range(count)])

    def finish(self):
        self.values = self.kept + self.moved.astype(f32)
        self.half //= 2

    def result(self):
        while self.live():
            self.start()
            self.finish()
        return self.values[0]


class Doubling:
    def __init__(self, values, name, sent_as=f32):
        self.values, self.name, self.sent_as = values, name, sent_as
        self.step = 1

    def live(self):
        return self.step < lax.axis_size(self.name)

    def start(self):
        count, step = lax.axis_size(self.name), self.step
        self.moved = lax.ppermute(
            self.values.astype(self.sent_as), self.name, [(i, i ^ step) for i in range(count)]
        )

    def finish(self):
        self.values = self.values + self.moved.astype(f32)
        self.step *= 2

    def result(self):
        while self.live():
            self.start()
            self.finish()
        return self.values


def begin(tasks):
    live = [t for t in tasks if t.live()]
    for t in live:
        t.start()
    return live


def settle(moved, extras, live):
    moved, extras, arrived = lax.optimization_barrier((moved, extras, [t.moved for t in live]))
    for t, value in zip(live, arrived):
        t.moved = value
        t.finish()
    return moved, extras


def ring_gather(own, use, tasks=()):
    tp = lax.axis_size("tp")
    pieces, results = [own], []
    for p in range(tp):
        if p < tp - 1:
            moved = hop(pieces[p])
            live = begin(tasks)
        result = use(p, pieces[p])
        if p < tp - 1:
            moved, result = settle(moved, result, live)
            pieces.append(moved)
        results.append(result)
    return pieces, results


def ring_scatter(part, fill=(), tasks=()):
    tp = lax.axis_size("tp")
    fill = list(fill)
    filled = []
    total = part(1 % tp)
    for p in range(2, tp + 1):
        low = total.astype(bf16)
        moved = hop(low)
        live = begin(tasks)
        term = part(p % tp)
        extra = [fill.pop(0)(low, tasks)] if fill else []
        moved, (term, extra) = settle(moved, (term, extra), live)
        filled += extra
        total = moved.astype(f32) + term
    for thunk in fill:
        filled.append(thunk(low, tasks))
    return total, filled


def ring_both(own, work, last=None, fill=None, tasks=()):
    tp = lax.axis_size("tp")
    pieces, filled = [own], []
    moved = hop(own)
    live = begin(tasks)
    first = work(0, own)
    moved, first = settle(moved, first, live)
    total, ahead = None, None
    for p in range(1, tp):
        pieces.append(moved)
        if p < tp - 1:
            moved = hop(pieces[p])
        elif last is not None:
            pieces[p], result = lax.optimization_barrier((pieces[p], last(pieces)))
            filled.append(result)
        live = begin(tasks)
        term = work(p, pieces[p])
        if total is not None:
            ahead, term = lax.optimization_barrier((ahead, term))
            term = ahead.astype(f32) + term
        total = term
        low = total.astype(bf16)
        ahead = hop(low)
        if p < tp - 1:
            moved, low = settle(moved, low, live)
        elif fill is not None:
            ahead, result = settle(ahead, fill(low), live)
            filled.append(result)
        else:
            ahead, _ = settle(ahead, (), live)
    return pieces, ahead.astype(f32) + first, filled


def doubling_gather(values, name):
    count = lax.axis_size(name)
    here = lax.axis_index(name)
    step = 1
    while step < count:
        moved = lax.ppermute(values, name, [(i, i ^ step) for i in range(count)])
        upper = (here & step) != 0
        values = jnp.concatenate(
            [jnp.where(upper, moved, values), jnp.where(upper, values, moved)], axis=0
        )
        step *= 2
    return values


def inverse_root(values):
    return lax.rsqrt(jnp.mean(values * values, axis=1, keepdims=True) + norm_eps)


def gather(values, axis=0):
    return lax.all_gather(values, "fsdp", axis=axis, tiled=True)


def scatter(values, axis=0):
    return lax.psum_scatter(values, "fsdp", scatter_dimension=axis, tiled=True)


def local(
    hidden,
    embed,
    lengths,
    attention_norm_gain,
    query_key_value_weight,
    attention_adapter_down,
    attention_adapter_up,
    attention_output_weight,
    feedforward_norm_gain,
    gate_up_weight,
    feedforward_adapter_down,
    feedforward_adapter_up,
    down_weight,
    mixer_norm_gain,
    gate_inner_weight,
    state_input_weight,
    step_projection,
    inner_conv_taps,
    state_conv_taps,
    head_step_bias,
    decay_log_rate,
    inner_skip_gains,
    gated_norm_gain,
    mixer_output_weight,
    output_cotangent,
):
    tp = lax.axis_size("tp")
    fsdp = lax.axis_size("fsdp")
    share, width = hidden.shape
    rows = share * tp
    here = lax.axis_index("tp").astype(jnp.int32)
    place = here.reshape(1)
    lengths = lengths.reshape(-1)
    rank = attention_adapter_down.shape[2]
    head_cols = query_key_value_weight.shape[2]
    units_here = gate_up_weight.shape[2]
    inner_cols = gate_inner_weight.shape[2]
    mixer_heads = inner_cols // HD
    states = state_input_weight.shape[2]
    count = inner_conv_taps.shape[0]
    inner_total = inner_cols * tp

    def piece(values, p):
        return values[p * share : (p + 1) * share]

    weight_qkv = gather(
        jnp.concatenate(
            [query_key_value_weight[:, j, :] for j in range(3)]
            + [attention_adapter_down[:, j, :] for j in range(3)],
            axis=1,
        )
    )
    ups = doubling_gather(
        jnp.concatenate(
            [attention_adapter_up[:, j, :] for j in range(3)]
            + [feedforward_adapter_up[:, j, :] for j in range(2)],
            axis=1,
        ),
        "fsdp",
    )
    fc_up = ups[:, 3 * head_cols :]
    weight_o = gather(attention_output_weight, 1)
    weight_fc1 = gather(
        jnp.concatenate(
            [gate_up_weight[:, j, :] for j in range(2)] + [feedforward_adapter_down], axis=1
        )
    )
    weight_fc2 = gather(down_weight, 1)
    weight_zx = gather(
        jnp.concatenate(
            [gate_inner_weight[:, j, :] for j in range(2)]
            + [jnp.pad(state_input_weight[:, j, :], ((0, 0), (0, LANES - states))) for j in range(2)]
            + [jnp.pad(step_projection, ((0, 0), (0, LANES - mixer_heads)))],
            axis=1,
        )
    )

    weight_out = gather(mixer_output_weight, 1)

    small = [
        attention_norm_gain,
        feedforward_norm_gain,
        mixer_norm_gain,
        inner_conv_taps.reshape(-1),
        state_conv_taps.reshape(-1),
        inner_skip_gains.reshape(-1),
        gated_norm_gain.reshape(-1),
    ]
    sizes = [v.shape[0] for v in small]
    padding = -sum(sizes) % LANES
    packed = jnp.concatenate(small + [jnp.zeros((padding,), bf16)]).reshape(1, -1)
    spread = gather(packed).astype(f32)
    cuts = [sum(sizes[:i]) for i in range(len(sizes) + 1)]
    parts = [spread[:, cuts[i] : cuts[i + 1]] for i in range(len(sizes))]
    gain_attn, gain_mlp, gain_mixer = (parts[i].reshape(1, -1) for i in range(3))
    taps_x = parts[3].reshape(fsdp, count, mixer_heads, -1)
    taps_x = jnp.transpose(taps_x, (1, 2, 0, 3)).reshape(count, inner_cols)
    taps_s = parts[4].reshape(fsdp, count, 2, -1)
    taps_s = jnp.transpose(taps_s, (1, 2, 0, 3)).reshape(count, 2, states)
    skip = jnp.transpose(parts[5].reshape(fsdp, mixer_heads, -1), (1, 0, 2)).reshape(1, inner_cols)
    gain_gate = jnp.transpose(parts[6].reshape(fsdp, mixer_heads, -1), (1, 0, 2)).reshape(1, inner_cols)
    wide = jnp.concatenate([taps_x, skip, gain_gate, jnp.zeros((2, inner_cols), f32)], axis=0)
    narrow = jnp.pad(taps_s, ((0, 8 - count), (0, 0), (0, LANES - states))).reshape(8, 2 * LANES)
    rates = jnp.pad(
        jnp.stack([head_step_bias, decay_log_rate]), ((0, 6), (0, LANES - mixer_heads))
    )

    places = jnp.arange(rows, dtype=jnp.int32)
    ends = [jnp.sum(lengths[: i + 1]) for i in range(lengths.shape[0] - 1)]
    position = places - starts_of(places, ends)
    freqs = jnp.exp(jnp.arange(HDA // 2, dtype=f32) * (-2.0 * math.log(10000.0) / HDA))
    angles = position.astype(f32)[:, None] * freqs[None, :]
    cosine = jnp.cos(angles)
    sine = jnp.sin(angles)
    cosine = jnp.concatenate([cosine, cosine], axis=1)
    sine = jnp.concatenate([-sine, sine], axis=1)

    def norm_rows(pair):
        pair = [v.astype(f32) for v in pair]
        squares = sum(jnp.sum(v * v, axis=1, keepdims=True) for v in pair)
        inv_root = lax.rsqrt(squares / (2 * width) + norm_eps)
        return [
            (v * inv_root * gain_attn[:, i * width : (i + 1) * width]).astype(bf16)
            for i, v in enumerate(pair)
        ]

    raw, normed = [(hidden, embed)], []
    for p in range(1, tp):
        moved = tuple(hop(v) for v in raw[-1])
        if p > 1:
            normed.append(norm_rows(raw[p - 2]))
            moved = tie(moved, normed[-1])
        raw.append(moved)
    normed += [norm_rows(v) for v in raw[len(normed) :]]

    out_grad = [tie(output_cotangent, raw[-1][0])]
    normed_parts, projected = [], []
    for i in range(tp - 1):
        moved = hop(out_grad[-1])
        if i < tp - 2:
            low, high = (tp * i) // (tp - 2), (tp * (i + 1)) // (tp - 2)
            normed_parts.append(jnp.concatenate([jnp.concatenate(v, axis=1) for v in normed[low:high]], axis=0))
            projected.append(mm(normed_parts[-1], weight_qkv))
            moved = tie(moved, projected)
        else:
            attended, queries, keys, values = attention_forward(
                place, lengths, tp, projected, ups, head_cols, cosine, sine
            )
            moved = tie(moved, attended)
        out_grad.append(moved)
    lora_rows = jnp.concatenate([v[:, 3 * head_cols :].astype(bf16) for v in projected], axis=0)
    attended, lora_rows, out_grad[-1] = lax.optimization_barrier((attended, lora_rows, moved))
    out_grad_rows = jnp.concatenate(out_grad, axis=0)
    normed_rows = jnp.concatenate(normed_parts, axis=0)
    mixed, _ = ring_scatter(lambda p: mm(piece(attended, p), weight_o))

    mlp_root = inverse_root(mixed)
    gate_up, fc_mid, units = [], [], []

    def feed(p, rows_in):
        wide_rows = mm(rows_in, weight_fc1)
        middle = wide_rows[:, 2 * units_here :].astype(bf16)
        both = (wide_rows[:, : 2 * units_here] + mm(middle, fc_up)).astype(bf16)
        gate, up = both[:, :units_here].astype(f32), both[:, units_here:].astype(f32)
        unit = (jax.nn.gelu(gate) * up).astype(bf16)
        fc_mid.append(middle)
        gate_up.append(both)
        units.append(unit)
        return mm(unit, weight_fc2)

    mlp_in, branch, _ = ring_both((mixed * mlp_root * gain_mlp).astype(bf16), feed)
    residual = hidden.astype(f32) + mixed + branch

    mixer_root = inverse_root(residual)
    kept = []

    def mix(p, rows_in):
        result = mm(rows_in, weight_zx)
        if p == 0:
            kept.append(mm_nt(tie(out_grad_rows, result), weight_out).astype(bf16))
        elif p == 1:
            kept.append(jnp.concatenate(tie(units, result), axis=0))
            kept.append(jnp.concatenate(tie(mlp_in, result), axis=0))
        return (result, kept[-1])

    mixer_in, zxs = ring_gather((residual * mixer_root * gain_mixer).astype(bf16), mix)
    zxs = [v[0] for v in zxs]
    grad_scaled, units_rows, mlp_rows = kept
    mixer_rows = jnp.concatenate(mixer_in, axis=0)
    zx = jnp.concatenate([v[:, : 2 * inner_cols].astype(bf16) for v in zxs], axis=0)
    sd = jnp.concatenate([v[:, 2 * inner_cols :] for v in zxs], axis=0)
    gated, chunk_states = mixer_forward(place, lengths, tp, zx, sd, wide, narrow, rates)
    gated_wide = gated.astype(f32)
    sums = jnp.stack(
        [
            jnp.sum(gated_wide * gated_wide, axis=1),
            jnp.sum(grad_scaled.astype(f32) * gain_gate * gated_wide, axis=1),
        ],
        axis=0,
    )
    sums = jnp.roll(jnp.flip(sums.reshape(2, tp, share), axis=1), here + 1, axis=1)
    sums = lax.psum(sums, "tp")
    sums = jnp.flip(jnp.roll(sums, -(here + 1), axis=1), axis=1).reshape(2, rows)
    gate_root = lax.rsqrt(sums[0] / inner_total + norm_eps)
    stats = jnp.stack([gate_root, gate_root**3 * sums[1] / inner_total], axis=1)
    scaled = (gated_wide * gate_root[:, None] * gain_gate).astype(bf16)
    out_rows, stats = lax.optimization_barrier((mm(scaled, weight_out).astype(bf16), stats))
    out_terms = [piece(out_rows, p) for p in range(tp)]
    out = hop(out_terms[1 % tp])

    grad_all, grad_wide, grad_narrow, grad_rates = mixer_backward(
        place, lengths, tp, zx, sd, grad_scaled, stats, chunk_states, wide, narrow, rates
    )
    out, grad_all = lax.optimization_barrier((out, grad_all))
    out = out.astype(f32) + out_terms[2 % tp].astype(f32)

    def by_fsdp(values):
        lead = values.shape[:-1]
        cut = values.reshape(lead + (fsdp, values.shape[-1] // fsdp))
        return jnp.moveaxis(cut, -2, 0).reshape(fsdp, -1)

    def small_gradients(token):
        taps, bars, sums_r = tie((grad_wide, grad_narrow, grad_rates), token)
        return [
            by_fsdp(taps[:count].reshape(count, mixer_heads, HD)),
            by_fsdp(taps[4].reshape(mixer_heads, HD)),
            by_fsdp(taps[5].reshape(mixer_heads, HD)),
            jnp.broadcast_to(sums_r[:2, :mixer_heads].reshape(1, -1), (fsdp, 2 * mixer_heads)),
            by_fsdp(bars[:count].reshape(count, 2, LANES)[:, :, :states]),
        ]

    grad_mixer_in, (sum_w_out, sum_w_zx, small) = ring_scatter(
        lambda p: mm_nt(piece(grad_all, p), weight_zx),
        [
            lambda t, _: mm_tn(tie(scaled, t), out_grad_rows).astype(bf16),
            lambda t, _: mm_tn(tie(mixer_rows, t), grad_all).astype(bf16),
            lambda t, _: small_gradients(t),
        ],
    )
    sum_w_out = scatter(sum_w_out, 1)
    sum_w_zx = scatter(sum_w_zx)
    small_sizes = [v.shape[1] for v in small]
    small_cuts = [sum(small_sizes[:i]) for i in range(len(small_sizes) + 1)]
    small_task = Halving(jnp.concatenate(small, axis=1), "fsdp")
    grad_residual, grad_residual_low, grad_gain_mixer = norm_back(
        [residual], grad_mixer_in, gain_mixer, output_cotangent, True
    )

    grad_gate_up = []

    def feed_back(p, grad_rows):
        grad_units = mm_nt(grad_rows, weight_fc2)
        gate = gate_up[p][:, :units_here].astype(f32)
        up = gate_up[p][:, units_here:].astype(f32)
        raised, back = jax.vjp(jax.nn.gelu, gate)
        both = jnp.concatenate(
            [back(grad_units * up)[0].astype(bf16), (grad_units * raised).astype(bf16)], axis=1
        )
        both = jnp.concatenate([both, mm_nt(both, fc_up).astype(bf16)], axis=1)
        grad_gate_up.append(both)
        return mm_nt(both, weight_fc1)

    grad_branch, grad_mlp_in, (sum_w_fc2, sum_w_fc1) = ring_both(
        grad_residual_low,
        feed_back,
        lambda pieces: mm_tn(tie(units_rows, sum_w_out), jnp.concatenate(pieces, axis=0)).astype(bf16),
        lambda t: mm_tn(tie(mlp_rows, t), jnp.concatenate(grad_gate_up, axis=0)).astype(bf16),
        [small_task],
    )
    sum_w_fc2 = scatter(sum_w_fc2, 1)
    sum_w_fc1 = scatter(sum_w_fc1)
    grad_gate_up_rows = jnp.concatenate(grad_gate_up, axis=0)
    _, grad_mixed_low, grad_gain_mlp = norm_back([mixed], grad_mlp_in, gain_mlp, grad_residual, True)
    gain_task = Halving(
        jnp.concatenate([grad_gain_mixer.reshape(fsdp, -1), grad_gain_mlp.reshape(fsdp, -1)], axis=1), "fsdp"
    )

    fc_ups = []

    def attended_back(p, rows_in):
        result = mm_nt(rows_in, weight_o).astype(bf16)
        if p == 0:
            fc_ups.append(
                mm_tn(tie(jnp.concatenate(fc_mid, axis=0), rows_in), grad_gate_up_rows[:, : 2 * units_here])
            )
            result = tie(result, fc_ups[0])
        return result

    grad_mixed, grad_attended = ring_gather(tie(grad_mixed_low, sum_w_zx), attended_back, [gain_task])
    sum_w_o = mm_tn(tie(attended, sum_w_fc2), jnp.concatenate(grad_mixed, axis=0)).astype(bf16)
    grad_attended[-1] = tie(grad_attended[-1], sum_w_o)
    sum_w_o = scatter(sum_w_o, 1)
    out = hop(out.astype(bf16))
    grad_projected = attention_backward(
        place, lengths, queries, keys, values, ups, grad_attended, cosine, sine
    )
    out, grad_projected, sum_w_fc1 = lax.optimization_barrier((out, grad_projected, sum_w_fc1))
    out = out.astype(f32) + out_terms[3 % tp].astype(f32)
    sum_w_qkv = mm_tn(normed_rows, grad_projected).astype(bf16)
    grad_projected = tie(grad_projected, sum_w_qkv)
    sum_w_qkv = scatter(sum_w_qkv)

    at_t = 2 * inner_cols + 2 * LANES

    def finish_out(token):
        total = tie(out, token)
        for p in range(4, tp + 1):
            total = hop(total.astype(bf16)).astype(f32) + out_terms[p % tp].astype(f32)
        return residual + total

    def finish_adapters(token, tasks):
        rows_in = tie(lora_rows, token)
        grad_up = [
            mm_tn(
                rows_in[:, j * rank : (j + 1) * rank],
                grad_projected[:, j * head_cols : (j + 1) * head_cols],
            )
            for j in range(3)
        ]
        ups_grad = jnp.concatenate(grad_up + fc_ups, axis=1)
        tasks.append(Halving(ups_grad.reshape(fsdp, -1, ups_grad.shape[1]), "fsdp", bf16))
        shared = jnp.concatenate([small_task.result()[small_cuts[4] :], gain_task.result()])
        tasks.append(Doubling(shared, "tp"))
        return ups_grad, shared

    def finish_mixer(token, tasks):
        zx_sum, w_out, w_fc2 = tie((sum_w_zx, sum_w_out, sum_w_fc2), token)
        zx_sum = zx_sum.astype(f32)
        bc_sums.append(zx_sum[:, 2 * inner_cols : at_t])
        return (
            stacked(zx_sum, inner_cols, 2),
            zx_sum[:, at_t : at_t + mixer_heads],
            w_out.astype(f32),
            w_fc2.astype(f32),
        )

    def finish_feed(token, tasks):
        fc1_sum, w_o = tie((sum_w_fc1, sum_w_o), token)
        fc1_sum = fc1_sum.astype(f32)
        tasks.append(
            Doubling(jnp.concatenate([bc_sums[0], fc1_sum[:, 2 * units_here :]], axis=1), "tp", bf16)
        )
        return (
            stacked(fc1_sum, units_here, 2),
            w_o.astype(f32),
            finish_out(token),
        )

    def stacked(values, each, parts):
        values = jnp.stack([values[:, j * each : (j + 1) * each] for j in range(parts)], axis=1)
        return with_layout_constraint(values, Layout(major_to_minor=(0, 1, 2)))

    tasks, bc_sums = [], []
    pair = mm_nt(grad_projected[share : 3 * share], weight_qkv)
    grad_normed, (_, mixer_sums, feed_sums) = ring_scatter(
        lambda p: piece(pair, p - 1) if p in (1, 2) else mm_nt(piece(grad_projected, p), weight_qkv),
        [finish_adapters, finish_mixer, finish_feed],
        tasks,
    )
    grad_w_zx, grad_w_dt, grad_w_out, grad_w_fc2 = mixer_sums
    grad_w_fc1, grad_w_o, out = feed_sums
    grad_hidden, grad_embed, grad_gain_attn = norm_back([hidden, embed], grad_normed, gain_attn, grad_residual)
    gain_first = Halving(grad_gain_attn.reshape(fsdp, -1), "fsdp")
    grad_gain_attn = Halving(gain_first.result().reshape(tp, -1), "tp").result()
    grad_down = Halving(
        sum_w_qkv[:, 3 * head_cols :].astype(f32).reshape(tp, -1, 3 * rank), "tp", bf16
    ).result()
    grad_w_qkv = jnp.stack(
        [sum_w_qkv[:, j * head_cols : (j + 1) * head_cols].astype(f32) for j in range(3)], axis=1
    )
    small_sum = small_task.result()
    small_parts = [small_sum[small_cuts[i] : small_cuts[i + 1]] for i in range(len(small_sizes))]
    grad_ups, tail = tasks[0].result(), tasks[1].result()
    shared = tasks[2].result()
    tail_sizes = [small_sizes[4], width // fsdp, width // fsdp]
    tail_cuts = [sum(tail_sizes[:i]) for i in range(4)]
    grad_conv_bc, sum_gain_mixer, sum_gain_mlp = (
        tail[tail_cuts[i] : tail_cuts[i + 1]] for i in range(3)
    )
    sum_rates = small_parts[3].reshape(2, mixer_heads)
    return (
        out,
        grad_hidden,
        grad_embed,
        grad_gain_attn,
        grad_w_qkv,
        grad_down.reshape(-1, 3, rank),
        grad_ups[:, : 3 * head_cols].reshape(-1, 3, head_cols),
        grad_w_o,
        sum_gain_mlp,
        grad_w_fc1,
        shared[:, 2 * LANES :],
        grad_ups[:, 3 * head_cols :].reshape(-1, 2, units_here),
        grad_w_fc2,
        sum_gain_mixer,
        grad_w_zx,
        shared[:, : 2 * LANES].reshape(-1, 2, LANES)[:, :, :states],
        grad_w_dt,
        small_parts[0].reshape(count, mixer_heads, -1),
        grad_conv_bc.reshape(count, 2, -1),
        sum_rates[0],
        sum_rates[1],
        small_parts[1].reshape(mixer_heads, -1),
        small_parts[2].reshape(mixer_heads, -1),
        grad_w_out,
    )


def solution(mesh):
    placed = (
        P(("fsdp", "tp"), None),
        P(("fsdp", "tp"), None),
        P("fsdp", None),
        P("fsdp"),
        P("fsdp", None, "tp"),
        P("fsdp", None, None),
        P("fsdp", None, "tp"),
        P("tp", "fsdp"),
        P("fsdp"),
        P("fsdp", None, "tp"),
        P("fsdp", None),
        P("fsdp", None, "tp"),
        P("tp", "fsdp"),
        P("fsdp"),
        P("fsdp", None, "tp"),
        P("fsdp", None, None),
        P("fsdp", "tp"),
        P(None, "tp", "fsdp"),
        P(None, None, "fsdp"),
        P("tp"),
        P("tp"),
        P("tp", "fsdp"),
        P("tp", "fsdp"),
        P("tp", "fsdp"),
        P(("fsdp", "tp"), None),
    )
    return jax.shard_map(
        local,
        mesh=mesh,
        in_specs=placed,
        out_specs=(
            P(("fsdp", "tp"), None),
            P(("fsdp", "tp"), None),
            P(("fsdp", "tp"), None),
            P(("fsdp", "tp")),
            P("fsdp", None, "tp"),
            P(("fsdp", "tp"), None, None),
            P("fsdp", None, "tp"),
            P("tp", "fsdp"),
            P("fsdp"),
            P("fsdp", None, "tp"),
            P("fsdp", None),
            P("fsdp", None, "tp"),
            P("tp", "fsdp"),
            P("fsdp"),
            P("fsdp", None, "tp"),
            P("fsdp", None, None),
            P("fsdp", "tp"),
            P(None, "tp", "fsdp"),
            P(None, None, "fsdp"),
            P("tp"),
            P("tp"),
            P("tp", "fsdp"),
            P("tp", "fsdp"),
            P("tp", "fsdp"),
        ),
        check_vma=False,
    )
```

```python
import functools
import math

import jax
import jax.numpy as jnp
from jax import lax
from jax.experimental import pallas as pl
from jax.experimental.layout import Layout, with_layout_constraint
from jax.experimental.pallas import tpu as pltpu
from jax.sharding import PartitionSpec as P

HDA = 128
HD = 64
LANES = 128
CHUNK = 128

norm_eps = 1e-05
f32 = jnp.float32
bf16 = jnp.bfloat16
HIGHEST = lax.Precision.HIGHEST
VMEM_LIMIT = 56 * 1024 * 1024


def mm(left, right):
    return jnp.dot(left, right, preferred_element_type=f32)


def mm_nt(left, right):
    return lax.dot_general(left, right, (((1,), (1,)), ((), ())), preferred_element_type=f32)


def mm_tn(left, right):
    return lax.dot_general(left, right, (((0,), (0,)), ((), ())), preferred_element_type=f32)


def starts_of(index, ends):
    start = jnp.zeros_like(index)
    for end in ends:
        start = jnp.where(index >= end, end, start)
    return start


def ends_of(lengths_ref):
    ends = []
    end = jnp.int32(0)
    for i in range(lengths_ref.shape[0] - 1):
        end = end + lengths_ref[i]
        ends.append(end)
    return ends


def iota(shape, axis):
    return lax.broadcasted_iota(jnp.int32, shape, axis)


def attention_forward_kernel(
    tp,
    parts,
    place_ref,
    lengths_ref,
    cosine_ref,
    sine_ref,
    q_up,
    k_up,
    v_up,
    *refs,
):
    pieces = refs[: 4 * parts]
    attended_ref, q_ref, k_ref, v_ref, held = refs[4 * parts :]
    rows = q_ref.shape[0]
    share = rows // tp
    rank = q_up.shape[0]
    here = place_ref[0]
    ends = ends_of(lengths_ref)
    for p in range(tp):
        owner = lax.rem(here - p + tp, tp)
        part = pl.ds(pl.multiple_of(owner * share, share), share)
        cosine, sine = cosine_ref[part, :], sine_ref[part, :]
        at = p * share
        source = 0
        while at >= pieces[4 * source].shape[0]:
            at -= pieces[4 * source].shape[0]
            source += 1
        mine = slice(at, at + share)
        for j, (up, target) in enumerate(((q_up, q_ref), (k_up, k_ref), (v_up, v_ref))):
            low = pieces[4 * source + 3][mine, j * rank : (j + 1) * rank].astype(bf16)
            value = pieces[4 * source + j][mine, :] + mm(low, up[...])
            if j < 2:
                value = value * cosine + pltpu.roll(value, HDA // 2, 1) * sine
            target[part, :] = value.astype(bf16)
    block = min(256, rows)
    scale = HDA ** (-0.5)
    for at in range(0, rows, block):
        upto = at + block
        scores = mm_nt(q_ref[at:upto, :], k_ref[:upto, :]) * scale
        query = at + iota((block, 1), 0)
        key = iota((1, upto), 1)
        seen = (key <= query) & (key >= starts_of(query, ends))
        scores = jnp.where(seen, scores, -1e30)
        raised = jnp.exp(scores - jnp.max(scores, axis=1, keepdims=True))
        probs = (raised * (1.0 / jnp.sum(raised, axis=1, keepdims=True))).astype(bf16)
        held[at:upto, :] = mm(probs, v_ref[:upto, :]).astype(bf16)
    for p in range(tp):
        owner = lax.rem(here - p + tp, tp)
        part = pl.ds(pl.multiple_of(owner * share, share), share)
        attended_ref[p * share : (p + 1) * share, :] = held[part, :]


def attention_forward(place, lengths, tp, projected, ups, columns, cosine, sine):
    rows = sum(v.shape[0] for v in projected)
    heads = columns // HDA
    rank = ups.shape[0]
    table_spec = pl.BlockSpec((rows, HDA), lambda h, *_: (0, 0))

    def head_spec(j, height=rows):
        return pl.BlockSpec((height, HDA), lambda h, *_: (0, j * heads + h))

    work = heads * rows * rows * HDA
    return pl.pallas_call(
        functools.partial(attention_forward_kernel, tp, len(projected)),
        out_shape=[jax.ShapeDtypeStruct((rows, columns), bf16)] * 4,
        grid_spec=pltpu.PrefetchScalarGridSpec(
            num_scalar_prefetch=2,
            grid=(heads,),
            in_specs=[table_spec, table_spec]
            + [head_spec(j, rank) for j in range(3)]
            + [
                pl.BlockSpec((v.shape[0], 3 * rank), lambda h, *_: (0, columns // rank))
                if j == 3
                else head_spec(j, v.shape[0])
                for v in projected
                for j in range(4)
            ],
            out_specs=[head_spec(0)] * 4,
            scratch_shapes=[pltpu.VMEM((rows, HDA), bf16)],
        ),
        compiler_params=pltpu.CompilerParams(vmem_limit_bytes=VMEM_LIMIT),
        cost_estimate=pl.CostEstimate(
            flops=4 * work, bytes_accessed=20 * rows * columns, transcendentals=heads * rows * rows
        ),
        name="attention_forward",
    )(place, lengths, cosine, sine, ups, ups, ups, *[v for v in projected for _ in range(4)])


def attention_backward_kernel(
    tp,
    heads,
    place_ref,
    lengths_ref,
    cosine_ref,
    sine_ref,
    q_ref,
    k_ref,
    v_ref,
    q_up,
    k_up,
    v_up,
    *refs,
):
    grad_in = refs[:tp]
    out_ref, held, dq, dk, dv, lora = refs[tp:]
    rows = q_ref.shape[0]
    share = rows // tp
    rank = q_up.shape[0]
    here = place_ref[0]
    head = pl.program_id(0)
    ends = ends_of(lengths_ref)
    for p in range(tp):
        owner = lax.rem(here - p + tp, tp)
        part = pl.ds(pl.multiple_of(owner * share, share), share)
        held[part, :] = grad_in[p][...]
    dk[...] = jnp.zeros_like(dk)
    dv[...] = jnp.zeros_like(dv)

    @pl.when(head == 0)
    def _():
        lora[...] = jnp.zeros_like(lora)

    block = min(256, rows)
    scale = HDA ** (-0.5)
    for at in range(0, rows, block):
        upto = at + block
        query_rows = q_ref[at:upto, :]
        grad_rows = held[at:upto, :]
        scores = mm_nt(k_ref[:upto, :], query_rows) * scale
        query = at + iota((1, block), 1)
        key = iota((upto, 1), 0)
        seen = (key <= query) & (key >= starts_of(query, ends))
        scores = jnp.where(seen, scores, -1e30)
        raised = jnp.exp(scores - jnp.max(scores, axis=0, keepdims=True))
        probs = raised * (1.0 / jnp.sum(raised, axis=0, keepdims=True))
        grad_probs = mm_nt(v_ref[:upto, :], grad_rows)
        cross = jnp.sum(probs * grad_probs, axis=0, keepdims=True)
        grad_scores = (probs * (grad_probs - cross)).astype(bf16)
        dv[:upto, :] += mm(probs.astype(bf16), grad_rows)
        dk[:upto, :] += mm(grad_scores, query_rows)
        dq[at:upto, :] = mm_tn(grad_scores, k_ref[:upto, :])
    for p in range(tp):
        owner = lax.rem(here - p + tp, tp)
        part = pl.ds(pl.multiple_of(owner * share, share), share)
        cosine, sine = cosine_ref[part, :], sine_ref[part, :]
        mine = slice(p * share, (p + 1) * share)
        for j, (source, up) in enumerate(((dq, q_up), (dk, k_up), (dv, v_up))):
            value = source[part, :]
            if j < 2:
                value = value * scale
                value = value * cosine - pltpu.roll(value, HDA // 2, 1) * sine
            low = value.astype(bf16)
            at = pl.multiple_of((j * heads + head) * HDA, HDA)
            out_ref[mine, pl.ds(at, HDA)] = low
            lora[mine, j * rank : (j + 1) * rank] += mm_nt(low, up[...])

    @pl.when(head == heads - 1)
    def _():
        out_ref[:, 3 * heads * HDA :] = lora[...].astype(bf16)


def attention_backward(place, lengths, queries, keys, values, ups, pieces, cosine, sine):
    tp = len(pieces)
    share, columns = pieces[0].shape
    rows = share * tp
    heads = columns // HDA
    rank = ups.shape[0]
    piece_spec = pl.BlockSpec((share, HDA), lambda h, *_: (0, h))
    table_spec = pl.BlockSpec((rows, HDA), lambda h, *_: (0, 0))
    head_spec = pl.BlockSpec((rows, HDA), lambda h, *_: (0, h))

    def up_spec(j):
        return pl.BlockSpec((rank, HDA), lambda h, *_: (0, j * heads + h))

    total = 3 * columns + 3 * rank
    work = heads * rows * rows * HDA
    return pl.pallas_call(
        functools.partial(attention_backward_kernel, tp, heads),
        out_shape=jax.ShapeDtypeStruct((rows, total), bf16),
        grid_spec=pltpu.PrefetchScalarGridSpec(
            num_scalar_prefetch=2,
            grid=(heads,),
            in_specs=[table_spec, table_spec]
            + [head_spec] * 3
            + [up_spec(j) for j in range(3)]
            + [piece_spec] * tp,
            out_specs=pl.BlockSpec((rows, total), lambda h, *_: (0, 0)),
            scratch_shapes=[pltpu.VMEM((rows, HDA), bf16)]
            + [pltpu.VMEM((rows, HDA), f32)] * 3
            + [pltpu.VMEM((rows, 3 * rank), f32)],
        ),
        compiler_params=pltpu.CompilerParams(vmem_limit_bytes=VMEM_LIMIT),
        cost_estimate=pl.CostEstimate(
            flops=10 * work, bytes_accessed=14 * rows * columns, transcendentals=heads * rows * rows
        ),
        name="attention_backward",
    )(place, lengths, cosine, sine, queries, keys, values, ups, ups, ups, *pieces)


def conv_rows(extended, taps, position):
    count = 4
    rows = extended.shape[0] - 8
    total = None
    for k in range(count):
        moved = extended[8 - k : 8 - k + rows, :]
        if k:
            moved = jnp.where(position >= k, moved, 0.0)
        term = taps[count - 1 - k : count - k, :] * moved
        total = term if total is None else total + term
    return total


def conv_back(extended, taps, position):
    count = 4
    rows = extended.shape[0] - 8
    total = None
    for k in range(count):
        kept = jnp.where(position >= k, extended, 0.0) if k else extended
        term = taps[count - 1 - k : count - k, :] * kept[k : k + rows, :]
        total = term if total is None else total + term
    return total


def taps_back(extended, grad, position, target):
    count = 4
    rows = extended.shape[0] - 8
    for k in range(count):
        moved = extended[8 - k : 8 - k + rows, :]
        if k:
            moved = jnp.where(position >= k, moved, 0.0)
        at = count - 1 - k
        target[at : at + 1, :] += jnp.sum(grad * moved, axis=0, keepdims=True)


def silu_grad(value, gate):
    return gate * (1.0 + value * (1.0 - gate))


class Chunk:
    def __init__(self, c0, ends, zx, before, sd, sd_before, wide, narrow, rates):
        rows = zx.shape[0]
        width = zx.shape[1] // 2
        self.rows, self.width = rows, width
        index = c0 + iota((rows, 1), 0)
        start = starts_of(index, ends)
        self.index, self.start = index, start
        self.position = index - start
        last_start = starts_of(c0 + rows - 1, ends)
        self.z = zx[:, :width].astype(f32)
        self.x_ext = jnp.concatenate(
            [before[...].astype(f32)[8:16, :], zx[:, width:].astype(f32)], axis=0
        )
        self.s_ext = jnp.concatenate([sd_before[:, : 2 * LANES], sd[:, : 2 * LANES]], axis=0)
        self.pre = conv_rows(self.x_ext, wide, self.position)
        self.gate_x = jax.nn.sigmoid(self.pre)
        self.xc = self.pre * self.gate_x
        self.pre_s = conv_rows(self.s_ext, narrow, self.position)
        self.gate_s = jax.nn.sigmoid(self.pre_s)
        sc = self.pre_s * self.gate_s
        self.b_low = sc[:, :HD].astype(bf16)
        self.c_low = sc[:, LANES : LANES + HD].astype(bf16)
        self.raw = sd[:, 2 * LANES : 3 * LANES] + rates[0:1, :]
        self.step = jnp.maximum(self.raw, 0.0) + jnp.log1p(jnp.exp(-jnp.abs(self.raw)))
        self.rate = jnp.exp(rates[1:2, :])
        row, col = iota((rows, rows), 0), iota((rows, rows), 1)
        below = (col <= row).astype(f32)
        self.cum = jnp.dot(below, -self.step * self.rate, precision=HIGHEST, preferred_element_type=f32)
        self.cum_t = self.cum.T
        self.allowed = (col <= row) & ((c0 + col) >= start)
        self.inner = jnp.where(self.allowed, mm_nt(self.c_low, self.b_low), 0.0)
        last = self.cum[rows - 1 : rows, :]
        self.into = jnp.exp(self.cum) * (start < c0).astype(f32)
        self.onto = jnp.exp(last - self.cum) * (index >= last_start).astype(f32)
        self.decay = jnp.exp(last) * (last_start < c0).astype(f32)
        self.low_half = iota((1, LANES), 1) < HD

    def pair(self, table, i):
        return jnp.where(self.low_half, table[:, 2 * i : 2 * i + 1], table[:, 2 * i + 1 : 2 * i + 2])

    def spread(self, h):
        return jnp.exp(jnp.minimum(self.cum[:, h : h + 1] - self.cum_t[h : h + 1, :], 0.0))


def mixer_forward_kernel(
    place_ref, lengths_ref, zx, before, sd, sd_before, wide, narrow, rates, gated, states, state
):
    rows = zx.shape[0]
    c0 = pl.program_id(0) * rows
    ends = ends_of(lengths_ref)

    @pl.when(pl.program_id(0) == 0)
    def _():
        state[...] = jnp.zeros_like(state)

    v = Chunk(c0, ends, zx, before, sd, sd_before, wide, narrow, rates)
    state_low = state[...].astype(bf16)
    states[...] = state_low
    for i in range(v.width // LANES):
        cols = slice(i * LANES, (i + 1) * LANES)
        xc = v.xc[:, cols]
        xs = v.pair(v.step, i) * xc
        xs_low = xs.astype(bf16)
        first = (v.spread(2 * i) * v.inner).astype(bf16)
        second = (v.spread(2 * i + 1) * v.inner).astype(bf16)
        y = jnp.where(v.low_half, mm(first, xs_low), mm(second, xs_low))
        y = y + v.pair(v.into, i) * mm(v.c_low, state_low[:, cols])
        y = y + wide[4:5, cols] * xc
        z = v.z[:, cols]
        gated[:, cols] = (y * z * jax.nn.sigmoid(z)).astype(bf16)
        state[:, cols] = v.pair(v.decay, i) * state[:, cols] + mm_tn(
            v.b_low, (v.pair(v.onto, i) * xs).astype(bf16)
        )


def split_sum(values, ones):
    high = values.astype(bf16)
    low = (values - high.astype(f32)).astype(bf16)
    return mm(high, ones) + mm(low, ones)


def mixer_backward_kernel(
    chunks,
    place_ref,
    lengths_ref,
    zx,
    before,
    sd,
    sd_before,
    grad_scaled,
    stats,
    states,
    wide,
    narrow,
    rates,
    grad_all,
    grad_wide,
    grad_narrow,
    grad_rates,
    grad_state,
    next_pre,
    next_pre_s,
    carry,
    products,
    directs,
    grad_pre,
):
    rows = zx.shape[0]
    turn = pl.program_id(0)
    c0 = (chunks - 1 - turn) * rows
    ends = ends_of(lengths_ref)

    @pl.when(turn == 0)
    def _():
        for ref in (grad_state, next_pre, next_pre_s, carry, grad_wide, grad_narrow, grad_rates):
            ref[...] = jnp.zeros_like(ref)

    v = Chunk(c0, ends, zx, before, sd, sd_before, wide, narrow, rates)
    width = v.width
    root, pull = stats[:, 0:1], stats[:, 1:2]
    grad_inner = jnp.zeros((rows, rows), f32)
    grad_b = jnp.zeros((rows, HD), f32)
    grad_c = jnp.zeros((rows, HD), f32)
    for i in range(width // LANES):
        cols = slice(i * LANES, (i + 1) * LANES)
        xc = v.xc[:, cols]
        step = v.pair(v.step, i)
        xs = step * xc
        xs_low = xs.astype(bf16)
        spread_a, spread_b = v.spread(2 * i), v.spread(2 * i + 1)
        first = (spread_a * v.inner).astype(bf16)
        second = (spread_b * v.inner).astype(bf16)
        state_low = states[:, cols]
        into, onto = v.pair(v.into, i), v.pair(v.onto, i)
        y = jnp.where(v.low_half, mm(first, xs_low), mm(second, xs_low))
        y = y + into * mm(v.c_low, state_low)
        skip, gain = wide[4:5, cols], wide[5:6, cols]
        whole = y + skip * xc
        z = v.z[:, cols]
        gate = jax.nn.sigmoid(z)
        gated = whole * z * gate
        incoming = grad_scaled[:, cols].astype(f32)
        rooted = incoming * root
        grad_wide[5:6, cols] += jnp.sum(rooted * gated, axis=0, keepdims=True)
        grad_gated = rooted * gain - gated * pull
        grad_y = grad_gated * z * gate
        grad_all[:, cols] = (grad_gated * whole * silu_grad(z, gate)).astype(bf16)
        grad_wide[4:5, cols] += jnp.sum(grad_y * xc, axis=0, keepdims=True)
        low = grad_y.astype(bf16)
        low_a = jnp.where(v.low_half, grad_y, 0.0).astype(bf16)
        low_b = jnp.where(v.low_half, 0.0, grad_y).astype(bf16)
        grad_inner = grad_inner + spread_a * mm_nt(low_a, xs_low) + spread_b * mm_nt(low_b, xs_low)
        grad_end = grad_state[:, cols]
        grad_end_low = grad_end.astype(bf16)
        grad_xs = jnp.where(v.low_half, mm_tn(first, low), mm_tn(second, low))
        grad_xs = grad_xs + onto * mm(v.b_low, grad_end_low)
        into_y = (into * grad_y).astype(bf16)
        onto_x = (onto * xs).astype(bf16)
        grad_b = grad_b + mm_nt(onto_x, grad_end_low)
        grad_c = grad_c + mm_nt(into_y, state_low)
        grad_state[:, cols] = v.pair(v.decay, i) * grad_end + mm_tn(v.c_low, into_y)
        products[:, cols] = low.astype(f32) * y - xs_low.astype(f32) * grad_xs
        directs[:, cols] = xc * grad_xs
        grad_xc = step * grad_xs + skip * grad_y
        grad_pre[:, cols] = grad_xc * silu_grad(v.pre[:, cols], v.gate_x[:, cols])
    grad_inner = jnp.where(v.allowed, grad_inner, 0.0).astype(bf16)
    grad_b = grad_b + mm_tn(grad_inner, v.c_low)
    grad_c = grad_c + mm(grad_inner, v.b_low)

    lane, head = iota((width, LANES), 0), iota((width, LANES), 1)
    ones = ((lane >= head * HD) & (lane < head * HD + HD)).astype(bf16)
    grad_cum = split_sum(products[...], ones)
    direct = split_sum(directs[...], ones)
    row, col = iota((rows, rows), 0), iota((rows, rows), 1)
    col_start = starts_of(c0 + iota((1, rows), 1), ends)
    above = ((col >= row) & (col_start <= c0 + row)).astype(f32)
    next_start = starts_of(c0 + rows, ends)
    reaches = (v.index >= next_start).astype(f32)
    after = jnp.dot(above, grad_cum, precision=HIGHEST, preferred_element_type=f32) + reaches * carry[0:1, :]
    flux = jnp.sum(grad_state[...] * states[...].astype(f32), axis=0, keepdims=True)
    carry[...] = split_sum(jnp.broadcast_to(flux, (8, width)), ones)
    grad_log = -v.step * v.rate * after
    grad_raw = (direct - v.rate * after) * jax.nn.sigmoid(v.raw)
    grad_rates[0:1, :] += jnp.sum(grad_raw, axis=0, keepdims=True)
    grad_rates[1:2, :] += jnp.sum(grad_log, axis=0, keepdims=True)

    index_ext = c0 + iota((rows + 8, 1), 0)
    position_ext = index_ext - starts_of(index_ext, ends)
    taps_back(v.x_ext, grad_pre[...], v.position, grad_wide)
    extended = jnp.concatenate([grad_pre[...], next_pre[...]], axis=0)
    grad_all[:, width : 2 * width] = conv_back(extended, wide, position_ext).astype(bf16)
    next_pre[...] = grad_pre[0:8, :]

    blank = jnp.zeros((rows, LANES - HD), f32)
    grad_sc = jnp.concatenate([grad_b, blank, grad_c, blank], axis=1)
    grad_pre_s = grad_sc * silu_grad(v.pre_s, v.gate_s)
    taps_back(v.s_ext, grad_pre_s, v.position, grad_narrow)
    extended_s = jnp.concatenate([grad_pre_s, next_pre_s[...]], axis=0)
    grad_all[:, 2 * width : 2 * width + 2 * LANES] = conv_back(extended_s, narrow, position_ext).astype(bf16)
    next_pre_s[...] = grad_pre_s[0:8, :]
    grad_all[:, 2 * width + 2 * LANES :] = grad_raw.astype(bf16)


def mixer_specs(tp, rows, width, order):
    share = rows // tp
    per_share = share // CHUNK

    def here(place, c):
        owner = lax.div(c, per_share)
        piece = lax.rem(place[0] - owner + tp, tp)
        return piece * per_share + lax.rem(c, per_share)

    def chunk_map(i, place, lengths):
        return (here(place, order(i)), 0)

    def before_map(unit, column):
        def index(i, place, lengths):
            c = order(i)
            previous = jnp.maximum(c - 1, 0)
            return (here(place, previous) * (CHUNK // unit) + CHUNK // unit - 1, column)

        return index

    def fixed(i, place, lengths):
        return (0, 0)

    return chunk_map, before_map, fixed


def mixer_forward(place, lengths, tp, zx, sd, wide, narrow, rates):
    rows, width = zx.shape[0], zx.shape[1] // 2
    chunks = rows // CHUNK
    chunk_map, before_map, fixed = mixer_specs(tp, rows, width, lambda i: i)
    work = rows * width * CHUNK
    return pl.pallas_call(
        mixer_forward_kernel,
        out_shape=[
            jax.ShapeDtypeStruct((rows, width), bf16),
            jax.ShapeDtypeStruct((chunks, HD, width), bf16),
        ],
        grid_spec=pltpu.PrefetchScalarGridSpec(
            num_scalar_prefetch=2,
            grid=(chunks,),
            in_specs=[
                pl.BlockSpec((CHUNK, 2 * width), chunk_map),
                pl.BlockSpec((16, width), before_map(16, 1)),
                pl.BlockSpec((CHUNK, 3 * LANES), chunk_map),
                pl.BlockSpec((8, 3 * LANES), before_map(8, 0)),
                pl.BlockSpec((8, width), fixed),
                pl.BlockSpec((8, 2 * LANES), fixed),
                pl.BlockSpec((8, LANES), fixed),
            ],
            out_specs=[
                pl.BlockSpec((CHUNK, width), chunk_map),
                pl.BlockSpec((None, HD, width), lambda i, *_: (i, 0, 0)),
            ],
            scratch_shapes=[pltpu.VMEM((HD, width), f32)],
        ),
        compiler_params=pltpu.CompilerParams(vmem_limit_bytes=VMEM_LIMIT),
        cost_estimate=pl.CostEstimate(
            flops=8 * work, bytes_accessed=8 * rows * width, transcendentals=4 * rows * width
        ),
        name="mixer_forward",
    )(place, lengths, zx, zx, sd, sd, wide, narrow, rates)


def mixer_backward(place, lengths, tp, zx, sd, grad_scaled, stats, states, wide, narrow, rates):
    rows, width = zx.shape[0], zx.shape[1] // 2
    chunks = rows // CHUNK
    chunk_map, before_map, fixed = mixer_specs(tp, rows, width, lambda i: chunks - 1 - i)
    work = rows * width * CHUNK
    return pl.pallas_call(
        functools.partial(mixer_backward_kernel, chunks),
        out_shape=[
            jax.ShapeDtypeStruct((rows, 2 * width + 3 * LANES), bf16),
            jax.ShapeDtypeStruct((8, width), f32),
            jax.ShapeDtypeStruct((8, 2 * LANES), f32),
            jax.ShapeDtypeStruct((8, LANES), f32),
        ],
        grid_spec=pltpu.PrefetchScalarGridSpec(
            num_scalar_prefetch=2,
            grid=(chunks,),
            in_specs=[
                pl.BlockSpec((CHUNK, 2 * width), chunk_map),
                pl.BlockSpec((16, width), before_map(16, 1)),
                pl.BlockSpec((CHUNK, 3 * LANES), chunk_map),
                pl.BlockSpec((8, 3 * LANES), before_map(8, 0)),
                pl.BlockSpec((CHUNK, width), chunk_map),
                pl.BlockSpec((CHUNK, 2), chunk_map),
                pl.BlockSpec((None, HD, width), lambda i, *_: (chunks - 1 - i, 0, 0)),
                pl.BlockSpec((8, width), fixed),
                pl.BlockSpec((8, 2 * LANES), fixed),
                pl.BlockSpec((8, LANES), fixed),
            ],
            out_specs=[
                pl.BlockSpec((CHUNK, 2 * width + 3 * LANES), chunk_map),
                pl.BlockSpec((8, width), fixed),
                pl.BlockSpec((8, 2 * LANES), fixed),
                pl.BlockSpec((8, LANES), fixed),
            ],
            scratch_shapes=[
                pltpu.VMEM((HD, width), f32),
                pltpu.VMEM((8, width), f32),
                pltpu.VMEM((8, 2 * LANES), f32),
                pltpu.VMEM((8, LANES), f32),
                pltpu.VMEM((CHUNK, width), f32),
                pltpu.VMEM((CHUNK, width), f32),
                pltpu.VMEM((CHUNK, width), f32),
            ],
        ),
        compiler_params=pltpu.CompilerParams(vmem_limit_bytes=VMEM_LIMIT),
        cost_estimate=pl.CostEstimate(
            flops=24 * work, bytes_accessed=12 * rows * width, transcendentals=5 * rows * width
        ),
        name="mixer_backward",
    )(place, lengths, zx, zx, sd, sd, grad_scaled, stats, states, wide, narrow, rates)


def norm_back_kernel(parts, with_base, with_low, with_gain, *refs):
    values, refs = refs[:parts], refs[parts:]
    grad, gain, refs = refs[0], refs[1], refs[2:]
    base, refs = (refs[0], refs[1:]) if with_base else (None, refs)
    outs, refs = refs[:parts], refs[parts:]
    low, refs = (refs[0], refs[1:]) if with_low else (None, refs)
    if with_gain:
        grad_gain = refs[0]

        @pl.when(pl.program_id(0) == 0)
        def _():
            grad_gain[...] = jnp.zeros_like(grad_gain)

    width = grad.shape[1]
    each = width // parts
    wide = [v[...].astype(f32) for v in values]
    squares = sum(jnp.sum(v * v, axis=1, keepdims=True) for v in wide)
    inv_root = lax.rsqrt(squares / width + norm_eps)
    units = [v * inv_root for v in wide]
    grads = [grad[:, i * each : (i + 1) * each] for i in range(parts)]
    grad_units = [g * gain[:, i * each : (i + 1) * each] for i, g in enumerate(grads)]
    cross = sum(jnp.sum(g * u, axis=1, keepdims=True) for g, u in zip(grad_units, units)) / width
    for i in range(parts):
        cols = slice(i * each, (i + 1) * each)
        if with_gain:
            grad_gain[0:1, cols] += jnp.sum(grads[i] * units[i], axis=0, keepdims=True)
        result = inv_root * (grad_units[i] - units[i] * cross)
        if with_base and i == 0:
            result = result + base[...].astype(f32)
        outs[i][...] = result
        if with_low and i == 0:
            low[...] = result.astype(bf16)


def norm_back(values, grad, gain, base=None, with_low=False, with_gain=True):
    rows, width = grad.shape
    parts = len(values)
    block = math.gcd(rows, 64)
    row_spec = pl.BlockSpec((block, width // parts), lambda i: (i, 0))
    full_spec = pl.BlockSpec((block, width), lambda i: (i, 0))
    operands = list(values) + [grad, gain] + ([base] if base is not None else [])
    shapes = [jax.ShapeDtypeStruct((rows, width // parts), f32)] * parts
    shapes += [jax.ShapeDtypeStruct((rows, width // parts), bf16)] if with_low else []
    results = pl.pallas_call(
        functools.partial(norm_back_kernel, parts, base is not None, with_low, with_gain),
        out_shape=shapes + [jax.ShapeDtypeStruct((8, width), f32)] * int(with_gain),
        grid=(rows // block,),
        in_specs=[row_spec] * parts
        + [full_spec, pl.BlockSpec((1, width), lambda i: (0, 0))]
        + ([row_spec] if base is not None else []),
        out_specs=[row_spec] * (parts + int(with_low))
        + [pl.BlockSpec((8, width), lambda i: (0, 0))] * int(with_gain),
        compiler_params=pltpu.CompilerParams(vmem_limit_bytes=VMEM_LIMIT),
        cost_estimate=pl.CostEstimate(
            flops=20 * rows * width, bytes_accessed=14 * rows * width, transcendentals=rows
        ),
        name="norm_back",
    )(*operands)
    return list(results[:-1]) + [results[-1][0]] if with_gain else list(results)


def tie(value, others):
    return lax.optimization_barrier((value, others))[0]


def after(value, token):
    return value if token is None else tie(value, token)


def ring_pairs():
    tp = lax.axis_size("tp")
    return [(i, (i + 1) % tp) for i in range(tp)]


def hop(values):
    return lax.ppermute(values, "tp", ring_pairs())


class Halving:
    def __init__(self, values, name, sent_as=f32):
        self.values, self.name, self.sent_as = values, name, sent_as
        self.half = lax.axis_size(name) // 2

    def live(self):
        return self.half > 0

    def start(self):
        count, half = lax.axis_size(self.name), self.half
        upper = (lax.axis_index(self.name) & half) != 0
        low, high = self.values[:half], self.values[half:]
        self.kept = jnp.where(upper, high, low)
        sent = jnp.where(upper, low, high).astype(self.sent_as)
        self.moved = lax.ppermute(sent, self.name, [(i, i ^ half) for i in range(count)])

    def finish(self):
        self.values = self.kept + self.moved.astype(f32)
        self.half //= 2

    def result(self):
        while self.live():
            self.start()
            self.finish()
        return self.values[0]


class Doubling:
    def __init__(self, values, name, sent_as=f32):
        self.values, self.name, self.sent_as = values, name, sent_as
        self.step = 1

    def live(self):
        return self.step < lax.axis_size(self.name)

    def start(self):
        count, step = lax.axis_size(self.name), self.step
        self.moved = lax.ppermute(
            self.values.astype(self.sent_as), self.name, [(i, i ^ step) for i in range(count)]
        )

    def finish(self):
        self.values = self.values + self.moved.astype(f32)
        self.step *= 2

    def result(self):
        while self.live():
            self.start()
            self.finish()
        return self.values


def begin(tasks):
    live = [t for t in tasks if t.live()]
    for t in live:
        t.start()
    return live


def settle(moved, extras, live):
    moved, extras, arrived = lax.optimization_barrier((moved, extras, [t.moved for t in live]))
    for t, value in zip(live, arrived):
        t.moved = value
        t.finish()
    return moved, extras


def ring_gather(own, use, tasks=()):
    tp = lax.axis_size("tp")
    pieces, results = [own], []
    for p in range(tp):
        if p < tp - 1:
            moved = hop(pieces[p])
            live = begin(tasks)
        result = use(p, pieces[p])
        if p < tp - 1:
            moved, result = settle(moved, result, live)
            pieces.append(moved)
        results.append(result)
    return pieces, results


def ring_scatter(part, fill=(), tasks=()):
    tp = lax.axis_size("tp")
    fill = list(fill)
    filled = []
    total = part(1 % tp, None)
    for p in range(2, tp + 1):
        low = total.astype(bf16)
        moved = hop(low)
        live = begin(tasks)
        term = part(p % tp, low)
        extra = [fill.pop(0)(low, tasks)] if fill else []
        moved, (term, extra) = settle(moved, (term, extra), live)
        filled += extra
        total = moved.astype(f32) + term
    for thunk in fill:
        filled.append(thunk(low, tasks))
    return total, filled


def ring_both(own, work, last=None, fill=None, tasks=()):
    tp = lax.axis_size("tp")
    pieces, filled = [own], []
    moved = hop(own)
    live = begin(tasks)
    first = work(0, own)
    moved, _ = settle(moved, (), live)
    total, ahead = None, None
    for p in range(1, tp):
        pieces.append(moved)
        if p < tp - 1:
            moved = hop(pieces[p])
        elif last is not None:
            pieces[p], result = lax.optimization_barrier((pieces[p], last(pieces)))
            filled.append(result)
        live = begin(tasks)
        term = work(p, pieces[p])
        if total is not None:
            ahead, term = lax.optimization_barrier((ahead, term))
            term = ahead.astype(f32) + term
        total = term
        low = total.astype(bf16)
        ahead = hop(low)
        if p < tp - 1:
            moved, (low, first) = settle(moved, (low, first), live)
        elif fill is not None:
            ahead, result = settle(ahead, fill(low), live)
            filled.append(result)
        else:
            ahead, _ = settle(ahead, (), live)
    return pieces, ahead.astype(f32) + first, filled


def doubling_gather(values, name):
    count = lax.axis_size(name)
    here = lax.axis_index(name)
    step = 1
    while step < count:
        moved = lax.ppermute(values, name, [(i, i ^ step) for i in range(count)])
        upper = (here & step) != 0
        values = jnp.concatenate(
            [jnp.where(upper, moved, values), jnp.where(upper, values, moved)], axis=0
        )
        step *= 2
    return values


def inverse_root(values):
    return lax.rsqrt(jnp.mean(values * values, axis=1, keepdims=True) + norm_eps)


def gather(values, axis=0):
    return lax.all_gather(values, "fsdp", axis=axis, tiled=True)


def scatter(values, axis=0):
    return lax.psum_scatter(values, "fsdp", scatter_dimension=axis, tiled=True)


def local(
    hidden,
    embed,
    lengths,
    attention_norm_gain,
    query_key_value_weight,
    attention_adapter_down,
    attention_adapter_up,
    attention_output_weight,
    feedforward_norm_gain,
    gate_up_weight,
    feedforward_adapter_down,
    feedforward_adapter_up,
    down_weight,
    mixer_norm_gain,
    gate_inner_weight,
    state_input_weight,
    step_projection,
    inner_conv_taps,
    state_conv_taps,
    head_step_bias,
    decay_log_rate,
    inner_skip_gains,
    gated_norm_gain,
    mixer_output_weight,
    output_cotangent,
):
    tp = lax.axis_size("tp")
    fsdp = lax.axis_size("fsdp")
    share, width = hidden.shape
    rows = share * tp
    here = lax.axis_index("tp").astype(jnp.int32)
    place = here.reshape(1)
    lengths = lengths.reshape(-1)
    rank = attention_adapter_down.shape[2]
    head_cols = query_key_value_weight.shape[2]
    units_here = gate_up_weight.shape[2]
    inner_cols = gate_inner_weight.shape[2]
    mixer_heads = inner_cols // HD
    states = state_input_weight.shape[2]
    count = inner_conv_taps.shape[0]
    inner_total = inner_cols * tp

    def piece(values, p):
        return values[p * share : (p + 1) * share]

    own_qkv = jnp.concatenate(
        [query_key_value_weight[:, j, :] for j in range(3)]
        + [attention_adapter_down[:, j, :] for j in range(3)],
        axis=1,
    )
    weight_qkv = gather(own_qkv)
    first_hop = tuple(hop(v) for v in (hidden, embed))

    small = [
        attention_norm_gain,
        feedforward_norm_gain,
        mixer_norm_gain,
        inner_conv_taps.reshape(-1),
        state_conv_taps.reshape(-1),
        inner_skip_gains.reshape(-1),
        gated_norm_gain.reshape(-1),
    ]
    sizes = [v.shape[0] for v in small]
    padding = -sum(sizes) % LANES
    packed = jnp.concatenate(small + [jnp.zeros((padding,), bf16)]).reshape(1, -1)
    spread = gather(packed).astype(f32)
    cuts = [sum(sizes[:i]) for i in range(len(sizes) + 1)]
    parts = [spread[:, cuts[i] : cuts[i + 1]] for i in range(len(sizes))]
    gain_attn, gain_mlp, gain_mixer = (parts[i].reshape(1, -1) for i in range(3))
    taps_x = parts[3].reshape(fsdp, count, mixer_heads, -1)
    taps_x = jnp.transpose(taps_x, (1, 2, 0, 3)).reshape(count, inner_cols)
    taps_s = parts[4].reshape(fsdp, count, 2, -1)
    taps_s = jnp.transpose(taps_s, (1, 2, 0, 3)).reshape(count, 2, states)
    skip = jnp.transpose(parts[5].reshape(fsdp, mixer_heads, -1), (1, 0, 2)).reshape(1, inner_cols)
    gain_gate = jnp.transpose(parts[6].reshape(fsdp, mixer_heads, -1), (1, 0, 2)).reshape(1, inner_cols)
    wide = jnp.concatenate([taps_x, skip, gain_gate, jnp.zeros((2, inner_cols), f32)], axis=0)
    narrow = jnp.pad(taps_s, ((0, 8 - count), (0, 0), (0, LANES - states))).reshape(8, 2 * LANES)
    rates = jnp.pad(
        jnp.stack([head_step_bias, decay_log_rate]), ((0, 6), (0, LANES - mixer_heads))
    )

    places = jnp.arange(rows, dtype=jnp.int32)
    ends = [jnp.sum(lengths[: i + 1]) for i in range(lengths.shape[0] - 1)]
    position = places - starts_of(places, ends)
    freqs = jnp.exp(jnp.arange(HDA // 2, dtype=f32) * (-2.0 * math.log(10000.0) / HDA))
    angles = position.astype(f32)[:, None] * freqs[None, :]
    cosine = jnp.cos(angles)
    sine = jnp.sin(angles)
    cosine = jnp.concatenate([cosine, cosine], axis=1)
    sine = jnp.concatenate([-sine, sine], axis=1)

    own_fc1 = jnp.concatenate(
        [gate_up_weight[:, j, :] for j in range(2)] + [feedforward_adapter_down], axis=1
    )
    own_zx = jnp.concatenate(
        [gate_inner_weight[:, j, :] for j in range(2)]
        + [jnp.pad(state_input_weight[:, j, :], ((0, 0), (0, LANES - states))) for j in range(2)]
        + [jnp.pad(step_projection, ((0, 0), (0, LANES - mixer_heads)))],
        axis=1,
    )
    weight_o = gather(attention_output_weight, 1)
    weight_fc1 = gather(own_fc1)
    weight_fc2 = gather(down_weight, 1)
    weight_zx = gather(own_zx)
    weight_out = gather(mixer_output_weight, 1)

    def norm_rows(pair):
        pair = [v.astype(f32) for v in pair]
        squares = sum(jnp.sum(v * v, axis=1, keepdims=True) for v in pair)
        inv_root = lax.rsqrt(squares / (2 * width) + norm_eps)
        return [
            (v * inv_root * gain_attn[:, i * width : (i + 1) * width]).astype(bf16)
            for i, v in enumerate(pair)
        ]

    raw, normed = [(hidden, embed), first_hop], []
    for p in range(2, tp):
        moved = tuple(hop(v) for v in raw[-1])
        normed.append(norm_rows(raw[p - 2]))
        raw.append(tie(moved, normed[-1]))
    normed += [norm_rows(v) for v in raw[len(normed) :]]

    own_ups = jnp.concatenate(
        [attention_adapter_up[:, j, :] for j in range(3)]
        + [feedforward_adapter_up[:, j, :] for j in range(2)],
        axis=1,
    )
    ups = doubling_gather(tie(own_ups, raw[-2]), "fsdp")
    fc_up = ups[:, 3 * head_cols :]
    out_grad = [tie(output_cotangent, raw[-1])]
    normed_parts, projected = [], []
    for i in range(tp - 1):
        moved = hop(out_grad[-1])
        if i < tp - 2:
            low, high = (tp * i) // (tp - 2), (tp * (i + 1)) // (tp - 2)
            normed_parts.append(jnp.concatenate([jnp.concatenate(v, axis=1) for v in normed[low:high]], axis=0))
            projected.append(mm(normed_parts[-1], weight_qkv))
            moved = tie(moved, projected)
        else:
            attended, queries, keys, values = attention_forward(
                place, lengths, tp, projected, ups, head_cols, cosine, sine
            )
            moved = tie(moved, attended)
        out_grad.append(moved)
    lora_rows = jnp.concatenate([v[:, 3 * head_cols :].astype(bf16) for v in projected], axis=0)
    attended, lora_rows, out_grad[-1] = lax.optimization_barrier((attended, lora_rows, moved))
    out_grad_rows = jnp.concatenate(out_grad, axis=0)
    normed_rows = jnp.concatenate(normed_parts, axis=0)
    mixed, _ = ring_scatter(lambda p, t: mm(piece(after(attended, t), p), weight_o))

    mlp_root = inverse_root(mixed)
    gate_up, fc_mid, units = [], [], []

    def feed(p, rows_in):
        wide_rows = mm(rows_in, weight_fc1)
        middle = wide_rows[:, 2 * units_here :].astype(bf16)
        both = (wide_rows[:, : 2 * units_here] + mm(middle, fc_up)).astype(bf16)
        gate, up = both[:, :units_here].astype(f32), both[:, units_here:].astype(f32)
        unit = (jax.nn.gelu(gate) * up).astype(bf16)
        fc_mid.append(middle)
        gate_up.append(both)
        units.append(unit)
        return mm(unit, weight_fc2)

    mlp_in, branch, _ = ring_both((mixed * mlp_root * gain_mlp).astype(bf16), feed)
    residual = hidden.astype(f32) + mixed + branch

    mixer_root = inverse_root(residual)
    kept = []

    def mix(p, rows_in):
        result = mm(rows_in, weight_zx)
        if p == 0:
            kept.append(mm_nt(tie(out_grad_rows, result), weight_out).astype(bf16))
        elif p == 1:
            kept.append(jnp.concatenate(tie(units, result), axis=0))
            kept.append(jnp.concatenate(tie(mlp_in, result), axis=0))
        return (result, kept[-1])

    mixer_in, zxs = ring_gather((residual * mixer_root * gain_mixer).astype(bf16), mix)
    zxs = [v[0] for v in zxs]
    grad_scaled, units_rows, mlp_rows = kept
    mixer_rows = jnp.concatenate(mixer_in, axis=0)
    zx = jnp.concatenate([v[:, : 2 * inner_cols].astype(bf16) for v in zxs], axis=0)
    sd = jnp.concatenate([v[:, 2 * inner_cols :] for v in zxs], axis=0)
    gated, chunk_states = mixer_forward(place, lengths, tp, zx, sd, wide, narrow, rates)
    gated_wide = gated.astype(f32)
    sums = jnp.stack(
        [
            jnp.sum(gated_wide * gated_wide, axis=1),
            jnp.sum(grad_scaled.astype(f32) * gain_gate * gated_wide, axis=1),
        ],
        axis=0,
    )
    sums = jnp.roll(jnp.flip(sums.reshape(2, tp, share), axis=1), here + 1, axis=1)
    sums = lax.psum(sums, "tp")
    sums = jnp.flip(jnp.roll(sums, -(here + 1), axis=1), axis=1).reshape(2, rows)
    gate_root = lax.rsqrt(sums[0] / inner_total + norm_eps)
    stats = jnp.stack([gate_root, gate_root**3 * sums[1] / inner_total], axis=1)
    scaled = (gated_wide * gate_root[:, None] * gain_gate).astype(bf16)
    out_rows, stats = lax.optimization_barrier((mm(scaled, weight_out).astype(bf16), stats))
    out_terms = [piece(out_rows, p) for p in range(tp)]
    out = hop(out_terms[1 % tp])

    grad_all, grad_wide, grad_narrow, grad_rates = mixer_backward(
        place, lengths, tp, zx, sd, grad_scaled, stats, chunk_states, wide, narrow, rates
    )
    out, grad_all = lax.optimization_barrier((out, grad_all))
    out = out.astype(f32) + out_terms[2 % tp].astype(f32)

    def by_fsdp(values):
        lead = values.shape[:-1]
        cut = values.reshape(lead + (fsdp, values.shape[-1] // fsdp))
        return jnp.moveaxis(cut, -2, 0).reshape(fsdp, -1)

    def small_gradients(token):
        taps, bars, sums_r = tie((grad_wide, grad_narrow, grad_rates), token)
        return [
            by_fsdp(taps[:count].reshape(count, mixer_heads, HD)),
            by_fsdp(taps[4].reshape(mixer_heads, HD)),
            by_fsdp(taps[5].reshape(mixer_heads, HD)),
            jnp.broadcast_to(sums_r[:2, :mixer_heads].reshape(1, -1), (fsdp, 2 * mixer_heads)),
            by_fsdp(bars[:count].reshape(count, 2, LANES)[:, :, :states]),
        ]

    grad_mixer_in, (sum_w_out, sum_w_zx, small) = ring_scatter(
        lambda p, t: mm_nt(piece(after(grad_all, t), p), weight_zx),
        [
            lambda t, _: mm_tn(tie(scaled, t), out_grad_rows).astype(bf16),
            lambda t, _: mm_tn(tie(mixer_rows, t), grad_all).astype(bf16),
            lambda t, _: small_gradients(t),
        ],
    )
    sum_w_out = scatter(sum_w_out, 1)
    sum_w_zx = scatter(sum_w_zx)
    small_sizes = [v.shape[1] for v in small]
    small_cuts = [sum(small_sizes[:i]) for i in range(len(small_sizes) + 1)]
    small_task = Halving(jnp.concatenate(small, axis=1), "fsdp")
    grad_residual, grad_residual_low, grad_gain_mixer = norm_back(
        [residual], grad_mixer_in, gain_mixer, output_cotangent, True
    )

    grad_gate_up = []

    def feed_back(p, grad_rows):
        grad_units = mm_nt(grad_rows, weight_fc2)
        gate = gate_up[p][:, :units_here].astype(f32)
        up = gate_up[p][:, units_here:].astype(f32)
        raised, back = jax.vjp(jax.nn.gelu, gate)
        both = jnp.concatenate(
            [back(grad_units * up)[0].astype(bf16), (grad_units * raised).astype(bf16)], axis=1
        )
        both = jnp.concatenate([both, mm_nt(both, fc_up).astype(bf16)], axis=1)
        grad_gate_up.append(both)
        return mm_nt(both, weight_fc1)

    grad_branch, grad_mlp_in, (sum_w_fc2, sum_w_fc1) = ring_both(
        grad_residual_low,
        feed_back,
        lambda pieces: mm_tn(tie(units_rows, sum_w_out), jnp.concatenate(pieces, axis=0)).astype(bf16),
        lambda t: mm_tn(tie(mlp_rows, t), jnp.concatenate(grad_gate_up, axis=0)).astype(bf16),
        [small_task],
    )
    sum_w_fc2 = scatter(sum_w_fc2, 1)
    sum_w_fc1 = scatter(sum_w_fc1)
    grad_gate_up_rows = jnp.concatenate(grad_gate_up, axis=0)
    _, grad_mixed_low, grad_gain_mlp = norm_back([mixed], grad_mlp_in, gain_mlp, grad_residual, True)
    gain_task = Halving(
        jnp.concatenate([grad_gain_mixer.reshape(fsdp, -1), grad_gain_mlp.reshape(fsdp, -1)], axis=1), "fsdp"
    )

    fc_ups = []

    def attended_back(p, rows_in):
        result = mm_nt(rows_in, weight_o).astype(bf16)
        if p == 0:
            fc_ups.append(
                mm_tn(tie(jnp.concatenate(fc_mid, axis=0), rows_in), grad_gate_up_rows[:, : 2 * units_here])
            )
            result = tie(result, fc_ups[0])
        return result

    grad_mixed, grad_attended = ring_gather(tie(grad_mixed_low, sum_w_zx), attended_back, [gain_task])
    sum_w_o = mm_tn(tie(attended, sum_w_fc2), jnp.concatenate(grad_mixed, axis=0)).astype(bf16)
    grad_attended[-1] = tie(grad_attended[-1], sum_w_o)
    sum_w_o = scatter(sum_w_o, 1)
    out = hop(out.astype(bf16))
    grad_projected = attention_backward(
        place, lengths, queries, keys, values, ups, grad_attended, cosine, sine
    )
    out, grad_projected, sum_w_fc1 = lax.optimization_barrier((out, grad_projected, sum_w_fc1))
    out = out.astype(f32) + out_terms[3 % tp].astype(f32)
    out = hop(out.astype(bf16))
    sum_w_qkv = mm_tn(normed_rows, grad_projected).astype(bf16)
    out, sum_w_qkv, grad_projected = lax.optimization_barrier((out, sum_w_qkv, grad_projected))
    sum_w_qkv = scatter(sum_w_qkv)

    at_t = 2 * inner_cols + 2 * LANES

    def finish_out(token):
        total = tie(out, token).astype(f32) + out_terms[4 % tp].astype(f32)
        for p in range(5, tp + 1):
            total = hop(total.astype(bf16)).astype(f32) + out_terms[p % tp].astype(f32)
        return residual + total

    def finish_adapters(token, tasks):
        rows_in = tie(lora_rows, token)
        grad_up = [
            mm_tn(
                rows_in[:, j * rank : (j + 1) * rank],
                grad_projected[:, j * head_cols : (j + 1) * head_cols],
            )
            for j in range(3)
        ]
        ups_grad = jnp.concatenate(grad_up + fc_ups, axis=1)
        tasks.append(Halving(ups_grad.reshape(fsdp, -1, ups_grad.shape[1]), "fsdp", bf16))
        shared = jnp.concatenate([small_task.result()[small_cuts[4] :], gain_task.result()])
        tasks.append(Doubling(shared, "tp"))
        return ups_grad, shared

    def finish_mixer(token, tasks):
        zx_sum, w_out, w_fc2 = tie((sum_w_zx, sum_w_out, sum_w_fc2), token)
        zx_sum = zx_sum.astype(f32)
        bc_sums.append(zx_sum[:, 2 * inner_cols : at_t])
        return (
            stacked(zx_sum, inner_cols, 2),
            zx_sum[:, at_t : at_t + mixer_heads],
            w_out.astype(f32),
            w_fc2.astype(f32),
        )

    def finish_feed(token, tasks):
        fc1_sum, w_o = tie((sum_w_fc1, sum_w_o), token)
        fc1_sum = fc1_sum.astype(f32)
        tasks.append(
            Doubling(jnp.concatenate([bc_sums[0], fc1_sum[:, 2 * units_here :]], axis=1), "tp", bf16)
        )
        return (
            stacked(fc1_sum, units_here, 2),
            w_o.astype(f32),
            finish_out(token),
        )

    def stacked(values, each, parts):
        values = jnp.stack([values[:, j * each : (j + 1) * each] for j in range(parts)], axis=1)
        return with_layout_constraint(values, Layout(major_to_minor=(0, 1, 2)))

    tasks, bc_sums = [], []
    pair = mm_nt(grad_projected[share : 3 * share], weight_qkv)
    grad_normed, (_, mixer_sums, feed_sums) = ring_scatter(
        lambda p, t: piece(pair, p - 1)
        if p in (1, 2)
        else mm_nt(piece(after(grad_projected, t), p), weight_qkv),
        [finish_adapters, finish_mixer, finish_feed],
        tasks,
    )
    grad_w_zx, grad_w_dt, grad_w_out, grad_w_fc2 = mixer_sums
    grad_w_fc1, grad_w_o, out = feed_sums
    grad_hidden, grad_embed = norm_back(
        [hidden, embed], grad_normed, gain_attn, grad_residual, with_gain=False
    )
    gain_rows = jnp.sum(sum_w_qkv.astype(f32) * own_qkv.astype(f32), axis=1)
    gain_rows = gain_rows / attention_norm_gain.astype(f32)
    down_task = Halving(sum_w_qkv[:, 3 * head_cols :].astype(f32).reshape(tp, -1, 3 * rank), "tp", bf16)
    gain_last = Halving(gain_rows.reshape(tp, -1), "tp")
    while down_task.live():
        for t in begin([down_task, gain_last]):
            t.finish()
    grad_down, grad_gain_attn = down_task.result(), gain_last.result()
    grad_w_qkv = jnp.stack(
        [sum_w_qkv[:, j * head_cols : (j + 1) * head_cols].astype(f32) for j in range(3)], axis=1
    )
    small_sum = small_task.result()
    small_parts = [small_sum[small_cuts[i] : small_cuts[i + 1]] for i in range(len(small_sizes))]
    grad_ups, tail = tasks[0].result(), tasks[1].result()
    shared = tasks[2].result()
    tail_sizes = [small_sizes[4], width // fsdp, width // fsdp]
    tail_cuts = [sum(tail_sizes[:i]) for i in range(4)]
    grad_conv_bc, sum_gain_mixer, sum_gain_mlp = (
        tail[tail_cuts[i] : tail_cuts[i + 1]] for i in range(3)
    )
    sum_rates = small_parts[3].reshape(2, mixer_heads)
    return (
        out,
        grad_hidden,
        grad_embed,
        grad_gain_attn,
        grad_w_qkv,
        grad_down.reshape(-1, 3, rank),
        grad_ups[:, : 3 * head_cols].reshape(-1, 3, head_cols),
        grad_w_o,
        sum_gain_mlp,
        grad_w_fc1,
        shared[:, 2 * LANES :],
        grad_ups[:, 3 * head_cols :].reshape(-1, 2, units_here),
        grad_w_fc2,
        sum_gain_mixer,
        grad_w_zx,
        shared[:, : 2 * LANES].reshape(-1, 2, LANES)[:, :, :states],
        grad_w_dt,
        small_parts[0].reshape(count, mixer_heads, -1),
        grad_conv_bc.reshape(count, 2, -1),
        sum_rates[0],
        sum_rates[1],
        small_parts[1].reshape(mixer_heads, -1),
        small_parts[2].reshape(mixer_heads, -1),
        grad_w_out,
    )


def solution(mesh):
    placed = (
        P(("fsdp", "tp"), None),
        P(("fsdp", "tp"), None),
        P("fsdp", None),
        P("fsdp"),
        P("fsdp", None, "tp"),
        P("fsdp", None, None),
        P("fsdp", None, "tp"),
        P("tp", "fsdp"),
        P("fsdp"),
        P("fsdp", None, "tp"),
        P("fsdp", None),
        P("fsdp", None, "tp"),
        P("tp", "fsdp"),
        P("fsdp"),
        P("fsdp", None, "tp"),
        P("fsdp", None, None),
        P("fsdp", "tp"),
        P(None, "tp", "fsdp"),
        P(None, None, "fsdp"),
        P("tp"),
        P("tp"),
        P("tp", "fsdp"),
        P("tp", "fsdp"),
        P("tp", "fsdp"),
        P(("fsdp", "tp"), None),
    )
    return jax.shard_map(
        local,
        mesh=mesh,
        in_specs=placed,
        out_specs=(
            P(("fsdp", "tp"), None),
            P(("fsdp", "tp"), None),
            P(("fsdp", "tp"), None),
            P(("fsdp", "tp")),
            P("fsdp", None, "tp"),
            P(("fsdp", "tp"), None, None),
            P("fsdp", None, "tp"),
            P("tp", "fsdp"),
            P("fsdp"),
            P("fsdp", None, "tp"),
            P("fsdp", None),
            P("fsdp", None, "tp"),
            P("tp", "fsdp"),
            P("fsdp"),
            P("fsdp", None, "tp"),
            P("fsdp", None, None),
            P("fsdp", "tp"),
            P(None, "tp", "fsdp"),
            P(None, None, "fsdp"),
            P("tp"),
            P("tp"),
            P("tp", "fsdp"),
            P("tp", "fsdp"),
            P("tp", "fsdp"),
        ),
        check_vma=False,
    )
```

```python
import functools
import math

import jax
import jax.numpy as jnp
from jax import lax
from jax.experimental import pallas as pl
from jax.experimental.layout import Layout, with_layout_constraint
from jax.experimental.pallas import tpu as pltpu
from jax.sharding import PartitionSpec as P

HDA = 128
HD = 64
LANES = 128
CHUNK = 128

norm_eps = 1e-05
f32 = jnp.float32
bf16 = jnp.bfloat16
HIGHEST = lax.Precision.HIGHEST
VMEM_LIMIT = 56 * 1024 * 1024


def mm(left, right):
    return jnp.dot(left, right, preferred_element_type=f32)


def mm_nt(left, right):
    return lax.dot_general(left, right, (((1,), (1,)), ((), ())), preferred_element_type=f32)


def mm_tn(left, right):
    return lax.dot_general(left, right, (((0,), (0,)), ((), ())), preferred_element_type=f32)


def starts_of(index, ends):
    start = jnp.zeros_like(index)
    for end in ends:
        start = jnp.where(index >= end, end, start)
    return start


def ends_of(lengths_ref):
    ends = []
    end = jnp.int32(0)
    for i in range(lengths_ref.shape[0] - 1):
        end = end + lengths_ref[i]
        ends.append(end)
    return ends


def iota(shape, axis):
    return lax.broadcasted_iota(jnp.int32, shape, axis)


def attention_forward_kernel(
    tp,
    parts,
    place_ref,
    lengths_ref,
    cosine_ref,
    sine_ref,
    q_up,
    k_up,
    v_up,
    *refs,
):
    pieces = refs[: 4 * parts]
    attended_ref, q_ref, k_ref, v_ref, held = refs[4 * parts :]
    rows = q_ref.shape[0]
    share = rows // tp
    rank = q_up.shape[0]
    here = place_ref[0]
    ends = ends_of(lengths_ref)
    for p in range(tp):
        owner = lax.rem(here - p + tp, tp)
        part = pl.ds(pl.multiple_of(owner * share, share), share)
        cosine, sine = cosine_ref[part, :], sine_ref[part, :]
        at = p * share
        source = 0
        while at >= pieces[4 * source].shape[0]:
            at -= pieces[4 * source].shape[0]
            source += 1
        mine = slice(at, at + share)
        for j, (up, target) in enumerate(((q_up, q_ref), (k_up, k_ref), (v_up, v_ref))):
            low = pieces[4 * source + 3][mine, j * rank : (j + 1) * rank].astype(bf16)
            value = pieces[4 * source + j][mine, :] + mm(low, up[...])
            if j < 2:
                value = value * cosine + pltpu.roll(value, HDA // 2, 1) * sine
            target[part, :] = value.astype(bf16)
    block = min(256, rows)
    scale = HDA ** (-0.5)
    for at in range(0, rows, block):
        upto = at + block
        scores = mm_nt(q_ref[at:upto, :], k_ref[:upto, :]) * scale
        query = at + iota((block, 1), 0)
        key = iota((1, upto), 1)
        seen = (key <= query) & (key >= starts_of(query, ends))
        scores = jnp.where(seen, scores, -1e30)
        raised = jnp.exp(scores - jnp.max(scores, axis=1, keepdims=True))
        probs = (raised * (1.0 / jnp.sum(raised, axis=1, keepdims=True))).astype(bf16)
        held[at:upto, :] = mm(probs, v_ref[:upto, :]).astype(bf16)
    for p in range(tp):
        owner = lax.rem(here - p + tp, tp)
        part = pl.ds(pl.multiple_of(owner * share, share), share)
        attended_ref[p * share : (p + 1) * share, :] = held[part, :]


def attention_forward(place, lengths, tp, projected, ups, columns, cosine, sine):
    rows = sum(v.shape[0] for v in projected)
    heads = columns // HDA
    rank = ups.shape[0]
    table_spec = pl.BlockSpec((rows, HDA), lambda h, *_: (0, 0))

    def head_spec(j, height=rows):
        return pl.BlockSpec((height, HDA), lambda h, *_: (0, j * heads + h))

    work = heads * rows * rows * HDA
    return pl.pallas_call(
        functools.partial(attention_forward_kernel, tp, len(projected)),
        out_shape=[jax.ShapeDtypeStruct((rows, columns), bf16)] * 4,
        grid_spec=pltpu.PrefetchScalarGridSpec(
            num_scalar_prefetch=2,
            grid=(heads,),
            in_specs=[table_spec, table_spec]
            + [head_spec(j, rank) for j in range(3)]
            + [
                pl.BlockSpec((v.shape[0], 3 * rank), lambda h, *_: (0, columns // rank))
                if j == 3
                else head_spec(j, v.shape[0])
                for v in projected
                for j in range(4)
            ],
            out_specs=[head_spec(0)] * 4,
            scratch_shapes=[pltpu.VMEM((rows, HDA), bf16)],
        ),
        compiler_params=pltpu.CompilerParams(vmem_limit_bytes=VMEM_LIMIT),
        cost_estimate=pl.CostEstimate(
            flops=4 * work, bytes_accessed=20 * rows * columns, transcendentals=heads * rows * rows
        ),
        name="attention_forward",
    )(place, lengths, cosine, sine, ups, ups, ups, *[v for v in projected for _ in range(4)])


def attention_backward_kernel(
    tp,
    heads,
    place_ref,
    lengths_ref,
    cosine_ref,
    sine_ref,
    q_ref,
    k_ref,
    v_ref,
    q_up,
    k_up,
    v_up,
    *refs,
):
    grad_in = refs[:tp]
    out_ref, held, dq, dk, dv, lora = refs[tp:]
    rows = q_ref.shape[0]
    share = rows // tp
    rank = q_up.shape[0]
    here = place_ref[0]
    head = pl.program_id(0)
    ends = ends_of(lengths_ref)
    for p in range(tp):
        owner = lax.rem(here - p + tp, tp)
        part = pl.ds(pl.multiple_of(owner * share, share), share)
        held[part, :] = grad_in[p][...]
    dk[...] = jnp.zeros_like(dk)
    dv[...] = jnp.zeros_like(dv)

    @pl.when(head == 0)
    def _():
        lora[...] = jnp.zeros_like(lora)

    block = min(256, rows)
    scale = HDA ** (-0.5)
    for at in range(0, rows, block):
        upto = at + block
        query_rows = q_ref[at:upto, :]
        grad_rows = held[at:upto, :]
        scores = mm_nt(k_ref[:upto, :], query_rows) * scale
        query = at + iota((1, block), 1)
        key = iota((upto, 1), 0)
        seen = (key <= query) & (key >= starts_of(query, ends))
        scores = jnp.where(seen, scores, -1e30)
        raised = jnp.exp(scores - jnp.max(scores, axis=0, keepdims=True))
        probs = raised * (1.0 / jnp.sum(raised, axis=0, keepdims=True))
        grad_probs = mm_nt(v_ref[:upto, :], grad_rows)
        cross = jnp.sum(probs * grad_probs, axis=0, keepdims=True)
        grad_scores = (probs * (grad_probs - cross)).astype(bf16)
        dv[:upto, :] += mm(probs.astype(bf16), grad_rows)
        dk[:upto, :] += mm(grad_scores, query_rows)
        dq[at:upto, :] = mm_tn(grad_scores, k_ref[:upto, :])
    for p in range(tp):
        owner = lax.rem(here - p + tp, tp)
        part = pl.ds(pl.multiple_of(owner * share, share), share)
        cosine, sine = cosine_ref[part, :], sine_ref[part, :]
        mine = slice(p * share, (p + 1) * share)
        for j, (source, up) in enumerate(((dq, q_up), (dk, k_up), (dv, v_up))):
            value = source[part, :]
            if j < 2:
                value = value * scale
                value = value * cosine - pltpu.roll(value, HDA // 2, 1) * sine
            low = value.astype(bf16)
            at = pl.multiple_of((j * heads + head) * HDA, HDA)
            out_ref[mine, pl.ds(at, HDA)] = low
            lora[mine, j * rank : (j + 1) * rank] += mm_nt(low, up[...])

    @pl.when(head == heads - 1)
    def _():
        out_ref[:, 3 * heads * HDA :] = lora[...].astype(bf16)


def attention_backward(place, lengths, queries, keys, values, ups, pieces, cosine, sine):
    tp = len(pieces)
    share, columns = pieces[0].shape
    rows = share * tp
    heads = columns // HDA
    rank = ups.shape[0]
    piece_spec = pl.BlockSpec((share, HDA), lambda h, *_: (0, h))
    table_spec = pl.BlockSpec((rows, HDA), lambda h, *_: (0, 0))
    head_spec = pl.BlockSpec((rows, HDA), lambda h, *_: (0, h))

    def up_spec(j):
        return pl.BlockSpec((rank, HDA), lambda h, *_: (0, j * heads + h))

    total = 3 * columns + 3 * rank
    work = heads * rows * rows * HDA
    return pl.pallas_call(
        functools.partial(attention_backward_kernel, tp, heads),
        out_shape=jax.ShapeDtypeStruct((rows, total), bf16),
        grid_spec=pltpu.PrefetchScalarGridSpec(
            num_scalar_prefetch=2,
            grid=(heads,),
            in_specs=[table_spec, table_spec]
            + [head_spec] * 3
            + [up_spec(j) for j in range(3)]
            + [piece_spec] * tp,
            out_specs=pl.BlockSpec((rows, total), lambda h, *_: (0, 0)),
            scratch_shapes=[pltpu.VMEM((rows, HDA), bf16)]
            + [pltpu.VMEM((rows, HDA), f32)] * 3
            + [pltpu.VMEM((rows, 3 * rank), f32)],
        ),
        compiler_params=pltpu.CompilerParams(vmem_limit_bytes=VMEM_LIMIT),
        cost_estimate=pl.CostEstimate(
            flops=10 * work, bytes_accessed=14 * rows * columns, transcendentals=heads * rows * rows
        ),
        name="attention_backward",
    )(place, lengths, cosine, sine, queries, keys, values, ups, ups, ups, *pieces)


def conv_rows(extended, taps, position):
    count = 4
    rows = extended.shape[0] - 8
    total = None
    for k in range(count):
        moved = extended[8 - k : 8 - k + rows, :]
        if k:
            moved = jnp.where(position >= k, moved, 0.0)
        term = taps[count - 1 - k : count - k, :] * moved
        total = term if total is None else total + term
    return total


def conv_back(extended, taps, position):
    count = 4
    rows = extended.shape[0] - 8
    total = None
    for k in range(count):
        kept = jnp.where(position >= k, extended, 0.0) if k else extended
        term = taps[count - 1 - k : count - k, :] * kept[k : k + rows, :]
        total = term if total is None else total + term
    return total


def taps_back(extended, grad, position, target):
    count = 4
    rows = extended.shape[0] - 8
    for k in range(count):
        moved = extended[8 - k : 8 - k + rows, :]
        if k:
            moved = jnp.where(position >= k, moved, 0.0)
        at = count - 1 - k
        target[at : at + 1, :] += jnp.sum(grad * moved, axis=0, keepdims=True)


def silu_grad(value, gate):
    return gate * (1.0 + value * (1.0 - gate))


class Chunk:
    def __init__(self, c0, ends, zx, before, sd, sd_before, wide, narrow, rates):
        rows = zx.shape[0]
        width = zx.shape[1] // 2
        self.rows, self.width = rows, width
        index = c0 + iota((rows, 1), 0)
        start = starts_of(index, ends)
        self.index, self.start = index, start
        self.position = index - start
        last_start = starts_of(c0 + rows - 1, ends)
        self.z = zx[:, :width].astype(f32)
        self.x_ext = jnp.concatenate(
            [before[...].astype(f32)[8:16, :], zx[:, width:].astype(f32)], axis=0
        )
        self.s_ext = jnp.concatenate([sd_before[:, : 2 * LANES], sd[:, : 2 * LANES]], axis=0)
        self.pre = conv_rows(self.x_ext, wide, self.position)
        self.gate_x = jax.nn.sigmoid(self.pre)
        self.xc = self.pre * self.gate_x
        self.pre_s = conv_rows(self.s_ext, narrow, self.position)
        self.gate_s = jax.nn.sigmoid(self.pre_s)
        sc = self.pre_s * self.gate_s
        self.b_low = sc[:, :HD].astype(bf16)
        self.c_low = sc[:, LANES : LANES + HD].astype(bf16)
        self.raw = sd[:, 2 * LANES : 3 * LANES] + rates[0:1, :]
        self.step = jnp.maximum(self.raw, 0.0) + jnp.log1p(jnp.exp(-jnp.abs(self.raw)))
        self.rate = jnp.exp(rates[1:2, :])
        row, col = iota((rows, rows), 0), iota((rows, rows), 1)
        below = (col <= row).astype(f32)
        self.cum = jnp.dot(below, -self.step * self.rate, precision=HIGHEST, preferred_element_type=f32)
        self.cum_t = self.cum.T
        self.allowed = (col <= row) & ((c0 + col) >= start)
        self.inner = jnp.where(self.allowed, mm_nt(self.c_low, self.b_low), 0.0)
        last = self.cum[rows - 1 : rows, :]
        self.into = jnp.exp(self.cum) * (start < c0).astype(f32)
        self.onto = jnp.exp(last - self.cum) * (index >= last_start).astype(f32)
        self.decay = jnp.exp(last) * (last_start < c0).astype(f32)
        self.low_half = iota((1, LANES), 1) < HD

    def pair(self, table, i):
        return jnp.where(self.low_half, table[:, 2 * i : 2 * i + 1], table[:, 2 * i + 1 : 2 * i + 2])

    def spread(self, h):
        return jnp.exp(jnp.minimum(self.cum[:, h : h + 1] - self.cum_t[h : h + 1, :], 0.0))


def mixer_forward_kernel(
    place_ref, lengths_ref, zx, before, sd, sd_before, wide, narrow, rates, gated, states, state
):
    rows = zx.shape[0]
    c0 = pl.program_id(0) * rows
    ends = ends_of(lengths_ref)

    @pl.when(pl.program_id(0) == 0)
    def _():
        state[...] = jnp.zeros_like(state)

    v = Chunk(c0, ends, zx, before, sd, sd_before, wide, narrow, rates)
    state_low = state[...].astype(bf16)
    states[...] = state_low
    for i in range(v.width // LANES):
        cols = slice(i * LANES, (i + 1) * LANES)
        xc = v.xc[:, cols]
        xs = v.pair(v.step, i) * xc
        xs_low = xs.astype(bf16)
        first = (v.spread(2 * i) * v.inner).astype(bf16)
        second = (v.spread(2 * i + 1) * v.inner).astype(bf16)
        y = jnp.where(v.low_half, mm(first, xs_low), mm(second, xs_low))
        y = y + v.pair(v.into, i) * mm(v.c_low, state_low[:, cols])
        y = y + wide[4:5, cols] * xc
        z = v.z[:, cols]
        gated[:, cols] = (y * z * jax.nn.sigmoid(z)).astype(bf16)
        state[:, cols] = v.pair(v.decay, i) * state[:, cols] + mm_tn(
            v.b_low, (v.pair(v.onto, i) * xs).astype(bf16)
        )


def split_sum(values, ones):
    high = values.astype(bf16)
    low = (values - high.astype(f32)).astype(bf16)
    return mm(high, ones) + mm(low, ones)


def mixer_backward_kernel(
    chunks,
    place_ref,
    lengths_ref,
    zx,
    before,
    sd,
    sd_before,
    grad_scaled,
    stats,
    states,
    wide,
    narrow,
    rates,
    grad_all,
    grad_wide,
    grad_narrow,
    grad_rates,
    grad_state,
    next_pre,
    next_pre_s,
    carry,
    products,
    directs,
    grad_pre,
):
    rows = zx.shape[0]
    turn = pl.program_id(0)
    c0 = (chunks - 1 - turn) * rows
    ends = ends_of(lengths_ref)

    @pl.when(turn == 0)
    def _():
        for ref in (grad_state, next_pre, next_pre_s, carry, grad_wide, grad_narrow, grad_rates):
            ref[...] = jnp.zeros_like(ref)

    v = Chunk(c0, ends, zx, before, sd, sd_before, wide, narrow, rates)
    width = v.width
    root, pull = stats[:, 0:1], stats[:, 1:2]
    grad_inner = jnp.zeros((rows, rows), f32)
    grad_b = jnp.zeros((rows, HD), f32)
    grad_c = jnp.zeros((rows, HD), f32)
    for i in range(width // LANES):
        cols = slice(i * LANES, (i + 1) * LANES)
        xc = v.xc[:, cols]
        step = v.pair(v.step, i)
        xs = step * xc
        xs_low = xs.astype(bf16)
        spread_a, spread_b = v.spread(2 * i), v.spread(2 * i + 1)
        first = (spread_a * v.inner).astype(bf16)
        second = (spread_b * v.inner).astype(bf16)
        state_low = states[:, cols]
        into, onto = v.pair(v.into, i), v.pair(v.onto, i)
        y = jnp.where(v.low_half, mm(first, xs_low), mm(second, xs_low))
        y = y + into * mm(v.c_low, state_low)
        skip, gain = wide[4:5, cols], wide[5:6, cols]
        whole = y + skip * xc
        z = v.z[:, cols]
        gate = jax.nn.sigmoid(z)
        gated = whole * z * gate
        incoming = grad_scaled[:, cols].astype(f32)
        rooted = incoming * root
        grad_wide[5:6, cols] += jnp.sum(rooted * gated, axis=0, keepdims=True)
        grad_gated = rooted * gain - gated * pull
        grad_y = grad_gated * z * gate
        grad_all[:, cols] = (grad_gated * whole * silu_grad(z, gate)).astype(bf16)
        grad_wide[4:5, cols] += jnp.sum(grad_y * xc, axis=0, keepdims=True)
        low = grad_y.astype(bf16)
        low_a = jnp.where(v.low_half, grad_y, 0.0).astype(bf16)
        low_b = jnp.where(v.low_half, 0.0, grad_y).astype(bf16)
        grad_inner = grad_inner + spread_a * mm_nt(low_a, xs_low) + spread_b * mm_nt(low_b, xs_low)
        grad_end = grad_state[:, cols]
        grad_end_low = grad_end.astype(bf16)
        grad_xs = jnp.where(v.low_half, mm_tn(first, low), mm_tn(second, low))
        grad_xs = grad_xs + onto * mm(v.b_low, grad_end_low)
        into_y = (into * grad_y).astype(bf16)
        onto_x = (onto * xs).astype(bf16)
        grad_b = grad_b + mm_nt(onto_x, grad_end_low)
        grad_c = grad_c + mm_nt(into_y, state_low)
        grad_state[:, cols] = v.pair(v.decay, i) * grad_end + mm_tn(v.c_low, into_y)
        products[:, cols] = low.astype(f32) * y - xs_low.astype(f32) * grad_xs
        directs[:, cols] = xc * grad_xs
        grad_xc = step * grad_xs + skip * grad_y
        grad_pre[:, cols] = grad_xc * silu_grad(v.pre[:, cols], v.gate_x[:, cols])
    grad_inner = jnp.where(v.allowed, grad_inner, 0.0).astype(bf16)
    grad_b = grad_b + mm_tn(grad_inner, v.c_low)
    grad_c = grad_c + mm(grad_inner, v.b_low)

    lane, head = iota((width, LANES), 0), iota((width, LANES), 1)
    ones = ((lane >= head * HD) & (lane < head * HD + HD)).astype(bf16)
    grad_cum = split_sum(products[...], ones)
    direct = split_sum(directs[...], ones)
    row, col = iota((rows, rows), 0), iota((rows, rows), 1)
    col_start = starts_of(c0 + iota((1, rows), 1), ends)
    above = ((col >= row) & (col_start <= c0 + row)).astype(f32)
    next_start = starts_of(c0 + rows, ends)
    reaches = (v.index >= next_start).astype(f32)
    after = jnp.dot(above, grad_cum, precision=HIGHEST, preferred_element_type=f32) + reaches * carry[0:1, :]
    flux = jnp.sum(grad_state[...] * states[...].astype(f32), axis=0, keepdims=True)
    carry[...] = split_sum(jnp.broadcast_to(flux, (8, width)), ones)
    grad_log = -v.step * v.rate * after
    grad_raw = (direct - v.rate * after) * jax.nn.sigmoid(v.raw)
    grad_rates[0:1, :] += jnp.sum(grad_raw, axis=0, keepdims=True)
    grad_rates[1:2, :] += jnp.sum(grad_log, axis=0, keepdims=True)

    index_ext = c0 + iota((rows + 8, 1), 0)
    position_ext = index_ext - starts_of(index_ext, ends)
    taps_back(v.x_ext, grad_pre[...], v.position, grad_wide)
    extended = jnp.concatenate([grad_pre[...], next_pre[...]], axis=0)
    grad_all[:, width : 2 * width] = conv_back(extended, wide, position_ext).astype(bf16)
    next_pre[...] = grad_pre[0:8, :]

    blank = jnp.zeros((rows, LANES - HD), f32)
    grad_sc = jnp.concatenate([grad_b, blank, grad_c, blank], axis=1)
    grad_pre_s = grad_sc * silu_grad(v.pre_s, v.gate_s)
    taps_back(v.s_ext, grad_pre_s, v.position, grad_narrow)
    extended_s = jnp.concatenate([grad_pre_s, next_pre_s[...]], axis=0)
    grad_all[:, 2 * width : 2 * width + 2 * LANES] = conv_back(extended_s, narrow, position_ext).astype(bf16)
    next_pre_s[...] = grad_pre_s[0:8, :]
    grad_all[:, 2 * width + 2 * LANES :] = grad_raw.astype(bf16)


def mixer_specs(tp, rows, width, order):
    share = rows // tp
    per_share = share // CHUNK

    def here(place, c):
        owner = lax.div(c, per_share)
        piece = lax.rem(place[0] - owner + tp, tp)
        return piece * per_share + lax.rem(c, per_share)

    def chunk_map(i, place, lengths):
        return (here(place, order(i)), 0)

    def before_map(unit, column):
        def index(i, place, lengths):
            c = order(i)
            previous = jnp.maximum(c - 1, 0)
            return (here(place, previous) * (CHUNK // unit) + CHUNK // unit - 1, column)

        return index

    def fixed(i, place, lengths):
        return (0, 0)

    return chunk_map, before_map, fixed


def mixer_forward(place, lengths, tp, zx, sd, wide, narrow, rates):
    rows, width = zx.shape[0], zx.shape[1] // 2
    chunks = rows // CHUNK
    chunk_map, before_map, fixed = mixer_specs(tp, rows, width, lambda i: i)
    work = rows * width * CHUNK
    return pl.pallas_call(
        mixer_forward_kernel,
        out_shape=[
            jax.ShapeDtypeStruct((rows, width), bf16),
            jax.ShapeDtypeStruct((chunks, HD, width), bf16),
        ],
        grid_spec=pltpu.PrefetchScalarGridSpec(
            num_scalar_prefetch=2,
            grid=(chunks,),
            in_specs=[
                pl.BlockSpec((CHUNK, 2 * width), chunk_map),
                pl.BlockSpec((16, width), before_map(16, 1)),
                pl.BlockSpec((CHUNK, 3 * LANES), chunk_map),
                pl.BlockSpec((8, 3 * LANES), before_map(8, 0)),
                pl.BlockSpec((8, width), fixed),
                pl.BlockSpec((8, 2 * LANES), fixed),
                pl.BlockSpec((8, LANES), fixed),
            ],
            out_specs=[
                pl.BlockSpec((CHUNK, width), chunk_map),
                pl.BlockSpec((None, HD, width), lambda i, *_: (i, 0, 0)),
            ],
            scratch_shapes=[pltpu.VMEM((HD, width), f32)],
        ),
        compiler_params=pltpu.CompilerParams(vmem_limit_bytes=VMEM_LIMIT),
        cost_estimate=pl.CostEstimate(
            flops=8 * work, bytes_accessed=8 * rows * width, transcendentals=4 * rows * width
        ),
        name="mixer_forward",
    )(place, lengths, zx, zx, sd, sd, wide, narrow, rates)


def mixer_backward(place, lengths, tp, zx, sd, grad_scaled, stats, states, wide, narrow, rates):
    rows, width = zx.shape[0], zx.shape[1] // 2
    chunks = rows // CHUNK
    chunk_map, before_map, fixed = mixer_specs(tp, rows, width, lambda i: chunks - 1 - i)
    work = rows * width * CHUNK
    return pl.pallas_call(
        functools.partial(mixer_backward_kernel, chunks),
        out_shape=[
            jax.ShapeDtypeStruct((rows, 2 * width + 3 * LANES), bf16),
            jax.ShapeDtypeStruct((8, width), f32),
            jax.ShapeDtypeStruct((8, 2 * LANES), f32),
            jax.ShapeDtypeStruct((8, LANES), f32),
        ],
        grid_spec=pltpu.PrefetchScalarGridSpec(
            num_scalar_prefetch=2,
            grid=(chunks,),
            in_specs=[
                pl.BlockSpec((CHUNK, 2 * width), chunk_map),
                pl.BlockSpec((16, width), before_map(16, 1)),
                pl.BlockSpec((CHUNK, 3 * LANES), chunk_map),
                pl.BlockSpec((8, 3 * LANES), before_map(8, 0)),
                pl.BlockSpec((CHUNK, width), chunk_map),
                pl.BlockSpec((CHUNK, 2), chunk_map),
                pl.BlockSpec((None, HD, width), lambda i, *_: (chunks - 1 - i, 0, 0)),
                pl.BlockSpec((8, width), fixed),
                pl.BlockSpec((8, 2 * LANES), fixed),
                pl.BlockSpec((8, LANES), fixed),
            ],
            out_specs=[
                pl.BlockSpec((CHUNK, 2 * width + 3 * LANES), chunk_map),
                pl.BlockSpec((8, width), fixed),
                pl.BlockSpec((8, 2 * LANES), fixed),
                pl.BlockSpec((8, LANES), fixed),
            ],
            scratch_shapes=[
                pltpu.VMEM((HD, width), f32),
                pltpu.VMEM((8, width), f32),
                pltpu.VMEM((8, 2 * LANES), f32),
                pltpu.VMEM((8, LANES), f32),
                pltpu.VMEM((CHUNK, width), f32),
                pltpu.VMEM((CHUNK, width), f32),
                pltpu.VMEM((CHUNK, width), f32),
            ],
        ),
        compiler_params=pltpu.CompilerParams(vmem_limit_bytes=VMEM_LIMIT),
        cost_estimate=pl.CostEstimate(
            flops=24 * work, bytes_accessed=12 * rows * width, transcendentals=5 * rows * width
        ),
        name="mixer_backward",
    )(place, lengths, zx, zx, sd, sd, grad_scaled, stats, states, wide, narrow, rates)


def norm_back_kernel(parts, with_base, with_low, with_gain, *refs):
    values, refs = refs[:parts], refs[parts:]
    grad, gain, refs = refs[0], refs[1], refs[2:]
    base, refs = (refs[0], refs[1:]) if with_base else (None, refs)
    outs, refs = refs[:parts], refs[parts:]
    low, refs = (refs[0], refs[1:]) if with_low else (None, refs)
    if with_gain:
        grad_gain = refs[0]

        @pl.when(pl.program_id(0) == 0)
        def _():
            grad_gain[...] = jnp.zeros_like(grad_gain)

    width = grad.shape[1]
    each = width // parts
    wide = [v[...].astype(f32) for v in values]
    squares = sum(jnp.sum(v * v, axis=1, keepdims=True) for v in wide)
    inv_root = lax.rsqrt(squares / width + norm_eps)
    units = [v * inv_root for v in wide]
    grads = [grad[:, i * each : (i + 1) * each] for i in range(parts)]
    grad_units = [g * gain[:, i * each : (i + 1) * each] for i, g in enumerate(grads)]
    cross = sum(jnp.sum(g * u, axis=1, keepdims=True) for g, u in zip(grad_units, units)) / width
    for i in range(parts):
        cols = slice(i * each, (i + 1) * each)
        if with_gain:
            grad_gain[0:1, cols] += jnp.sum(grads[i] * units[i], axis=0, keepdims=True)
        result = inv_root * (grad_units[i] - units[i] * cross)
        if with_base and i == 0:
            result = result + base[...].astype(f32)
        outs[i][...] = result
        if with_low and i == 0:
            low[...] = result.astype(bf16)


def norm_back(values, grad, gain, base=None, with_low=False, with_gain=True):
    rows, width = grad.shape
    parts = len(values)
    block = math.gcd(rows, 64)
    row_spec = pl.BlockSpec((block, width // parts), lambda i: (i, 0))
    full_spec = pl.BlockSpec((block, width), lambda i: (i, 0))
    operands = list(values) + [grad, gain] + ([base] if base is not None else [])
    shapes = [jax.ShapeDtypeStruct((rows, width // parts), f32)] * parts
    shapes += [jax.ShapeDtypeStruct((rows, width // parts), bf16)] if with_low else []
    results = pl.pallas_call(
        functools.partial(norm_back_kernel, parts, base is not None, with_low, with_gain),
        out_shape=shapes + [jax.ShapeDtypeStruct((8, width), f32)] * int(with_gain),
        grid=(rows // block,),
        in_specs=[row_spec] * parts
        + [full_spec, pl.BlockSpec((1, width), lambda i: (0, 0))]
        + ([row_spec] if base is not None else []),
        out_specs=[row_spec] * (parts + int(with_low))
        + [pl.BlockSpec((8, width), lambda i: (0, 0))] * int(with_gain),
        compiler_params=pltpu.CompilerParams(vmem_limit_bytes=VMEM_LIMIT),
        cost_estimate=pl.CostEstimate(
            flops=20 * rows * width, bytes_accessed=14 * rows * width, transcendentals=rows
        ),
        name="norm_back",
    )(*operands)
    return list(results[:-1]) + [results[-1][0]] if with_gain else list(results)


def tie(value, others):
    return lax.optimization_barrier((value, others))[0]


def after(value, token):
    return value if token is None else tie(value, token)


def ring_pairs():
    tp = lax.axis_size("tp")
    return [(i, (i + 1) % tp) for i in range(tp)]


def hop(values):
    return lax.ppermute(values, "tp", ring_pairs())


class Halving:
    def __init__(self, values, name, sent_as=f32):
        self.values, self.name, self.sent_as = values, name, sent_as
        self.half = lax.axis_size(name) // 2

    def live(self):
        return self.half > 0

    def start(self):
        count, half = lax.axis_size(self.name), self.half
        upper = (lax.axis_index(self.name) & half) != 0
        low, high = self.values[:half], self.values[half:]
        self.kept = jnp.where(upper, high, low)
        sent = jnp.where(upper, low, high).astype(self.sent_as)
        self.moved = lax.ppermute(sent, self.name, [(i, i ^ half) for i in range(count)])

    def finish(self):
        self.values = self.kept + self.moved.astype(f32)
        self.half //= 2

    def result(self):
        while self.live():
            self.start()
            self.finish()
        return self.values[0]


class Doubling:
    def __init__(self, values, name, sent_as=f32):
        self.values, self.name, self.sent_as = values, name, sent_as
        self.step = 1

    def live(self):
        return self.step < lax.axis_size(self.name)

    def start(self):
        count, step = lax.axis_size(self.name), self.step
        self.moved = lax.ppermute(
            self.values.astype(self.sent_as), self.name, [(i, i ^ step) for i in range(count)]
        )

    def finish(self):
        self.values = self.values + self.moved.astype(f32)
        self.step *= 2

    def result(self):
        while self.live():
            self.start()
            self.finish()
        return self.values


def begin(tasks):
    live = [t for t in tasks if t.live()]
    for t in live:
        t.start()
    return live


def settle(moved, extras, live):
    moved, extras, arrived = lax.optimization_barrier((moved, extras, [t.moved for t in live]))
    for t, value in zip(live, arrived):
        t.moved = value
        t.finish()
    return moved, extras


def ring_gather(own, use, tasks=()):
    tp = lax.axis_size("tp")
    pieces, results = [own], []
    for p in range(tp):
        if p < tp - 1:
            moved = hop(pieces[p])
            live = begin(tasks)
        result = use(p, pieces[p])
        if p < tp - 1:
            moved, result = settle(moved, result, live)
            pieces.append(moved)
        results.append(result)
    return pieces, results


def ring_scatter(part, fill=(), tasks=()):
    tp = lax.axis_size("tp")
    fill = list(fill)
    filled = []
    total = part(1 % tp, None)
    for p in range(2, tp + 1):
        low = total.astype(bf16)
        moved = hop(low)
        live = begin(tasks)
        term = part(p % tp, low)
        extra = [fill.pop(0)(low, tasks)] if fill else []
        moved, (term, extra) = settle(moved, (term, extra), live)
        filled += extra
        total = moved.astype(f32) + term
    for thunk in fill:
        filled.append(thunk(low, tasks))
    return total, filled


def ring_both(own, work, last=None, fill=None, tasks=()):
    tp = lax.axis_size("tp")
    pieces, filled = [own], []
    moved = hop(own)
    live = begin(tasks)
    first = work(0, own)
    moved, _ = settle(moved, (), live)
    total, ahead = None, None
    for p in range(1, tp):
        pieces.append(moved)
        if p < tp - 1:
            moved = hop(pieces[p])
        elif last is not None:
            pieces[p], result = lax.optimization_barrier((pieces[p], last(pieces)))
            filled.append(result)
        live = begin(tasks)
        term = work(p, pieces[p])
        if total is not None:
            ahead, term = lax.optimization_barrier((ahead, term))
            term = ahead.astype(f32) + term
        total = term
        low = total.astype(bf16)
        ahead = hop(low)
        if p < tp - 1:
            moved, (low, first) = settle(moved, (low, first), live)
        elif fill is not None:
            ahead, result = settle(ahead, fill(low), live)
            filled.append(result)
        else:
            ahead, _ = settle(ahead, (), live)
    return pieces, ahead.astype(f32) + first, filled


def doubling_gather(values, name):
    count = lax.axis_size(name)
    here = lax.axis_index(name)
    step = 1
    while step < count:
        moved = lax.ppermute(values, name, [(i, i ^ step) for i in range(count)])
        upper = (here & step) != 0
        values = jnp.concatenate(
            [jnp.where(upper, moved, values), jnp.where(upper, values, moved)], axis=0
        )
        step *= 2
    return values


def inverse_root(values):
    return lax.rsqrt(jnp.mean(values * values, axis=1, keepdims=True) + norm_eps)


def gather(values, axis=0):
    return lax.all_gather(values, "fsdp", axis=axis, tiled=True)


def scatter(values, axis=0):
    return lax.psum_scatter(values, "fsdp", scatter_dimension=axis, tiled=True)


def local(
    hidden,
    embed,
    lengths,
    attention_norm_gain,
    query_key_value_weight,
    attention_adapter_down,
    attention_adapter_up,
    attention_output_weight,
    feedforward_norm_gain,
    gate_up_weight,
    feedforward_adapter_down,
    feedforward_adapter_up,
    down_weight,
    mixer_norm_gain,
    gate_inner_weight,
    state_input_weight,
    step_projection,
    inner_conv_taps,
    state_conv_taps,
    head_step_bias,
    decay_log_rate,
    inner_skip_gains,
    gated_norm_gain,
    mixer_output_weight,
    output_cotangent,
):
    tp = lax.axis_size("tp")
    fsdp = lax.axis_size("fsdp")
    share, width = hidden.shape
    rows = share * tp
    here = lax.axis_index("tp").astype(jnp.int32)
    place = here.reshape(1)
    lengths = lengths.reshape(-1)
    rank = attention_adapter_down.shape[2]
    head_cols = query_key_value_weight.shape[2]
    units_here = gate_up_weight.shape[2]
    inner_cols = gate_inner_weight.shape[2]
    mixer_heads = inner_cols // HD
    states = state_input_weight.shape[2]
    count = inner_conv_taps.shape[0]
    inner_total = inner_cols * tp

    def piece(values, p):
        return values[p * share : (p + 1) * share]

    own_qkv = jnp.concatenate(
        [query_key_value_weight[:, j, :] for j in range(3)]
        + [attention_adapter_down[:, j, :] for j in range(3)],
        axis=1,
    )
    weight_qkv = gather(own_qkv)
    first_hop = tuple(hop(v) for v in (hidden, embed))

    small = [
        attention_norm_gain,
        feedforward_norm_gain,
        mixer_norm_gain,
        inner_conv_taps.reshape(-1),
        state_conv_taps.reshape(-1),
        inner_skip_gains.reshape(-1),
        gated_norm_gain.reshape(-1),
    ]
    sizes = [v.shape[0] for v in small]
    padding = -sum(sizes) % LANES
    packed = jnp.concatenate(small + [jnp.zeros((padding,), bf16)]).reshape(1, -1)
    spread = gather(packed).astype(f32)
    cuts = [sum(sizes[:i]) for i in range(len(sizes) + 1)]
    parts = [spread[:, cuts[i] : cuts[i + 1]] for i in range(len(sizes))]
    gain_attn, gain_mlp, gain_mixer = (parts[i].reshape(1, -1) for i in range(3))
    taps_x = parts[3].reshape(fsdp, count, mixer_heads, -1)
    taps_x = jnp.transpose(taps_x, (1, 2, 0, 3)).reshape(count, inner_cols)
    taps_s = parts[4].reshape(fsdp, count, 2, -1)
    taps_s = jnp.transpose(taps_s, (1, 2, 0, 3)).reshape(count, 2, states)
    skip = jnp.transpose(parts[5].reshape(fsdp, mixer_heads, -1), (1, 0, 2)).reshape(1, inner_cols)
    gain_gate = jnp.transpose(parts[6].reshape(fsdp, mixer_heads, -1), (1, 0, 2)).reshape(1, inner_cols)
    wide = jnp.concatenate([taps_x, skip, gain_gate, jnp.zeros((2, inner_cols), f32)], axis=0)
    narrow = jnp.pad(taps_s, ((0, 8 - count), (0, 0), (0, LANES - states))).reshape(8, 2 * LANES)
    rates = jnp.pad(
        jnp.stack([head_step_bias, decay_log_rate]), ((0, 6), (0, LANES - mixer_heads))
    )

    places = jnp.arange(rows, dtype=jnp.int32)
    ends = [jnp.sum(lengths[: i + 1]) for i in range(lengths.shape[0] - 1)]
    position = places - starts_of(places, ends)
    freqs = jnp.exp(jnp.arange(HDA // 2, dtype=f32) * (-2.0 * math.log(10000.0) / HDA))
    angles = position.astype(f32)[:, None] * freqs[None, :]
    cosine = jnp.cos(angles)
    sine = jnp.sin(angles)
    cosine = jnp.concatenate([cosine, cosine], axis=1)
    sine = jnp.concatenate([-sine, sine], axis=1)

    own_fc1 = jnp.concatenate(
        [gate_up_weight[:, j, :] for j in range(2)] + [feedforward_adapter_down], axis=1
    )
    own_zx = jnp.concatenate(
        [gate_inner_weight[:, j, :] for j in range(2)]
        + [jnp.pad(state_input_weight[:, j, :], ((0, 0), (0, LANES - states))) for j in range(2)]
        + [jnp.pad(step_projection, ((0, 0), (0, LANES - mixer_heads)))],
        axis=1,
    )
    weight_o = gather(attention_output_weight, 1)
    weight_fc1 = gather(own_fc1)
    weight_fc2 = gather(down_weight, 1)
    weight_zx = gather(own_zx)
    weight_out = gather(mixer_output_weight, 1)

    def norm_rows(pair):
        pair = [v.astype(f32) for v in pair]
        squares = sum(jnp.sum(v * v, axis=1, keepdims=True) for v in pair)
        inv_root = lax.rsqrt(squares / (2 * width) + norm_eps)
        return [
            (v * inv_root * gain_attn[:, i * width : (i + 1) * width]).astype(bf16)
            for i, v in enumerate(pair)
        ]

    raw, normed = [(hidden, embed), first_hop], []
    for p in range(2, tp):
        moved = tuple(hop(v) for v in raw[-1])
        normed.append(norm_rows(raw[p - 2]))
        raw.append(tie(moved, normed[-1]))
    normed += [norm_rows(v) for v in raw[len(normed) :]]

    own_ups = jnp.concatenate(
        [attention_adapter_up[:, j, :] for j in range(3)]
        + [feedforward_adapter_up[:, j, :] for j in range(2)],
        axis=1,
    )
    ups = doubling_gather(tie(own_ups, raw[-2]), "fsdp")
    fc_up = ups[:, 3 * head_cols :]
    out_grad = [tie(output_cotangent, raw[-1])]
    normed_parts, projected = [], []
    for i in range(tp - 1):
        moved = hop(out_grad[-1])
        if i < tp - 2:
            low, high = (tp * i) // (tp - 2), (tp * (i + 1)) // (tp - 2)
            normed_parts.append(jnp.concatenate([jnp.concatenate(v, axis=1) for v in normed[low:high]], axis=0))
            projected.append(mm(normed_parts[-1], weight_qkv))
            moved = tie(moved, projected)
        else:
            attended, queries, keys, values = attention_forward(
                place, lengths, tp, projected, ups, head_cols, cosine, sine
            )
            moved = tie(moved, attended)
        out_grad.append(moved)
    lora_rows = jnp.concatenate([v[:, 3 * head_cols :].astype(bf16) for v in projected], axis=0)
    attended, lora_rows, out_grad[-1] = lax.optimization_barrier((attended, lora_rows, moved))
    out_grad_rows = jnp.concatenate(out_grad, axis=0)
    mixed, (normed_rows,) = ring_scatter(
        lambda p, t: mm(piece(after(attended, t), p), weight_o),
        [lambda t, _: jnp.concatenate(tie(normed_parts, t), axis=0)],
    )

    mlp_root = inverse_root(mixed)
    gate_up, fc_mid, units = [], [], []

    def feed(p, rows_in):
        wide_rows = mm(rows_in, weight_fc1)
        middle = wide_rows[:, 2 * units_here :].astype(bf16)
        both = (wide_rows[:, : 2 * units_here] + mm(middle, fc_up)).astype(bf16)
        gate, up = both[:, :units_here].astype(f32), both[:, units_here:].astype(f32)
        unit = (jax.nn.gelu(gate) * up).astype(bf16)
        fc_mid.append(middle)
        gate_up.append(both)
        units.append(unit)
        return mm(unit, weight_fc2)

    mlp_in, branch, _ = ring_both((mixed * mlp_root * gain_mlp).astype(bf16), feed)
    residual = hidden.astype(f32) + mixed + branch

    mixer_root = inverse_root(residual)
    kept = []

    def mix(p, rows_in):
        result = mm(rows_in, weight_zx)
        if p == 0:
            kept.append(mm_nt(tie(out_grad_rows, result), weight_out).astype(bf16))
        elif p == 1:
            kept.append(jnp.concatenate(tie(units, result), axis=0))
            kept.append(jnp.concatenate(tie(mlp_in, result), axis=0))
        return (result, kept[-1])

    mixer_in, zxs = ring_gather((residual * mixer_root * gain_mixer).astype(bf16), mix)
    zxs = [v[0] for v in zxs]
    grad_scaled, units_rows, mlp_rows = kept
    mixer_rows = jnp.concatenate(mixer_in, axis=0)
    zx = jnp.concatenate([v[:, : 2 * inner_cols].astype(bf16) for v in zxs], axis=0)
    sd = jnp.concatenate([v[:, 2 * inner_cols :] for v in zxs], axis=0)
    gated, chunk_states = mixer_forward(place, lengths, tp, zx, sd, wide, narrow, rates)
    gated_wide = gated.astype(f32)
    sums = jnp.stack(
        [
            jnp.sum(gated_wide * gated_wide, axis=1),
            jnp.sum(grad_scaled.astype(f32) * gain_gate * gated_wide, axis=1),
        ],
        axis=0,
    )
    sums = jnp.roll(jnp.flip(sums.reshape(2, tp, share), axis=1), here + 1, axis=1)
    sums = lax.psum(sums, "tp")
    sums = jnp.flip(jnp.roll(sums, -(here + 1), axis=1), axis=1).reshape(2, rows)
    gate_root = lax.rsqrt(sums[0] / inner_total + norm_eps)
    stats = jnp.stack([gate_root, gate_root**3 * sums[1] / inner_total], axis=1)
    scaled = (gated_wide * gate_root[:, None] * gain_gate).astype(bf16)
    out_rows, stats = lax.optimization_barrier((mm(scaled, weight_out).astype(bf16), stats))
    out_terms = [piece(out_rows, p) for p in range(tp)]
    out = hop(out_terms[1 % tp])

    grad_all, grad_wide, grad_narrow, grad_rates = mixer_backward(
        place, lengths, tp, zx, sd, grad_scaled, stats, chunk_states, wide, narrow, rates
    )
    out, grad_all = lax.optimization_barrier((out, grad_all))
    out = out.astype(f32) + out_terms[2 % tp].astype(f32)

    def by_fsdp(values):
        lead = values.shape[:-1]
        cut = values.reshape(lead + (fsdp, values.shape[-1] // fsdp))
        return jnp.moveaxis(cut, -2, 0).reshape(fsdp, -1)

    def small_gradients(token):
        taps, bars, sums_r = tie((grad_wide, grad_narrow, grad_rates), token)
        return [
            by_fsdp(taps[:count].reshape(count, mixer_heads, HD)),
            by_fsdp(taps[4].reshape(mixer_heads, HD)),
            by_fsdp(taps[5].reshape(mixer_heads, HD)),
            jnp.broadcast_to(sums_r[:2, :mixer_heads].reshape(1, -1), (fsdp, 2 * mixer_heads)),
            by_fsdp(bars[:count].reshape(count, 2, LANES)[:, :, :states]),
        ]

    grad_mixer_in, (sum_w_out, sum_w_zx, small) = ring_scatter(
        lambda p, t: mm_nt(piece(after(grad_all, t), p), weight_zx),
        [
            lambda t, _: mm_tn(tie(scaled, t), out_grad_rows).astype(bf16),
            lambda t, _: mm_tn(tie(mixer_rows, t), grad_all).astype(bf16),
            lambda t, _: small_gradients(t),
        ],
    )
    sum_w_out = scatter(sum_w_out, 1)
    sum_w_zx = scatter(sum_w_zx)
    small_sizes = [v.shape[1] for v in small]
    small_cuts = [sum(small_sizes[:i]) for i in range(len(small_sizes) + 1)]
    small_task = Halving(jnp.concatenate(small, axis=1), "fsdp")
    grad_residual, grad_residual_low, grad_gain_mixer = norm_back(
        [residual], grad_mixer_in, gain_mixer, output_cotangent, True
    )

    grad_gate_up = []

    def feed_back(p, grad_rows):
        grad_units = mm_nt(grad_rows, weight_fc2)
        gate = gate_up[p][:, :units_here].astype(f32)
        up = gate_up[p][:, units_here:].astype(f32)
        raised, back = jax.vjp(jax.nn.gelu, gate)
        both = jnp.concatenate(
            [back(grad_units * up)[0].astype(bf16), (grad_units * raised).astype(bf16)], axis=1
        )
        both = jnp.concatenate([both, mm_nt(both, fc_up).astype(bf16)], axis=1)
        grad_gate_up.append(both)
        return mm_nt(both, weight_fc1)

    def fc2_fill(token, _):
        rows_in = tie(units_rows, (sum_w_out, token))
        return mm_tn(rows_in, jnp.concatenate(grad_branch, axis=0)).astype(bf16)

    def fc1_fill(token, _):
        return mm_tn(tie(mlp_rows, token), jnp.concatenate(grad_gate_up, axis=0)).astype(bf16)

    grad_branch, back_terms = ring_gather(
        grad_residual_low, lambda p, v: feed_back(p, v) if p < tp - 1 else (), [small_task]
    )
    grad_mlp_in, filled = ring_scatter(
        lambda p, t: back_terms[p] if p < tp - 1 else feed_back(p, after(grad_branch[p], t)),
        [fc2_fill] + [lambda t, _: ()] * (tp - 3) + [fc1_fill],
    )
    sum_w_fc2, sum_w_fc1 = filled[0], filled[-1]
    sum_w_fc2 = scatter(sum_w_fc2, 1)
    sum_w_fc1 = scatter(sum_w_fc1)
    grad_gate_up_rows = jnp.concatenate(grad_gate_up, axis=0)
    _, grad_mixed_low, grad_gain_mlp = norm_back([mixed], grad_mlp_in, gain_mlp, grad_residual, True)
    gain_task = Halving(
        jnp.concatenate([grad_gain_mixer.reshape(fsdp, -1), grad_gain_mlp.reshape(fsdp, -1)], axis=1), "fsdp"
    )

    fc_ups = []

    def attended_back(p, rows_in):
        result = mm_nt(rows_in, weight_o).astype(bf16)
        if p == 0:
            fc_ups.append(
                mm_tn(tie(jnp.concatenate(fc_mid, axis=0), rows_in), grad_gate_up_rows[:, : 2 * units_here])
            )
            result = tie(result, fc_ups[0])
        return result

    grad_mixed, grad_attended = ring_gather(tie(grad_mixed_low, sum_w_zx), attended_back, [gain_task])
    sum_w_o = mm_tn(tie(attended, sum_w_fc2), jnp.concatenate(grad_mixed, axis=0)).astype(bf16)
    grad_attended[-1] = tie(grad_attended[-1], sum_w_o)
    sum_w_o = scatter(sum_w_o, 1)
    out = hop(out.astype(bf16))
    grad_projected = attention_backward(
        place, lengths, queries, keys, values, ups, grad_attended, cosine, sine
    )
    out, grad_projected, sum_w_fc1 = lax.optimization_barrier((out, grad_projected, sum_w_fc1))
    out = out.astype(f32) + out_terms[3 % tp].astype(f32)
    out = hop(out.astype(bf16))
    sum_w_qkv = mm_tn(normed_rows, grad_projected).astype(bf16)
    out, sum_w_qkv, grad_projected = lax.optimization_barrier((out, sum_w_qkv, grad_projected))
    sum_w_qkv = scatter(sum_w_qkv)

    at_t = 2 * inner_cols + 2 * LANES

    def finish_out(token):
        total = tie(out, token).astype(f32) + out_terms[4 % tp].astype(f32)
        for p in range(5, tp + 1):
            total = hop(total.astype(bf16)).astype(f32) + out_terms[p % tp].astype(f32)
        return residual + total

    def finish_adapters(token, tasks):
        rows_in = tie(lora_rows, token)
        grad_up = [
            mm_tn(
                rows_in[:, j * rank : (j + 1) * rank],
                grad_projected[:, j * head_cols : (j + 1) * head_cols],
            )
            for j in range(3)
        ]
        ups_grad = jnp.concatenate(grad_up + fc_ups, axis=1)
        tasks.append(Halving(ups_grad.reshape(fsdp, -1, ups_grad.shape[1]), "fsdp", bf16))
        shared = jnp.concatenate([small_task.result()[small_cuts[4] :], gain_task.result()])
        tasks.append(Doubling(shared, "tp"))
        return ups_grad, shared

    def finish_mixer(token, tasks):
        zx_sum, w_out, w_fc2 = tie((sum_w_zx, sum_w_out, sum_w_fc2), token)
        zx_sum = zx_sum.astype(f32)
        bc_sums.append(zx_sum[:, 2 * inner_cols : at_t])
        return (
            stacked(zx_sum, inner_cols, 2),
            zx_sum[:, at_t : at_t + mixer_heads],
            w_out.astype(f32),
            w_fc2.astype(f32),
        )

    def finish_feed(token, tasks):
        fc1_sum, w_o = tie((sum_w_fc1, sum_w_o), token)
        fc1_sum = fc1_sum.astype(f32)
        tasks.append(
            Doubling(jnp.concatenate([bc_sums[0], fc1_sum[:, 2 * units_here :]], axis=1), "tp", bf16)
        )
        return (
            stacked(fc1_sum, units_here, 2),
            w_o.astype(f32),
            finish_out(token),
        )

    def stacked(values, each, parts):
        values = jnp.stack([values[:, j * each : (j + 1) * each] for j in range(parts)], axis=1)
        return with_layout_constraint(values, Layout(major_to_minor=(0, 1, 2)))

    tasks, bc_sums = [], []
    normed_terms = {}
    pair = mm_nt(grad_projected[share : 3 * share], weight_qkv)
    normed_terms[1], normed_terms[2] = piece(pair, 0), piece(pair, 1)

    def normed_back(p, token):
        if p not in normed_terms:
            normed_terms[p] = mm_nt(piece(after(grad_projected, token), p), weight_qkv)
        return normed_terms[p]

    grad_normed, ((_, mixer_sums, _), feed_sums) = ring_scatter(
        normed_back,
        [lambda t, k: (finish_adapters(t, k), finish_mixer(t, k), normed_back(3 % tp, t)), finish_feed],
        tasks,
    )
    grad_w_zx, grad_w_dt, grad_w_out, grad_w_fc2 = mixer_sums
    grad_w_fc1, grad_w_o, out = feed_sums
    grad_hidden, grad_embed = norm_back(
        [hidden, embed], grad_normed, gain_attn, grad_residual, with_gain=False
    )
    gain_rows = jnp.sum(sum_w_qkv.astype(f32) * own_qkv.astype(f32), axis=1)
    gain_rows = gain_rows / attention_norm_gain.astype(f32)
    down_task = Halving(sum_w_qkv[:, 3 * head_cols :].astype(f32).reshape(tp, -1, 3 * rank), "tp", bf16)
    gain_last = Halving(gain_rows.reshape(tp, -1), "tp")
    while down_task.live():
        for t in begin([down_task, gain_last]):
            t.finish()
    grad_down, grad_gain_attn = down_task.result(), gain_last.result()
    grad_w_qkv = jnp.stack(
        [sum_w_qkv[:, j * head_cols : (j + 1) * head_cols].astype(f32) for j in range(3)], axis=1
    )
    small_sum = small_task.result()
    small_parts = [small_sum[small_cuts[i] : small_cuts[i + 1]] for i in range(len(small_sizes))]
    grad_ups, tail = tasks[0].result(), tasks[1].result()
    shared = tasks[2].result()
    tail_sizes = [small_sizes[4], width // fsdp, width // fsdp]
    tail_cuts = [sum(tail_sizes[:i]) for i in range(4)]
    grad_conv_bc, sum_gain_mixer, sum_gain_mlp = (
        tail[tail_cuts[i] : tail_cuts[i + 1]] for i in range(3)
    )
    sum_rates = small_parts[3].reshape(2, mixer_heads)
    return (
        out,
        grad_hidden,
        grad_embed,
        grad_gain_attn,
        grad_w_qkv,
        grad_down.reshape(-1, 3, rank),
        grad_ups[:, : 3 * head_cols].reshape(-1, 3, head_cols),
        grad_w_o,
        sum_gain_mlp,
        grad_w_fc1,
        shared[:, 2 * LANES :],
        grad_ups[:, 3 * head_cols :].reshape(-1, 2, units_here),
        grad_w_fc2,
        sum_gain_mixer,
        grad_w_zx,
        shared[:, : 2 * LANES].reshape(-1, 2, LANES)[:, :, :states],
        grad_w_dt,
        small_parts[0].reshape(count, mixer_heads, -1),
        grad_conv_bc.reshape(count, 2, -1),
        sum_rates[0],
        sum_rates[1],
        small_parts[1].reshape(mixer_heads, -1),
        small_parts[2].reshape(mixer_heads, -1),
        grad_w_out,
    )


def solution(mesh):
    placed = (
        P(("fsdp", "tp"), None),
        P(("fsdp", "tp"), None),
        P("fsdp", None),
        P("fsdp"),
        P("fsdp", None, "tp"),
        P("fsdp", None, None),
        P("fsdp", None, "tp"),
        P("tp", "fsdp"),
        P("fsdp"),
        P("fsdp", None, "tp"),
        P("fsdp", None),
        P("fsdp", None, "tp"),
        P("tp", "fsdp"),
        P("fsdp"),
        P("fsdp", None, "tp"),
        P("fsdp", None, None),
        P("fsdp", "tp"),
        P(None, "tp", "fsdp"),
        P(None, None, "fsdp"),
        P("tp"),
        P("tp"),
        P("tp", "fsdp"),
        P("tp", "fsdp"),
        P("tp", "fsdp"),
        P(("fsdp", "tp"), None),
    )
    return jax.shard_map(
        local,
        mesh=mesh,
        in_specs=placed,
        out_specs=(
            P(("fsdp", "tp"), None),
            P(("fsdp", "tp"), None),
            P(("fsdp", "tp"), None),
            P(("fsdp", "tp")),
            P("fsdp", None, "tp"),
            P(("fsdp", "tp"), None, None),
            P("fsdp", None, "tp"),
            P("tp", "fsdp"),
            P("fsdp"),
            P("fsdp", None, "tp"),
            P("fsdp", None),
            P("fsdp", None, "tp"),
            P("tp", "fsdp"),
            P("fsdp"),
            P("fsdp", None, "tp"),
            P("fsdp", None, None),
            P("fsdp", "tp"),
            P(None, "tp", "fsdp"),
            P(None, None, "fsdp"),
            P("tp"),
            P("tp"),
            P("tp", "fsdp"),
            P("tp", "fsdp"),
            P("tp", "fsdp"),
        ),
        check_vma=False,
    )
```

```python
import functools
import math

import jax
import jax.numpy as jnp
from jax import lax
from jax.experimental import pallas as pl
from jax.experimental.layout import Layout, with_layout_constraint
from jax.experimental.pallas import tpu as pltpu
from jax.sharding import PartitionSpec as P

HDA = 128
HD = 64
LANES = 128
CHUNK = 128

norm_eps = 1e-05
f32 = jnp.float32
bf16 = jnp.bfloat16
HIGHEST = lax.Precision.HIGHEST
VMEM_LIMIT = 56 * 1024 * 1024


def mm(left, right):
    return jnp.dot(left, right, preferred_element_type=f32)


def mm_nt(left, right):
    return lax.dot_general(left, right, (((1,), (1,)), ((), ())), preferred_element_type=f32)


def mm_tn(left, right):
    return lax.dot_general(left, right, (((0,), (0,)), ((), ())), preferred_element_type=f32)


def starts_of(index, ends):
    start = jnp.zeros_like(index)
    for end in ends:
        start = jnp.where(index >= end, end, start)
    return start


def ends_of(lengths_ref):
    ends = []
    end = jnp.int32(0)
    for i in range(lengths_ref.shape[0] - 1):
        end = end + lengths_ref[i]
        ends.append(end)
    return ends


def iota(shape, axis):
    return lax.broadcasted_iota(jnp.int32, shape, axis)


def attention_forward_kernel(
    tp,
    parts,
    place_ref,
    lengths_ref,
    cosine_ref,
    sine_ref,
    q_up,
    k_up,
    v_up,
    *refs,
):
    pieces = refs[: 4 * parts]
    attended_ref, q_ref, k_ref, v_ref, held = refs[4 * parts :]
    rows = q_ref.shape[0]
    share = rows // tp
    rank = q_up.shape[0]
    here = place_ref[0]
    ends = ends_of(lengths_ref)
    for p in range(tp):
        owner = lax.rem(here - p + tp, tp)
        part = pl.ds(pl.multiple_of(owner * share, share), share)
        cosine, sine = cosine_ref[part, :], sine_ref[part, :]
        at = p * share
        source = 0
        while at >= pieces[4 * source].shape[0]:
            at -= pieces[4 * source].shape[0]
            source += 1
        mine = slice(at, at + share)
        for j, (up, target) in enumerate(((q_up, q_ref), (k_up, k_ref), (v_up, v_ref))):
            low = pieces[4 * source + 3][mine, j * rank : (j + 1) * rank].astype(bf16)
            value = pieces[4 * source + j][mine, :] + mm(low, up[...])
            if j < 2:
                value = value * cosine + pltpu.roll(value, HDA // 2, 1) * sine
            target[part, :] = value.astype(bf16)
    block = min(256, rows)
    scale = HDA ** (-0.5)
    for at in range(0, rows, block):
        upto = at + block
        scores = mm_nt(k_ref[:upto, :], q_ref[at:upto, :]) * scale
        query = at + iota((1, block), 1)
        key = iota((upto, 1), 0)
        seen = (key <= query) & (key >= starts_of(query, ends))
        scores = jnp.where(seen, scores, -1e30)
        raised = jnp.exp(scores - jnp.max(scores, axis=0, keepdims=True))
        probs = (raised * (1.0 / jnp.sum(raised, axis=0, keepdims=True))).astype(bf16)
        held[at:upto, :] = mm_tn(probs, v_ref[:upto, :]).astype(bf16)
    for p in range(tp):
        owner = lax.rem(here - p + tp, tp)
        part = pl.ds(pl.multiple_of(owner * share, share), share)
        attended_ref[p * share : (p + 1) * share, :] = held[part, :]


def attention_forward(place, lengths, tp, projected, ups, columns, cosine, sine):
    rows = sum(v.shape[0] for v in projected)
    heads = columns // HDA
    rank = ups.shape[0]
    table_spec = pl.BlockSpec((rows, HDA), lambda h, *_: (0, 0))

    def head_spec(j, height=rows):
        return pl.BlockSpec((height, HDA), lambda h, *_: (0, j * heads + h))

    work = heads * rows * rows * HDA
    return pl.pallas_call(
        functools.partial(attention_forward_kernel, tp, len(projected)),
        out_shape=[jax.ShapeDtypeStruct((rows, columns), bf16)] * 4,
        grid_spec=pltpu.PrefetchScalarGridSpec(
            num_scalar_prefetch=2,
            grid=(heads,),
            in_specs=[table_spec, table_spec]
            + [head_spec(j, rank) for j in range(3)]
            + [
                pl.BlockSpec((v.shape[0], 3 * rank), lambda h, *_: (0, columns // rank))
                if j == 3
                else head_spec(j, v.shape[0])
                for v in projected
                for j in range(4)
            ],
            out_specs=[head_spec(0)] * 4,
            scratch_shapes=[pltpu.VMEM((rows, HDA), bf16)],
        ),
        compiler_params=pltpu.CompilerParams(vmem_limit_bytes=VMEM_LIMIT),
        cost_estimate=pl.CostEstimate(
            flops=4 * work, bytes_accessed=20 * rows * columns, transcendentals=heads * rows * rows
        ),
        name="attention_forward",
    )(place, lengths, cosine, sine, ups, ups, ups, *[v for v in projected for _ in range(4)])


def attention_backward_kernel(
    tp,
    heads,
    place_ref,
    lengths_ref,
    cosine_ref,
    sine_ref,
    q_ref,
    k_ref,
    v_ref,
    q_up,
    k_up,
    v_up,
    *refs,
):
    grad_in = refs[:tp]
    out_ref, held, dq, dk, dv, lora = refs[tp:]
    rows = q_ref.shape[0]
    share = rows // tp
    rank = q_up.shape[0]
    here = place_ref[0]
    head = pl.program_id(0)
    ends = ends_of(lengths_ref)
    for p in range(tp):
        owner = lax.rem(here - p + tp, tp)
        part = pl.ds(pl.multiple_of(owner * share, share), share)
        held[part, :] = grad_in[p][...]
    dk[...] = jnp.zeros_like(dk)
    dv[...] = jnp.zeros_like(dv)

    @pl.when(head == 0)
    def _():
        lora[...] = jnp.zeros_like(lora)

    block = min(256, rows)
    scale = HDA ** (-0.5)
    for at in range(0, rows, block):
        upto = at + block
        query_rows = q_ref[at:upto, :]
        grad_rows = held[at:upto, :]
        scores = mm_nt(k_ref[:upto, :], query_rows) * scale
        query = at + iota((1, block), 1)
        key = iota((upto, 1), 0)
        seen = (key <= query) & (key >= starts_of(query, ends))
        scores = jnp.where(seen, scores, -1e30)
        raised = jnp.exp(scores - jnp.max(scores, axis=0, keepdims=True))
        probs = raised * (1.0 / jnp.sum(raised, axis=0, keepdims=True))
        grad_probs = mm_nt(v_ref[:upto, :], grad_rows)
        cross = jnp.sum(probs * grad_probs, axis=0, keepdims=True)
        grad_scores = (probs * (grad_probs - cross)).astype(bf16)
        dv[:upto, :] += mm(probs.astype(bf16), grad_rows)
        dk[:upto, :] += mm(grad_scores, query_rows)
        dq[at:upto, :] = mm_tn(grad_scores, k_ref[:upto, :])
    for p in range(tp):
        owner = lax.rem(here - p + tp, tp)
        part = pl.ds(pl.multiple_of(owner * share, share), share)
        cosine, sine = cosine_ref[part, :], sine_ref[part, :]
        mine = slice(p * share, (p + 1) * share)
        for j, (source, up) in enumerate(((dq, q_up), (dk, k_up), (dv, v_up))):
            value = source[part, :]
            if j < 2:
                value = value * scale
                value = value * cosine - pltpu.roll(value, HDA // 2, 1) * sine
            low = value.astype(bf16)
            at = pl.multiple_of((j * heads + head) * HDA, HDA)
            out_ref[mine, pl.ds(at, HDA)] = low
            lora[mine, j * rank : (j + 1) * rank] += mm_nt(low, up[...])

    @pl.when(head == heads - 1)
    def _():
        out_ref[:, 3 * heads * HDA :] = lora[...].astype(bf16)


def attention_backward(place, lengths, queries, keys, values, ups, pieces, cosine, sine):
    tp = len(pieces)
    share, columns = pieces[0].shape
    rows = share * tp
    heads = columns // HDA
    rank = ups.shape[0]
    piece_spec = pl.BlockSpec((share, HDA), lambda h, *_: (0, h))
    table_spec = pl.BlockSpec((rows, HDA), lambda h, *_: (0, 0))
    head_spec = pl.BlockSpec((rows, HDA), lambda h, *_: (0, h))

    def up_spec(j):
        return pl.BlockSpec((rank, HDA), lambda h, *_: (0, j * heads + h))

    total = 3 * columns + 3 * rank
    work = heads * rows * rows * HDA
    return pl.pallas_call(
        functools.partial(attention_backward_kernel, tp, heads),
        out_shape=jax.ShapeDtypeStruct((rows, total), bf16),
        grid_spec=pltpu.PrefetchScalarGridSpec(
            num_scalar_prefetch=2,
            grid=(heads,),
            in_specs=[table_spec, table_spec]
            + [head_spec] * 3
            + [up_spec(j) for j in range(3)]
            + [piece_spec] * tp,
            out_specs=pl.BlockSpec((rows, total), lambda h, *_: (0, 0)),
            scratch_shapes=[pltpu.VMEM((rows, HDA), bf16)]
            + [pltpu.VMEM((rows, HDA), f32)] * 3
            + [pltpu.VMEM((rows, 3 * rank), f32)],
        ),
        compiler_params=pltpu.CompilerParams(vmem_limit_bytes=VMEM_LIMIT),
        cost_estimate=pl.CostEstimate(
            flops=10 * work, bytes_accessed=14 * rows * columns, transcendentals=heads * rows * rows
        ),
        name="attention_backward",
    )(place, lengths, cosine, sine, queries, keys, values, ups, ups, ups, *pieces)


def conv_rows(extended, taps, position):
    count = 4
    rows = extended.shape[0] - 8
    total = None
    for k in range(count):
        moved = extended[8 - k : 8 - k + rows, :]
        if k:
            moved = jnp.where(position >= k, moved, 0.0)
        term = taps[count - 1 - k : count - k, :] * moved
        total = term if total is None else total + term
    return total


def conv_back(extended, taps, position):
    count = 4
    rows = extended.shape[0] - 8
    total = None
    for k in range(count):
        kept = jnp.where(position >= k, extended, 0.0) if k else extended
        term = taps[count - 1 - k : count - k, :] * kept[k : k + rows, :]
        total = term if total is None else total + term
    return total


def taps_back(extended, grad, position, target):
    count = 4
    rows = extended.shape[0] - 8
    for k in range(count):
        moved = extended[8 - k : 8 - k + rows, :]
        if k:
            moved = jnp.where(position >= k, moved, 0.0)
        at = count - 1 - k
        target[at : at + 1, :] += jnp.sum(grad * moved, axis=0, keepdims=True)


def silu_grad(value, gate):
    return gate * (1.0 + value * (1.0 - gate))


class Chunk:
    def __init__(self, c0, ends, zx, before, sd, sd_before, wide, narrow, rates):
        rows = zx.shape[0]
        width = zx.shape[1] // 2
        self.rows, self.width = rows, width
        index = c0 + iota((rows, 1), 0)
        start = starts_of(index, ends)
        self.index, self.start = index, start
        self.position = index - start
        last_start = starts_of(c0 + rows - 1, ends)
        self.z = zx[:, :width].astype(f32)
        self.x_ext = jnp.concatenate(
            [before[...].astype(f32)[8:16, :], zx[:, width:].astype(f32)], axis=0
        )
        self.s_ext = jnp.concatenate([sd_before[:, : 2 * LANES], sd[:, : 2 * LANES]], axis=0)
        self.pre = conv_rows(self.x_ext, wide, self.position)
        self.gate_x = jax.nn.sigmoid(self.pre)
        self.xc = self.pre * self.gate_x
        self.pre_s = conv_rows(self.s_ext, narrow, self.position)
        self.gate_s = jax.nn.sigmoid(self.pre_s)
        sc = self.pre_s * self.gate_s
        self.b_low = sc[:, :HD].astype(bf16)
        self.c_low = sc[:, LANES : LANES + HD].astype(bf16)
        self.raw = sd[:, 2 * LANES : 3 * LANES] + rates[0:1, :]
        self.step = jnp.maximum(self.raw, 0.0) + jnp.log1p(jnp.exp(-jnp.abs(self.raw)))
        self.rate = jnp.exp(rates[1:2, :])
        row, col = iota((rows, rows), 0), iota((rows, rows), 1)
        below = (col <= row).astype(f32)
        self.cum = jnp.dot(below, -self.step * self.rate, precision=HIGHEST, preferred_element_type=f32)
        self.cum_t = self.cum.T
        self.allowed = (col <= row) & ((c0 + col) >= start)
        self.inner = jnp.where(self.allowed, mm_nt(self.c_low, self.b_low), 0.0)
        last = self.cum[rows - 1 : rows, :]
        self.into = jnp.exp(self.cum) * (start < c0).astype(f32)
        self.onto = jnp.exp(last - self.cum) * (index >= last_start).astype(f32)
        self.decay = jnp.exp(last) * (last_start < c0).astype(f32)
        self.low_half = iota((1, LANES), 1) < HD

    def pair(self, table, i):
        return jnp.where(self.low_half, table[:, 2 * i : 2 * i + 1], table[:, 2 * i + 1 : 2 * i + 2])

    def spread(self, h):
        return jnp.exp(jnp.minimum(self.cum[:, h : h + 1] - self.cum_t[h : h + 1, :], 0.0))


def mixer_forward_kernel(
    place_ref, lengths_ref, zx, before, sd, sd_before, wide, narrow, rates, gated, states, state
):
    rows = zx.shape[0]
    c0 = pl.program_id(0) * rows
    ends = ends_of(lengths_ref)

    @pl.when(pl.program_id(0) == 0)
    def _():
        state[...] = jnp.zeros_like(state)

    v = Chunk(c0, ends, zx, before, sd, sd_before, wide, narrow, rates)
    state_low = state[...].astype(bf16)
    states[...] = state_low
    for i in range(v.width // LANES):
        cols = slice(i * LANES, (i + 1) * LANES)
        xc = v.xc[:, cols]
        xs = v.pair(v.step, i) * xc
        xs_low = xs.astype(bf16)
        first = (v.spread(2 * i) * v.inner).astype(bf16)
        second = (v.spread(2 * i + 1) * v.inner).astype(bf16)
        y = jnp.where(v.low_half, mm(first, xs_low), mm(second, xs_low))
        y = y + v.pair(v.into, i) * mm(v.c_low, state_low[:, cols])
        y = y + wide[4:5, cols] * xc
        z = v.z[:, cols]
        gated[:, cols] = (y * z * jax.nn.sigmoid(z)).astype(bf16)
        state[:, cols] = v.pair(v.decay, i) * state[:, cols] + mm_tn(
            v.b_low, (v.pair(v.onto, i) * xs).astype(bf16)
        )


def split_sum(values, ones):
    high = values.astype(bf16)
    low = (values - high.astype(f32)).astype(bf16)
    return mm(high, ones) + mm(low, ones)


def mixer_backward_kernel(
    chunks,
    place_ref,
    lengths_ref,
    zx,
    before,
    sd,
    sd_before,
    grad_scaled,
    stats,
    states,
    wide,
    narrow,
    rates,
    grad_all,
    grad_wide,
    grad_narrow,
    grad_rates,
    grad_state,
    next_pre,
    next_pre_s,
    carry,
    products,
    directs,
    grad_pre,
):
    rows = zx.shape[0]
    turn = pl.program_id(0)
    c0 = (chunks - 1 - turn) * rows
    ends = ends_of(lengths_ref)

    @pl.when(turn == 0)
    def _():
        for ref in (grad_state, next_pre, next_pre_s, carry, grad_wide, grad_narrow, grad_rates):
            ref[...] = jnp.zeros_like(ref)

    v = Chunk(c0, ends, zx, before, sd, sd_before, wide, narrow, rates)
    width = v.width
    root, pull = stats[:, 0:1], stats[:, 1:2]
    grad_inner = jnp.zeros((rows, rows), f32)
    grad_b = jnp.zeros((rows, HD), f32)
    grad_c = jnp.zeros((rows, HD), f32)
    for i in range(width // LANES):
        cols = slice(i * LANES, (i + 1) * LANES)
        xc = v.xc[:, cols]
        step = v.pair(v.step, i)
        xs = step * xc
        xs_low = xs.astype(bf16)
        spread_a, spread_b = v.spread(2 * i), v.spread(2 * i + 1)
        first = (spread_a * v.inner).astype(bf16)
        second = (spread_b * v.inner).astype(bf16)
        state_low = states[:, cols]
        into, onto = v.pair(v.into, i), v.pair(v.onto, i)
        y = jnp.where(v.low_half, mm(first, xs_low), mm(second, xs_low))
        y = y + into * mm(v.c_low, state_low)
        skip, gain = wide[4:5, cols], wide[5:6, cols]
        whole = y + skip * xc
        z = v.z[:, cols]
        gate = jax.nn.sigmoid(z)
        gated = whole * z * gate
        incoming = grad_scaled[:, cols].astype(f32)
        rooted = incoming * root
        grad_wide[5:6, cols] += jnp.sum(rooted * gated, axis=0, keepdims=True)
        grad_gated = rooted * gain - gated * pull
        grad_y = grad_gated * z * gate
        grad_all[:, cols] = (grad_gated * whole * silu_grad(z, gate)).astype(bf16)
        grad_wide[4:5, cols] += jnp.sum(grad_y * xc, axis=0, keepdims=True)
        low = grad_y.astype(bf16)
        low_a = jnp.where(v.low_half, grad_y, 0.0).astype(bf16)
        low_b = jnp.where(v.low_half, 0.0, grad_y).astype(bf16)
        grad_inner = grad_inner + spread_a * mm_nt(low_a, xs_low) + spread_b * mm_nt(low_b, xs_low)
        grad_end = grad_state[:, cols]
        grad_end_low = grad_end.astype(bf16)
        grad_xs = jnp.where(v.low_half, mm_tn(first, low), mm_tn(second, low))
        grad_xs = grad_xs + onto * mm(v.b_low, grad_end_low)
        into_y = (into * grad_y).astype(bf16)
        onto_x = (onto * xs).astype(bf16)
        grad_b = grad_b + mm_nt(onto_x, grad_end_low)
        grad_c = grad_c + mm_nt(into_y, state_low)
        grad_state[:, cols] = v.pair(v.decay, i) * grad_end + mm_tn(v.c_low, into_y)
        products[:, cols] = low.astype(f32) * y - xs_low.astype(f32) * grad_xs
        directs[:, cols] = xc * grad_xs
        grad_xc = step * grad_xs + skip * grad_y
        grad_pre[:, cols] = grad_xc * silu_grad(v.pre[:, cols], v.gate_x[:, cols])
    grad_inner = jnp.where(v.allowed, grad_inner, 0.0).astype(bf16)
    grad_b = grad_b + mm_tn(grad_inner, v.c_low)
    grad_c = grad_c + mm(grad_inner, v.b_low)

    lane, head = iota((width, LANES), 0), iota((width, LANES), 1)
    ones = ((lane >= head * HD) & (lane < head * HD + HD)).astype(bf16)
    grad_cum = split_sum(products[...], ones)
    direct = split_sum(directs[...], ones)
    row, col = iota((rows, rows), 0), iota((rows, rows), 1)
    col_start = starts_of(c0 + iota((1, rows), 1), ends)
    above = ((col >= row) & (col_start <= c0 + row)).astype(f32)
    next_start = starts_of(c0 + rows, ends)
    reaches = (v.index >= next_start).astype(f32)
    after = jnp.dot(above, grad_cum, precision=HIGHEST, preferred_element_type=f32) + reaches * carry[0:1, :]
    flux = jnp.sum(grad_state[...] * states[...].astype(f32), axis=0, keepdims=True)
    carry[...] = split_sum(jnp.broadcast_to(flux, (8, width)), ones)
    grad_log = -v.step * v.rate * after
    grad_raw = (direct - v.rate * after) * jax.nn.sigmoid(v.raw)
    grad_rates[0:1, :] += jnp.sum(grad_raw, axis=0, keepdims=True)
    grad_rates[1:2, :] += jnp.sum(grad_log, axis=0, keepdims=True)

    index_ext = c0 + iota((rows + 8, 1), 0)
    position_ext = index_ext - starts_of(index_ext, ends)
    taps_back(v.x_ext, grad_pre[...], v.position, grad_wide)
    extended = jnp.concatenate([grad_pre[...], next_pre[...]], axis=0)
    grad_all[:, width : 2 * width] = conv_back(extended, wide, position_ext).astype(bf16)
    next_pre[...] = grad_pre[0:8, :]

    blank = jnp.zeros((rows, LANES - HD), f32)
    grad_sc = jnp.concatenate([grad_b, blank, grad_c, blank], axis=1)
    grad_pre_s = grad_sc * silu_grad(v.pre_s, v.gate_s)
    taps_back(v.s_ext, grad_pre_s, v.position, grad_narrow)
    extended_s = jnp.concatenate([grad_pre_s, next_pre_s[...]], axis=0)
    grad_all[:, 2 * width : 2 * width + 2 * LANES] = conv_back(extended_s, narrow, position_ext).astype(bf16)
    next_pre_s[...] = grad_pre_s[0:8, :]
    grad_all[:, 2 * width + 2 * LANES :] = grad_raw.astype(bf16)


def chunk_of(tp, rows):
    return math.gcd(rows // tp, CHUNK)


def mixer_specs(tp, rows, chunk, order):
    share = rows // tp
    per_share = share // chunk

    def here(place, c):
        owner = lax.div(c, per_share)
        piece = lax.rem(place[0] - owner + tp, tp)
        return piece * per_share + lax.rem(c, per_share)

    def chunk_map(i, place, lengths):
        return (here(place, order(i)), 0)

    def before_map(unit, column):
        def index(i, place, lengths):
            c = order(i)
            previous = jnp.maximum(c - 1, 0)
            return (here(place, previous) * (chunk // unit) + chunk // unit - 1, column)

        return index

    def fixed(i, place, lengths):
        return (0, 0)

    return chunk_map, before_map, fixed


def mixer_forward(place, lengths, tp, zx, sd, wide, narrow, rates):
    rows, width = zx.shape[0], zx.shape[1] // 2
    chunk = chunk_of(tp, rows)
    chunks = rows // chunk
    chunk_map, before_map, fixed = mixer_specs(tp, rows, chunk, lambda i: i)
    work = rows * width * chunk
    return pl.pallas_call(
        mixer_forward_kernel,
        out_shape=[
            jax.ShapeDtypeStruct((rows, width), bf16),
            jax.ShapeDtypeStruct((chunks, HD, width), bf16),
        ],
        grid_spec=pltpu.PrefetchScalarGridSpec(
            num_scalar_prefetch=2,
            grid=(chunks,),
            in_specs=[
                pl.BlockSpec((chunk, 2 * width), chunk_map),
                pl.BlockSpec((16, width), before_map(16, 1)),
                pl.BlockSpec((chunk, 3 * LANES), chunk_map),
                pl.BlockSpec((8, 3 * LANES), before_map(8, 0)),
                pl.BlockSpec((8, width), fixed),
                pl.BlockSpec((8, 2 * LANES), fixed),
                pl.BlockSpec((8, LANES), fixed),
            ],
            out_specs=[
                pl.BlockSpec((chunk, width), chunk_map),
                pl.BlockSpec((None, HD, width), lambda i, *_: (i, 0, 0)),
            ],
            scratch_shapes=[pltpu.VMEM((HD, width), f32)],
        ),
        compiler_params=pltpu.CompilerParams(vmem_limit_bytes=VMEM_LIMIT),
        cost_estimate=pl.CostEstimate(
            flops=8 * work, bytes_accessed=8 * rows * width, transcendentals=4 * rows * width
        ),
        name="mixer_forward",
    )(place, lengths, zx, zx, sd, sd, wide, narrow, rates)


def mixer_backward(place, lengths, tp, zx, sd, grad_scaled, stats, states, wide, narrow, rates):
    rows, width = zx.shape[0], zx.shape[1] // 2
    chunk = chunk_of(tp, rows)
    chunks = rows // chunk
    chunk_map, before_map, fixed = mixer_specs(tp, rows, chunk, lambda i: chunks - 1 - i)
    work = rows * width * chunk
    return pl.pallas_call(
        functools.partial(mixer_backward_kernel, chunks),
        out_shape=[
            jax.ShapeDtypeStruct((rows, 2 * width + 3 * LANES), bf16),
            jax.ShapeDtypeStruct((8, width), f32),
            jax.ShapeDtypeStruct((8, 2 * LANES), f32),
            jax.ShapeDtypeStruct((8, LANES), f32),
        ],
        grid_spec=pltpu.PrefetchScalarGridSpec(
            num_scalar_prefetch=2,
            grid=(chunks,),
            in_specs=[
                pl.BlockSpec((chunk, 2 * width), chunk_map),
                pl.BlockSpec((16, width), before_map(16, 1)),
                pl.BlockSpec((chunk, 3 * LANES), chunk_map),
                pl.BlockSpec((8, 3 * LANES), before_map(8, 0)),
                pl.BlockSpec((chunk, width), chunk_map),
                pl.BlockSpec((chunk, 2), chunk_map),
                pl.BlockSpec((None, HD, width), lambda i, *_: (chunks - 1 - i, 0, 0)),
                pl.BlockSpec((8, width), fixed),
                pl.BlockSpec((8, 2 * LANES), fixed),
                pl.BlockSpec((8, LANES), fixed),
            ],
            out_specs=[
                pl.BlockSpec((chunk, 2 * width + 3 * LANES), chunk_map),
                pl.BlockSpec((8, width), fixed),
                pl.BlockSpec((8, 2 * LANES), fixed),
                pl.BlockSpec((8, LANES), fixed),
            ],
            scratch_shapes=[
                pltpu.VMEM((HD, width), f32),
                pltpu.VMEM((8, width), f32),
                pltpu.VMEM((8, 2 * LANES), f32),
                pltpu.VMEM((8, LANES), f32),
                pltpu.VMEM((chunk, width), f32),
                pltpu.VMEM((chunk, width), f32),
                pltpu.VMEM((chunk, width), f32),
            ],
        ),
        compiler_params=pltpu.CompilerParams(vmem_limit_bytes=VMEM_LIMIT),
        cost_estimate=pl.CostEstimate(
            flops=24 * work, bytes_accessed=12 * rows * width, transcendentals=5 * rows * width
        ),
        name="mixer_backward",
    )(place, lengths, zx, zx, sd, sd, grad_scaled, stats, states, wide, narrow, rates)


def norm_back_kernel(parts, with_base, with_low, with_gain, *refs):
    values, refs = refs[:parts], refs[parts:]
    grad, gain, refs = refs[0], refs[1], refs[2:]
    base, refs = (refs[0], refs[1:]) if with_base else (None, refs)
    outs, refs = refs[:parts], refs[parts:]
    low, refs = (refs[0], refs[1:]) if with_low else (None, refs)
    if with_gain:
        grad_gain = refs[0]

        @pl.when(pl.program_id(0) == 0)
        def _():
            grad_gain[...] = jnp.zeros_like(grad_gain)

    width = grad.shape[1]
    each = width // parts
    wide = [v[...].astype(f32) for v in values]
    squares = sum(jnp.sum(v * v, axis=1, keepdims=True) for v in wide)
    inv_root = lax.rsqrt(squares / width + norm_eps)
    units = [v * inv_root for v in wide]
    grads = [grad[:, i * each : (i + 1) * each] for i in range(parts)]
    grad_units = [g * gain[:, i * each : (i + 1) * each] for i, g in enumerate(grads)]
    cross = sum(jnp.sum(g * u, axis=1, keepdims=True) for g, u in zip(grad_units, units)) / width
    for i in range(parts):
        cols = slice(i * each, (i + 1) * each)
        if with_gain:
            grad_gain[0:1, cols] += jnp.sum(grads[i] * units[i], axis=0, keepdims=True)
        result = inv_root * (grad_units[i] - units[i] * cross)
        if with_base and i == 0:
            result = result + base[...].astype(f32)
        outs[i][...] = result
        if with_low and i == 0:
            low[...] = result.astype(bf16)


def norm_back(values, grad, gain, base=None, with_low=False, with_gain=True):
    rows, width = grad.shape
    parts = len(values)
    block = math.gcd(rows, 64)
    row_spec = pl.BlockSpec((block, width // parts), lambda i: (i, 0))
    full_spec = pl.BlockSpec((block, width), lambda i: (i, 0))
    operands = list(values) + [grad, gain] + ([base] if base is not None else [])
    shapes = [jax.ShapeDtypeStruct((rows, width // parts), f32)] * parts
    shapes += [jax.ShapeDtypeStruct((rows, width // parts), bf16)] if with_low else []
    results = pl.pallas_call(
        functools.partial(norm_back_kernel, parts, base is not None, with_low, with_gain),
        out_shape=shapes + [jax.ShapeDtypeStruct((8, width), f32)] * int(with_gain),
        grid=(rows // block,),
        in_specs=[row_spec] * parts
        + [full_spec, pl.BlockSpec((1, width), lambda i: (0, 0))]
        + ([row_spec] if base is not None else []),
        out_specs=[row_spec] * (parts + int(with_low))
        + [pl.BlockSpec((8, width), lambda i: (0, 0))] * int(with_gain),
        compiler_params=pltpu.CompilerParams(vmem_limit_bytes=VMEM_LIMIT),
        cost_estimate=pl.CostEstimate(
            flops=20 * rows * width, bytes_accessed=14 * rows * width, transcendentals=rows
        ),
        name="norm_back",
    )(*operands)
    return list(results[:-1]) + [results[-1][0]] if with_gain else list(results)


def tie(value, others):
    return lax.optimization_barrier((value, others))[0]


def after(value, token):
    return value if token is None else tie(value, token)


def ring_pairs():
    tp = lax.axis_size("tp")
    return [(i, (i + 1) % tp) for i in range(tp)]


def hop(values):
    return lax.ppermute(values, "tp", ring_pairs())


class Halving:
    def __init__(self, values, name, sent_as=f32):
        self.values, self.name, self.sent_as = values, name, sent_as
        self.half = lax.axis_size(name) // 2

    def live(self):
        return self.half > 0

    def start(self):
        count, half = lax.axis_size(self.name), self.half
        upper = (lax.axis_index(self.name) & half) != 0
        low, high = self.values[:half], self.values[half:]
        self.kept = jnp.where(upper, high, low)
        sent = jnp.where(upper, low, high).astype(self.sent_as)
        self.moved = lax.ppermute(sent, self.name, [(i, i ^ half) for i in range(count)])

    def finish(self):
        self.values = self.kept + self.moved.astype(f32)
        self.half //= 2

    def result(self):
        while self.live():
            self.start()
            self.finish()
        return self.values[0]


class Doubling:
    def __init__(self, values, name, sent_as=f32):
        self.values, self.name, self.sent_as = values, name, sent_as
        self.step = 1

    def live(self):
        return self.step < lax.axis_size(self.name)

    def start(self):
        count, step = lax.axis_size(self.name), self.step
        self.moved = lax.ppermute(
            self.values.astype(self.sent_as), self.name, [(i, i ^ step) for i in range(count)]
        )

    def finish(self):
        self.values = self.values + self.moved.astype(f32)
        self.step *= 2

    def result(self):
        while self.live():
            self.start()
            self.finish()
        return self.values


def direct(values, name, sent_as=f32):
    count = lax.axis_size(name)
    here = lax.axis_index(name)

    def block(at):
        return lax.dynamic_index_in_dim(values, lax.rem(at, count), 0, keepdims=False)

    total = block(here)
    for step in range(1, count):
        sent = block(here + step).astype(sent_as)
        moved = lax.ppermute(sent, name, [(i, (i + step) % count) for i in range(count)])
        total = total + moved.astype(f32)
    return total


def begin(tasks):
    live = [t for t in tasks if t.live()]
    for t in live:
        t.start()
    return live


def settle(moved, extras, live):
    moved, extras, arrived = lax.optimization_barrier((moved, extras, [t.moved for t in live]))
    for t, value in zip(live, arrived):
        t.moved = value
        t.finish()
    return moved, extras


def ring_gather(own, use, tasks=()):
    tp = lax.axis_size("tp")
    pieces, results = [own], []
    for p in range(tp):
        if p < tp - 1:
            moved = hop(pieces[p])
            live = begin(tasks)
        result = use(p, pieces[p])
        if p < tp - 1:
            moved, result = settle(moved, result, live)
            pieces.append(moved)
        results.append(result)
    return pieces, results


def ring_scatter(part, fill=(), tasks=()):
    tp = lax.axis_size("tp")
    fill = list(fill)
    filled = []
    total = part(1 % tp, None)
    for p in range(2, tp + 1):
        low = total.astype(bf16)
        moved = hop(low)
        live = begin(tasks)
        term = part(p % tp, low)
        extra = [fill.pop(0)(low, tasks)] if fill else []
        moved, (term, extra) = settle(moved, (term, extra), live)
        filled += extra
        total = moved.astype(f32) + term
    for thunk in fill:
        filled.append(thunk(low, tasks))
    return total, filled


def ring_both(own, work, last=None, fill=None, tasks=()):
    tp = lax.axis_size("tp")
    pieces, filled = [own], []
    moved = hop(own)
    live = begin(tasks)
    first = work(0, own)
    moved, _ = settle(moved, (), live)
    total, ahead = None, None
    for p in range(1, tp):
        pieces.append(moved)
        if p < tp - 1:
            moved = hop(pieces[p])
        elif last is not None:
            pieces[p], result = lax.optimization_barrier((pieces[p], last(pieces)))
            filled.append(result)
        live = begin(tasks)
        term = work(p, pieces[p])
        if total is not None:
            ahead, term = lax.optimization_barrier((ahead, term))
            term = ahead.astype(f32) + term
        total = term
        low = total.astype(bf16)
        ahead = hop(low)
        if p < tp - 1:
            moved, (low, first) = settle(moved, (low, first), live)
        elif fill is not None:
            ahead, result = settle(ahead, fill(low), live)
            filled.append(result)
        else:
            ahead, _ = settle(ahead, (), live)
    return pieces, ahead.astype(f32) + first, filled


def doubling_gather(values, name):
    count = lax.axis_size(name)
    here = lax.axis_index(name)
    step = 1
    while step < count:
        moved = lax.ppermute(values, name, [(i, i ^ step) for i in range(count)])
        upper = (here & step) != 0
        values = jnp.concatenate(
            [jnp.where(upper, moved, values), jnp.where(upper, values, moved)], axis=0
        )
        step *= 2
    return values


def inverse_root(values):
    return lax.rsqrt(jnp.mean(values * values, axis=1, keepdims=True) + norm_eps)


def gather(values, axis=0):
    return lax.all_gather(values, "fsdp", axis=axis, tiled=True)


def scatter(values, axis=0):
    return lax.psum_scatter(values, "fsdp", scatter_dimension=axis, tiled=True)


def local(
    hidden,
    embed,
    lengths,
    attention_norm_gain,
    query_key_value_weight,
    attention_adapter_down,
    attention_adapter_up,
    attention_output_weight,
    feedforward_norm_gain,
    gate_up_weight,
    feedforward_adapter_down,
    feedforward_adapter_up,
    down_weight,
    mixer_norm_gain,
    gate_inner_weight,
    state_input_weight,
    step_projection,
    inner_conv_taps,
    state_conv_taps,
    head_step_bias,
    decay_log_rate,
    inner_skip_gains,
    gated_norm_gain,
    mixer_output_weight,
    output_cotangent,
):
    tp = lax.axis_size("tp")
    fsdp = lax.axis_size("fsdp")
    share, width = hidden.shape
    rows = share * tp
    here = lax.axis_index("tp").astype(jnp.int32)
    place = here.reshape(1)
    lengths = lengths.reshape(-1)
    rank = attention_adapter_down.shape[2]
    head_cols = query_key_value_weight.shape[2]
    units_here = gate_up_weight.shape[2]
    inner_cols = gate_inner_weight.shape[2]
    mixer_heads = inner_cols // HD
    states = state_input_weight.shape[2]
    count = inner_conv_taps.shape[0]
    inner_total = inner_cols * tp

    def piece(values, p):
        return values[p * share : (p + 1) * share]

    own_qkv = jnp.concatenate(
        [query_key_value_weight[:, j, :] for j in range(3)]
        + [attention_adapter_down[:, j, :] for j in range(3)],
        axis=1,
    )
    weight_qkv = gather(own_qkv)
    first_hop = tuple(hop(v) for v in (hidden, embed))

    small = [
        attention_norm_gain,
        feedforward_norm_gain,
        mixer_norm_gain,
        inner_conv_taps.reshape(-1),
        state_conv_taps.reshape(-1),
        inner_skip_gains.reshape(-1),
        gated_norm_gain.reshape(-1),
    ]
    sizes = [v.shape[0] for v in small]
    padding = -sum(sizes) % LANES
    packed = jnp.concatenate(small + [jnp.zeros((padding,), bf16)]).reshape(1, -1)
    spread = gather(packed).astype(f32)
    cuts = [sum(sizes[:i]) for i in range(len(sizes) + 1)]
    parts = [spread[:, cuts[i] : cuts[i + 1]] for i in range(len(sizes))]
    gain_attn, gain_mlp, gain_mixer = (parts[i].reshape(1, -1) for i in range(3))
    taps_x = parts[3].reshape(fsdp, count, mixer_heads, -1)
    taps_x = jnp.transpose(taps_x, (1, 2, 0, 3)).reshape(count, inner_cols)
    taps_s = parts[4].reshape(fsdp, count, 2, -1)
    taps_s = jnp.transpose(taps_s, (1, 2, 0, 3)).reshape(count, 2, states)
    skip = jnp.transpose(parts[5].reshape(fsdp, mixer_heads, -1), (1, 0, 2)).reshape(1, inner_cols)
    gain_gate = jnp.transpose(parts[6].reshape(fsdp, mixer_heads, -1), (1, 0, 2)).reshape(1, inner_cols)
    wide = jnp.concatenate([taps_x, skip, gain_gate, jnp.zeros((2, inner_cols), f32)], axis=0)
    narrow = jnp.pad(taps_s, ((0, 8 - count), (0, 0), (0, LANES - states))).reshape(8, 2 * LANES)
    rates = jnp.pad(
        jnp.stack([head_step_bias, decay_log_rate]), ((0, 6), (0, LANES - mixer_heads))
    )

    places = jnp.arange(rows, dtype=jnp.int32)
    ends = [jnp.sum(lengths[: i + 1]) for i in range(lengths.shape[0] - 1)]
    position = places - starts_of(places, ends)
    freqs = jnp.exp(jnp.arange(HDA // 2, dtype=f32) * (-2.0 * math.log(10000.0) / HDA))
    angles = position.astype(f32)[:, None] * freqs[None, :]
    cosine = jnp.cos(angles)
    sine = jnp.sin(angles)
    cosine = jnp.concatenate([cosine, cosine], axis=1)
    sine = jnp.concatenate([-sine, sine], axis=1)

    own_fc1 = jnp.concatenate(
        [gate_up_weight[:, j, :] for j in range(2)] + [feedforward_adapter_down], axis=1
    )
    own_zx = jnp.concatenate(
        [gate_inner_weight[:, j, :] for j in range(2)]
        + [jnp.pad(state_input_weight[:, j, :], ((0, 0), (0, LANES - states))) for j in range(2)]
        + [jnp.pad(step_projection, ((0, 0), (0, LANES - mixer_heads)))],
        axis=1,
    )
    weight_o = gather(attention_output_weight, 1)
    weight_fc1 = gather(own_fc1)
    weight_fc2 = gather(down_weight, 1)
    weight_zx = gather(own_zx)
    weight_out = gather(mixer_output_weight, 1)

    def norm_rows(pair):
        pair = [v.astype(f32) for v in pair]
        squares = sum(jnp.sum(v * v, axis=1, keepdims=True) for v in pair)
        inv_root = lax.rsqrt(squares / (2 * width) + norm_eps)
        return [
            (v * inv_root * gain_attn[:, i * width : (i + 1) * width]).astype(bf16)
            for i, v in enumerate(pair)
        ]

    raw, normed = [(hidden, embed), first_hop], []
    for p in range(2, tp):
        moved = tuple(hop(v) for v in raw[-1])
        normed.append(norm_rows(raw[p - 2]))
        raw.append(tie(moved, normed[-1]))
    normed += [norm_rows(v) for v in raw[len(normed) :]]

    own_ups = jnp.concatenate(
        [attention_adapter_up[:, j, :] for j in range(3)]
        + [feedforward_adapter_up[:, j, :] for j in range(2)],
        axis=1,
    )
    ups = doubling_gather(tie(own_ups, raw[-2]), "fsdp")
    fc_up = ups[:, 3 * head_cols :]
    out_grad = [tie(output_cotangent, raw[-1])]
    normed_parts, projected = [], []
    for i in range(tp - 1):
        moved = hop(out_grad[-1])
        if i < tp - 2:
            low, high = (tp * i) // (tp - 2), (tp * (i + 1)) // (tp - 2)
            normed_parts.append(jnp.concatenate([jnp.concatenate(v, axis=1) for v in normed[low:high]], axis=0))
            projected.append(mm(normed_parts[-1], weight_qkv))
            moved = tie(moved, projected)
        else:
            attended, queries, keys, values = attention_forward(
                place, lengths, tp, projected, ups, head_cols, cosine, sine
            )
            moved = tie(moved, attended)
        out_grad.append(moved)
    lora_rows = jnp.concatenate([v[:, 3 * head_cols :].astype(bf16) for v in projected], axis=0)
    attended, lora_rows, out_grad[-1] = lax.optimization_barrier((attended, lora_rows, moved))
    out_grad_rows = jnp.concatenate(out_grad, axis=0)
    mixed, (normed_rows,) = ring_scatter(
        lambda p, t: mm(piece(after(attended, t), p), weight_o),
        [lambda t, _: jnp.concatenate(tie(normed_parts, t), axis=0)],
    )

    mlp_root = inverse_root(mixed)
    gate_up, fc_mid, units = [], [], []

    def feed(p, rows_in):
        wide_rows = mm(rows_in, weight_fc1)
        middle = wide_rows[:, 2 * units_here :].astype(bf16)
        both = (wide_rows[:, : 2 * units_here] + mm(middle, fc_up)).astype(bf16)
        gate, up = both[:, :units_here].astype(f32), both[:, units_here:].astype(f32)
        unit = (jax.nn.gelu(gate) * up).astype(bf16)
        fc_mid.append(middle)
        gate_up.append(both)
        units.append(unit)
        return mm(unit, weight_fc2)

    mlp_in, branch, _ = ring_both((mixed * mlp_root * gain_mlp).astype(bf16), feed)
    residual = hidden.astype(f32) + mixed + branch

    mixer_root = inverse_root(residual)
    kept = []

    def mix(p, rows_in):
        result = mm(rows_in, weight_zx)
        if p == 0:
            kept.append(mm_nt(tie(out_grad_rows, result), weight_out).astype(bf16))
        elif p == 1:
            kept.append(jnp.concatenate(tie(units, result), axis=0))
            kept.append(jnp.concatenate(tie(mlp_in, result), axis=0))
        return (result, kept[-1])

    mixer_in, zxs = ring_gather((residual * mixer_root * gain_mixer).astype(bf16), mix)
    zxs = [v[0] for v in zxs]
    grad_scaled, units_rows, mlp_rows = kept
    mixer_rows = jnp.concatenate(mixer_in, axis=0)
    zx = jnp.concatenate([v[:, : 2 * inner_cols].astype(bf16) for v in zxs], axis=0)
    sd = jnp.concatenate([v[:, 2 * inner_cols :] for v in zxs], axis=0)
    gated, chunk_states = mixer_forward(place, lengths, tp, zx, sd, wide, narrow, rates)
    gated_wide = gated.astype(f32)
    sums = jnp.stack(
        [
            jnp.sum(gated_wide * gated_wide, axis=1),
            jnp.sum(grad_scaled.astype(f32) * gain_gate * gated_wide, axis=1),
        ],
        axis=0,
    )
    sums = jnp.roll(jnp.flip(sums.reshape(2, tp, share), axis=1), here + 1, axis=1)
    sums = lax.psum(sums, "tp")
    sums = jnp.flip(jnp.roll(sums, -(here + 1), axis=1), axis=1).reshape(2, rows)
    gate_root = lax.rsqrt(sums[0] / inner_total + norm_eps)
    stats = jnp.stack([gate_root, gate_root**3 * sums[1] / inner_total], axis=1)
    scaled = (gated_wide * gate_root[:, None] * gain_gate).astype(bf16)
    out_rows, stats = lax.optimization_barrier((mm(scaled, weight_out).astype(bf16), stats))
    out_terms = [piece(out_rows, p) for p in range(tp)]
    out = hop(out_terms[1 % tp])

    grad_all, grad_wide, grad_narrow, grad_rates = mixer_backward(
        place, lengths, tp, zx, sd, grad_scaled, stats, chunk_states, wide, narrow, rates
    )
    out, grad_all = lax.optimization_barrier((out, grad_all))
    out = out.astype(f32) + out_terms[2 % tp].astype(f32)

    def by_fsdp(values):
        lead = values.shape[:-1]
        cut = values.reshape(lead + (fsdp, values.shape[-1] // fsdp))
        return jnp.moveaxis(cut, -2, 0).reshape(fsdp, -1)

    def small_gradients(token):
        taps, bars, sums_r = tie((grad_wide, grad_narrow, grad_rates), token)
        return [
            by_fsdp(taps[:count].reshape(count, mixer_heads, HD)),
            by_fsdp(taps[4].reshape(mixer_heads, HD)),
            by_fsdp(taps[5].reshape(mixer_heads, HD)),
            jnp.broadcast_to(sums_r[:2, :mixer_heads].reshape(1, -1), (fsdp, 2 * mixer_heads)),
            by_fsdp(bars[:count].reshape(count, 2, LANES)[:, :, :states]),
        ]

    grad_mixer_in, (sum_w_out, sum_w_zx, small) = ring_scatter(
        lambda p, t: mm_nt(piece(after(grad_all, t), p), weight_zx),
        [
            lambda t, _: mm_tn(tie(scaled, t), out_grad_rows).astype(bf16),
            lambda t, _: mm_tn(tie(mixer_rows, t), grad_all).astype(bf16),
            lambda t, _: small_gradients(t),
        ],
    )
    sum_w_out = scatter(sum_w_out, 1)
    sum_w_zx = scatter(sum_w_zx)
    small_sizes = [v.shape[1] for v in small]
    small_cuts = [sum(small_sizes[:i]) for i in range(len(small_sizes) + 1)]
    small_task = Halving(jnp.concatenate(small, axis=1), "fsdp")
    grad_residual, grad_residual_low, grad_gain_mixer = norm_back(
        [residual], grad_mixer_in, gain_mixer, output_cotangent, True
    )

    grad_gate_up = []

    def feed_back(p, grad_rows):
        grad_units = mm_nt(grad_rows, weight_fc2)
        gate = gate_up[p][:, :units_here].astype(f32)
        up = gate_up[p][:, units_here:].astype(f32)
        raised, back = jax.vjp(jax.nn.gelu, gate)
        both = jnp.concatenate(
            [back(grad_units * up)[0].astype(bf16), (grad_units * raised).astype(bf16)], axis=1
        )
        both = jnp.concatenate([both, mm_nt(both, fc_up).astype(bf16)], axis=1)
        grad_gate_up.append(both)
        return mm_nt(both, weight_fc1)

    def fc2_fill(token, _):
        rows_in = tie(units_rows, (sum_w_out, token))
        return mm_tn(rows_in, jnp.concatenate(grad_branch, axis=0)).astype(bf16)

    def fc1_fill(token, _):
        return mm_tn(tie(mlp_rows, token), jnp.concatenate(grad_gate_up, axis=0)).astype(bf16)

    grad_branch, back_terms = ring_gather(
        grad_residual_low, lambda p, v: feed_back(p, v) if p < tp - 1 else (), [small_task]
    )
    grad_mlp_in, filled = ring_scatter(
        lambda p, t: feed_back(p, after(grad_branch[p], t))
        if p == tp - 1
        else tie(back_terms[p], grad_branch[-1]),
        [fc2_fill] + [lambda t, _: ()] * (tp - 3) + [fc1_fill],
    )
    sum_w_fc2, sum_w_fc1 = filled[0], filled[-1]
    sum_w_fc2 = scatter(sum_w_fc2, 1)
    sum_w_fc1 = scatter(sum_w_fc1)
    grad_gate_up_rows = jnp.concatenate(grad_gate_up, axis=0)
    _, grad_mixed_low, grad_gain_mlp = norm_back([mixed], grad_mlp_in, gain_mlp, grad_residual, True)
    gain_task = Halving(
        jnp.concatenate([grad_gain_mixer.reshape(fsdp, -1), grad_gain_mlp.reshape(fsdp, -1)], axis=1), "fsdp"
    )

    fc_ups = []

    def attended_back(p, rows_in):
        result = mm_nt(rows_in, weight_o).astype(bf16)
        if p == 0:
            fc_ups.append(
                mm_tn(tie(jnp.concatenate(fc_mid, axis=0), rows_in), grad_gate_up_rows[:, : 2 * units_here])
            )
            result = tie(result, fc_ups[0])
        return result

    grad_mixed, grad_attended = ring_gather(tie(grad_mixed_low, sum_w_zx), attended_back, [gain_task])
    sum_w_o = mm_tn(tie(attended, sum_w_fc2), jnp.concatenate(grad_mixed, axis=0)).astype(bf16)
    grad_attended[-1] = tie(grad_attended[-1], sum_w_o)
    sum_w_o = scatter(sum_w_o, 1)
    out = hop(out.astype(bf16))
    grad_projected = attention_backward(
        place, lengths, queries, keys, values, ups, grad_attended, cosine, sine
    )
    out, grad_projected, sum_w_fc1 = lax.optimization_barrier((out, grad_projected, sum_w_fc1))
    out = out.astype(f32) + out_terms[3 % tp].astype(f32)
    out = hop(out.astype(bf16))
    sum_w_qkv = mm_tn(normed_rows, grad_projected).astype(bf16)
    out, sum_w_qkv, grad_projected = lax.optimization_barrier((out, sum_w_qkv, grad_projected))
    sum_w_qkv = scatter(sum_w_qkv)

    at_t = 2 * inner_cols + 2 * LANES

    def finish_out(token):
        total = tie(out, token).astype(f32) + out_terms[4 % tp].astype(f32)
        for p in range(5, tp + 1):
            total = hop(total.astype(bf16)).astype(f32) + out_terms[p % tp].astype(f32)
        return residual + total

    def finish_adapters(token, tasks):
        rows_in = tie(lora_rows, token)
        grad_up = [
            mm_tn(
                rows_in[:, j * rank : (j + 1) * rank],
                grad_projected[:, j * head_cols : (j + 1) * head_cols],
            )
            for j in range(3)
        ]
        ups_grad = jnp.concatenate(grad_up + fc_ups, axis=1)
        tasks.append(Halving(ups_grad.reshape(fsdp, -1, ups_grad.shape[1]), "fsdp", bf16))
        shared = jnp.concatenate([small_task.result()[small_cuts[4] :], gain_task.result()])
        tasks.append(Doubling(shared, "tp"))
        return ups_grad, shared

    def finish_mixer(token, tasks):
        zx_sum, w_out, w_fc2 = tie((sum_w_zx, sum_w_out, sum_w_fc2), token)
        zx_sum = zx_sum.astype(f32)
        bc_sums.append(zx_sum[:, 2 * inner_cols : at_t])
        return (
            stacked(zx_sum, inner_cols, 2),
            zx_sum[:, at_t : at_t + mixer_heads],
            w_out.astype(f32),
            w_fc2.astype(f32),
        )

    def finish_feed(token, tasks):
        fc1_sum, w_o = tie((sum_w_fc1, sum_w_o), token)
        fc1_sum = fc1_sum.astype(f32)
        tasks.append(
            Doubling(jnp.concatenate([bc_sums[0], fc1_sum[:, 2 * units_here :]], axis=1), "tp", bf16)
        )
        return (
            stacked(fc1_sum, units_here, 2),
            w_o.astype(f32),
            finish_out(token),
        )

    def stacked(values, each, parts):
        values = jnp.stack([values[:, j * each : (j + 1) * each] for j in range(parts)], axis=1)
        return with_layout_constraint(values, Layout(major_to_minor=(0, 1, 2)))

    tasks, bc_sums = [], []
    normed_terms = {}
    pair = mm_nt(grad_projected[share : 3 * share], weight_qkv)
    normed_terms[1], normed_terms[2] = piece(pair, 0), piece(pair, 1)

    def normed_back(p, token):
        if p not in normed_terms:
            normed_terms[p] = mm_nt(piece(after(grad_projected, token), p), weight_qkv)
        return normed_terms[p]

    grad_normed, ((_, mixer_sums, _), feed_sums) = ring_scatter(
        normed_back,
        [lambda t, k: (finish_adapters(t, k), finish_mixer(t, k), normed_back(3 % tp, t)), finish_feed],
        tasks,
    )
    grad_w_zx, grad_w_dt, grad_w_out, grad_w_fc2 = mixer_sums
    grad_w_fc1, grad_w_o, out = feed_sums
    grad_hidden, grad_embed = norm_back(
        [hidden, embed], grad_normed, gain_attn, grad_residual, with_gain=False
    )
    gain_rows = jnp.sum(sum_w_qkv.astype(f32) * own_qkv.astype(f32), axis=1)
    gain_rows = gain_rows / attention_norm_gain.astype(f32)
    grad_down = direct(sum_w_qkv[:, 3 * head_cols :].astype(f32).reshape(tp, -1, 3 * rank), "tp", bf16)
    grad_gain_attn = direct(gain_rows.reshape(tp, -1), "tp")
    grad_w_qkv = jnp.stack(
        [sum_w_qkv[:, j * head_cols : (j + 1) * head_cols].astype(f32) for j in range(3)], axis=1
    )
    small_sum = small_task.result()
    small_parts = [small_sum[small_cuts[i] : small_cuts[i + 1]] for i in range(len(small_sizes))]
    grad_ups, tail = tasks[0].result(), tasks[1].result()
    shared = tasks[2].result()
    tail_sizes = [small_sizes[4], width // fsdp, width // fsdp]
    tail_cuts = [sum(tail_sizes[:i]) for i in range(4)]
    grad_conv_bc, sum_gain_mixer, sum_gain_mlp = (
        tail[tail_cuts[i] : tail_cuts[i + 1]] for i in range(3)
    )
    sum_rates = small_parts[3].reshape(2, mixer_heads)
    return (
        out,
        grad_hidden,
        grad_embed,
        grad_gain_attn,
        grad_w_qkv,
        grad_down.reshape(-1, 3, rank),
        grad_ups[:, : 3 * head_cols].reshape(-1, 3, head_cols),
        grad_w_o,
        sum_gain_mlp,
        grad_w_fc1,
        shared[:, 2 * LANES :],
        grad_ups[:, 3 * head_cols :].reshape(-1, 2, units_here),
        grad_w_fc2,
        sum_gain_mixer,
        grad_w_zx,
        shared[:, : 2 * LANES].reshape(-1, 2, LANES)[:, :, :states],
        grad_w_dt,
        small_parts[0].reshape(count, mixer_heads, -1),
        grad_conv_bc.reshape(count, 2, -1),
        sum_rates[0],
        sum_rates[1],
        small_parts[1].reshape(mixer_heads, -1),
        small_parts[2].reshape(mixer_heads, -1),
        grad_w_out,
    )


def solution(mesh):
    placed = (
        P(("fsdp", "tp"), None),
        P(("fsdp", "tp"), None),
        P("fsdp", None),
        P("fsdp"),
        P("fsdp", None, "tp"),
        P("fsdp", None, None),
        P("fsdp", None, "tp"),
        P("tp", "fsdp"),
        P("fsdp"),
        P("fsdp", None, "tp"),
        P("fsdp", None),
        P("fsdp", None, "tp"),
        P("tp", "fsdp"),
        P("fsdp"),
        P("fsdp", None, "tp"),
        P("fsdp", None, None),
        P("fsdp", "tp"),
        P(None, "tp", "fsdp"),
        P(None, None, "fsdp"),
        P("tp"),
        P("tp"),
        P("tp", "fsdp"),
        P("tp", "fsdp"),
        P("tp", "fsdp"),
        P(("fsdp", "tp"), None),
    )
    return jax.shard_map(
        local,
        mesh=mesh,
        in_specs=placed,
        out_specs=(
            P(("fsdp", "tp"), None),
            P(("fsdp", "tp"), None),
            P(("fsdp", "tp"), None),
            P(("fsdp", "tp")),
            P("fsdp", None, "tp"),
            P(("fsdp", "tp"), None, None),
            P("fsdp", None, "tp"),
            P("tp", "fsdp"),
            P("fsdp"),
            P("fsdp", None, "tp"),
            P("fsdp", None),
            P("fsdp", None, "tp"),
            P("tp", "fsdp"),
            P("fsdp"),
            P("fsdp", None, "tp"),
            P("fsdp", None, None),
            P("fsdp", "tp"),
            P(None, "tp", "fsdp"),
            P(None, None, "fsdp"),
            P("tp"),
            P("tp"),
            P("tp", "fsdp"),
            P("tp", "fsdp"),
            P("tp", "fsdp"),
        ),
        check_vma=False,
    )
```

```python
import functools
import math

import jax
import jax.numpy as jnp
from jax import lax
from jax.experimental import pallas as pl
from jax.experimental.layout import Layout, with_layout_constraint
from jax.experimental.pallas import tpu as pltpu
from jax.sharding import PartitionSpec as P

HDA = 128
HD = 64
LANES = 128
CHUNK = 128

norm_eps = 1e-05
f32 = jnp.float32
bf16 = jnp.bfloat16
HIGHEST = lax.Precision.HIGHEST
VMEM_LIMIT = 56 * 1024 * 1024


def mm(left, right):
    return jnp.dot(left, right, preferred_element_type=f32)


def mm_nt(left, right):
    return lax.dot_general(left, right, (((1,), (1,)), ((), ())), preferred_element_type=f32)


def mm_tn(left, right):
    return lax.dot_general(left, right, (((0,), (0,)), ((), ())), preferred_element_type=f32)


def starts_of(index, ends):
    start = jnp.zeros_like(index)
    for end in ends:
        start = jnp.where(index >= end, end, start)
    return start


def ends_of(lengths_ref):
    ends = []
    end = jnp.int32(0)
    for i in range(lengths_ref.shape[0] - 1):
        end = end + lengths_ref[i]
        ends.append(end)
    return ends


def iota(shape, axis):
    return lax.broadcasted_iota(jnp.int32, shape, axis)


def attention_forward_kernel(
    tp,
    parts,
    place_ref,
    lengths_ref,
    cosine_ref,
    sine_ref,
    q_up,
    k_up,
    v_up,
    *refs,
):
    pieces = refs[: 4 * parts]
    attended_ref, q_ref, k_ref, v_ref, held = refs[4 * parts :]
    rows = q_ref.shape[0]
    share = rows // tp
    rank = q_up.shape[0]
    here = place_ref[0]
    ends = ends_of(lengths_ref)
    for p in range(tp):
        owner = lax.rem(here - p + tp, tp)
        part = pl.ds(pl.multiple_of(owner * share, share), share)
        cosine, sine = cosine_ref[part, :], sine_ref[part, :]
        at = p * share
        source = 0
        while at >= pieces[4 * source].shape[0]:
            at -= pieces[4 * source].shape[0]
            source += 1
        mine = slice(at, at + share)
        for j, (up, target) in enumerate(((q_up, q_ref), (k_up, k_ref), (v_up, v_ref))):
            low = pieces[4 * source + 3][mine, j * rank : (j + 1) * rank].astype(bf16)
            value = pieces[4 * source + j][mine, :] + mm(low, up[...])
            if j < 2:
                value = value * cosine + pltpu.roll(value, HDA // 2, 1) * sine
            target[part, :] = value.astype(bf16)
    block = min(256, rows)
    scale = HDA ** (-0.5)
    for at in range(0, rows, block):
        upto = at + block
        scores = mm_nt(k_ref[:upto, :], q_ref[at:upto, :]) * scale
        query = at + iota((1, block), 1)
        key = iota((upto, 1), 0)
        seen = (key <= query) & (key >= starts_of(query, ends))
        scores = jnp.where(seen, scores, -1e30)
        raised = jnp.exp(scores - jnp.max(scores, axis=0, keepdims=True))
        probs = (raised * (1.0 / jnp.sum(raised, axis=0, keepdims=True))).astype(bf16)
        held[at:upto, :] = mm_tn(probs, v_ref[:upto, :]).astype(bf16)
    for p in range(tp):
        owner = lax.rem(here - p + tp, tp)
        part = pl.ds(pl.multiple_of(owner * share, share), share)
        attended_ref[p * share : (p + 1) * share, :] = held[part, :]


def attention_forward(place, lengths, tp, projected, ups, columns, cosine, sine):
    rows = sum(v.shape[0] for v in projected)
    heads = columns // HDA
    rank = ups.shape[0]
    table_spec = pl.BlockSpec((rows, HDA), lambda h, *_: (0, 0))

    def head_spec(j, height=rows):
        return pl.BlockSpec((height, HDA), lambda h, *_: (0, j * heads + h))

    work = heads * rows * rows * HDA
    return pl.pallas_call(
        functools.partial(attention_forward_kernel, tp, len(projected)),
        out_shape=[jax.ShapeDtypeStruct((rows, columns), bf16)] * 4,
        grid_spec=pltpu.PrefetchScalarGridSpec(
            num_scalar_prefetch=2,
            grid=(heads,),
            in_specs=[table_spec, table_spec]
            + [head_spec(j, rank) for j in range(3)]
            + [
                pl.BlockSpec((v.shape[0], 3 * rank), lambda h, *_: (0, columns // rank))
                if j == 3
                else head_spec(j, v.shape[0])
                for v in projected
                for j in range(4)
            ],
            out_specs=[head_spec(0)] * 4,
            scratch_shapes=[pltpu.VMEM((rows, HDA), bf16)],
        ),
        compiler_params=pltpu.CompilerParams(vmem_limit_bytes=VMEM_LIMIT),
        cost_estimate=pl.CostEstimate(
            flops=4 * work, bytes_accessed=20 * rows * columns, transcendentals=heads * rows * rows
        ),
        name="attention_forward",
    )(place, lengths, cosine, sine, ups, ups, ups, *[v for v in projected for _ in range(4)])


def attention_backward_kernel(
    tp,
    heads,
    place_ref,
    lengths_ref,
    cosine_ref,
    sine_ref,
    q_ref,
    k_ref,
    v_ref,
    q_up,
    k_up,
    v_up,
    *refs,
):
    grad_in = refs[:tp]
    out_ref, held, dq, dk, dv, lora = refs[tp:]
    rows = q_ref.shape[0]
    share = rows // tp
    rank = q_up.shape[0]
    here = place_ref[0]
    head = pl.program_id(0)
    ends = ends_of(lengths_ref)
    for p in range(tp):
        owner = lax.rem(here - p + tp, tp)
        part = pl.ds(pl.multiple_of(owner * share, share), share)
        held[part, :] = grad_in[p][...]
    dk[...] = jnp.zeros_like(dk)
    dv[...] = jnp.zeros_like(dv)

    @pl.when(head == 0)
    def _():
        lora[...] = jnp.zeros_like(lora)

    block = min(256, rows)
    scale = HDA ** (-0.5)
    for at in range(0, rows, block):
        upto = at + block
        query_rows = q_ref[at:upto, :]
        grad_rows = held[at:upto, :]
        scores = mm_nt(k_ref[:upto, :], query_rows) * scale
        query = at + iota((1, block), 1)
        key = iota((upto, 1), 0)
        seen = (key <= query) & (key >= starts_of(query, ends))
        scores = jnp.where(seen, scores, -1e30)
        raised = jnp.exp(scores - jnp.max(scores, axis=0, keepdims=True))
        probs = raised * (1.0 / jnp.sum(raised, axis=0, keepdims=True))
        grad_probs = mm_nt(v_ref[:upto, :], grad_rows)
        cross = jnp.sum(probs * grad_probs, axis=0, keepdims=True)
        grad_scores = (probs * (grad_probs - cross)).astype(bf16)
        dv[:upto, :] += mm(probs.astype(bf16), grad_rows)
        dk[:upto, :] += mm(grad_scores, query_rows)
        dq[at:upto, :] = mm_tn(grad_scores, k_ref[:upto, :])
    for p in range(tp):
        owner = lax.rem(here - p + tp, tp)
        part = pl.ds(pl.multiple_of(owner * share, share), share)
        cosine, sine = cosine_ref[part, :], sine_ref[part, :]
        mine = slice(p * share, (p + 1) * share)
        for j, (source, up) in enumerate(((dq, q_up), (dk, k_up), (dv, v_up))):
            value = source[part, :]
            if j < 2:
                value = value * scale
                value = value * cosine - pltpu.roll(value, HDA // 2, 1) * sine
            low = value.astype(bf16)
            at = pl.multiple_of((j * heads + head) * HDA, HDA)
            out_ref[mine, pl.ds(at, HDA)] = low
            lora[mine, j * rank : (j + 1) * rank] += mm_nt(low, up[...])

    @pl.when(head == heads - 1)
    def _():
        out_ref[:, 3 * heads * HDA :] = lora[...].astype(bf16)


def attention_backward(place, lengths, queries, keys, values, ups, pieces, cosine, sine):
    tp = len(pieces)
    share, columns = pieces[0].shape
    rows = share * tp
    heads = columns // HDA
    rank = ups.shape[0]
    piece_spec = pl.BlockSpec((share, HDA), lambda h, *_: (0, h))
    table_spec = pl.BlockSpec((rows, HDA), lambda h, *_: (0, 0))
    head_spec = pl.BlockSpec((rows, HDA), lambda h, *_: (0, h))

    def up_spec(j):
        return pl.BlockSpec((rank, HDA), lambda h, *_: (0, j * heads + h))

    total = 3 * columns + 3 * rank
    work = heads * rows * rows * HDA
    return pl.pallas_call(
        functools.partial(attention_backward_kernel, tp, heads),
        out_shape=jax.ShapeDtypeStruct((rows, total), bf16),
        grid_spec=pltpu.PrefetchScalarGridSpec(
            num_scalar_prefetch=2,
            grid=(heads,),
            in_specs=[table_spec, table_spec]
            + [head_spec] * 3
            + [up_spec(j) for j in range(3)]
            + [piece_spec] * tp,
            out_specs=pl.BlockSpec((rows, total), lambda h, *_: (0, 0)),
            scratch_shapes=[pltpu.VMEM((rows, HDA), bf16)]
            + [pltpu.VMEM((rows, HDA), f32)] * 3
            + [pltpu.VMEM((rows, 3 * rank), f32)],
        ),
        compiler_params=pltpu.CompilerParams(vmem_limit_bytes=VMEM_LIMIT),
        cost_estimate=pl.CostEstimate(
            flops=10 * work, bytes_accessed=14 * rows * columns, transcendentals=heads * rows * rows
        ),
        name="attention_backward",
    )(place, lengths, cosine, sine, queries, keys, values, ups, ups, ups, *pieces)


def conv_rows(extended, taps, position):
    count = 4
    rows = extended.shape[0] - 8
    total = None
    for k in range(count):
        moved = extended[8 - k : 8 - k + rows, :]
        if k:
            moved = jnp.where(position >= k, moved, 0.0)
        term = taps[count - 1 - k : count - k, :] * moved
        total = term if total is None else total + term
    return total


def conv_back(extended, taps, position):
    count = 4
    rows = extended.shape[0] - 8
    total = None
    for k in range(count):
        kept = jnp.where(position >= k, extended, 0.0) if k else extended
        term = taps[count - 1 - k : count - k, :] * kept[k : k + rows, :]
        total = term if total is None else total + term
    return total


def taps_back(extended, grad, position, target):
    count = 4
    rows = extended.shape[0] - 8
    for k in range(count):
        moved = extended[8 - k : 8 - k + rows, :]
        if k:
            moved = jnp.where(position >= k, moved, 0.0)
        at = count - 1 - k
        target[at : at + 1, :] += jnp.sum(grad * moved, axis=0, keepdims=True)


def silu_grad(value, gate):
    return gate * (1.0 + value * (1.0 - gate))


class Chunk:
    def __init__(self, c0, ends, zx, before, sd, sd_before, wide, narrow, rates):
        rows = zx.shape[0]
        width = zx.shape[1] // 2
        self.rows, self.width = rows, width
        index = c0 + iota((rows, 1), 0)
        start = starts_of(index, ends)
        self.index, self.start = index, start
        self.position = index - start
        last_start = starts_of(c0 + rows - 1, ends)
        self.z = zx[:, :width].astype(f32)
        self.x_ext = jnp.concatenate(
            [before[...].astype(f32)[8:16, :], zx[:, width:].astype(f32)], axis=0
        )
        self.s_ext = jnp.concatenate([sd_before[:, : 2 * LANES], sd[:, : 2 * LANES]], axis=0)
        self.pre = conv_rows(self.x_ext, wide, self.position)
        self.gate_x = jax.nn.sigmoid(self.pre)
        self.xc = self.pre * self.gate_x
        self.pre_s = conv_rows(self.s_ext, narrow, self.position)
        self.gate_s = jax.nn.sigmoid(self.pre_s)
        sc = self.pre_s * self.gate_s
        self.b_low = sc[:, :HD].astype(bf16)
        self.c_low = sc[:, LANES : LANES + HD].astype(bf16)
        self.raw = sd[:, 2 * LANES : 3 * LANES] + rates[0:1, :]
        self.step = jnp.maximum(self.raw, 0.0) + jnp.log1p(jnp.exp(-jnp.abs(self.raw)))
        self.rate = jnp.exp(rates[1:2, :])
        row, col = iota((rows, rows), 0), iota((rows, rows), 1)
        below = (col <= row).astype(f32)
        self.cum = jnp.dot(below, -self.step * self.rate, precision=HIGHEST, preferred_element_type=f32)
        self.cum_t = self.cum.T
        self.allowed = (col <= row) & ((c0 + col) >= start)
        self.inner = jnp.where(self.allowed, mm_nt(self.c_low, self.b_low), 0.0)
        last = self.cum[rows - 1 : rows, :]
        self.into = jnp.exp(self.cum) * (start < c0).astype(f32)
        self.onto = jnp.exp(last - self.cum) * (index >= last_start).astype(f32)
        self.decay = jnp.exp(last) * (last_start < c0).astype(f32)
        self.low_half = iota((1, LANES), 1) < HD

    def pair(self, table, i):
        return jnp.where(self.low_half, table[:, 2 * i : 2 * i + 1], table[:, 2 * i + 1 : 2 * i + 2])

    def spread(self, h):
        return jnp.exp(jnp.minimum(self.cum[:, h : h + 1] - self.cum_t[h : h + 1, :], 0.0))


def mixer_forward_kernel(
    place_ref, lengths_ref, zx, before, sd, sd_before, wide, narrow, rates, gated, states, state
):
    rows = zx.shape[0]
    c0 = pl.program_id(0) * rows
    ends = ends_of(lengths_ref)

    @pl.when(pl.program_id(0) == 0)
    def _():
        state[...] = jnp.zeros_like(state)

    v = Chunk(c0, ends, zx, before, sd, sd_before, wide, narrow, rates)
    state_low = state[...].astype(bf16)
    states[...] = state_low
    for i in range(v.width // LANES):
        cols = slice(i * LANES, (i + 1) * LANES)
        xc = v.xc[:, cols]
        xs = v.pair(v.step, i) * xc
        xs_low = xs.astype(bf16)
        first = (v.spread(2 * i) * v.inner).astype(bf16)
        second = (v.spread(2 * i + 1) * v.inner).astype(bf16)
        y = jnp.where(v.low_half, mm(first, xs_low), mm(second, xs_low))
        y = y + v.pair(v.into, i) * mm(v.c_low, state_low[:, cols])
        y = y + wide[4:5, cols] * xc
        z = v.z[:, cols]
        gated[:, cols] = (y * z * jax.nn.sigmoid(z)).astype(bf16)
        state[:, cols] = v.pair(v.decay, i) * state[:, cols] + mm_tn(
            v.b_low, (v.pair(v.onto, i) * xs).astype(bf16)
        )


def split_sum(values, ones):
    high = values.astype(bf16)
    low = (values - high.astype(f32)).astype(bf16)
    return mm(high, ones) + mm(low, ones)


def mixer_backward_kernel(
    chunks,
    place_ref,
    lengths_ref,
    zx,
    before,
    sd,
    sd_before,
    grad_scaled,
    stats,
    states,
    wide,
    narrow,
    rates,
    grad_all,
    grad_wide,
    grad_narrow,
    grad_rates,
    grad_state,
    next_pre,
    next_pre_s,
    carry,
    products,
    directs,
    grad_pre,
):
    rows = zx.shape[0]
    turn = pl.program_id(0)
    c0 = (chunks - 1 - turn) * rows
    ends = ends_of(lengths_ref)

    @pl.when(turn == 0)
    def _():
        for ref in (grad_state, next_pre, next_pre_s, carry, grad_wide, grad_narrow, grad_rates):
            ref[...] = jnp.zeros_like(ref)

    v = Chunk(c0, ends, zx, before, sd, sd_before, wide, narrow, rates)
    width = v.width
    root, pull = stats[:, 0:1], stats[:, 1:2]
    grad_inner = jnp.zeros((rows, rows), f32)
    grad_b = jnp.zeros((rows, HD), f32)
    grad_c = jnp.zeros((rows, HD), f32)
    for i in range(width // LANES):
        cols = slice(i * LANES, (i + 1) * LANES)
        xc = v.xc[:, cols]
        step = v.pair(v.step, i)
        xs = step * xc
        xs_low = xs.astype(bf16)
        spread_a, spread_b = v.spread(2 * i), v.spread(2 * i + 1)
        first = (spread_a * v.inner).astype(bf16)
        second = (spread_b * v.inner).astype(bf16)
        state_low = states[:, cols]
        into, onto = v.pair(v.into, i), v.pair(v.onto, i)
        y = jnp.where(v.low_half, mm(first, xs_low), mm(second, xs_low))
        y = y + into * mm(v.c_low, state_low)
        skip, gain = wide[4:5, cols], wide[5:6, cols]
        whole = y + skip * xc
        z = v.z[:, cols]
        gate = jax.nn.sigmoid(z)
        gated = whole * z * gate
        incoming = grad_scaled[:, cols].astype(f32)
        rooted = incoming * root
        grad_wide[5:6, cols] += jnp.sum(rooted * gated, axis=0, keepdims=True)
        grad_gated = rooted * gain - gated * pull
        grad_y = grad_gated * z * gate
        grad_all[:, cols] = (grad_gated * whole * silu_grad(z, gate)).astype(bf16)
        grad_wide[4:5, cols] += jnp.sum(grad_y * xc, axis=0, keepdims=True)
        low = grad_y.astype(bf16)
        low_a = jnp.where(v.low_half, grad_y, 0.0).astype(bf16)
        low_b = jnp.where(v.low_half, 0.0, grad_y).astype(bf16)
        grad_inner = grad_inner + spread_a * mm_nt(low_a, xs_low) + spread_b * mm_nt(low_b, xs_low)
        grad_end = grad_state[:, cols]
        grad_end_low = grad_end.astype(bf16)
        grad_xs = jnp.where(v.low_half, mm_tn(first, low), mm_tn(second, low))
        grad_xs = grad_xs + onto * mm(v.b_low, grad_end_low)
        into_y = (into * grad_y).astype(bf16)
        onto_x = (onto * xs).astype(bf16)
        grad_b = grad_b + mm_nt(onto_x, grad_end_low)
        grad_c = grad_c + mm_nt(into_y, state_low)
        grad_state[:, cols] = v.pair(v.decay, i) * grad_end + mm_tn(v.c_low, into_y)
        products[:, cols] = low.astype(f32) * y - xs_low.astype(f32) * grad_xs
        directs[:, cols] = xc * grad_xs
        grad_xc = step * grad_xs + skip * grad_y
        grad_pre[:, cols] = grad_xc * silu_grad(v.pre[:, cols], v.gate_x[:, cols])
    grad_inner = jnp.where(v.allowed, grad_inner, 0.0).astype(bf16)
    grad_b = grad_b + mm_tn(grad_inner, v.c_low)
    grad_c = grad_c + mm(grad_inner, v.b_low)

    lane, head = iota((width, LANES), 0), iota((width, LANES), 1)
    ones = ((lane >= head * HD) & (lane < head * HD + HD)).astype(bf16)
    grad_cum = split_sum(products[...], ones)
    direct = split_sum(directs[...], ones)
    row, col = iota((rows, rows), 0), iota((rows, rows), 1)
    col_start = starts_of(c0 + iota((1, rows), 1), ends)
    above = ((col >= row) & (col_start <= c0 + row)).astype(f32)
    next_start = starts_of(c0 + rows, ends)
    reaches = (v.index >= next_start).astype(f32)
    after = jnp.dot(above, grad_cum, precision=HIGHEST, preferred_element_type=f32) + reaches * carry[0:1, :]
    flux = jnp.sum(grad_state[...] * states[...].astype(f32), axis=0, keepdims=True)
    carry[...] = split_sum(jnp.broadcast_to(flux, (8, width)), ones)
    grad_log = -v.step * v.rate * after
    grad_raw = (direct - v.rate * after) * jax.nn.sigmoid(v.raw)
    grad_rates[0:1, :] += jnp.sum(grad_raw, axis=0, keepdims=True)
    grad_rates[1:2, :] += jnp.sum(grad_log, axis=0, keepdims=True)

    index_ext = c0 + iota((rows + 8, 1), 0)
    position_ext = index_ext - starts_of(index_ext, ends)
    taps_back(v.x_ext, grad_pre[...], v.position, grad_wide)
    extended = jnp.concatenate([grad_pre[...], next_pre[...]], axis=0)
    grad_all[:, width : 2 * width] = conv_back(extended, wide, position_ext).astype(bf16)
    next_pre[...] = grad_pre[0:8, :]

    blank = jnp.zeros((rows, LANES - HD), f32)
    grad_sc = jnp.concatenate([grad_b, blank, grad_c, blank], axis=1)
    grad_pre_s = grad_sc * silu_grad(v.pre_s, v.gate_s)
    taps_back(v.s_ext, grad_pre_s, v.position, grad_narrow)
    extended_s = jnp.concatenate([grad_pre_s, next_pre_s[...]], axis=0)
    grad_all[:, 2 * width : 2 * width + 2 * LANES] = conv_back(extended_s, narrow, position_ext).astype(bf16)
    next_pre_s[...] = grad_pre_s[0:8, :]
    grad_all[:, 2 * width + 2 * LANES :] = grad_raw.astype(bf16)


def chunk_of(tp, rows):
    return math.gcd(rows // tp, CHUNK)


def mixer_specs(tp, rows, chunk, order):
    share = rows // tp
    per_share = share // chunk

    def here(place, c):
        owner = lax.div(c, per_share)
        piece = lax.rem(place[0] - owner + tp, tp)
        return piece * per_share + lax.rem(c, per_share)

    def chunk_map(i, place, lengths):
        return (here(place, order(i)), 0)

    def before_map(unit, column):
        def index(i, place, lengths):
            c = order(i)
            previous = jnp.maximum(c - 1, 0)
            return (here(place, previous) * (chunk // unit) + chunk // unit - 1, column)

        return index

    def fixed(i, place, lengths):
        return (0, 0)

    return chunk_map, before_map, fixed


def mixer_forward(place, lengths, tp, zx, sd, wide, narrow, rates):
    rows, width = zx.shape[0], zx.shape[1] // 2
    chunk = chunk_of(tp, rows)
    chunks = rows // chunk
    chunk_map, before_map, fixed = mixer_specs(tp, rows, chunk, lambda i: i)
    work = rows * width * chunk
    return pl.pallas_call(
        mixer_forward_kernel,
        out_shape=[
            jax.ShapeDtypeStruct((rows, width), bf16),
            jax.ShapeDtypeStruct((chunks, HD, width), bf16),
        ],
        grid_spec=pltpu.PrefetchScalarGridSpec(
            num_scalar_prefetch=2,
            grid=(chunks,),
            in_specs=[
                pl.BlockSpec((chunk, 2 * width), chunk_map),
                pl.BlockSpec((16, width), before_map(16, 1)),
                pl.BlockSpec((chunk, 3 * LANES), chunk_map),
                pl.BlockSpec((8, 3 * LANES), before_map(8, 0)),
                pl.BlockSpec((8, width), fixed),
                pl.BlockSpec((8, 2 * LANES), fixed),
                pl.BlockSpec((8, LANES), fixed),
            ],
            out_specs=[
                pl.BlockSpec((chunk, width), chunk_map),
                pl.BlockSpec((None, HD, width), lambda i, *_: (i, 0, 0)),
            ],
            scratch_shapes=[pltpu.VMEM((HD, width), f32)],
        ),
        compiler_params=pltpu.CompilerParams(vmem_limit_bytes=VMEM_LIMIT),
        cost_estimate=pl.CostEstimate(
            flops=8 * work, bytes_accessed=8 * rows * width, transcendentals=4 * rows * width
        ),
        name="mixer_forward",
    )(place, lengths, zx, zx, sd, sd, wide, narrow, rates)


def mixer_backward(place, lengths, tp, zx, sd, grad_scaled, stats, states, wide, narrow, rates):
    rows, width = zx.shape[0], zx.shape[1] // 2
    chunk = chunk_of(tp, rows)
    chunks = rows // chunk
    chunk_map, before_map, fixed = mixer_specs(tp, rows, chunk, lambda i: chunks - 1 - i)
    work = rows * width * chunk
    return pl.pallas_call(
        functools.partial(mixer_backward_kernel, chunks),
        out_shape=[
            jax.ShapeDtypeStruct((rows, 2 * width + 3 * LANES), bf16),
            jax.ShapeDtypeStruct((8, width), f32),
            jax.ShapeDtypeStruct((8, 2 * LANES), f32),
            jax.ShapeDtypeStruct((8, LANES), f32),
        ],
        grid_spec=pltpu.PrefetchScalarGridSpec(
            num_scalar_prefetch=2,
            grid=(chunks,),
            in_specs=[
                pl.BlockSpec((chunk, 2 * width), chunk_map),
                pl.BlockSpec((16, width), before_map(16, 1)),
                pl.BlockSpec((chunk, 3 * LANES), chunk_map),
                pl.BlockSpec((8, 3 * LANES), before_map(8, 0)),
                pl.BlockSpec((chunk, width), chunk_map),
                pl.BlockSpec((chunk, 2), chunk_map),
                pl.BlockSpec((None, HD, width), lambda i, *_: (chunks - 1 - i, 0, 0)),
                pl.BlockSpec((8, width), fixed),
                pl.BlockSpec((8, 2 * LANES), fixed),
                pl.BlockSpec((8, LANES), fixed),
            ],
            out_specs=[
                pl.BlockSpec((chunk, 2 * width + 3 * LANES), chunk_map),
                pl.BlockSpec((8, width), fixed),
                pl.BlockSpec((8, 2 * LANES), fixed),
                pl.BlockSpec((8, LANES), fixed),
            ],
            scratch_shapes=[
                pltpu.VMEM((HD, width), f32),
                pltpu.VMEM((8, width), f32),
                pltpu.VMEM((8, 2 * LANES), f32),
                pltpu.VMEM((8, LANES), f32),
                pltpu.VMEM((chunk, width), f32),
                pltpu.VMEM((chunk, width), f32),
                pltpu.VMEM((chunk, width), f32),
            ],
        ),
        compiler_params=pltpu.CompilerParams(vmem_limit_bytes=VMEM_LIMIT),
        cost_estimate=pl.CostEstimate(
            flops=24 * work, bytes_accessed=12 * rows * width, transcendentals=5 * rows * width
        ),
        name="mixer_backward",
    )(place, lengths, zx, zx, sd, sd, grad_scaled, stats, states, wide, narrow, rates)


def norm_pairs_kernel(pairs, gain, *refs):
    out = refs[2 * pairs]
    width = refs[0].shape[1]
    for j in range(pairs):
        both = [refs[2 * j + i][...].astype(f32) for i in range(2)]
        squares = sum(jnp.sum(v * v, axis=1, keepdims=True) for v in both)
        inv_root = lax.rsqrt(squares / (2 * width) + norm_eps)
        for i, v in enumerate(both):
            cols = slice(i * width, (i + 1) * width)
            out[j, :, cols] = (v * inv_root * gain[:, cols]).astype(bf16)


def norm_pairs(pairs, gain):
    rows, width = pairs[0][0].shape
    block = math.gcd(rows, 64)
    count = len(pairs)
    result = pl.pallas_call(
        functools.partial(norm_pairs_kernel, count),
        out_shape=jax.ShapeDtypeStruct((count, rows, 2 * width), bf16),
        grid=(rows // block,),
        in_specs=[pl.BlockSpec((1, 2 * width), lambda i: (0, 0))]
        + [pl.BlockSpec((block, width), lambda i: (i, 0))] * (2 * count),
        out_specs=pl.BlockSpec((count, block, 2 * width), lambda i: (0, i, 0)),
        compiler_params=pltpu.CompilerParams(vmem_limit_bytes=VMEM_LIMIT),
        cost_estimate=pl.CostEstimate(
            flops=10 * count * rows * width, bytes_accessed=8 * count * rows * width, transcendentals=rows
        ),
        name="norm_pairs",
    )(gain, *[v for pair in pairs for v in pair])
    return result.reshape(count * rows, 2 * width)


def norm_back_kernel(parts, with_base, with_low, with_gain, *refs):
    values, refs = refs[:parts], refs[parts:]
    grad, gain, refs = refs[0], refs[1], refs[2:]
    base, refs = (refs[0], refs[1:]) if with_base else (None, refs)
    outs, refs = refs[:parts], refs[parts:]
    low, refs = (refs[0], refs[1:]) if with_low else (None, refs)
    if with_gain:
        grad_gain = refs[0]

        @pl.when(pl.program_id(0) == 0)
        def _():
            grad_gain[...] = jnp.zeros_like(grad_gain)

    width = grad.shape[1]
    each = width // parts
    wide = [v[...].astype(f32) for v in values]
    squares = sum(jnp.sum(v * v, axis=1, keepdims=True) for v in wide)
    inv_root = lax.rsqrt(squares / width + norm_eps)
    units = [v * inv_root for v in wide]
    grads = [grad[:, i * each : (i + 1) * each] for i in range(parts)]
    grad_units = [g * gain[:, i * each : (i + 1) * each] for i, g in enumerate(grads)]
    cross = sum(jnp.sum(g * u, axis=1, keepdims=True) for g, u in zip(grad_units, units)) / width
    for i in range(parts):
        cols = slice(i * each, (i + 1) * each)
        if with_gain:
            grad_gain[0:1, cols] += jnp.sum(grads[i] * units[i], axis=0, keepdims=True)
        result = inv_root * (grad_units[i] - units[i] * cross)
        if with_base and i == 0:
            result = result + base[...].astype(f32)
        outs[i][...] = result
        if with_low and i == 0:
            low[...] = result.astype(bf16)


def norm_back(values, grad, gain, base=None, with_low=False, with_gain=True):
    rows, width = grad.shape
    parts = len(values)
    block = math.gcd(rows, 64)
    row_spec = pl.BlockSpec((block, width // parts), lambda i: (i, 0))
    full_spec = pl.BlockSpec((block, width), lambda i: (i, 0))
    operands = list(values) + [grad, gain] + ([base] if base is not None else [])
    shapes = [jax.ShapeDtypeStruct((rows, width // parts), f32)] * parts
    shapes += [jax.ShapeDtypeStruct((rows, width // parts), bf16)] if with_low else []
    results = pl.pallas_call(
        functools.partial(norm_back_kernel, parts, base is not None, with_low, with_gain),
        out_shape=shapes + [jax.ShapeDtypeStruct((8, width), f32)] * int(with_gain),
        grid=(rows // block,),
        in_specs=[row_spec] * parts
        + [full_spec, pl.BlockSpec((1, width), lambda i: (0, 0))]
        + ([row_spec] if base is not None else []),
        out_specs=[row_spec] * (parts + int(with_low))
        + [pl.BlockSpec((8, width), lambda i: (0, 0))] * int(with_gain),
        compiler_params=pltpu.CompilerParams(vmem_limit_bytes=VMEM_LIMIT),
        cost_estimate=pl.CostEstimate(
            flops=20 * rows * width, bytes_accessed=14 * rows * width, transcendentals=rows
        ),
        name="norm_back",
    )(*operands)
    return list(results[:-1]) + [results[-1][0]] if with_gain else list(results)


def tie(value, others):
    return lax.optimization_barrier((value, others))[0]


def after(value, token):
    return value if token is None else tie(value, token)


def ring_pairs():
    tp = lax.axis_size("tp")
    return [(i, (i + 1) % tp) for i in range(tp)]


def hop(values):
    return lax.ppermute(values, "tp", ring_pairs())


class Halving:
    def __init__(self, values, name, sent_as=f32):
        self.values, self.name, self.sent_as = values, name, sent_as
        self.half = lax.axis_size(name) // 2

    def live(self):
        return self.half > 0

    def start(self):
        count, half = lax.axis_size(self.name), self.half
        upper = (lax.axis_index(self.name) & half) != 0
        low, high = self.values[:half], self.values[half:]
        self.kept = jnp.where(upper, high, low)
        sent = jnp.where(upper, low, high).astype(self.sent_as)
        self.moved = lax.ppermute(sent, self.name, [(i, i ^ half) for i in range(count)])

    def finish(self):
        self.values = self.kept + self.moved.astype(f32)
        self.half //= 2

    def result(self):
        while self.live():
            self.start()
            self.finish()
        return self.values[0]


class Doubling:
    def __init__(self, values, name, sent_as=f32):
        self.values, self.name, self.sent_as = values, name, sent_as
        self.step = 1

    def live(self):
        return self.step < lax.axis_size(self.name)

    def start(self):
        count, step = lax.axis_size(self.name), self.step
        self.moved = lax.ppermute(
            self.values.astype(self.sent_as), self.name, [(i, i ^ step) for i in range(count)]
        )

    def finish(self):
        self.values = self.values + self.moved.astype(f32)
        self.step *= 2

    def result(self):
        while self.live():
            self.start()
            self.finish()
        return self.values


def direct_send(values, name, sent_as=f32):
    count = lax.axis_size(name)
    here = lax.axis_index(name)

    def block(at):
        return lax.dynamic_index_in_dim(values, lax.rem(at, count), 0, keepdims=False)

    blocks = [block(here)] + [block(here + step).astype(sent_as) for step in range(1, count)]
    blocks = lax.optimization_barrier(blocks)
    return [
        lax.ppermute(sent, name, [(i, (i + step) % count) for i in range(count)]) if step else sent
        for step, sent in enumerate(blocks)
    ]


def begin(tasks):
    live = [t for t in tasks if t.live()]
    for t in live:
        t.start()
    return live


def settle(moved, extras, live):
    moved, extras, arrived = lax.optimization_barrier((moved, extras, [t.moved for t in live]))
    for t, value in zip(live, arrived):
        t.moved = value
        t.finish()
    return moved, extras


def ring_gather(own, use, tasks=()):
    tp = lax.axis_size("tp")
    pieces, results = [own], []
    for p in range(tp):
        if p < tp - 1:
            moved = hop(pieces[p])
            live = begin(tasks)
        result = use(p, pieces[p])
        if p < tp - 1:
            moved, result = settle(moved, result, live)
            pieces.append(moved)
        results.append(result)
    return pieces, results


def ring_scatter(part, fill=(), tasks=()):
    tp = lax.axis_size("tp")
    fill = list(fill)
    filled = []
    total = part(1 % tp, None)
    for p in range(2, tp + 1):
        low = total.astype(bf16)
        moved = hop(low)
        live = begin(tasks)
        term = part(p % tp, low)
        extra = [fill.pop(0)(low, tasks)] if fill else []
        moved, (term, extra) = settle(moved, (term, extra), live)
        filled += extra
        total = moved.astype(f32) + term
    for thunk in fill:
        filled.append(thunk(low, tasks))
    return total, filled


def ring_both(own, work, last=None, fill=None, tasks=()):
    tp = lax.axis_size("tp")
    pieces, filled = [own], []
    moved = hop(own)
    live = begin(tasks)
    first = work(0, own)
    moved, _ = settle(moved, (), live)
    total, ahead = None, None
    for p in range(1, tp):
        pieces.append(moved)
        if p < tp - 1:
            moved = hop(pieces[p])
        elif last is not None:
            pieces[p], result = lax.optimization_barrier((pieces[p], last(pieces)))
            filled.append(result)
        live = begin(tasks)
        term = work(p, pieces[p])
        if total is not None:
            ahead, term = lax.optimization_barrier((ahead, term))
            term = ahead.astype(f32) + term
        total = term
        low = total.astype(bf16)
        ahead = hop(low)
        if p < tp - 1:
            moved, (low, first) = settle(moved, (low, first), live)
        elif fill is not None:
            ahead, result = settle(ahead, fill(low), live)
            filled.append(result)
        else:
            ahead, _ = settle(ahead, (), live)
    return pieces, ahead.astype(f32) + first, filled


def doubling_gather(values, name):
    count = lax.axis_size(name)
    here = lax.axis_index(name)
    step = 1
    while step < count:
        moved = lax.ppermute(values, name, [(i, i ^ step) for i in range(count)])
        upper = (here & step) != 0
        values = jnp.concatenate(
            [jnp.where(upper, moved, values), jnp.where(upper, values, moved)], axis=0
        )
        step *= 2
    return values


def inverse_root(values):
    return lax.rsqrt(jnp.mean(values * values, axis=1, keepdims=True) + norm_eps)


def gather(values, axis=0):
    return lax.all_gather(values, "fsdp", axis=axis, tiled=True)


def scatter(values, axis=0):
    return lax.psum_scatter(values, "fsdp", scatter_dimension=axis, tiled=True)


def local(
    hidden,
    embed,
    lengths,
    attention_norm_gain,
    query_key_value_weight,
    attention_adapter_down,
    attention_adapter_up,
    attention_output_weight,
    feedforward_norm_gain,
    gate_up_weight,
    feedforward_adapter_down,
    feedforward_adapter_up,
    down_weight,
    mixer_norm_gain,
    gate_inner_weight,
    state_input_weight,
    step_projection,
    inner_conv_taps,
    state_conv_taps,
    head_step_bias,
    decay_log_rate,
    inner_skip_gains,
    gated_norm_gain,
    mixer_output_weight,
    output_cotangent,
):
    tp = lax.axis_size("tp")
    fsdp = lax.axis_size("fsdp")
    share, width = hidden.shape
    rows = share * tp
    here = lax.axis_index("tp").astype(jnp.int32)
    place = here.reshape(1)
    lengths = lengths.reshape(-1)
    rank = attention_adapter_down.shape[2]
    head_cols = query_key_value_weight.shape[2]
    units_here = gate_up_weight.shape[2]
    inner_cols = gate_inner_weight.shape[2]
    mixer_heads = inner_cols // HD
    states = state_input_weight.shape[2]
    count = inner_conv_taps.shape[0]
    inner_total = inner_cols * tp

    def piece(values, p):
        return values[p * share : (p + 1) * share]

    own_qkv = jnp.concatenate(
        [query_key_value_weight[:, j, :] for j in range(3)]
        + [attention_adapter_down[:, j, :] for j in range(3)],
        axis=1,
    )
    weight_qkv = gather(own_qkv)
    first_hop = tuple(hop(v) for v in (hidden, embed))

    small = [
        attention_norm_gain,
        feedforward_norm_gain,
        mixer_norm_gain,
        inner_conv_taps.reshape(-1),
        state_conv_taps.reshape(-1),
        inner_skip_gains.reshape(-1),
        gated_norm_gain.reshape(-1),
    ]
    sizes = [v.shape[0] for v in small]
    padding = -sum(sizes) % LANES
    packed = jnp.concatenate(small + [jnp.zeros((padding,), bf16)]).reshape(1, -1)
    spread = gather(packed).astype(f32)
    cuts = [sum(sizes[:i]) for i in range(len(sizes) + 1)]
    parts = [spread[:, cuts[i] : cuts[i + 1]] for i in range(len(sizes))]
    gain_attn, gain_mlp, gain_mixer = (parts[i].reshape(1, -1) for i in range(3))
    taps_x = parts[3].reshape(fsdp, count, mixer_heads, -1)
    taps_x = jnp.transpose(taps_x, (1, 2, 0, 3)).reshape(count, inner_cols)
    taps_s = parts[4].reshape(fsdp, count, 2, -1)
    taps_s = jnp.transpose(taps_s, (1, 2, 0, 3)).reshape(count, 2, states)
    skip = jnp.transpose(parts[5].reshape(fsdp, mixer_heads, -1), (1, 0, 2)).reshape(1, inner_cols)
    gain_gate = jnp.transpose(parts[6].reshape(fsdp, mixer_heads, -1), (1, 0, 2)).reshape(1, inner_cols)
    wide = jnp.concatenate([taps_x, skip, gain_gate, jnp.zeros((2, inner_cols), f32)], axis=0)
    narrow = jnp.pad(taps_s, ((0, 8 - count), (0, 0), (0, LANES - states))).reshape(8, 2 * LANES)
    rates = jnp.pad(
        jnp.stack([head_step_bias, decay_log_rate]), ((0, 6), (0, LANES - mixer_heads))
    )

    places = jnp.arange(rows, dtype=jnp.int32)
    ends = [jnp.sum(lengths[: i + 1]) for i in range(lengths.shape[0] - 1)]
    position = places - starts_of(places, ends)
    freqs = jnp.exp(jnp.arange(HDA // 2, dtype=f32) * (-2.0 * math.log(10000.0) / HDA))
    angles = position.astype(f32)[:, None] * freqs[None, :]
    cosine = jnp.cos(angles)
    sine = jnp.sin(angles)
    cosine = jnp.concatenate([cosine, cosine], axis=1)
    sine = jnp.concatenate([-sine, sine], axis=1)

    own_fc1 = jnp.concatenate(
        [gate_up_weight[:, j, :] for j in range(2)] + [feedforward_adapter_down], axis=1
    )
    own_zx = jnp.concatenate(
        [gate_inner_weight[:, j, :] for j in range(2)]
        + [jnp.pad(state_input_weight[:, j, :], ((0, 0), (0, LANES - states))) for j in range(2)]
        + [jnp.pad(step_projection, ((0, 0), (0, LANES - mixer_heads)))],
        axis=1,
    )
    weight_o = gather(attention_output_weight, 1)
    weight_fc1 = gather(own_fc1)
    weight_fc2 = gather(down_weight, 1)
    weight_zx = gather(own_zx)
    weight_out = gather(mixer_output_weight, 1)

    raw, normed_parts = [(hidden, embed), first_hop], []
    spans = [((tp * i) // (tp - 2), (tp * (i + 1)) // (tp - 2)) for i in range(tp - 2)]

    def norm_ready(count):
        fresh = [norm_pairs(raw[low:high], gain_attn) for low, high in spans[len(normed_parts) :] if high <= count]
        normed_parts.extend(fresh)
        return fresh

    for p in range(2, tp):
        moved = tuple(hop(v) for v in raw[-1])
        raw.append(tie(moved, norm_ready(p)))
    norm_ready(tp)

    own_ups = jnp.concatenate(
        [attention_adapter_up[:, j, :] for j in range(3)]
        + [feedforward_adapter_up[:, j, :] for j in range(2)],
        axis=1,
    )
    ups = doubling_gather(tie(own_ups, raw[-2]), "fsdp")
    fc_up = ups[:, 3 * head_cols :]
    out_grad = [tie(output_cotangent, raw[-1])]
    projected = []
    for i in range(tp - 1):
        moved = hop(out_grad[-1])
        if i < tp - 2:
            projected.append(mm(normed_parts[i], weight_qkv))
            moved = tie(moved, projected)
        else:
            attended, queries, keys, values = attention_forward(
                place, lengths, tp, projected, ups, head_cols, cosine, sine
            )
            moved = tie(moved, attended)
        out_grad.append(moved)
    lora_rows = jnp.concatenate([v[:, 3 * head_cols :].astype(bf16) for v in projected], axis=0)
    attended, lora_rows, out_grad[-1] = lax.optimization_barrier((attended, lora_rows, moved))
    out_grad_rows = jnp.concatenate(out_grad, axis=0)
    mixed, (normed_rows,) = ring_scatter(
        lambda p, t: mm(piece(after(attended, t), p), weight_o),
        [lambda t, _: jnp.concatenate(tie(normed_parts, t), axis=0)],
    )

    mlp_root = inverse_root(mixed)
    gate_up, fc_mid, units = [], [], []

    def feed(p, rows_in):
        wide_rows = mm(rows_in, weight_fc1)
        middle = wide_rows[:, 2 * units_here :].astype(bf16)
        both = (wide_rows[:, : 2 * units_here] + mm(middle, fc_up)).astype(bf16)
        gate, up = both[:, :units_here].astype(f32), both[:, units_here:].astype(f32)
        unit = (jax.nn.gelu(gate) * up).astype(bf16)
        fc_mid.append(middle)
        gate_up.append(both)
        units.append(unit)
        return mm(unit, weight_fc2)

    mlp_in, branch, _ = ring_both((mixed * mlp_root * gain_mlp).astype(bf16), feed)
    residual = hidden.astype(f32) + mixed + branch

    mixer_root = inverse_root(residual)
    kept = []

    def mix(p, rows_in):
        result = mm(rows_in, weight_zx)
        if p == 0:
            kept.append(mm_nt(tie(out_grad_rows, result), weight_out).astype(bf16))
        elif p == 1:
            kept.append(jnp.concatenate(tie(units, result), axis=0))
            kept.append(jnp.concatenate(tie(mlp_in, result), axis=0))
        return (result, kept[-1])

    mixer_in, zxs = ring_gather((residual * mixer_root * gain_mixer).astype(bf16), mix)
    zxs = [v[0] for v in zxs]
    grad_scaled, units_rows, mlp_rows = kept
    zx = jnp.concatenate([v[:, : 2 * inner_cols].astype(bf16) for v in zxs], axis=0)
    sd = jnp.concatenate([v[:, 2 * inner_cols :] for v in zxs], axis=0)
    gated, chunk_states = mixer_forward(place, lengths, tp, zx, sd, wide, narrow, rates)
    gated_wide = gated.astype(f32)
    sums = jnp.stack(
        [
            jnp.sum(gated_wide * gated_wide, axis=1),
            jnp.sum(grad_scaled.astype(f32) * gain_gate * gated_wide, axis=1),
        ],
        axis=0,
    )
    sums = jnp.roll(jnp.flip(sums.reshape(2, tp, share), axis=1), here + 1, axis=1)
    sums = lax.psum(sums, "tp")
    sums = jnp.flip(jnp.roll(sums, -(here + 1), axis=1), axis=1).reshape(2, rows)
    gate_root = lax.rsqrt(sums[0] / inner_total + norm_eps)
    stats = jnp.stack([gate_root, gate_root**3 * sums[1] / inner_total], axis=1)
    scaled = (gated_wide * gate_root[:, None] * gain_gate).astype(bf16)
    out_rows, stats = lax.optimization_barrier((mm(scaled, weight_out).astype(bf16), stats))
    out_terms = [piece(out_rows, p) for p in range(tp)]
    out = hop(out_terms[1 % tp])

    grad_all, grad_wide, grad_narrow, grad_rates = mixer_backward(
        place, lengths, tp, zx, sd, grad_scaled, stats, chunk_states, wide, narrow, rates
    )
    out, grad_all = lax.optimization_barrier((out, grad_all))
    out = out.astype(f32) + out_terms[2 % tp].astype(f32)

    def by_fsdp(values):
        lead = values.shape[:-1]
        cut = values.reshape(lead + (fsdp, values.shape[-1] // fsdp))
        return jnp.moveaxis(cut, -2, 0).reshape(fsdp, -1)

    def small_gradients(token):
        taps, bars, sums_r = tie((grad_wide, grad_narrow, grad_rates), token)
        return [
            by_fsdp(taps[:count].reshape(count, mixer_heads, HD)),
            by_fsdp(taps[4].reshape(mixer_heads, HD)),
            by_fsdp(taps[5].reshape(mixer_heads, HD)),
            jnp.broadcast_to(sums_r[:2, :mixer_heads].reshape(1, -1), (fsdp, 2 * mixer_heads)),
            by_fsdp(bars[:count].reshape(count, 2, LANES)[:, :, :states]),
        ]

    mixer_rows = []

    def out_fill(token, _):
        mixer_rows.append(jnp.concatenate(tie(mixer_in, token), axis=0))
        return mm_tn(tie(scaled, token), out_grad_rows).astype(bf16), mixer_rows[0]

    grad_mixer_in, ((sum_w_out, _), sum_w_zx, small) = ring_scatter(
        lambda p, t: mm_nt(piece(after(grad_all, t), p), weight_zx),
        [
            out_fill,
            lambda t, _: mm_tn(tie(mixer_rows[0], t), grad_all).astype(bf16),
            lambda t, _: small_gradients(t),
        ],
    )
    sum_w_out = scatter(sum_w_out, 1)
    sum_w_zx = scatter(sum_w_zx)
    small_sizes = [v.shape[1] for v in small]
    small_cuts = [sum(small_sizes[:i]) for i in range(len(small_sizes) + 1)]
    small_task = Halving(jnp.concatenate(small, axis=1), "fsdp")
    grad_residual, grad_residual_low, grad_gain_mixer = norm_back(
        [residual], grad_mixer_in, gain_mixer, output_cotangent, True
    )

    grad_gate_up = []

    def feed_back(p, grad_rows):
        grad_units = mm_nt(grad_rows, weight_fc2)
        gate = gate_up[p][:, :units_here].astype(f32)
        up = gate_up[p][:, units_here:].astype(f32)
        raised, back = jax.vjp(jax.nn.gelu, gate)
        both = jnp.concatenate(
            [back(grad_units * up)[0].astype(bf16), (grad_units * raised).astype(bf16)], axis=1
        )
        both = jnp.concatenate([both, mm_nt(both, fc_up).astype(bf16)], axis=1)
        grad_gate_up.append(both)
        return mm_nt(both, weight_fc1)

    def fc2_fill(token, _):
        rows_in = tie(units_rows, (sum_w_out, token))
        return mm_tn(rows_in, jnp.concatenate(grad_branch, axis=0)).astype(bf16)

    def fc1_fill(token, _):
        return mm_tn(tie(mlp_rows, token), jnp.concatenate(grad_gate_up, axis=0)).astype(bf16)

    grad_branch, back_terms = ring_gather(
        grad_residual_low, lambda p, v: feed_back(p, v) if p < tp - 1 else (), [small_task]
    )
    grad_mlp_in, filled = ring_scatter(
        lambda p, t: feed_back(p, after(grad_branch[p], t))
        if p == tp - 1
        else tie(back_terms[p], grad_branch[-1]),
        [fc2_fill] + [lambda t, _: ()] * (tp - 3) + [fc1_fill],
    )
    sum_w_fc2, sum_w_fc1 = filled[0], filled[-1]
    sum_w_fc2 = scatter(sum_w_fc2, 1)
    sum_w_fc1 = scatter(sum_w_fc1)
    grad_gate_up_rows = jnp.concatenate(grad_gate_up, axis=0)
    _, grad_mixed_low, grad_gain_mlp = norm_back([mixed], grad_mlp_in, gain_mlp, grad_residual, True)
    gain_tasks = []

    fc_ups = []

    def attended_back(p, rows_in):
        result = mm_nt(rows_in, weight_o).astype(bf16)
        if p == 0:
            middle, first, second = tie((fc_mid, grad_gain_mixer, grad_gain_mlp), rows_in)
            fc_ups.append(
                mm_tn(jnp.concatenate(middle, axis=0), grad_gate_up_rows[:, : 2 * units_here])
            )
            gains = jnp.concatenate([first.reshape(fsdp, -1), second.reshape(fsdp, -1)], axis=1)
            result, gains = tie((result, gains), fc_ups[0])
            gain_tasks.append(Halving(gains, "fsdp"))
        return result

    grad_mixed, grad_attended = ring_gather(tie(grad_mixed_low, sum_w_zx), attended_back, gain_tasks)
    sum_w_o = mm_tn(tie(attended, sum_w_fc2), jnp.concatenate(grad_mixed, axis=0)).astype(bf16)
    grad_attended[-1] = tie(grad_attended[-1], sum_w_o)
    sum_w_o = scatter(sum_w_o, 1)
    out = hop(out.astype(bf16))
    grad_projected = attention_backward(
        place, lengths, queries, keys, values, ups, grad_attended, cosine, sine
    )
    out, grad_projected, sum_w_fc1 = lax.optimization_barrier((out, grad_projected, sum_w_fc1))
    out = out.astype(f32) + out_terms[3 % tp].astype(f32)
    out = hop(out.astype(bf16))
    sum_w_qkv = mm_tn(normed_rows, grad_projected).astype(bf16)
    out, sum_w_qkv, grad_projected = lax.optimization_barrier((out, sum_w_qkv, grad_projected))
    sum_w_qkv = scatter(sum_w_qkv)

    at_t = 2 * inner_cols + 2 * LANES

    def finish_out(token):
        total = tie(out, token).astype(f32) + out_terms[4 % tp].astype(f32)
        for p in range(5, tp + 1):
            total = hop(total.astype(bf16)).astype(f32) + out_terms[p % tp].astype(f32)
        return residual + total

    def finish_adapters(token, tasks):
        rows_in = tie(lora_rows, token)
        grad_up = [
            mm_tn(
                rows_in[:, j * rank : (j + 1) * rank],
                grad_projected[:, j * head_cols : (j + 1) * head_cols],
            )
            for j in range(3)
        ]
        ups_grad = jnp.concatenate(grad_up + fc_ups, axis=1)
        tasks.append(Halving(ups_grad.reshape(fsdp, -1, ups_grad.shape[1]), "fsdp", bf16))
        shared = jnp.concatenate([small_task.result()[small_cuts[4] :], gain_tasks[0].result()])
        tasks.append(Doubling(shared, "tp"))
        return ups_grad, shared

    def finish_mixer(token, tasks):
        zx_sum, w_out, w_fc2 = tie((sum_w_zx, sum_w_out, sum_w_fc2), token)
        zx_sum = zx_sum.astype(f32)
        bc_sums.append(zx_sum[:, 2 * inner_cols : at_t])
        return (
            stacked(zx_sum, inner_cols, 2),
            zx_sum[:, at_t : at_t + mixer_heads],
            w_out.astype(f32),
            w_fc2.astype(f32),
        )

    def finish_feed(token, tasks):
        fc1_sum, w_o = tie((sum_w_fc1, sum_w_o), token)
        fc1_sum = fc1_sum.astype(f32)
        tasks.append(
            Doubling(jnp.concatenate([bc_sums[0], fc1_sum[:, 2 * units_here :]], axis=1), "tp", bf16)
        )
        return (
            stacked(fc1_sum, units_here, 2),
            w_o.astype(f32),
            finish_out(token),
        )

    def stacked(values, each, parts):
        values = jnp.stack([values[:, j * each : (j + 1) * each] for j in range(parts)], axis=1)
        return with_layout_constraint(values, Layout(major_to_minor=(0, 1, 2)))

    tasks, bc_sums = [], []
    normed_terms = {}
    pair = mm_nt(grad_projected[share : 3 * share], weight_qkv)
    normed_terms[1], normed_terms[2] = piece(pair, 0), piece(pair, 1)

    def normed_back(p, token):
        if p not in normed_terms:
            normed_terms[p] = mm_nt(piece(after(grad_projected, token), p), weight_qkv)
        return normed_terms[p]

    grad_normed, ((_, mixer_sums, _), feed_sums) = ring_scatter(
        normed_back,
        [lambda t, k: (finish_adapters(t, k), finish_mixer(t, k), normed_back(3 % tp, t)), finish_feed],
        tasks,
    )
    grad_w_zx, grad_w_dt, grad_w_out, grad_w_fc2 = mixer_sums
    grad_w_fc1, grad_w_o, out = feed_sums
    grad_hidden, grad_embed = norm_back(
        [hidden, embed], grad_normed, gain_attn, grad_residual, with_gain=False
    )
    gain_rows = jnp.sum(sum_w_qkv.astype(f32) * own_qkv.astype(f32), axis=1)
    gain_rows = gain_rows / attention_norm_gain.astype(f32)
    down_blocks = direct_send(
        sum_w_qkv[:, 3 * head_cols :].astype(f32).reshape(tp, -1, 3 * rank), "tp", bf16
    )
    gain_blocks = direct_send(gain_rows.reshape(tp, -1), "tp")
    sum_w_qkv = tie(sum_w_qkv, (down_blocks[0], gain_blocks[0]))
    grad_w_qkv = jnp.stack(
        [sum_w_qkv[:, j * head_cols : (j + 1) * head_cols].astype(f32) for j in range(3)], axis=1
    )
    down_blocks, gain_blocks, grad_w_qkv = lax.optimization_barrier((down_blocks, gain_blocks, grad_w_qkv))
    grad_down = sum(v.astype(f32) for v in down_blocks)
    grad_gain_attn = sum(gain_blocks)
    small_sum = small_task.result()
    small_parts = [small_sum[small_cuts[i] : small_cuts[i + 1]] for i in range(len(small_sizes))]
    grad_ups, tail = tasks[0].result(), tasks[1].result()
    shared = tasks[2].result()
    tail_sizes = [small_sizes[4], width // fsdp, width // fsdp]
    tail_cuts = [sum(tail_sizes[:i]) for i in range(4)]
    grad_conv_bc, sum_gain_mixer, sum_gain_mlp = (
        tail[tail_cuts[i] : tail_cuts[i + 1]] for i in range(3)
    )
    sum_rates = small_parts[3].reshape(2, mixer_heads)
    return (
        out,
        grad_hidden,
        grad_embed,
        grad_gain_attn,
        grad_w_qkv,
        grad_down.reshape(-1, 3, rank),
        grad_ups[:, : 3 * head_cols].reshape(-1, 3, head_cols),
        grad_w_o,
        sum_gain_mlp,
        grad_w_fc1,
        shared[:, 2 * LANES :],
        grad_ups[:, 3 * head_cols :].reshape(-1, 2, units_here),
        grad_w_fc2,
        sum_gain_mixer,
        grad_w_zx,
        shared[:, : 2 * LANES].reshape(-1, 2, LANES)[:, :, :states],
        grad_w_dt,
        small_parts[0].reshape(count, mixer_heads, -1),
        grad_conv_bc.reshape(count, 2, -1),
        sum_rates[0],
        sum_rates[1],
        small_parts[1].reshape(mixer_heads, -1),
        small_parts[2].reshape(mixer_heads, -1),
        grad_w_out,
    )


def solution(mesh):
    placed = (
        P(("fsdp", "tp"), None),
        P(("fsdp", "tp"), None),
        P("fsdp", None),
        P("fsdp"),
        P("fsdp", None, "tp"),
        P("fsdp", None, None),
        P("fsdp", None, "tp"),
        P("tp", "fsdp"),
        P("fsdp"),
        P("fsdp", None, "tp"),
        P("fsdp", None),
        P("fsdp", None, "tp"),
        P("tp", "fsdp"),
        P("fsdp"),
        P("fsdp", None, "tp"),
        P("fsdp", None, None),
        P("fsdp", "tp"),
        P(None, "tp", "fsdp"),
        P(None, None, "fsdp"),
        P("tp"),
        P("tp"),
        P("tp", "fsdp"),
        P("tp", "fsdp"),
        P("tp", "fsdp"),
        P(("fsdp", "tp"), None),
    )
    return jax.shard_map(
        local,
        mesh=mesh,
        in_specs=placed,
        out_specs=(
            P(("fsdp", "tp"), None),
            P(("fsdp", "tp"), None),
            P(("fsdp", "tp"), None),
            P(("fsdp", "tp")),
            P("fsdp", None, "tp"),
            P(("fsdp", "tp"), None, None),
            P("fsdp", None, "tp"),
            P("tp", "fsdp"),
            P("fsdp"),
            P("fsdp", None, "tp"),
            P("fsdp", None),
            P("fsdp", None, "tp"),
            P("tp", "fsdp"),
            P("fsdp"),
            P("fsdp", None, "tp"),
            P("fsdp", None, None),
            P("fsdp", "tp"),
            P(None, "tp", "fsdp"),
            P(None, None, "fsdp"),
            P("tp"),
            P("tp"),
            P("tp", "fsdp"),
            P("tp", "fsdp"),
            P("tp", "fsdp"),
        ),
        check_vma=False,
    )
```

```python
import functools
import math

import jax
import jax.numpy as jnp
from jax import lax
from jax.experimental import pallas as pl
from jax.experimental.layout import Layout, with_layout_constraint
from jax.experimental.pallas import tpu as pltpu
from jax.sharding import PartitionSpec as P

HDA = 128
HD = 64
LANES = 128
CHUNK = 128

norm_eps = 1e-05
f32 = jnp.float32
bf16 = jnp.bfloat16
HIGHEST = lax.Precision.HIGHEST
VMEM_LIMIT = 56 * 1024 * 1024


def mm(left, right):
    return jnp.dot(left, right, preferred_element_type=f32)


def mm_nt(left, right):
    return lax.dot_general(left, right, (((1,), (1,)), ((), ())), preferred_element_type=f32)


def mm_tn(left, right):
    return lax.dot_general(left, right, (((0,), (0,)), ((), ())), preferred_element_type=f32)


def starts_of(index, ends):
    start = jnp.zeros_like(index)
    for end in ends:
        start = jnp.where(index >= end, end, start)
    return start


def ends_of(lengths_ref):
    ends = []
    end = jnp.int32(0)
    for i in range(lengths_ref.shape[0] - 1):
        end = end + lengths_ref[i]
        ends.append(end)
    return ends


def iota(shape, axis):
    return lax.broadcasted_iota(jnp.int32, shape, axis)


def attention_forward_kernel(
    tp,
    parts,
    place_ref,
    lengths_ref,
    cosine_ref,
    sine_ref,
    q_up,
    k_up,
    v_up,
    *refs,
):
    pieces = refs[: 4 * parts]
    attended_ref, q_ref, k_ref, v_ref, held = refs[4 * parts :]
    rows = q_ref.shape[0]
    share = rows // tp
    rank = q_up.shape[0]
    here = place_ref[0]
    ends = ends_of(lengths_ref)
    for p in range(tp):
        owner = lax.rem(here - p + tp, tp)
        part = pl.ds(pl.multiple_of(owner * share, share), share)
        cosine, sine = cosine_ref[part, :], sine_ref[part, :]
        at = p * share
        source = 0
        while at >= pieces[4 * source].shape[0]:
            at -= pieces[4 * source].shape[0]
            source += 1
        mine = slice(at, at + share)
        for j, (up, target) in enumerate(((q_up, q_ref), (k_up, k_ref), (v_up, v_ref))):
            low = pieces[4 * source + 3][mine, j * rank : (j + 1) * rank].astype(bf16)
            value = pieces[4 * source + j][mine, :] + mm(low, up[...])
            if j < 2:
                value = value * cosine + pltpu.roll(value, HDA // 2, 1) * sine
            target[part, :] = value.astype(bf16)
    block = min(256, rows)
    scale = HDA ** (-0.5)
    for at in range(0, rows, block):
        upto = at + block
        scores = mm_nt(k_ref[:upto, :], q_ref[at:upto, :]) * scale
        query = at + iota((1, block), 1)
        key = iota((upto, 1), 0)
        seen = (key <= query) & (key >= starts_of(query, ends))
        scores = jnp.where(seen, scores, -1e30)
        raised = jnp.exp(scores - jnp.max(scores, axis=0, keepdims=True))
        probs = (raised * (1.0 / jnp.sum(raised, axis=0, keepdims=True))).astype(bf16)
        held[at:upto, :] = mm_tn(probs, v_ref[:upto, :]).astype(bf16)
    for p in range(tp):
        owner = lax.rem(here - p + tp, tp)
        part = pl.ds(pl.multiple_of(owner * share, share), share)
        attended_ref[p * share : (p + 1) * share, :] = held[part, :]


def attention_forward(place, lengths, tp, projected, ups, columns, cosine, sine):
    rows = sum(v.shape[0] for v in projected)
    heads = columns // HDA
    rank = ups.shape[0]
    table_spec = pl.BlockSpec((rows, HDA), lambda h, *_: (0, 0))

    def head_spec(j, height=rows):
        return pl.BlockSpec((height, HDA), lambda h, *_: (0, j * heads + h))

    work = heads * rows * rows * HDA
    return pl.pallas_call(
        functools.partial(attention_forward_kernel, tp, len(projected)),
        out_shape=[jax.ShapeDtypeStruct((rows, columns), bf16)] * 4,
        grid_spec=pltpu.PrefetchScalarGridSpec(
            num_scalar_prefetch=2,
            grid=(heads,),
            in_specs=[table_spec, table_spec]
            + [head_spec(j, rank) for j in range(3)]
            + [
                pl.BlockSpec((v.shape[0], 3 * rank), lambda h, *_: (0, columns // rank))
                if j == 3
                else head_spec(j, v.shape[0])
                for v in projected
                for j in range(4)
            ],
            out_specs=[head_spec(0)] * 4,
            scratch_shapes=[pltpu.VMEM((rows, HDA), bf16)],
        ),
        compiler_params=pltpu.CompilerParams(vmem_limit_bytes=VMEM_LIMIT),
        cost_estimate=pl.CostEstimate(
            flops=4 * work, bytes_accessed=20 * rows * columns, transcendentals=heads * rows * rows
        ),
        name="attention_forward",
    )(place, lengths, cosine, sine, ups, ups, ups, *[v for v in projected for _ in range(4)])


def attention_backward_kernel(
    tp,
    heads,
    place_ref,
    lengths_ref,
    cosine_ref,
    sine_ref,
    q_ref,
    k_ref,
    v_ref,
    q_up,
    k_up,
    v_up,
    *refs,
):
    grad_in = refs[:tp]
    out_ref, held, dq, dk, dv, lora = refs[tp:]
    rows = q_ref.shape[0]
    share = rows // tp
    rank = q_up.shape[0]
    here = place_ref[0]
    head = pl.program_id(0)
    ends = ends_of(lengths_ref)
    for p in range(tp):
        owner = lax.rem(here - p + tp, tp)
        part = pl.ds(pl.multiple_of(owner * share, share), share)
        held[part, :] = grad_in[p][...]
    dk[...] = jnp.zeros_like(dk)
    dv[...] = jnp.zeros_like(dv)

    @pl.when(head == 0)
    def _():
        lora[...] = jnp.zeros_like(lora)

    block = min(256, rows)
    scale = HDA ** (-0.5)
    for at in range(0, rows, block):
        upto = at + block
        query_rows = q_ref[at:upto, :]
        grad_rows = held[at:upto, :]
        scores = mm_nt(k_ref[:upto, :], query_rows) * scale
        query = at + iota((1, block), 1)
        key = iota((upto, 1), 0)
        seen = (key <= query) & (key >= starts_of(query, ends))
        scores = jnp.where(seen, scores, -1e30)
        raised = jnp.exp(scores - jnp.max(scores, axis=0, keepdims=True))
        probs = raised * (1.0 / jnp.sum(raised, axis=0, keepdims=True))
        grad_probs = mm_nt(v_ref[:upto, :], grad_rows)
        cross = jnp.sum(probs * grad_probs, axis=0, keepdims=True)
        grad_scores = (probs * (grad_probs - cross)).astype(bf16)
        dv[:upto, :] += mm(probs.astype(bf16), grad_rows)
        dk[:upto, :] += mm(grad_scores, query_rows)
        dq[at:upto, :] = mm_tn(grad_scores, k_ref[:upto, :])
    for p in range(tp):
        owner = lax.rem(here - p + tp, tp)
        part = pl.ds(pl.multiple_of(owner * share, share), share)
        cosine, sine = cosine_ref[part, :], sine_ref[part, :]
        mine = slice(p * share, (p + 1) * share)
        for j, (source, up) in enumerate(((dq, q_up), (dk, k_up), (dv, v_up))):
            value = source[part, :]
            if j < 2:
                value = value * scale
                value = value * cosine - pltpu.roll(value, HDA // 2, 1) * sine
            low = value.astype(bf16)
            at = pl.multiple_of((j * heads + head) * HDA, HDA)
            out_ref[mine, pl.ds(at, HDA)] = low
            lora[mine, j * rank : (j + 1) * rank] += mm_nt(low, up[...])

    @pl.when(head == heads - 1)
    def _():
        out_ref[:, 3 * heads * HDA :] = lora[...].astype(bf16)


def attention_backward(place, lengths, queries, keys, values, ups, pieces, cosine, sine):
    tp = len(pieces)
    share, columns = pieces[0].shape
    rows = share * tp
    heads = columns // HDA
    rank = ups.shape[0]
    piece_spec = pl.BlockSpec((share, HDA), lambda h, *_: (0, h))
    table_spec = pl.BlockSpec((rows, HDA), lambda h, *_: (0, 0))
    head_spec = pl.BlockSpec((rows, HDA), lambda h, *_: (0, h))

    def up_spec(j):
        return pl.BlockSpec((rank, HDA), lambda h, *_: (0, j * heads + h))

    total = 3 * columns + 3 * rank
    work = heads * rows * rows * HDA
    return pl.pallas_call(
        functools.partial(attention_backward_kernel, tp, heads),
        out_shape=jax.ShapeDtypeStruct((rows, total), bf16),
        grid_spec=pltpu.PrefetchScalarGridSpec(
            num_scalar_prefetch=2,
            grid=(heads,),
            in_specs=[table_spec, table_spec]
            + [head_spec] * 3
            + [up_spec(j) for j in range(3)]
            + [piece_spec] * tp,
            out_specs=pl.BlockSpec((rows, total), lambda h, *_: (0, 0)),
            scratch_shapes=[pltpu.VMEM((rows, HDA), bf16)]
            + [pltpu.VMEM((rows, HDA), f32)] * 3
            + [pltpu.VMEM((rows, 3 * rank), f32)],
        ),
        compiler_params=pltpu.CompilerParams(vmem_limit_bytes=VMEM_LIMIT),
        cost_estimate=pl.CostEstimate(
            flops=10 * work, bytes_accessed=14 * rows * columns, transcendentals=heads * rows * rows
        ),
        name="attention_backward",
    )(place, lengths, cosine, sine, queries, keys, values, ups, ups, ups, *pieces)


def conv_rows(extended, taps, position):
    count = 4
    rows = extended.shape[0] - 8
    total = None
    for k in range(count):
        moved = extended[8 - k : 8 - k + rows, :]
        if k:
            moved = jnp.where(position >= k, moved, 0.0)
        term = taps[count - 1 - k : count - k, :] * moved
        total = term if total is None else total + term
    return total


def conv_back(extended, taps, position):
    count = 4
    rows = extended.shape[0] - 8
    total = None
    for k in range(count):
        kept = jnp.where(position >= k, extended, 0.0) if k else extended
        term = taps[count - 1 - k : count - k, :] * kept[k : k + rows, :]
        total = term if total is None else total + term
    return total


def taps_back(extended, grad, position, target):
    count = 4
    rows = extended.shape[0] - 8
    for k in range(count):
        moved = extended[8 - k : 8 - k + rows, :]
        if k:
            moved = jnp.where(position >= k, moved, 0.0)
        at = count - 1 - k
        target[at : at + 1, :] += jnp.sum(grad * moved, axis=0, keepdims=True)


def silu_grad(value, gate):
    return gate * (1.0 + value * (1.0 - gate))


class Chunk:
    def __init__(self, c0, ends, zx, before, sd, sd_before, wide, narrow, rates):
        rows = zx.shape[0]
        width = zx.shape[1] // 2
        self.rows, self.width = rows, width
        index = c0 + iota((rows, 1), 0)
        start = starts_of(index, ends)
        self.index, self.start = index, start
        self.position = index - start
        last_start = starts_of(c0 + rows - 1, ends)
        self.z = zx[:, :width].astype(f32)
        self.x_ext = jnp.concatenate(
            [before[...].astype(f32)[8:16, :], zx[:, width:].astype(f32)], axis=0
        )
        self.s_ext = jnp.concatenate([sd_before[:, : 2 * LANES], sd[:, : 2 * LANES]], axis=0)
        self.pre = conv_rows(self.x_ext, wide, self.position)
        self.gate_x = jax.nn.sigmoid(self.pre)
        self.xc = self.pre * self.gate_x
        self.pre_s = conv_rows(self.s_ext, narrow, self.position)
        self.gate_s = jax.nn.sigmoid(self.pre_s)
        sc = self.pre_s * self.gate_s
        self.b_low = sc[:, :HD].astype(bf16)
        self.c_low = sc[:, LANES : LANES + HD].astype(bf16)
        self.raw = sd[:, 2 * LANES : 3 * LANES] + rates[0:1, :]
        self.step = jnp.maximum(self.raw, 0.0) + jnp.log1p(jnp.exp(-jnp.abs(self.raw)))
        self.rate = jnp.exp(rates[1:2, :])
        row, col = iota((rows, rows), 0), iota((rows, rows), 1)
        below = (col <= row).astype(f32)
        self.cum = jnp.dot(below, -self.step * self.rate, precision=HIGHEST, preferred_element_type=f32)
        self.cum_t = self.cum.T
        self.allowed = (col <= row) & ((c0 + col) >= start)
        self.inner = jnp.where(self.allowed, mm_nt(self.c_low, self.b_low), 0.0)
        last = self.cum[rows - 1 : rows, :]
        self.into = jnp.exp(self.cum) * (start < c0).astype(f32)
        self.onto = jnp.exp(last - self.cum) * (index >= last_start).astype(f32)
        self.decay = jnp.exp(last) * (last_start < c0).astype(f32)
        self.low_half = iota((1, LANES), 1) < HD

    def pair(self, table, i):
        return jnp.where(self.low_half, table[:, 2 * i : 2 * i + 1], table[:, 2 * i + 1 : 2 * i + 2])

    def spread(self, h):
        return jnp.exp(jnp.minimum(self.cum[:, h : h + 1] - self.cum_t[h : h + 1, :], 0.0))


def mixer_forward_kernel(
    place_ref, lengths_ref, zx, before, sd, sd_before, wide, narrow, rates, gated, states, state
):
    rows = zx.shape[0]
    c0 = pl.program_id(0) * rows
    ends = ends_of(lengths_ref)

    @pl.when(pl.program_id(0) == 0)
    def _():
        state[...] = jnp.zeros_like(state)

    v = Chunk(c0, ends, zx, before, sd, sd_before, wide, narrow, rates)
    state_low = state[...].astype(bf16)
    states[...] = state_low
    for i in range(v.width // LANES):
        cols = slice(i * LANES, (i + 1) * LANES)
        xc = v.xc[:, cols]
        xs = v.pair(v.step, i) * xc
        xs_low = xs.astype(bf16)
        first = (v.spread(2 * i) * v.inner).astype(bf16)
        second = (v.spread(2 * i + 1) * v.inner).astype(bf16)
        y = jnp.where(v.low_half, mm(first, xs_low), mm(second, xs_low))
        y = y + v.pair(v.into, i) * mm(v.c_low, state_low[:, cols])
        y = y + wide[4:5, cols] * xc
        z = v.z[:, cols]
        gated[:, cols] = (y * z * jax.nn.sigmoid(z)).astype(bf16)
        state[:, cols] = v.pair(v.decay, i) * state[:, cols] + mm_tn(
            v.b_low, (v.pair(v.onto, i) * xs).astype(bf16)
        )


def split_sum(values, ones):
    high = values.astype(bf16)
    low = (values - high.astype(f32)).astype(bf16)
    return mm(high, ones) + mm(low, ones)


def mixer_backward_kernel(
    chunks,
    place_ref,
    lengths_ref,
    zx,
    before,
    sd,
    sd_before,
    grad_scaled,
    stats,
    states,
    wide,
    narrow,
    rates,
    grad_all,
    grad_wide,
    grad_narrow,
    grad_rates,
    grad_state,
    next_pre,
    next_pre_s,
    carry,
    products,
    directs,
    grad_pre,
):
    rows = zx.shape[0]
    turn = pl.program_id(0)
    c0 = (chunks - 1 - turn) * rows
    ends = ends_of(lengths_ref)

    @pl.when(turn == 0)
    def _():
        for ref in (grad_state, next_pre, next_pre_s, carry, grad_wide, grad_narrow, grad_rates):
            ref[...] = jnp.zeros_like(ref)

    v = Chunk(c0, ends, zx, before, sd, sd_before, wide, narrow, rates)
    width = v.width
    root, pull = stats[:, 0:1], stats[:, 1:2]
    grad_inner = jnp.zeros((rows, rows), f32)
    grad_b = jnp.zeros((rows, HD), f32)
    grad_c = jnp.zeros((rows, HD), f32)
    for i in range(width // LANES):
        cols = slice(i * LANES, (i + 1) * LANES)
        xc = v.xc[:, cols]
        step = v.pair(v.step, i)
        xs = step * xc
        xs_low = xs.astype(bf16)
        spread_a, spread_b = v.spread(2 * i), v.spread(2 * i + 1)
        first = (spread_a * v.inner).astype(bf16)
        second = (spread_b * v.inner).astype(bf16)
        state_low = states[:, cols]
        into, onto = v.pair(v.into, i), v.pair(v.onto, i)
        y = jnp.where(v.low_half, mm(first, xs_low), mm(second, xs_low))
        y = y + into * mm(v.c_low, state_low)
        skip, gain = wide[4:5, cols], wide[5:6, cols]
        whole = y + skip * xc
        z = v.z[:, cols]
        gate = jax.nn.sigmoid(z)
        gated = whole * z * gate
        incoming = grad_scaled[:, cols].astype(f32)
        rooted = incoming * root
        grad_wide[5:6, cols] += jnp.sum(rooted * gated, axis=0, keepdims=True)
        grad_gated = rooted * gain - gated * pull
        grad_y = grad_gated * z * gate
        grad_all[:, cols] = (grad_gated * whole * silu_grad(z, gate)).astype(bf16)
        grad_wide[4:5, cols] += jnp.sum(grad_y * xc, axis=0, keepdims=True)
        low = grad_y.astype(bf16)
        low_a = jnp.where(v.low_half, grad_y, 0.0).astype(bf16)
        low_b = jnp.where(v.low_half, 0.0, grad_y).astype(bf16)
        grad_inner = grad_inner + spread_a * mm_nt(low_a, xs_low) + spread_b * mm_nt(low_b, xs_low)
        grad_end = grad_state[:, cols]
        grad_end_low = grad_end.astype(bf16)
        grad_xs = jnp.where(v.low_half, mm_tn(first, low), mm_tn(second, low))
        grad_xs = grad_xs + onto * mm(v.b_low, grad_end_low)
        into_y = (into * grad_y).astype(bf16)
        onto_x = (onto * xs).astype(bf16)
        grad_b = grad_b + mm_nt(onto_x, grad_end_low)
        grad_c = grad_c + mm_nt(into_y, state_low)
        grad_state[:, cols] = v.pair(v.decay, i) * grad_end + mm_tn(v.c_low, into_y)
        products[:, cols] = low.astype(f32) * y - xs_low.astype(f32) * grad_xs
        directs[:, cols] = xc * grad_xs
        grad_xc = step * grad_xs + skip * grad_y
        grad_pre[:, cols] = grad_xc * silu_grad(v.pre[:, cols], v.gate_x[:, cols])
    grad_inner = jnp.where(v.allowed, grad_inner, 0.0).astype(bf16)
    grad_b = grad_b + mm_tn(grad_inner, v.c_low)
    grad_c = grad_c + mm(grad_inner, v.b_low)

    lane, head = iota((width, LANES), 0), iota((width, LANES), 1)
    ones = ((lane >= head * HD) & (lane < head * HD + HD)).astype(bf16)
    grad_cum = split_sum(products[...], ones)
    direct = split_sum(directs[...], ones)
    row, col = iota((rows, rows), 0), iota((rows, rows), 1)
    col_start = starts_of(c0 + iota((1, rows), 1), ends)
    above = ((col >= row) & (col_start <= c0 + row)).astype(f32)
    next_start = starts_of(c0 + rows, ends)
    reaches = (v.index >= next_start).astype(f32)
    after = jnp.dot(above, grad_cum, precision=HIGHEST, preferred_element_type=f32) + reaches * carry[0:1, :]
    flux = jnp.sum(grad_state[...] * states[...].astype(f32), axis=0, keepdims=True)
    carry[...] = split_sum(jnp.broadcast_to(flux, (8, width)), ones)
    grad_log = -v.step * v.rate * after
    grad_raw = (direct - v.rate * after) * jax.nn.sigmoid(v.raw)
    grad_rates[0:1, :] += jnp.sum(grad_raw, axis=0, keepdims=True)
    grad_rates[1:2, :] += jnp.sum(grad_log, axis=0, keepdims=True)

    index_ext = c0 + iota((rows + 8, 1), 0)
    position_ext = index_ext - starts_of(index_ext, ends)
    taps_back(v.x_ext, grad_pre[...], v.position, grad_wide)
    extended = jnp.concatenate([grad_pre[...], next_pre[...]], axis=0)
    grad_all[:, width : 2 * width] = conv_back(extended, wide, position_ext).astype(bf16)
    next_pre[...] = grad_pre[0:8, :]

    blank = jnp.zeros((rows, LANES - HD), f32)
    grad_sc = jnp.concatenate([grad_b, blank, grad_c, blank], axis=1)
    grad_pre_s = grad_sc * silu_grad(v.pre_s, v.gate_s)
    taps_back(v.s_ext, grad_pre_s, v.position, grad_narrow)
    extended_s = jnp.concatenate([grad_pre_s, next_pre_s[...]], axis=0)
    grad_all[:, 2 * width : 2 * width + 2 * LANES] = conv_back(extended_s, narrow, position_ext).astype(bf16)
    next_pre_s[...] = grad_pre_s[0:8, :]
    grad_all[:, 2 * width + 2 * LANES :] = grad_raw.astype(bf16)


def chunk_of(tp, rows):
    return math.gcd(rows // tp, CHUNK)


def mixer_specs(tp, rows, chunk, order):
    share = rows // tp
    per_share = share // chunk

    def here(place, c):
        owner = lax.div(c, per_share)
        piece = lax.rem(place[0] - owner + tp, tp)
        return piece * per_share + lax.rem(c, per_share)

    def chunk_map(i, place, lengths):
        return (here(place, order(i)), 0)

    def before_map(unit, column):
        def index(i, place, lengths):
            c = order(i)
            previous = jnp.maximum(c - 1, 0)
            return (here(place, previous) * (chunk // unit) + chunk // unit - 1, column)

        return index

    def fixed(i, place, lengths):
        return (0, 0)

    return chunk_map, before_map, fixed


def mixer_forward(place, lengths, tp, zx, sd, wide, narrow, rates):
    rows, width = zx.shape[0], zx.shape[1] // 2
    chunk = chunk_of(tp, rows)
    chunks = rows // chunk
    chunk_map, before_map, fixed = mixer_specs(tp, rows, chunk, lambda i: i)
    work = rows * width * chunk
    return pl.pallas_call(
        mixer_forward_kernel,
        out_shape=[
            jax.ShapeDtypeStruct((rows, width), bf16),
            jax.ShapeDtypeStruct((chunks, HD, width), bf16),
        ],
        grid_spec=pltpu.PrefetchScalarGridSpec(
            num_scalar_prefetch=2,
            grid=(chunks,),
            in_specs=[
                pl.BlockSpec((chunk, 2 * width), chunk_map),
                pl.BlockSpec((16, width), before_map(16, 1)),
                pl.BlockSpec((chunk, 3 * LANES), chunk_map),
                pl.BlockSpec((8, 3 * LANES), before_map(8, 0)),
                pl.BlockSpec((8, width), fixed),
                pl.BlockSpec((8, 2 * LANES), fixed),
                pl.BlockSpec((8, LANES), fixed),
            ],
            out_specs=[
                pl.BlockSpec((chunk, width), chunk_map),
                pl.BlockSpec((None, HD, width), lambda i, *_: (i, 0, 0)),
            ],
            scratch_shapes=[pltpu.VMEM((HD, width), f32)],
        ),
        compiler_params=pltpu.CompilerParams(vmem_limit_bytes=VMEM_LIMIT),
        cost_estimate=pl.CostEstimate(
            flops=8 * work, bytes_accessed=8 * rows * width, transcendentals=4 * rows * width
        ),
        name="mixer_forward",
    )(place, lengths, zx, zx, sd, sd, wide, narrow, rates)


def mixer_backward(place, lengths, tp, zx, sd, grad_scaled, stats, states, wide, narrow, rates):
    rows, width = zx.shape[0], zx.shape[1] // 2
    chunk = chunk_of(tp, rows)
    chunks = rows // chunk
    chunk_map, before_map, fixed = mixer_specs(tp, rows, chunk, lambda i: chunks - 1 - i)
    work = rows * width * chunk
    return pl.pallas_call(
        functools.partial(mixer_backward_kernel, chunks),
        out_shape=[
            jax.ShapeDtypeStruct((rows, 2 * width + 3 * LANES), bf16),
            jax.ShapeDtypeStruct((8, width), f32),
            jax.ShapeDtypeStruct((8, 2 * LANES), f32),
            jax.ShapeDtypeStruct((8, LANES), f32),
        ],
        grid_spec=pltpu.PrefetchScalarGridSpec(
            num_scalar_prefetch=2,
            grid=(chunks,),
            in_specs=[
                pl.BlockSpec((chunk, 2 * width), chunk_map),
                pl.BlockSpec((16, width), before_map(16, 1)),
                pl.BlockSpec((chunk, 3 * LANES), chunk_map),
                pl.BlockSpec((8, 3 * LANES), before_map(8, 0)),
                pl.BlockSpec((chunk, width), chunk_map),
                pl.BlockSpec((chunk, 2), chunk_map),
                pl.BlockSpec((None, HD, width), lambda i, *_: (chunks - 1 - i, 0, 0)),
                pl.BlockSpec((8, width), fixed),
                pl.BlockSpec((8, 2 * LANES), fixed),
                pl.BlockSpec((8, LANES), fixed),
            ],
            out_specs=[
                pl.BlockSpec((chunk, 2 * width + 3 * LANES), chunk_map),
                pl.BlockSpec((8, width), fixed),
                pl.BlockSpec((8, 2 * LANES), fixed),
                pl.BlockSpec((8, LANES), fixed),
            ],
            scratch_shapes=[
                pltpu.VMEM((HD, width), f32),
                pltpu.VMEM((8, width), f32),
                pltpu.VMEM((8, 2 * LANES), f32),
                pltpu.VMEM((8, LANES), f32),
                pltpu.VMEM((chunk, width), f32),
                pltpu.VMEM((chunk, width), f32),
                pltpu.VMEM((chunk, width), f32),
            ],
        ),
        compiler_params=pltpu.CompilerParams(vmem_limit_bytes=VMEM_LIMIT),
        cost_estimate=pl.CostEstimate(
            flops=24 * work, bytes_accessed=12 * rows * width, transcendentals=5 * rows * width
        ),
        name="mixer_backward",
    )(place, lengths, zx, zx, sd, sd, grad_scaled, stats, states, wide, narrow, rates)


def norm_pairs_kernel(pairs, gain, *refs):
    out = refs[2 * pairs]
    width = refs[0].shape[1]
    for j in range(pairs):
        both = [refs[2 * j + i][...].astype(f32) for i in range(2)]
        squares = sum(jnp.sum(v * v, axis=1, keepdims=True) for v in both)
        inv_root = lax.rsqrt(squares / (2 * width) + norm_eps)
        for i, v in enumerate(both):
            cols = slice(i * width, (i + 1) * width)
            out[j, :, cols] = (v * inv_root * gain[:, cols]).astype(bf16)


def norm_pairs(pairs, gain):
    rows, width = pairs[0][0].shape
    block = math.gcd(rows, 64)
    count = len(pairs)
    result = pl.pallas_call(
        functools.partial(norm_pairs_kernel, count),
        out_shape=jax.ShapeDtypeStruct((count, rows, 2 * width), bf16),
        grid=(rows // block,),
        in_specs=[pl.BlockSpec((1, 2 * width), lambda i: (0, 0))]
        + [pl.BlockSpec((block, width), lambda i: (i, 0))] * (2 * count),
        out_specs=pl.BlockSpec((count, block, 2 * width), lambda i: (0, i, 0)),
        compiler_params=pltpu.CompilerParams(vmem_limit_bytes=VMEM_LIMIT),
        cost_estimate=pl.CostEstimate(
            flops=10 * count * rows * width, bytes_accessed=8 * count * rows * width, transcendentals=rows
        ),
        name="norm_pairs",
    )(gain, *[v for pair in pairs for v in pair])
    return result.reshape(count * rows, 2 * width)


def norm_back_kernel(parts, with_base, with_low, with_gain, *refs):
    values, refs = refs[:parts], refs[parts:]
    grad, gain, refs = refs[0], refs[1], refs[2:]
    base, refs = (refs[0], refs[1:]) if with_base else (None, refs)
    outs, refs = refs[:parts], refs[parts:]
    low, refs = (refs[0], refs[1:]) if with_low else (None, refs)
    if with_gain:
        grad_gain = refs[0]

        @pl.when(pl.program_id(0) == 0)
        def _():
            grad_gain[...] = jnp.zeros_like(grad_gain)

    width = grad.shape[1]
    each = width // parts
    wide = [v[...].astype(f32) for v in values]
    squares = sum(jnp.sum(v * v, axis=1, keepdims=True) for v in wide)
    inv_root = lax.rsqrt(squares / width + norm_eps)
    units = [v * inv_root for v in wide]
    grads = [grad[:, i * each : (i + 1) * each] for i in range(parts)]
    grad_units = [g * gain[:, i * each : (i + 1) * each] for i, g in enumerate(grads)]
    cross = sum(jnp.sum(g * u, axis=1, keepdims=True) for g, u in zip(grad_units, units)) / width
    for i in range(parts):
        cols = slice(i * each, (i + 1) * each)
        if with_gain:
            grad_gain[0:1, cols] += jnp.sum(grads[i] * units[i], axis=0, keepdims=True)
        result = inv_root * (grad_units[i] - units[i] * cross)
        if with_base and i == 0:
            result = result + base[...].astype(f32)
        outs[i][...] = result
        if with_low and i == 0:
            low[...] = result.astype(bf16)


def norm_back(values, grad, gain, base=None, with_low=False, with_gain=True):
    rows, width = grad.shape
    parts = len(values)
    block = math.gcd(rows, 64)
    row_spec = pl.BlockSpec((block, width // parts), lambda i: (i, 0))
    full_spec = pl.BlockSpec((block, width), lambda i: (i, 0))
    operands = list(values) + [grad, gain] + ([base] if base is not None else [])
    shapes = [jax.ShapeDtypeStruct((rows, width // parts), f32)] * parts
    shapes += [jax.ShapeDtypeStruct((rows, width // parts), bf16)] if with_low else []
    results = pl.pallas_call(
        functools.partial(norm_back_kernel, parts, base is not None, with_low, with_gain),
        out_shape=shapes + [jax.ShapeDtypeStruct((8, width), f32)] * int(with_gain),
        grid=(rows // block,),
        in_specs=[row_spec] * parts
        + [full_spec, pl.BlockSpec((1, width), lambda i: (0, 0))]
        + ([row_spec] if base is not None else []),
        out_specs=[row_spec] * (parts + int(with_low))
        + [pl.BlockSpec((8, width), lambda i: (0, 0))] * int(with_gain),
        compiler_params=pltpu.CompilerParams(vmem_limit_bytes=VMEM_LIMIT),
        cost_estimate=pl.CostEstimate(
            flops=20 * rows * width, bytes_accessed=14 * rows * width, transcendentals=rows
        ),
        name="norm_back",
    )(*operands)
    return list(results[:-1]) + [results[-1][0]] if with_gain else list(results)


def tie(value, others):
    return lax.optimization_barrier((value, others))[0]


def after(value, token):
    return value if token is None else tie(value, token)


def ring_pairs():
    tp = lax.axis_size("tp")
    return [(i, (i + 1) % tp) for i in range(tp)]


def hop(values):
    return lax.ppermute(values, "tp", ring_pairs())


class Halving:
    def __init__(self, values, name, sent_as=f32):
        self.values, self.name, self.sent_as = values, name, sent_as
        self.half = lax.axis_size(name) // 2

    def live(self):
        return self.half > 0

    def start(self):
        count, half = lax.axis_size(self.name), self.half
        upper = (lax.axis_index(self.name) & half) != 0
        low, high = self.values[:half], self.values[half:]
        self.kept = jnp.where(upper, high, low)
        sent = jnp.where(upper, low, high).astype(self.sent_as)
        self.moved = lax.ppermute(sent, self.name, [(i, i ^ half) for i in range(count)])

    def finish(self):
        self.values = self.kept + self.moved.astype(f32)
        self.half //= 2

    def result(self):
        while self.live():
            self.start()
            self.finish()
        return self.values[0]


class Doubling:
    def __init__(self, values, name, sent_as=f32):
        self.values, self.name, self.sent_as = values, name, sent_as
        self.step = 1

    def live(self):
        return self.step < lax.axis_size(self.name)

    def start(self):
        count, step = lax.axis_size(self.name), self.step
        self.moved = lax.ppermute(
            self.values.astype(self.sent_as), self.name, [(i, i ^ step) for i in range(count)]
        )

    def finish(self):
        self.values = self.values + self.moved.astype(f32)
        self.step *= 2

    def result(self):
        while self.live():
            self.start()
            self.finish()
        return self.values


def direct(values, name, sent_as=f32):
    count = lax.axis_size(name)
    here = lax.axis_index(name)

    def block(at):
        return lax.dynamic_index_in_dim(values, lax.rem(at, count), 0, keepdims=False)

    total = block(here)
    for step in range(1, count):
        sent = block(here + step).astype(sent_as)
        moved = lax.ppermute(sent, name, [(i, (i + step) % count) for i in range(count)])
        total = total + moved.astype(f32)
    return total


def begin(tasks):
    live = [t for t in tasks if t.live()]
    for t in live:
        t.start()
    return live


def settle(moved, extras, live):
    moved, extras, arrived = lax.optimization_barrier((moved, extras, [t.moved for t in live]))
    for t, value in zip(live, arrived):
        t.moved = value
        t.finish()
    return moved, extras


def ring_gather(own, use, tasks=()):
    tp = lax.axis_size("tp")
    pieces, results = [own], []
    for p in range(tp):
        if p < tp - 1:
            moved = hop(pieces[p])
            live = begin(tasks)
        result = use(p, pieces[p])
        if p < tp - 1:
            moved, result = settle(moved, result, live)
            pieces.append(moved)
        results.append(result)
    return pieces, results


def ring_scatter(part, fill=(), tasks=()):
    tp = lax.axis_size("tp")
    fill = list(fill)
    filled = []
    total = part(1 % tp, None)
    for p in range(2, tp + 1):
        low = total.astype(bf16)
        moved = hop(low)
        live = begin(tasks)
        term = part(p % tp, low)
        extra = [fill.pop(0)(low, tasks)] if fill else []
        moved, (term, extra) = settle(moved, (term, extra), live)
        filled += extra
        total = moved.astype(f32) + term
    for thunk in fill:
        filled.append(thunk(low, tasks))
    return total, filled


def ring_both(own, work, last=None, fill=None, tasks=()):
    tp = lax.axis_size("tp")
    pieces, filled = [own], []
    moved = hop(own)
    live = begin(tasks)
    first = work(0, own)
    moved, _ = settle(moved, (), live)
    total, ahead = None, None
    for p in range(1, tp):
        pieces.append(moved)
        if p < tp - 1:
            moved = hop(pieces[p])
        elif last is not None:
            pieces[p], result = lax.optimization_barrier((pieces[p], last(pieces)))
            filled.append(result)
        live = begin(tasks)
        term = work(p, pieces[p])
        if total is not None:
            ahead, term = lax.optimization_barrier((ahead, term))
            term = ahead.astype(f32) + term
        total = term
        low = total.astype(bf16)
        ahead = hop(low)
        if p < tp - 1:
            moved, (low, first) = settle(moved, (low, first), live)
        elif fill is not None:
            ahead, result = settle(ahead, fill(low), live)
            filled.append(result)
        else:
            ahead, _ = settle(ahead, (), live)
    return pieces, ahead.astype(f32) + first, filled


def doubling_gather(values, name):
    count = lax.axis_size(name)
    here = lax.axis_index(name)
    step = 1
    while step < count:
        moved = lax.ppermute(values, name, [(i, i ^ step) for i in range(count)])
        upper = (here & step) != 0
        values = jnp.concatenate(
            [jnp.where(upper, moved, values), jnp.where(upper, values, moved)], axis=0
        )
        step *= 2
    return values


def inverse_root(values):
    return lax.rsqrt(jnp.mean(values * values, axis=1, keepdims=True) + norm_eps)


def gather(values, axis=0):
    return lax.all_gather(values, "fsdp", axis=axis, tiled=True)


def scatter(values, axis=0):
    return lax.psum_scatter(values, "fsdp", scatter_dimension=axis, tiled=True)


def local(
    hidden,
    embed,
    lengths,
    attention_norm_gain,
    query_key_value_weight,
    attention_adapter_down,
    attention_adapter_up,
    attention_output_weight,
    feedforward_norm_gain,
    gate_up_weight,
    feedforward_adapter_down,
    feedforward_adapter_up,
    down_weight,
    mixer_norm_gain,
    gate_inner_weight,
    state_input_weight,
    step_projection,
    inner_conv_taps,
    state_conv_taps,
    head_step_bias,
    decay_log_rate,
    inner_skip_gains,
    gated_norm_gain,
    mixer_output_weight,
    output_cotangent,
):
    tp = lax.axis_size("tp")
    fsdp = lax.axis_size("fsdp")
    share, width = hidden.shape
    rows = share * tp
    here = lax.axis_index("tp").astype(jnp.int32)
    place = here.reshape(1)
    lengths = lengths.reshape(-1)
    rank = attention_adapter_down.shape[2]
    head_cols = query_key_value_weight.shape[2]
    units_here = gate_up_weight.shape[2]
    inner_cols = gate_inner_weight.shape[2]
    mixer_heads = inner_cols // HD
    states = state_input_weight.shape[2]
    count = inner_conv_taps.shape[0]
    inner_total = inner_cols * tp

    def piece(values, p):
        return values[p * share : (p + 1) * share]

    own_qkv = jnp.concatenate(
        [query_key_value_weight[:, j, :] for j in range(3)]
        + [attention_adapter_down[:, j, :] for j in range(3)],
        axis=1,
    )
    weight_qkv = gather(own_qkv)
    first_hop = tuple(hop(v) for v in (hidden, embed))

    small = [
        attention_norm_gain,
        feedforward_norm_gain,
        mixer_norm_gain,
        inner_conv_taps.reshape(-1),
        state_conv_taps.reshape(-1),
        inner_skip_gains.reshape(-1),
        gated_norm_gain.reshape(-1),
    ]
    sizes = [v.shape[0] for v in small]
    padding = -sum(sizes) % LANES
    packed = jnp.concatenate(small + [jnp.zeros((padding,), bf16)]).reshape(1, -1)
    spread = gather(packed).astype(f32)
    cuts = [sum(sizes[:i]) for i in range(len(sizes) + 1)]
    parts = [spread[:, cuts[i] : cuts[i + 1]] for i in range(len(sizes))]
    gain_attn, gain_mlp, gain_mixer = (parts[i].reshape(1, -1) for i in range(3))
    taps_x = parts[3].reshape(fsdp, count, mixer_heads, -1)
    taps_x = jnp.transpose(taps_x, (1, 2, 0, 3)).reshape(count, inner_cols)
    taps_s = parts[4].reshape(fsdp, count, 2, -1)
    taps_s = jnp.transpose(taps_s, (1, 2, 0, 3)).reshape(count, 2, states)
    skip = jnp.transpose(parts[5].reshape(fsdp, mixer_heads, -1), (1, 0, 2)).reshape(1, inner_cols)
    gain_gate = jnp.transpose(parts[6].reshape(fsdp, mixer_heads, -1), (1, 0, 2)).reshape(1, inner_cols)
    wide = jnp.concatenate([taps_x, skip, gain_gate, jnp.zeros((2, inner_cols), f32)], axis=0)
    narrow = jnp.pad(taps_s, ((0, 8 - count), (0, 0), (0, LANES - states))).reshape(8, 2 * LANES)
    rates = jnp.pad(
        jnp.stack([head_step_bias, decay_log_rate]), ((0, 6), (0, LANES - mixer_heads))
    )

    places = jnp.arange(rows, dtype=jnp.int32)
    ends = [jnp.sum(lengths[: i + 1]) for i in range(lengths.shape[0] - 1)]
    position = places - starts_of(places, ends)
    freqs = jnp.exp(jnp.arange(HDA // 2, dtype=f32) * (-2.0 * math.log(10000.0) / HDA))
    angles = position.astype(f32)[:, None] * freqs[None, :]
    cosine = jnp.cos(angles)
    sine = jnp.sin(angles)
    cosine = jnp.concatenate([cosine, cosine], axis=1)
    sine = jnp.concatenate([-sine, sine], axis=1)

    own_fc1 = jnp.concatenate(
        [gate_up_weight[:, j, :] for j in range(2)] + [feedforward_adapter_down], axis=1
    )
    own_zx = jnp.concatenate(
        [gate_inner_weight[:, j, :] for j in range(2)]
        + [jnp.pad(state_input_weight[:, j, :], ((0, 0), (0, LANES - states))) for j in range(2)]
        + [jnp.pad(step_projection, ((0, 0), (0, LANES - mixer_heads)))],
        axis=1,
    )
    weight_o = gather(attention_output_weight, 1)
    weight_fc1 = gather(own_fc1)
    weight_fc2 = gather(down_weight, 1)
    weight_zx = gather(own_zx)
    weight_out = gather(mixer_output_weight, 1)

    raw, normed_parts = [(hidden, embed), first_hop], []
    spans = [((tp * i) // (tp - 2), (tp * (i + 1)) // (tp - 2)) for i in range(tp - 2)]

    def norm_ready(count):
        fresh = [norm_pairs(raw[low:high], gain_attn) for low, high in spans[len(normed_parts) :] if high <= count]
        normed_parts.extend(fresh)
        return fresh

    for p in range(2, tp):
        moved = tuple(hop(v) for v in raw[-1])
        raw.append(tie(moved, norm_ready(p)))
    norm_ready(tp)

    own_ups = jnp.concatenate(
        [attention_adapter_up[:, j, :] for j in range(3)]
        + [feedforward_adapter_up[:, j, :] for j in range(2)],
        axis=1,
    )
    ups = doubling_gather(tie(own_ups, raw[-2]), "fsdp")
    fc_up = ups[:, 3 * head_cols :]
    out_grad = [tie(output_cotangent, raw[-1])]
    projected = []
    for i in range(tp - 1):
        moved = hop(out_grad[-1])
        if i < tp - 2:
            projected.append(mm(normed_parts[i], weight_qkv))
            moved = tie(moved, projected)
        else:
            attended, queries, keys, values = attention_forward(
                place, lengths, tp, projected, ups, head_cols, cosine, sine
            )
            moved = tie(moved, attended)
        out_grad.append(moved)
    lora_rows = jnp.concatenate([v[:, 3 * head_cols :].astype(bf16) for v in projected], axis=0)
    attended, lora_rows, out_grad[-1] = lax.optimization_barrier((attended, lora_rows, moved))
    out_grad_rows = jnp.concatenate(out_grad, axis=0)
    mixed, (normed_rows,) = ring_scatter(
        lambda p, t: mm(piece(after(attended, t), p), weight_o),
        [lambda t, _: jnp.concatenate(tie(normed_parts, t), axis=0)],
    )

    mlp_root = inverse_root(mixed)
    gate_up, fc_mid, units = [], [], []

    def feed(p, rows_in):
        wide_rows = mm(rows_in, weight_fc1)
        middle = wide_rows[:, 2 * units_here :].astype(bf16)
        both = (wide_rows[:, : 2 * units_here] + mm(middle, fc_up)).astype(bf16)
        gate, up = both[:, :units_here].astype(f32), both[:, units_here:].astype(f32)
        unit = (jax.nn.gelu(gate) * up).astype(bf16)
        fc_mid.append(middle)
        gate_up.append(both)
        units.append(unit)
        return mm(unit, weight_fc2)

    mlp_in, branch, _ = ring_both((mixed * mlp_root * gain_mlp).astype(bf16), feed)
    residual = hidden.astype(f32) + mixed + branch

    mixer_root = inverse_root(residual)
    kept = []

    def mix(p, rows_in):
        result = mm(rows_in, weight_zx)
        if p == 0:
            kept.append(mm_nt(tie(out_grad_rows, result), weight_out).astype(bf16))
        elif p == 1:
            kept.append(jnp.concatenate(tie(units, result), axis=0))
            kept.append(jnp.concatenate(tie(mlp_in, result), axis=0))
        return (result, kept[-1])

    mixer_in, zxs = ring_gather((residual * mixer_root * gain_mixer).astype(bf16), mix)
    zxs = [v[0] for v in zxs]
    grad_scaled, units_rows, mlp_rows = kept
    zx = jnp.concatenate([v[:, : 2 * inner_cols].astype(bf16) for v in zxs], axis=0)
    sd = jnp.concatenate([v[:, 2 * inner_cols :] for v in zxs], axis=0)
    gated, chunk_states = mixer_forward(place, lengths, tp, zx, sd, wide, narrow, rates)
    gated_wide = gated.astype(f32)
    sums = jnp.stack(
        [
            jnp.sum(gated_wide * gated_wide, axis=1),
            jnp.sum(grad_scaled.astype(f32) * gain_gate * gated_wide, axis=1),
        ],
        axis=0,
    )
    sums = jnp.roll(jnp.flip(sums.reshape(2, tp, share), axis=1), here + 1, axis=1)
    sums = lax.psum(sums, "tp")
    sums = jnp.flip(jnp.roll(sums, -(here + 1), axis=1), axis=1).reshape(2, rows)
    gate_root = lax.rsqrt(sums[0] / inner_total + norm_eps)
    stats = jnp.stack([gate_root, gate_root**3 * sums[1] / inner_total], axis=1)
    scaled = (gated_wide * gate_root[:, None] * gain_gate).astype(bf16)
    out_rows, stats = lax.optimization_barrier((mm(scaled, weight_out).astype(bf16), stats))
    out_terms = [piece(out_rows, p) for p in range(tp)]
    out = hop(out_terms[1 % tp])

    grad_all, grad_wide, grad_narrow, grad_rates = mixer_backward(
        place, lengths, tp, zx, sd, grad_scaled, stats, chunk_states, wide, narrow, rates
    )
    out, grad_all = lax.optimization_barrier((out, grad_all))
    out = out.astype(f32) + out_terms[2 % tp].astype(f32)

    def by_fsdp(values):
        lead = values.shape[:-1]
        cut = values.reshape(lead + (fsdp, values.shape[-1] // fsdp))
        return jnp.moveaxis(cut, -2, 0).reshape(fsdp, -1)

    def small_gradients(token):
        taps, bars, sums_r = tie((grad_wide, grad_narrow, grad_rates), token)
        return [
            by_fsdp(taps[:count].reshape(count, mixer_heads, HD)),
            by_fsdp(taps[4].reshape(mixer_heads, HD)),
            by_fsdp(taps[5].reshape(mixer_heads, HD)),
            jnp.broadcast_to(sums_r[:2, :mixer_heads].reshape(1, -1), (fsdp, 2 * mixer_heads)),
            by_fsdp(bars[:count].reshape(count, 2, LANES)[:, :, :states]),
        ]

    mixer_rows = []

    def out_fill(token, _):
        mixer_rows.append(jnp.concatenate(tie(mixer_in, token), axis=0))
        return mm_tn(tie(scaled, token), out_grad_rows).astype(bf16), mixer_rows[0]

    grad_mixer_in, ((sum_w_out, _), sum_w_zx, small) = ring_scatter(
        lambda p, t: mm_nt(piece(after(grad_all, t), p), weight_zx),
        [
            out_fill,
            lambda t, _: mm_tn(tie(mixer_rows[0], t), grad_all).astype(bf16),
            lambda t, _: small_gradients(t),
        ],
    )
    sum_w_out = scatter(sum_w_out, 1)
    sum_w_zx = scatter(sum_w_zx)
    small_sizes = [v.shape[1] for v in small]
    small_cuts = [sum(small_sizes[:i]) for i in range(len(small_sizes) + 1)]
    small_task = Halving(jnp.concatenate(small, axis=1), "fsdp")
    grad_residual, grad_residual_low, grad_gain_mixer = norm_back(
        [residual], grad_mixer_in, gain_mixer, output_cotangent, True
    )

    grad_gate_up = []

    def feed_back(p, grad_rows):
        grad_units = mm_nt(grad_rows, weight_fc2)
        gate = gate_up[p][:, :units_here].astype(f32)
        up = gate_up[p][:, units_here:].astype(f32)
        raised, back = jax.vjp(jax.nn.gelu, gate)
        both = jnp.concatenate(
            [back(grad_units * up)[0].astype(bf16), (grad_units * raised).astype(bf16)], axis=1
        )
        both = jnp.concatenate([both, mm_nt(both, fc_up).astype(bf16)], axis=1)
        grad_gate_up.append(both)
        return mm_nt(both, weight_fc1)

    def fc2_fill(token, _):
        rows_in = tie(units_rows, (sum_w_out, token))
        return mm_tn(rows_in, jnp.concatenate(grad_branch, axis=0)).astype(bf16)

    def fc1_fill(token, _):
        return mm_tn(tie(mlp_rows, token), jnp.concatenate(grad_gate_up, axis=0)).astype(bf16)

    grad_branch, back_terms = ring_gather(
        grad_residual_low, lambda p, v: feed_back(p, v) if p < tp - 1 else (), [small_task]
    )
    grad_mlp_in, filled = ring_scatter(
        lambda p, t: feed_back(p, after(grad_branch[p], t))
        if p == tp - 1
        else tie(back_terms[p], grad_branch[-1]),
        [fc2_fill] + [lambda t, _: ()] * (tp - 3) + [fc1_fill],
    )
    sum_w_fc2, sum_w_fc1 = filled[0], filled[-1]
    sum_w_fc2 = scatter(sum_w_fc2, 1)
    sum_w_fc1 = scatter(sum_w_fc1)
    grad_gate_up_rows = jnp.concatenate(grad_gate_up, axis=0)
    _, grad_mixed_low, grad_gain_mlp = norm_back([mixed], grad_mlp_in, gain_mlp, grad_residual, True)
    gain_tasks = []

    fc_ups = []

    def attended_back(p, rows_in):
        result = mm_nt(rows_in, weight_o).astype(bf16)
        if p == 0:
            middle, first, second = tie((fc_mid, grad_gain_mixer, grad_gain_mlp), rows_in)
            fc_ups.append(
                mm_tn(jnp.concatenate(middle, axis=0), grad_gate_up_rows[:, : 2 * units_here])
            )
            gains = jnp.concatenate([first.reshape(fsdp, -1), second.reshape(fsdp, -1)], axis=1)
            result, gains = tie((result, gains), fc_ups[0])
            gain_tasks.append(Halving(gains, "fsdp"))
        return result

    grad_mixed, grad_attended = ring_gather(tie(grad_mixed_low, sum_w_zx), attended_back, gain_tasks)
    sum_w_o = mm_tn(tie(attended, sum_w_fc2), jnp.concatenate(grad_mixed, axis=0)).astype(bf16)
    grad_attended[-1] = tie(grad_attended[-1], sum_w_o)
    sum_w_o = scatter(sum_w_o, 1)
    out = hop(out.astype(bf16))
    grad_projected = attention_backward(
        place, lengths, queries, keys, values, ups, grad_attended, cosine, sine
    )
    out, grad_projected, sum_w_fc1 = lax.optimization_barrier((out, grad_projected, sum_w_fc1))
    out = out.astype(f32) + out_terms[3 % tp].astype(f32)
    out = hop(out.astype(bf16))
    sum_w_qkv = mm_tn(normed_rows, grad_projected).astype(bf16)
    out, sum_w_qkv, grad_projected = lax.optimization_barrier((out, sum_w_qkv, grad_projected))
    sum_w_qkv = scatter(sum_w_qkv)

    at_t = 2 * inner_cols + 2 * LANES

    def finish_out(token):
        total = tie(out, token).astype(f32) + out_terms[4 % tp].astype(f32)
        for p in range(5, tp + 1):
            total = hop(total.astype(bf16)).astype(f32) + out_terms[p % tp].astype(f32)
        return residual + total

    def finish_adapters(token, tasks):
        rows_in = tie(lora_rows, token)
        grad_up = [
            mm_tn(
                rows_in[:, j * rank : (j + 1) * rank],
                grad_projected[:, j * head_cols : (j + 1) * head_cols],
            )
            for j in range(3)
        ]
        ups_grad = jnp.concatenate(grad_up + fc_ups, axis=1)
        ups_tasks.append(Halving(ups_grad.reshape(fsdp, -1, ups_grad.shape[1]), "fsdp", bf16))
        ups_tasks[0].start()
        shared = jnp.concatenate([small_task.result()[small_cuts[4] :], gain_tasks[0].result()])
        tasks.append(Doubling(shared, "tp"))
        return ups_grad, shared

    def finish_mixer(token, tasks):
        zx_sum, w_out, w_fc2 = tie((sum_w_zx, sum_w_out, sum_w_fc2), token)
        zx_sum = zx_sum.astype(f32)
        bc_sums.append(zx_sum[:, 2 * inner_cols : at_t])
        return (
            stacked(zx_sum, inner_cols, 2),
            zx_sum[:, at_t : at_t + mixer_heads],
            w_out.astype(f32),
            w_fc2.astype(f32),
        )

    def finish_feed(token, tasks):
        fc1_sum, w_o = tie((sum_w_fc1, sum_w_o), token)
        fc1_sum = fc1_sum.astype(f32)
        tasks.append(
            Doubling(jnp.concatenate([bc_sums[0], fc1_sum[:, 2 * units_here :]], axis=1), "tp", bf16)
        )
        return (
            stacked(fc1_sum, units_here, 2),
            w_o.astype(f32),
            finish_out(token),
        )

    def stacked(values, each, parts):
        values = jnp.stack([values[:, j * each : (j + 1) * each] for j in range(parts)], axis=1)
        return with_layout_constraint(values, Layout(major_to_minor=(0, 1, 2)))

    tasks, ups_tasks, bc_sums = [], [], []
    normed_terms = {}
    pair = mm_nt(grad_projected[share : 3 * share], weight_qkv)
    normed_terms[1], normed_terms[2] = piece(pair, 0), piece(pair, 1)

    def normed_back(p, token):
        if p not in normed_terms:
            normed_terms[p] = mm_nt(piece(after(grad_projected, token), p), weight_qkv)
        return normed_terms[p]

    grad_normed, ((_, mixer_sums, _), feed_sums) = ring_scatter(
        normed_back,
        [lambda t, k: (finish_adapters(t, k), finish_mixer(t, k), normed_back(3 % tp, t)), finish_feed],
        tasks,
    )
    grad_w_zx, grad_w_dt, grad_w_out, grad_w_fc2 = mixer_sums
    grad_w_fc1, grad_w_o, out = feed_sums
    grad_hidden, grad_embed = norm_back(
        [hidden, embed], grad_normed, gain_attn, grad_residual, with_gain=False
    )
    ups_tasks[0].finish()
    grad_ups = ups_tasks[0].result()
    sum_w_qkv = tie(sum_w_qkv, grad_ups)
    gain_rows = jnp.sum(sum_w_qkv.astype(f32) * own_qkv.astype(f32), axis=1)
    gain_rows = gain_rows / attention_norm_gain.astype(f32)
    grad_down = direct(sum_w_qkv[:, 3 * head_cols :].astype(f32).reshape(tp, -1, 3 * rank), "tp", bf16)
    grad_gain_attn = direct(gain_rows.reshape(tp, -1), "tp")
    grad_w_qkv = jnp.stack(
        [sum_w_qkv[:, j * head_cols : (j + 1) * head_cols].astype(f32) for j in range(3)], axis=1
    )
    small_sum = small_task.result()
    small_parts = [small_sum[small_cuts[i] : small_cuts[i + 1]] for i in range(len(small_sizes))]
    tail = tasks[0].result()
    shared = tasks[1].result()
    tail_sizes = [small_sizes[4], width // fsdp, width // fsdp]
    tail_cuts = [sum(tail_sizes[:i]) for i in range(4)]
    grad_conv_bc, sum_gain_mixer, sum_gain_mlp = (
        tail[tail_cuts[i] : tail_cuts[i + 1]] for i in range(3)
    )
    sum_rates = small_parts[3].reshape(2, mixer_heads)
    return (
        out,
        grad_hidden,
        grad_embed,
        grad_gain_attn,
        grad_w_qkv,
        grad_down.reshape(-1, 3, rank),
        grad_ups[:, : 3 * head_cols].reshape(-1, 3, head_cols),
        grad_w_o,
        sum_gain_mlp,
        grad_w_fc1,
        shared[:, 2 * LANES :],
        grad_ups[:, 3 * head_cols :].reshape(-1, 2, units_here),
        grad_w_fc2,
        sum_gain_mixer,
        grad_w_zx,
        shared[:, : 2 * LANES].reshape(-1, 2, LANES)[:, :, :states],
        grad_w_dt,
        small_parts[0].reshape(count, mixer_heads, -1),
        grad_conv_bc.reshape(count, 2, -1),
        sum_rates[0],
        sum_rates[1],
        small_parts[1].reshape(mixer_heads, -1),
        small_parts[2].reshape(mixer_heads, -1),
        grad_w_out,
    )


def solution(mesh):
    placed = (
        P(("fsdp", "tp"), None),
        P(("fsdp", "tp"), None),
        P("fsdp", None),
        P("fsdp"),
        P("fsdp", None, "tp"),
        P("fsdp", None, None),
        P("fsdp", None, "tp"),
        P("tp", "fsdp"),
        P("fsdp"),
        P("fsdp", None, "tp"),
        P("fsdp", None),
        P("fsdp", None, "tp"),
        P("tp", "fsdp"),
        P("fsdp"),
        P("fsdp", None, "tp"),
        P("fsdp", None, None),
        P("fsdp", "tp"),
        P(None, "tp", "fsdp"),
        P(None, None, "fsdp"),
        P("tp"),
        P("tp"),
        P("tp", "fsdp"),
        P("tp", "fsdp"),
        P("tp", "fsdp"),
        P(("fsdp", "tp"), None),
    )
    return jax.shard_map(
        local,
        mesh=mesh,
        in_specs=placed,
        out_specs=(
            P(("fsdp", "tp"), None),
            P(("fsdp", "tp"), None),
            P(("fsdp", "tp"), None),
            P(("fsdp", "tp")),
            P("fsdp", None, "tp"),
            P(("fsdp", "tp"), None, None),
            P("fsdp", None, "tp"),
            P("tp", "fsdp"),
            P("fsdp"),
            P("fsdp", None, "tp"),
            P("fsdp", None),
            P("fsdp", None, "tp"),
            P("tp", "fsdp"),
            P("fsdp"),
            P("fsdp", None, "tp"),
            P("fsdp", None, None),
            P("fsdp", "tp"),
            P(None, "tp", "fsdp"),
            P(None, None, "fsdp"),
            P("tp"),
            P("tp"),
            P("tp", "fsdp"),
            P("tp", "fsdp"),
            P("tp", "fsdp"),
        ),
        check_vma=False,
    )
```

```python
import functools
import math

import jax
import jax.numpy as jnp
from jax import lax
from jax.experimental import pallas as pl
from jax.experimental.layout import Layout, with_layout_constraint
from jax.experimental.pallas import tpu as pltpu
from jax.sharding import PartitionSpec as P

HDA = 128
HD = 64
LANES = 128
CHUNK = 128

norm_eps = 1e-05
f32 = jnp.float32
bf16 = jnp.bfloat16
HIGHEST = lax.Precision.HIGHEST
VMEM_LIMIT = 56 * 1024 * 1024


def mm(left, right):
    return jnp.dot(left, right, preferred_element_type=f32)


def mm_nt(left, right):
    return lax.dot_general(left, right, (((1,), (1,)), ((), ())), preferred_element_type=f32)


def mm_tn(left, right):
    return lax.dot_general(left, right, (((0,), (0,)), ((), ())), preferred_element_type=f32)


def starts_of(index, ends):
    start = jnp.zeros_like(index)
    for end in ends:
        start = jnp.where(index >= end, end, start)
    return start


def ends_of(lengths_ref):
    ends = []
    end = jnp.int32(0)
    for i in range(lengths_ref.shape[0] - 1):
        end = end + lengths_ref[i]
        ends.append(end)
    return ends


def iota(shape, axis):
    return lax.broadcasted_iota(jnp.int32, shape, axis)


def attention_forward_kernel(
    tp,
    parts,
    place_ref,
    lengths_ref,
    cosine_ref,
    sine_ref,
    q_up,
    k_up,
    v_up,
    *refs,
):
    pieces = refs[: 4 * parts]
    attended_ref, q_ref, k_ref, v_ref, held = refs[4 * parts :]
    rows = q_ref.shape[0]
    share = rows // tp
    rank = q_up.shape[0]
    here = place_ref[0]
    ends = ends_of(lengths_ref)
    for p in range(tp):
        owner = lax.rem(here - p + tp, tp)
        part = pl.ds(pl.multiple_of(owner * share, share), share)
        cosine, sine = cosine_ref[part, :], sine_ref[part, :]
        at = p * share
        source = 0
        while at >= pieces[4 * source].shape[0]:
            at -= pieces[4 * source].shape[0]
            source += 1
        mine = slice(at, at + share)
        for j, (up, target) in enumerate(((q_up, q_ref), (k_up, k_ref), (v_up, v_ref))):
            low = pieces[4 * source + 3][mine, j * rank : (j + 1) * rank].astype(bf16)
            value = pieces[4 * source + j][mine, :] + mm(low, up[...])
            if j < 2:
                value = value * cosine + pltpu.roll(value, HDA // 2, 1) * sine
            target[part, :] = value.astype(bf16)
    block = min(256, rows)
    scale = HDA ** (-0.5)
    for at in range(0, rows, block):
        upto = at + block
        scores = mm_nt(k_ref[:upto, :], q_ref[at:upto, :]) * scale
        query = at + iota((1, block), 1)
        key = iota((upto, 1), 0)
        seen = (key <= query) & (key >= starts_of(query, ends))
        scores = jnp.where(seen, scores, -1e30)
        raised = jnp.exp(scores - jnp.max(scores, axis=0, keepdims=True))
        probs = (raised * (1.0 / jnp.sum(raised, axis=0, keepdims=True))).astype(bf16)
        held[at:upto, :] = mm_tn(probs, v_ref[:upto, :]).astype(bf16)
    for p in range(tp):
        owner = lax.rem(here - p + tp, tp)
        part = pl.ds(pl.multiple_of(owner * share, share), share)
        attended_ref[p * share : (p + 1) * share, :] = held[part, :]


def attention_forward(place, lengths, tp, projected, ups, columns, cosine, sine):
    rows = sum(v.shape[0] for v in projected)
    heads = columns // HDA
    rank = ups.shape[0]
    table_spec = pl.BlockSpec((rows, HDA), lambda h, *_: (0, 0))

    def head_spec(j, height=rows):
        return pl.BlockSpec((height, HDA), lambda h, *_: (0, j * heads + h))

    work = heads * rows * rows * HDA
    return pl.pallas_call(
        functools.partial(attention_forward_kernel, tp, len(projected)),
        out_shape=[jax.ShapeDtypeStruct((rows, columns), bf16)] * 4,
        grid_spec=pltpu.PrefetchScalarGridSpec(
            num_scalar_prefetch=2,
            grid=(heads,),
            in_specs=[table_spec, table_spec]
            + [head_spec(j, rank) for j in range(3)]
            + [
                pl.BlockSpec((v.shape[0], 3 * rank), lambda h, *_: (0, columns // rank))
                if j == 3
                else head_spec(j, v.shape[0])
                for v in projected
                for j in range(4)
            ],
            out_specs=[head_spec(0)] * 4,
            scratch_shapes=[pltpu.VMEM((rows, HDA), bf16)],
        ),
        compiler_params=pltpu.CompilerParams(vmem_limit_bytes=VMEM_LIMIT),
        cost_estimate=pl.CostEstimate(
            flops=4 * work, bytes_accessed=20 * rows * columns, transcendentals=heads * rows * rows
        ),
        name="attention_forward",
    )(place, lengths, cosine, sine, ups, ups, ups, *[v for v in projected for _ in range(4)])


def attention_backward_kernel(
    tp,
    heads,
    place_ref,
    lengths_ref,
    cosine_ref,
    sine_ref,
    q_ref,
    k_ref,
    v_ref,
    q_up,
    k_up,
    v_up,
    *refs,
):
    grad_in = refs[:tp]
    out_ref, held, dq, dk, dv, lora = refs[tp:]
    rows = q_ref.shape[0]
    share = rows // tp
    rank = q_up.shape[0]
    here = place_ref[0]
    head = pl.program_id(0)
    ends = ends_of(lengths_ref)
    for p in range(tp):
        owner = lax.rem(here - p + tp, tp)
        part = pl.ds(pl.multiple_of(owner * share, share), share)
        held[part, :] = grad_in[p][...]
    dk[...] = jnp.zeros_like(dk)
    dv[...] = jnp.zeros_like(dv)

    @pl.when(head == 0)
    def _():
        lora[...] = jnp.zeros_like(lora)

    block = min(256, rows)
    scale = HDA ** (-0.5)
    for at in range(0, rows, block):
        upto = at + block
        query_rows = q_ref[at:upto, :]
        grad_rows = held[at:upto, :]
        scores = mm_nt(k_ref[:upto, :], query_rows) * scale
        query = at + iota((1, block), 1)
        key = iota((upto, 1), 0)
        seen = (key <= query) & (key >= starts_of(query, ends))
        scores = jnp.where(seen, scores, -1e30)
        raised = jnp.exp(scores - jnp.max(scores, axis=0, keepdims=True))
        probs = raised * (1.0 / jnp.sum(raised, axis=0, keepdims=True))
        grad_probs = mm_nt(v_ref[:upto, :], grad_rows)
        cross = jnp.sum(probs * grad_probs, axis=0, keepdims=True)
        grad_scores = (probs * (grad_probs - cross)).astype(bf16)
        dv[:upto, :] += mm(probs.astype(bf16), grad_rows)
        dk[:upto, :] += mm(grad_scores, query_rows)
        dq[at:upto, :] = mm_tn(grad_scores, k_ref[:upto, :])
    for p in range(tp):
        owner = lax.rem(here - p + tp, tp)
        part = pl.ds(pl.multiple_of(owner * share, share), share)
        cosine, sine = cosine_ref[part, :], sine_ref[part, :]
        mine = slice(p * share, (p + 1) * share)
        for j, (source, up) in enumerate(((dq, q_up), (dk, k_up), (dv, v_up))):
            value = source[part, :]
            if j < 2:
                value = value * scale
                value = value * cosine - pltpu.roll(value, HDA // 2, 1) * sine
            low = value.astype(bf16)
            at = pl.multiple_of((j * heads + head) * HDA, HDA)
            out_ref[mine, pl.ds(at, HDA)] = low
            lora[mine, j * rank : (j + 1) * rank] += mm_nt(low, up[...])

    @pl.when(head == heads - 1)
    def _():
        out_ref[:, 3 * heads * HDA :] = lora[...].astype(bf16)


def attention_backward(place, lengths, queries, keys, values, ups, pieces, cosine, sine):
    tp = len(pieces)
    share, columns = pieces[0].shape
    rows = share * tp
    heads = columns // HDA
    rank = ups.shape[0]
    piece_spec = pl.BlockSpec((share, HDA), lambda h, *_: (0, h))
    table_spec = pl.BlockSpec((rows, HDA), lambda h, *_: (0, 0))
    head_spec = pl.BlockSpec((rows, HDA), lambda h, *_: (0, h))

    def up_spec(j):
        return pl.BlockSpec((rank, HDA), lambda h, *_: (0, j * heads + h))

    total = 3 * columns + 3 * rank
    work = heads * rows * rows * HDA
    return pl.pallas_call(
        functools.partial(attention_backward_kernel, tp, heads),
        out_shape=jax.ShapeDtypeStruct((rows, total), bf16),
        grid_spec=pltpu.PrefetchScalarGridSpec(
            num_scalar_prefetch=2,
            grid=(heads,),
            in_specs=[table_spec, table_spec]
            + [head_spec] * 3
            + [up_spec(j) for j in range(3)]
            + [piece_spec] * tp,
            out_specs=pl.BlockSpec((rows, total), lambda h, *_: (0, 0)),
            scratch_shapes=[pltpu.VMEM((rows, HDA), bf16)]
            + [pltpu.VMEM((rows, HDA), f32)] * 3
            + [pltpu.VMEM((rows, 3 * rank), f32)],
        ),
        compiler_params=pltpu.CompilerParams(vmem_limit_bytes=VMEM_LIMIT),
        cost_estimate=pl.CostEstimate(
            flops=10 * work, bytes_accessed=14 * rows * columns, transcendentals=heads * rows * rows
        ),
        name="attention_backward",
    )(place, lengths, cosine, sine, queries, keys, values, ups, ups, ups, *pieces)


def conv_rows(extended, taps, position):
    count = 4
    rows = extended.shape[0] - 8
    total = None
    for k in range(count):
        moved = extended[8 - k : 8 - k + rows, :]
        if k:
            moved = jnp.where(position >= k, moved, 0.0)
        term = taps[count - 1 - k : count - k, :] * moved
        total = term if total is None else total + term
    return total


def conv_back(extended, taps, position):
    count = 4
    rows = extended.shape[0] - 8
    total = None
    for k in range(count):
        kept = jnp.where(position >= k, extended, 0.0) if k else extended
        term = taps[count - 1 - k : count - k, :] * kept[k : k + rows, :]
        total = term if total is None else total + term
    return total


def taps_back(extended, grad, position, target):
    count = 4
    rows = extended.shape[0] - 8
    for k in range(count):
        moved = extended[8 - k : 8 - k + rows, :]
        if k:
            moved = jnp.where(position >= k, moved, 0.0)
        at = count - 1 - k
        target[at : at + 1, :] += jnp.sum(grad * moved, axis=0, keepdims=True)


def silu_grad(value, gate):
    return gate * (1.0 + value * (1.0 - gate))


class Chunk:
    def __init__(self, c0, ends, zx, before, sd, sd_before, wide, narrow, rates):
        rows = zx.shape[0]
        width = zx.shape[1] // 2
        self.rows, self.width = rows, width
        index = c0 + iota((rows, 1), 0)
        start = starts_of(index, ends)
        self.index, self.start = index, start
        self.position = index - start
        last_start = starts_of(c0 + rows - 1, ends)
        self.z = zx[:, :width].astype(f32)
        self.x_ext = jnp.concatenate(
            [before[...].astype(f32)[8:16, :], zx[:, width:].astype(f32)], axis=0
        )
        self.s_ext = jnp.concatenate([sd_before[:, : 2 * LANES], sd[:, : 2 * LANES]], axis=0)
        self.pre = conv_rows(self.x_ext, wide, self.position)
        self.gate_x = jax.nn.sigmoid(self.pre)
        self.xc = self.pre * self.gate_x
        self.pre_s = conv_rows(self.s_ext, narrow, self.position)
        self.gate_s = jax.nn.sigmoid(self.pre_s)
        sc = self.pre_s * self.gate_s
        self.b_low = sc[:, :HD].astype(bf16)
        self.c_low = sc[:, LANES : LANES + HD].astype(bf16)
        self.raw = sd[:, 2 * LANES : 3 * LANES] + rates[0:1, :]
        self.step = jnp.maximum(self.raw, 0.0) + jnp.log1p(jnp.exp(-jnp.abs(self.raw)))
        self.rate = jnp.exp(rates[1:2, :])
        row, col = iota((rows, rows), 0), iota((rows, rows), 1)
        below = (col <= row).astype(f32)
        self.cum = jnp.dot(below, -self.step * self.rate, precision=HIGHEST, preferred_element_type=f32)
        self.cum_t = self.cum.T
        self.allowed = (col <= row) & ((c0 + col) >= start)
        self.inner = jnp.where(self.allowed, mm_nt(self.c_low, self.b_low), 0.0)
        last = self.cum[rows - 1 : rows, :]
        self.into = jnp.exp(self.cum) * (start < c0).astype(f32)
        self.onto = jnp.exp(last - self.cum) * (index >= last_start).astype(f32)
        self.decay = jnp.exp(last) * (last_start < c0).astype(f32)
        self.low_half = iota((1, LANES), 1) < HD

    def pair(self, table, i):
        return jnp.where(self.low_half, table[:, 2 * i : 2 * i + 1], table[:, 2 * i + 1 : 2 * i + 2])

    def spread(self, h):
        return jnp.exp(jnp.minimum(self.cum[:, h : h + 1] - self.cum_t[h : h + 1, :], 0.0))


def mixer_forward_kernel(
    place_ref, lengths_ref, zx, before, sd, sd_before, wide, narrow, rates, gated, states, state
):
    rows = zx.shape[0]
    c0 = pl.program_id(0) * rows
    ends = ends_of(lengths_ref)

    @pl.when(pl.program_id(0) == 0)
    def _():
        state[...] = jnp.zeros_like(state)

    v = Chunk(c0, ends, zx, before, sd, sd_before, wide, narrow, rates)
    state_low = state[...].astype(bf16)
    states[...] = state_low
    for i in range(v.width // LANES):
        cols = slice(i * LANES, (i + 1) * LANES)
        xc = v.xc[:, cols]
        xs = v.pair(v.step, i) * xc
        xs_low = xs.astype(bf16)
        first = (v.spread(2 * i) * v.inner).astype(bf16)
        second = (v.spread(2 * i + 1) * v.inner).astype(bf16)
        y = jnp.where(v.low_half, mm(first, xs_low), mm(second, xs_low))
        y = y + v.pair(v.into, i) * mm(v.c_low, state_low[:, cols])
        y = y + wide[4:5, cols] * xc
        z = v.z[:, cols]
        gated[:, cols] = (y * z * jax.nn.sigmoid(z)).astype(bf16)
        state[:, cols] = v.pair(v.decay, i) * state[:, cols] + mm_tn(
            v.b_low, (v.pair(v.onto, i) * xs).astype(bf16)
        )


def split_sum(values, ones):
    high = values.astype(bf16)
    low = (values - high.astype(f32)).astype(bf16)
    return mm(high, ones) + mm(low, ones)


def mixer_backward_kernel(
    chunks,
    place_ref,
    lengths_ref,
    zx,
    before,
    sd,
    sd_before,
    grad_scaled,
    stats,
    states,
    wide,
    narrow,
    rates,
    grad_all,
    grad_wide,
    grad_narrow,
    grad_rates,
    grad_state,
    next_pre,
    next_pre_s,
    carry,
    products,
    directs,
    grad_pre,
):
    rows = zx.shape[0]
    turn = pl.program_id(0)
    c0 = (chunks - 1 - turn) * rows
    ends = ends_of(lengths_ref)

    @pl.when(turn == 0)
    def _():
        for ref in (grad_state, next_pre, next_pre_s, carry, grad_wide, grad_narrow, grad_rates):
            ref[...] = jnp.zeros_like(ref)

    v = Chunk(c0, ends, zx, before, sd, sd_before, wide, narrow, rates)
    width = v.width
    root, pull = stats[:, 0:1], stats[:, 1:2]
    grad_inner = jnp.zeros((rows, rows), f32)
    grad_b = jnp.zeros((rows, HD), f32)
    grad_c = jnp.zeros((rows, HD), f32)
    for i in range(width // LANES):
        cols = slice(i * LANES, (i + 1) * LANES)
        xc = v.xc[:, cols]
        step = v.pair(v.step, i)
        xs = step * xc
        xs_low = xs.astype(bf16)
        spread_a, spread_b = v.spread(2 * i), v.spread(2 * i + 1)
        first = (spread_a * v.inner).astype(bf16)
        second = (spread_b * v.inner).astype(bf16)
        state_low = states[:, cols]
        into, onto = v.pair(v.into, i), v.pair(v.onto, i)
        y = jnp.where(v.low_half, mm(first, xs_low), mm(second, xs_low))
        y = y + into * mm(v.c_low, state_low)
        skip, gain = wide[4:5, cols], wide[5:6, cols]
        whole = y + skip * xc
        z = v.z[:, cols]
        gate = jax.nn.sigmoid(z)
        gated = whole * z * gate
        incoming = grad_scaled[:, cols].astype(f32)
        rooted = incoming * root
        grad_wide[5:6, cols] += jnp.sum(rooted * gated, axis=0, keepdims=True)
        grad_gated = rooted * gain - gated * pull
        grad_y = grad_gated * z * gate
        grad_all[:, cols] = (grad_gated * whole * silu_grad(z, gate)).astype(bf16)
        grad_wide[4:5, cols] += jnp.sum(grad_y * xc, axis=0, keepdims=True)
        low = grad_y.astype(bf16)
        low_a = jnp.where(v.low_half, grad_y, 0.0).astype(bf16)
        low_b = jnp.where(v.low_half, 0.0, grad_y).astype(bf16)
        grad_inner = grad_inner + spread_a * mm_nt(low_a, xs_low) + spread_b * mm_nt(low_b, xs_low)
        grad_end = grad_state[:, cols]
        grad_end_low = grad_end.astype(bf16)
        grad_xs = jnp.where(v.low_half, mm_tn(first, low), mm_tn(second, low))
        grad_xs = grad_xs + onto * mm(v.b_low, grad_end_low)
        into_y = (into * grad_y).astype(bf16)
        onto_x = (onto * xs).astype(bf16)
        grad_b = grad_b + mm_nt(onto_x, grad_end_low)
        grad_c = grad_c + mm_nt(into_y, state_low)
        grad_state[:, cols] = v.pair(v.decay, i) * grad_end + mm_tn(v.c_low, into_y)
        products[:, cols] = low.astype(f32) * y - xs_low.astype(f32) * grad_xs
        directs[:, cols] = xc * grad_xs
        grad_xc = step * grad_xs + skip * grad_y
        grad_pre[:, cols] = grad_xc * silu_grad(v.pre[:, cols], v.gate_x[:, cols])
    grad_inner = jnp.where(v.allowed, grad_inner, 0.0).astype(bf16)
    grad_b = grad_b + mm_tn(grad_inner, v.c_low)
    grad_c = grad_c + mm(grad_inner, v.b_low)

    lane, head = iota((width, LANES), 0), iota((width, LANES), 1)
    ones = ((lane >= head * HD) & (lane < head * HD + HD)).astype(bf16)
    grad_cum = split_sum(products[...], ones)
    direct = split_sum(directs[...], ones)
    row, col = iota((rows, rows), 0), iota((rows, rows), 1)
    col_start = starts_of(c0 + iota((1, rows), 1), ends)
    above = ((col >= row) & (col_start <= c0 + row)).astype(f32)
    next_start = starts_of(c0 + rows, ends)
    reaches = (v.index >= next_start).astype(f32)
    after = jnp.dot(above, grad_cum, precision=HIGHEST, preferred_element_type=f32) + reaches * carry[0:1, :]
    flux = jnp.sum(grad_state[...] * states[...].astype(f32), axis=0, keepdims=True)
    carry[...] = split_sum(jnp.broadcast_to(flux, (8, width)), ones)
    grad_log = -v.step * v.rate * after
    grad_raw = (direct - v.rate * after) * jax.nn.sigmoid(v.raw)
    grad_rates[0:1, :] += jnp.sum(grad_raw, axis=0, keepdims=True)
    grad_rates[1:2, :] += jnp.sum(grad_log, axis=0, keepdims=True)

    index_ext = c0 + iota((rows + 8, 1), 0)
    position_ext = index_ext - starts_of(index_ext, ends)
    taps_back(v.x_ext, grad_pre[...], v.position, grad_wide)
    extended = jnp.concatenate([grad_pre[...], next_pre[...]], axis=0)
    grad_all[:, width : 2 * width] = conv_back(extended, wide, position_ext).astype(bf16)
    next_pre[...] = grad_pre[0:8, :]

    blank = jnp.zeros((rows, LANES - HD), f32)
    grad_sc = jnp.concatenate([grad_b, blank, grad_c, blank], axis=1)
    grad_pre_s = grad_sc * silu_grad(v.pre_s, v.gate_s)
    taps_back(v.s_ext, grad_pre_s, v.position, grad_narrow)
    extended_s = jnp.concatenate([grad_pre_s, next_pre_s[...]], axis=0)
    grad_all[:, 2 * width : 2 * width + 2 * LANES] = conv_back(extended_s, narrow, position_ext).astype(bf16)
    next_pre_s[...] = grad_pre_s[0:8, :]
    grad_all[:, 2 * width + 2 * LANES :] = grad_raw.astype(bf16)


def chunk_of(tp, rows):
    return math.gcd(rows // tp, CHUNK)


def mixer_specs(tp, rows, chunk, order):
    share = rows // tp
    per_share = share // chunk

    def here(place, c):
        owner = lax.div(c, per_share)
        piece = lax.rem(place[0] - owner + tp, tp)
        return piece * per_share + lax.rem(c, per_share)

    def chunk_map(i, place, lengths):
        return (here(place, order(i)), 0)

    def before_map(unit, column):
        def index(i, place, lengths):
            c = order(i)
            previous = jnp.maximum(c - 1, 0)
            return (here(place, previous) * (chunk // unit) + chunk // unit - 1, column)

        return index

    def fixed(i, place, lengths):
        return (0, 0)

    return chunk_map, before_map, fixed


def mixer_forward(place, lengths, tp, zx, sd, wide, narrow, rates):
    rows, width = zx.shape[0], zx.shape[1] // 2
    chunk = chunk_of(tp, rows)
    chunks = rows // chunk
    chunk_map, before_map, fixed = mixer_specs(tp, rows, chunk, lambda i: i)
    work = rows * width * chunk
    return pl.pallas_call(
        mixer_forward_kernel,
        out_shape=[
            jax.ShapeDtypeStruct((rows, width), bf16),
            jax.ShapeDtypeStruct((chunks, HD, width), bf16),
        ],
        grid_spec=pltpu.PrefetchScalarGridSpec(
            num_scalar_prefetch=2,
            grid=(chunks,),
            in_specs=[
                pl.BlockSpec((chunk, 2 * width), chunk_map),
                pl.BlockSpec((16, width), before_map(16, 1)),
                pl.BlockSpec((chunk, 3 * LANES), chunk_map),
                pl.BlockSpec((8, 3 * LANES), before_map(8, 0)),
                pl.BlockSpec((8, width), fixed),
                pl.BlockSpec((8, 2 * LANES), fixed),
                pl.BlockSpec((8, LANES), fixed),
            ],
            out_specs=[
                pl.BlockSpec((chunk, width), chunk_map),
                pl.BlockSpec((None, HD, width), lambda i, *_: (i, 0, 0)),
            ],
            scratch_shapes=[pltpu.VMEM((HD, width), f32)],
        ),
        compiler_params=pltpu.CompilerParams(vmem_limit_bytes=VMEM_LIMIT),
        cost_estimate=pl.CostEstimate(
            flops=8 * work, bytes_accessed=8 * rows * width, transcendentals=4 * rows * width
        ),
        name="mixer_forward",
    )(place, lengths, zx, zx, sd, sd, wide, narrow, rates)


def mixer_backward(place, lengths, tp, zx, sd, grad_scaled, stats, states, wide, narrow, rates):
    rows, width = zx.shape[0], zx.shape[1] // 2
    chunk = chunk_of(tp, rows)
    chunks = rows // chunk
    chunk_map, before_map, fixed = mixer_specs(tp, rows, chunk, lambda i: chunks - 1 - i)
    work = rows * width * chunk
    return pl.pallas_call(
        functools.partial(mixer_backward_kernel, chunks),
        out_shape=[
            jax.ShapeDtypeStruct((rows, 2 * width + 3 * LANES), bf16),
            jax.ShapeDtypeStruct((8, width), f32),
            jax.ShapeDtypeStruct((8, 2 * LANES), f32),
            jax.ShapeDtypeStruct((8, LANES), f32),
        ],
        grid_spec=pltpu.PrefetchScalarGridSpec(
            num_scalar_prefetch=2,
            grid=(chunks,),
            in_specs=[
                pl.BlockSpec((chunk, 2 * width), chunk_map),
                pl.BlockSpec((16, width), before_map(16, 1)),
                pl.BlockSpec((chunk, 3 * LANES), chunk_map),
                pl.BlockSpec((8, 3 * LANES), before_map(8, 0)),
                pl.BlockSpec((chunk, width), chunk_map),
                pl.BlockSpec((chunk, 2), chunk_map),
                pl.BlockSpec((None, HD, width), lambda i, *_: (chunks - 1 - i, 0, 0)),
                pl.BlockSpec((8, width), fixed),
                pl.BlockSpec((8, 2 * LANES), fixed),
                pl.BlockSpec((8, LANES), fixed),
            ],
            out_specs=[
                pl.BlockSpec((chunk, 2 * width + 3 * LANES), chunk_map),
                pl.BlockSpec((8, width), fixed),
                pl.BlockSpec((8, 2 * LANES), fixed),
                pl.BlockSpec((8, LANES), fixed),
            ],
            scratch_shapes=[
                pltpu.VMEM((HD, width), f32),
                pltpu.VMEM((8, width), f32),
                pltpu.VMEM((8, 2 * LANES), f32),
                pltpu.VMEM((8, LANES), f32),
                pltpu.VMEM((chunk, width), f32),
                pltpu.VMEM((chunk, width), f32),
                pltpu.VMEM((chunk, width), f32),
            ],
        ),
        compiler_params=pltpu.CompilerParams(vmem_limit_bytes=VMEM_LIMIT),
        cost_estimate=pl.CostEstimate(
            flops=24 * work, bytes_accessed=12 * rows * width, transcendentals=5 * rows * width
        ),
        name="mixer_backward",
    )(place, lengths, zx, zx, sd, sd, grad_scaled, stats, states, wide, narrow, rates)


def norm_pairs_kernel(pairs, gain, *refs):
    out = refs[2 * pairs]
    width = refs[0].shape[1]
    for j in range(pairs):
        both = [refs[2 * j + i][...].astype(f32) for i in range(2)]
        squares = sum(jnp.sum(v * v, axis=1, keepdims=True) for v in both)
        inv_root = lax.rsqrt(squares / (2 * width) + norm_eps)
        for i, v in enumerate(both):
            cols = slice(i * width, (i + 1) * width)
            out[j, :, cols] = (v * inv_root * gain[:, cols]).astype(bf16)


def norm_pairs(pairs, gain):
    rows, width = pairs[0][0].shape
    block = math.gcd(rows, 64)
    count = len(pairs)
    result = pl.pallas_call(
        functools.partial(norm_pairs_kernel, count),
        out_shape=jax.ShapeDtypeStruct((count, rows, 2 * width), bf16),
        grid=(rows // block,),
        in_specs=[pl.BlockSpec((1, 2 * width), lambda i: (0, 0))]
        + [pl.BlockSpec((block, width), lambda i: (i, 0))] * (2 * count),
        out_specs=pl.BlockSpec((count, block, 2 * width), lambda i: (0, i, 0)),
        compiler_params=pltpu.CompilerParams(vmem_limit_bytes=VMEM_LIMIT),
        cost_estimate=pl.CostEstimate(
            flops=10 * count * rows * width, bytes_accessed=8 * count * rows * width, transcendentals=rows
        ),
        name="norm_pairs",
    )(gain, *[v for pair in pairs for v in pair])
    return result.reshape(count * rows, 2 * width)


def norm_back_kernel(parts, with_base, with_low, with_gain, *refs):
    values, refs = refs[:parts], refs[parts:]
    grad, gain, refs = refs[0], refs[1], refs[2:]
    base, refs = (refs[0], refs[1:]) if with_base else (None, refs)
    outs, refs = refs[:parts], refs[parts:]
    low, refs = (refs[0], refs[1:]) if with_low else (None, refs)
    if with_gain:
        grad_gain = refs[0]

        @pl.when(pl.program_id(0) == 0)
        def _():
            grad_gain[...] = jnp.zeros_like(grad_gain)

    width = grad.shape[1]
    each = width // parts
    wide = [v[...].astype(f32) for v in values]
    squares = sum(jnp.sum(v * v, axis=1, keepdims=True) for v in wide)
    inv_root = lax.rsqrt(squares / width + norm_eps)
    units = [v * inv_root for v in wide]
    grads = [grad[:, i * each : (i + 1) * each] for i in range(parts)]
    grad_units = [g * gain[:, i * each : (i + 1) * each] for i, g in enumerate(grads)]
    cross = sum(jnp.sum(g * u, axis=1, keepdims=True) for g, u in zip(grad_units, units)) / width
    for i in range(parts):
        cols = slice(i * each, (i + 1) * each)
        if with_gain:
            grad_gain[0:1, cols] += jnp.sum(grads[i] * units[i], axis=0, keepdims=True)
        result = inv_root * (grad_units[i] - units[i] * cross)
        if with_base and i == 0:
            result = result + base[...].astype(f32)
        outs[i][...] = result
        if with_low and i == 0:
            low[...] = result.astype(bf16)


def norm_back(values, grad, gain, base=None, with_low=False, with_gain=True):
    rows, width = grad.shape
    parts = len(values)
    block = math.gcd(rows, 64)
    row_spec = pl.BlockSpec((block, width // parts), lambda i: (i, 0))
    full_spec = pl.BlockSpec((block, width), lambda i: (i, 0))
    operands = list(values) + [grad, gain] + ([base] if base is not None else [])
    shapes = [jax.ShapeDtypeStruct((rows, width // parts), f32)] * parts
    shapes += [jax.ShapeDtypeStruct((rows, width // parts), bf16)] if with_low else []
    results = pl.pallas_call(
        functools.partial(norm_back_kernel, parts, base is not None, with_low, with_gain),
        out_shape=shapes + [jax.ShapeDtypeStruct((8, width), f32)] * int(with_gain),
        grid=(rows // block,),
        in_specs=[row_spec] * parts
        + [full_spec, pl.BlockSpec((1, width), lambda i: (0, 0))]
        + ([row_spec] if base is not None else []),
        out_specs=[row_spec] * (parts + int(with_low))
        + [pl.BlockSpec((8, width), lambda i: (0, 0))] * int(with_gain),
        compiler_params=pltpu.CompilerParams(vmem_limit_bytes=VMEM_LIMIT),
        cost_estimate=pl.CostEstimate(
            flops=20 * rows * width, bytes_accessed=14 * rows * width, transcendentals=rows
        ),
        name="norm_back",
    )(*operands)
    return list(results[:-1]) + [results[-1][0]] if with_gain else list(results)


def tie(value, others):
    return lax.optimization_barrier((value, others))[0]


def after(value, token):
    return value if token is None else tie(value, token)


def ring_pairs():
    tp = lax.axis_size("tp")
    return [(i, (i + 1) % tp) for i in range(tp)]


def hop(values):
    return lax.ppermute(values, "tp", ring_pairs())


class Halving:
    def __init__(self, values, name, sent_as=f32):
        self.values, self.name, self.sent_as = values, name, sent_as
        self.half = lax.axis_size(name) // 2

    def live(self):
        return self.half > 0

    def start(self):
        count, half = lax.axis_size(self.name), self.half
        upper = (lax.axis_index(self.name) & half) != 0
        low, high = self.values[:half], self.values[half:]
        self.kept = jnp.where(upper, high, low)
        sent = jnp.where(upper, low, high).astype(self.sent_as)
        self.moved = lax.ppermute(sent, self.name, [(i, i ^ half) for i in range(count)])

    def finish(self):
        self.values = self.kept + self.moved.astype(f32)
        self.half //= 2

    def result(self):
        while self.live():
            self.start()
            self.finish()
        return self.values[0]


class Doubling:
    def __init__(self, values, name, sent_as=f32):
        self.values, self.name, self.sent_as = values, name, sent_as
        self.step = 1

    def live(self):
        return self.step < lax.axis_size(self.name)

    def start(self):
        count, step = lax.axis_size(self.name), self.step
        self.moved = lax.ppermute(
            self.values.astype(self.sent_as), self.name, [(i, i ^ step) for i in range(count)]
        )

    def finish(self):
        self.values = self.values + self.moved.astype(f32)
        self.step *= 2

    def result(self):
        while self.live():
            self.start()
            self.finish()
        return self.values


def direct(values, name, sent_as=f32):
    count = lax.axis_size(name)
    here = lax.axis_index(name)

    def block(at):
        return lax.dynamic_index_in_dim(values, lax.rem(at, count), 0, keepdims=False)

    total = block(here)
    for step in range(1, count):
        sent = block(here + step).astype(sent_as)
        moved = lax.ppermute(sent, name, [(i, (i + step) % count) for i in range(count)])
        total = total + moved.astype(f32)
    return total


def begin(tasks):
    live = [t for t in tasks if t.live()]
    for t in live:
        t.start()
    return live


def settle(moved, extras, live):
    moved, extras, arrived = lax.optimization_barrier((moved, extras, [t.moved for t in live]))
    for t, value in zip(live, arrived):
        t.moved = value
        t.finish()
    return moved, extras


def ring_gather(own, use, tasks=()):
    tp = lax.axis_size("tp")
    pieces, results = [own], []
    for p in range(tp):
        if p < tp - 1:
            moved = hop(pieces[p])
            live = begin(tasks)
        result = use(p, pieces[p])
        if p < tp - 1:
            moved, result = settle(moved, result, live)
            pieces.append(moved)
        results.append(result)
    return pieces, results


def ring_scatter(part, fill=(), tasks=()):
    tp = lax.axis_size("tp")
    fill = list(fill)
    filled = []
    total = part(1 % tp, None)
    for p in range(2, tp + 1):
        low = total.astype(bf16)
        moved = hop(low)
        live = begin(tasks)
        term = part(p % tp, low)
        extra = [fill.pop(0)(low, tasks)] if fill else []
        moved, (term, extra) = settle(moved, (term, extra), live)
        filled += extra
        total = moved.astype(f32) + term
    for thunk in fill:
        filled.append(thunk(low, tasks))
    return total, filled


def ring_both(own, work, last=None, fill=None, tasks=()):
    tp = lax.axis_size("tp")
    pieces, filled = [own], []
    moved = hop(own)
    live = begin(tasks)
    first = work(0, own)
    moved, _ = settle(moved, (), live)
    total, ahead = None, None
    for p in range(1, tp):
        pieces.append(moved)
        if p < tp - 1:
            moved = hop(pieces[p])
        elif last is not None:
            pieces[p], result = lax.optimization_barrier((pieces[p], last(pieces)))
            filled.append(result)
        live = begin(tasks)
        term = work(p, pieces[p])
        if total is not None:
            ahead, term = lax.optimization_barrier((ahead, term))
            term = ahead.astype(f32) + term
        total = term
        low = total.astype(bf16)
        ahead = hop(low)
        if p < tp - 1:
            moved, (low, first) = settle(moved, (low, first), live)
        elif fill is not None:
            ahead, result = settle(ahead, fill(low), live)
            filled.append(result)
        else:
            ahead, _ = settle(ahead, (), live)
    return pieces, ahead.astype(f32) + first, filled


def doubling_gather(values, name):
    count = lax.axis_size(name)
    here = lax.axis_index(name)
    step = 1
    while step < count:
        moved = lax.ppermute(values, name, [(i, i ^ step) for i in range(count)])
        upper = (here & step) != 0
        values = jnp.concatenate(
            [jnp.where(upper, moved, values), jnp.where(upper, values, moved)], axis=0
        )
        step *= 2
    return values


def inverse_root(values):
    return lax.rsqrt(jnp.mean(values * values, axis=1, keepdims=True) + norm_eps)


def gather(values, axis=0):
    return lax.all_gather(values, "fsdp", axis=axis, tiled=True)


def scatter(values, axis=0):
    return lax.psum_scatter(values, "fsdp", scatter_dimension=axis, tiled=True)


def local(
    hidden,
    embed,
    lengths,
    attention_norm_gain,
    query_key_value_weight,
    attention_adapter_down,
    attention_adapter_up,
    attention_output_weight,
    feedforward_norm_gain,
    gate_up_weight,
    feedforward_adapter_down,
    feedforward_adapter_up,
    down_weight,
    mixer_norm_gain,
    gate_inner_weight,
    state_input_weight,
    step_projection,
    inner_conv_taps,
    state_conv_taps,
    head_step_bias,
    decay_log_rate,
    inner_skip_gains,
    gated_norm_gain,
    mixer_output_weight,
    output_cotangent,
):
    tp = lax.axis_size("tp")
    fsdp = lax.axis_size("fsdp")
    share, width = hidden.shape
    rows = share * tp
    here = lax.axis_index("tp").astype(jnp.int32)
    place = here.reshape(1)
    lengths = lengths.reshape(-1)
    rank = attention_adapter_down.shape[2]
    head_cols = query_key_value_weight.shape[2]
    units_here = gate_up_weight.shape[2]
    inner_cols = gate_inner_weight.shape[2]
    mixer_heads = inner_cols // HD
    states = state_input_weight.shape[2]
    count = inner_conv_taps.shape[0]
    inner_total = inner_cols * tp

    def piece(values, p):
        return values[p * share : (p + 1) * share]

    own_qkv = jnp.concatenate(
        [query_key_value_weight[:, j, :] for j in range(3)]
        + [attention_adapter_down[:, j, :] for j in range(3)],
        axis=1,
    )
    weight_qkv = gather(own_qkv)
    first_hop = tuple(hop(v) for v in (hidden, embed))

    small = [
        attention_norm_gain,
        feedforward_norm_gain,
        mixer_norm_gain,
        inner_conv_taps.reshape(-1),
        state_conv_taps.reshape(-1),
        inner_skip_gains.reshape(-1),
        gated_norm_gain.reshape(-1),
    ]
    sizes = [v.shape[0] for v in small]
    padding = -sum(sizes) % LANES
    packed = jnp.concatenate(small + [jnp.zeros((padding,), bf16)]).reshape(1, -1)
    spread = gather(packed).astype(f32)
    cuts = [sum(sizes[:i]) for i in range(len(sizes) + 1)]
    parts = [spread[:, cuts[i] : cuts[i + 1]] for i in range(len(sizes))]
    gain_attn, gain_mlp, gain_mixer = (parts[i].reshape(1, -1) for i in range(3))
    taps_x = parts[3].reshape(fsdp, count, mixer_heads, -1)
    taps_x = jnp.transpose(taps_x, (1, 2, 0, 3)).reshape(count, inner_cols)
    taps_s = parts[4].reshape(fsdp, count, 2, -1)
    taps_s = jnp.transpose(taps_s, (1, 2, 0, 3)).reshape(count, 2, states)
    skip = jnp.transpose(parts[5].reshape(fsdp, mixer_heads, -1), (1, 0, 2)).reshape(1, inner_cols)
    gain_gate = jnp.transpose(parts[6].reshape(fsdp, mixer_heads, -1), (1, 0, 2)).reshape(1, inner_cols)
    wide = jnp.concatenate([taps_x, skip, gain_gate, jnp.zeros((2, inner_cols), f32)], axis=0)
    narrow = jnp.pad(taps_s, ((0, 8 - count), (0, 0), (0, LANES - states))).reshape(8, 2 * LANES)
    rates = jnp.pad(
        jnp.stack([head_step_bias, decay_log_rate]), ((0, 6), (0, LANES - mixer_heads))
    )

    places = jnp.arange(rows, dtype=jnp.int32)
    ends = [jnp.sum(lengths[: i + 1]) for i in range(lengths.shape[0] - 1)]
    position = places - starts_of(places, ends)
    freqs = jnp.exp(jnp.arange(HDA // 2, dtype=f32) * (-2.0 * math.log(10000.0) / HDA))
    angles = position.astype(f32)[:, None] * freqs[None, :]
    cosine = jnp.cos(angles)
    sine = jnp.sin(angles)
    cosine = jnp.concatenate([cosine, cosine], axis=1)
    sine = jnp.concatenate([-sine, sine], axis=1)

    own_fc1 = jnp.concatenate(
        [gate_up_weight[:, j, :] for j in range(2)] + [feedforward_adapter_down], axis=1
    )
    own_zx = jnp.concatenate(
        [gate_inner_weight[:, j, :] for j in range(2)]
        + [jnp.pad(state_input_weight[:, j, :], ((0, 0), (0, LANES - states))) for j in range(2)]
        + [jnp.pad(step_projection, ((0, 0), (0, LANES - mixer_heads)))],
        axis=1,
    )
    weight_o = gather(attention_output_weight, 1)
    weight_fc1 = gather(own_fc1)
    weight_fc2 = gather(down_weight, 1)
    weight_zx = gather(own_zx)
    weight_out = gather(mixer_output_weight, 1)

    raw, normed_parts = [(hidden, embed), first_hop], []
    spans = [((tp * i) // (tp - 2), (tp * (i + 1)) // (tp - 2)) for i in range(tp - 2)]

    def norm_ready(count):
        fresh = [norm_pairs(raw[low:high], gain_attn) for low, high in spans[len(normed_parts) :] if high <= count]
        normed_parts.extend(fresh)
        return fresh

    for p in range(2, tp):
        moved = tuple(hop(v) for v in raw[-1])
        raw.append(tie(moved, norm_ready(p)))
    norm_ready(tp)

    own_ups = jnp.concatenate(
        [attention_adapter_up[:, j, :] for j in range(3)]
        + [feedforward_adapter_up[:, j, :] for j in range(2)],
        axis=1,
    )
    ups = doubling_gather(tie(own_ups, raw[-2]), "fsdp")
    fc_up = ups[:, 3 * head_cols :]
    out_grad = [tie(output_cotangent, raw[-1])]
    projected = []
    for i in range(tp - 1):
        moved = hop(out_grad[-1])
        if i < tp - 2:
            projected.append(mm(normed_parts[i], weight_qkv))
            moved = tie(moved, projected)
        else:
            attended, queries, keys, values = attention_forward(
                place, lengths, tp, projected, ups, head_cols, cosine, sine
            )
            moved = tie(moved, attended)
        out_grad.append(moved)
    lora_rows = jnp.concatenate([v[:, 3 * head_cols :].astype(bf16) for v in projected], axis=0)
    attended, lora_rows, out_grad[-1] = lax.optimization_barrier((attended, lora_rows, moved))
    out_grad_rows = jnp.concatenate(out_grad, axis=0)
    mixed, (normed_rows,) = ring_scatter(
        lambda p, t: mm(piece(after(attended, t), p), weight_o),
        [lambda t, _: jnp.concatenate(tie(normed_parts, t), axis=0)],
    )

    mlp_root = inverse_root(mixed)
    gate_up, fc_mid, units = [], [], []

    def feed(p, rows_in):
        wide_rows = mm(rows_in, weight_fc1)
        middle = wide_rows[:, 2 * units_here :].astype(bf16)
        both = (wide_rows[:, : 2 * units_here] + mm(middle, fc_up)).astype(bf16)
        gate, up = both[:, :units_here].astype(f32), both[:, units_here:].astype(f32)
        unit = (jax.nn.gelu(gate) * up).astype(bf16)
        fc_mid.append(middle)
        gate_up.append(both)
        units.append(unit)
        return mm(unit, weight_fc2)

    mlp_in, branch, _ = ring_both((mixed * mlp_root * gain_mlp).astype(bf16), feed)
    residual = hidden.astype(f32) + mixed + branch

    mixer_root = inverse_root(residual)
    kept = []

    def mix(p, rows_in):
        result = mm(rows_in, weight_zx)
        if p == 0:
            kept.append(mm_nt(tie(out_grad_rows, result), weight_out).astype(bf16))
        elif p == 1:
            kept.append(jnp.concatenate(tie(units, result), axis=0))
            kept.append(jnp.concatenate(tie(mlp_in, result), axis=0))
        return (result, kept[-1])

    mixer_in, zxs = ring_gather((residual * mixer_root * gain_mixer).astype(bf16), mix)
    zxs = [v[0] for v in zxs]
    grad_scaled, units_rows, mlp_rows = kept
    mixer_rows = jnp.concatenate(mixer_in, axis=0)
    zx = jnp.concatenate([v[:, : 2 * inner_cols].astype(bf16) for v in zxs], axis=0)
    sd = jnp.concatenate([v[:, 2 * inner_cols :] for v in zxs], axis=0)
    gated, chunk_states = mixer_forward(place, lengths, tp, zx, sd, wide, narrow, rates)
    gated_wide = gated.astype(f32)
    sums = jnp.stack(
        [
            jnp.sum(gated_wide * gated_wide, axis=1),
            jnp.sum(grad_scaled.astype(f32) * gain_gate * gated_wide, axis=1),
        ],
        axis=0,
    )
    sums = jnp.roll(jnp.flip(sums.reshape(2, tp, share), axis=1), here + 1, axis=1)
    sums = lax.psum(sums, "tp")
    sums = jnp.flip(jnp.roll(sums, -(here + 1), axis=1), axis=1).reshape(2, rows)
    gate_root = lax.rsqrt(sums[0] / inner_total + norm_eps)
    stats = jnp.stack([gate_root, gate_root**3 * sums[1] / inner_total], axis=1)
    scaled = (gated_wide * gate_root[:, None] * gain_gate).astype(bf16)
    out_rows, stats = lax.optimization_barrier((mm(scaled, weight_out).astype(bf16), stats))
    out_terms = [piece(out_rows, p) for p in range(tp)]
    out = hop(out_terms[1 % tp])

    grad_all, grad_wide, grad_narrow, grad_rates = mixer_backward(
        place, lengths, tp, zx, sd, grad_scaled, stats, chunk_states, wide, narrow, rates
    )
    out, grad_all = lax.optimization_barrier((out, grad_all))
    out = out.astype(f32) + out_terms[2 % tp].astype(f32)

    def by_fsdp(values):
        lead = values.shape[:-1]
        cut = values.reshape(lead + (fsdp, values.shape[-1] // fsdp))
        return jnp.moveaxis(cut, -2, 0).reshape(fsdp, -1)

    def small_gradients(token):
        taps, bars, sums_r = tie((grad_wide, grad_narrow, grad_rates), token)
        return [
            by_fsdp(taps[:count].reshape(count, mixer_heads, HD)),
            by_fsdp(taps[4].reshape(mixer_heads, HD)),
            by_fsdp(taps[5].reshape(mixer_heads, HD)),
            jnp.broadcast_to(sums_r[:2, :mixer_heads].reshape(1, -1), (fsdp, 2 * mixer_heads)),
            by_fsdp(bars[:count].reshape(count, 2, LANES)[:, :, :states]),
        ]

    grad_mixer_in, (sum_w_out, sum_w_zx, small) = ring_scatter(
        lambda p, t: mm_nt(piece(after(grad_all, t), p), weight_zx),
        [
            lambda t, _: mm_tn(tie(scaled, t), out_grad_rows).astype(bf16),
            lambda t, _: mm_tn(tie(mixer_rows, t), grad_all).astype(bf16),
            lambda t, _: small_gradients(t),
        ],
    )
    sum_w_out = scatter(sum_w_out, 1)
    sum_w_zx = scatter(sum_w_zx)
    small_sizes = [v.shape[1] for v in small]
    small_cuts = [sum(small_sizes[:i]) for i in range(len(small_sizes) + 1)]
    small_task = Halving(jnp.concatenate(small, axis=1), "fsdp")
    grad_residual, grad_residual_low, grad_gain_mixer = norm_back(
        [residual], grad_mixer_in, gain_mixer, output_cotangent, True
    )

    grad_gate_up = []

    def feed_back(p, grad_rows):
        grad_units = mm_nt(grad_rows, weight_fc2)
        gate = gate_up[p][:, :units_here].astype(f32)
        up = gate_up[p][:, units_here:].astype(f32)
        raised, back = jax.vjp(jax.nn.gelu, gate)
        both = jnp.concatenate(
            [back(grad_units * up)[0].astype(bf16), (grad_units * raised).astype(bf16)], axis=1
        )
        both = jnp.concatenate([both, mm_nt(both, fc_up).astype(bf16)], axis=1)
        grad_gate_up.append(both)
        return mm_nt(both, weight_fc1)

    def fc2_fill(token, _):
        rows_in = tie(units_rows, (sum_w_out, token))
        return mm_tn(rows_in, jnp.concatenate(grad_branch, axis=0)).astype(bf16)

    def fc1_fill(token, _):
        return mm_tn(tie(mlp_rows, token), jnp.concatenate(grad_gate_up, axis=0)).astype(bf16)

    grad_branch, back_terms = ring_gather(
        grad_residual_low, lambda p, v: feed_back(p, v) if p < tp - 1 else (), [small_task]
    )
    grad_mlp_in, filled = ring_scatter(
        lambda p, t: feed_back(p, after(grad_branch[p], t))
        if p == tp - 1
        else tie(back_terms[p], grad_branch[-1]),
        [fc2_fill] + [lambda t, _: ()] * (tp - 3) + [fc1_fill],
    )
    sum_w_fc2, sum_w_fc1 = filled[0], filled[-1]
    sum_w_fc2 = scatter(sum_w_fc2, 1)
    sum_w_fc1 = scatter(sum_w_fc1)
    grad_gate_up_rows = jnp.concatenate(grad_gate_up, axis=0)
    _, grad_mixed_low, grad_gain_mlp = norm_back([mixed], grad_mlp_in, gain_mlp, grad_residual, True)
    gain_task = Halving(
        jnp.concatenate([grad_gain_mixer.reshape(fsdp, -1), grad_gain_mlp.reshape(fsdp, -1)], axis=1), "fsdp"
    )

    fc_ups = []

    def attended_back(p, rows_in):
        result = mm_nt(rows_in, weight_o).astype(bf16)
        if p == 0:
            fc_ups.append(
                mm_tn(tie(jnp.concatenate(fc_mid, axis=0), rows_in), grad_gate_up_rows[:, : 2 * units_here])
            )
            result = tie(result, fc_ups[0])
        return result

    grad_mixed, grad_attended = ring_gather(tie(grad_mixed_low, sum_w_zx), attended_back, [gain_task])
    sum_w_o = mm_tn(tie(attended, sum_w_fc2), jnp.concatenate(grad_mixed, axis=0)).astype(bf16)
    grad_attended[-1] = tie(grad_attended[-1], sum_w_o)
    sum_w_o = scatter(sum_w_o, 1)
    out = hop(out.astype(bf16))
    grad_projected = attention_backward(
        place, lengths, queries, keys, values, ups, grad_attended, cosine, sine
    )
    out, grad_projected, sum_w_fc1 = lax.optimization_barrier((out, grad_projected, sum_w_fc1))
    out = out.astype(f32) + out_terms[3 % tp].astype(f32)
    out = hop(out.astype(bf16))
    sum_w_qkv = mm_tn(normed_rows, grad_projected).astype(bf16)
    out, sum_w_qkv, grad_projected = lax.optimization_barrier((out, sum_w_qkv, grad_projected))
    sum_w_qkv = scatter(sum_w_qkv)

    at_t = 2 * inner_cols + 2 * LANES

    def finish_out(token):
        total = tie(out, token).astype(f32) + out_terms[4 % tp].astype(f32)
        for p in range(5, tp + 1):
            total = hop(total.astype(bf16)).astype(f32) + out_terms[p % tp].astype(f32)
        return residual + total

    def finish_adapters(token, tasks):
        rows_in = tie(lora_rows, token)
        grad_up = [
            mm_tn(
                rows_in[:, j * rank : (j + 1) * rank],
                grad_projected[:, j * head_cols : (j + 1) * head_cols],
            )
            for j in range(3)
        ]
        ups_grad = jnp.concatenate(grad_up + fc_ups, axis=1)
        tasks.append(Halving(ups_grad.reshape(fsdp, -1, ups_grad.shape[1]), "fsdp", bf16))
        shared = jnp.concatenate([small_task.result()[small_cuts[4] :], gain_task.result()])
        tasks.append(Doubling(shared, "tp"))
        return ups_grad, shared

    def finish_mixer(token, tasks):
        zx_sum, w_out, w_fc2 = tie((sum_w_zx, sum_w_out, sum_w_fc2), token)
        zx_sum = zx_sum.astype(f32)
        bc_sums.append(zx_sum[:, 2 * inner_cols : at_t])
        return (
            stacked(zx_sum, inner_cols, 2),
            zx_sum[:, at_t : at_t + mixer_heads],
            w_out.astype(f32),
            w_fc2.astype(f32),
        )

    def finish_feed(token, tasks):
        fc1_sum, w_o = tie((sum_w_fc1, sum_w_o), token)
        fc1_sum = fc1_sum.astype(f32)
        tasks.append(
            Doubling(jnp.concatenate([bc_sums[0], fc1_sum[:, 2 * units_here :]], axis=1), "tp", bf16)
        )
        return (
            stacked(fc1_sum, units_here, 2),
            w_o.astype(f32),
            finish_out(token),
        )

    def stacked(values, each, parts):
        values = jnp.stack([values[:, j * each : (j + 1) * each] for j in range(parts)], axis=1)
        return with_layout_constraint(values, Layout(major_to_minor=(0, 1, 2)))

    tasks, bc_sums = [], []
    normed_terms = {}
    pair = mm_nt(grad_projected[share : 3 * share], weight_qkv)
    normed_terms[1], normed_terms[2] = piece(pair, 0), piece(pair, 1)

    def normed_back(p, token):
        if p not in normed_terms:
            normed_terms[p] = mm_nt(piece(after(grad_projected, token), p), weight_qkv)
        return normed_terms[p]

    grad_normed, ((_, mixer_sums, _), feed_sums) = ring_scatter(
        normed_back,
        [lambda t, k: (finish_adapters(t, k), finish_mixer(t, k), normed_back(3 % tp, t)), finish_feed],
        tasks,
    )
    grad_w_zx, grad_w_dt, grad_w_out, grad_w_fc2 = mixer_sums
    grad_w_fc1, grad_w_o, out = feed_sums
    grad_hidden, grad_embed = norm_back(
        [hidden, embed], grad_normed, gain_attn, grad_residual, with_gain=False
    )
    gain_rows = jnp.sum(sum_w_qkv.astype(f32) * own_qkv.astype(f32), axis=1)
    gain_rows = gain_rows / attention_norm_gain.astype(f32)
    grad_down = direct(sum_w_qkv[:, 3 * head_cols :].astype(f32).reshape(tp, -1, 3 * rank), "tp", bf16)
    grad_gain_attn = direct(gain_rows.reshape(tp, -1), "tp")
    grad_w_qkv = jnp.stack(
        [sum_w_qkv[:, j * head_cols : (j + 1) * head_cols].astype(f32) for j in range(3)], axis=1
    )
    small_sum = small_task.result()
    small_parts = [small_sum[small_cuts[i] : small_cuts[i + 1]] for i in range(len(small_sizes))]
    grad_ups, tail = tasks[0].result(), tasks[1].result()
    shared = tasks[2].result()
    tail_sizes = [small_sizes[4], width // fsdp, width // fsdp]
    tail_cuts = [sum(tail_sizes[:i]) for i in range(4)]
    grad_conv_bc, sum_gain_mixer, sum_gain_mlp = (
        tail[tail_cuts[i] : tail_cuts[i + 1]] for i in range(3)
    )
    sum_rates = small_parts[3].reshape(2, mixer_heads)
    return (
        out,
        grad_hidden,
        grad_embed,
        grad_gain_attn,
        grad_w_qkv,
        grad_down.reshape(-1, 3, rank),
        grad_ups[:, : 3 * head_cols].reshape(-1, 3, head_cols),
        grad_w_o,
        sum_gain_mlp,
        grad_w_fc1,
        shared[:, 2 * LANES :],
        grad_ups[:, 3 * head_cols :].reshape(-1, 2, units_here),
        grad_w_fc2,
        sum_gain_mixer,
        grad_w_zx,
        shared[:, : 2 * LANES].reshape(-1, 2, LANES)[:, :, :states],
        grad_w_dt,
        small_parts[0].reshape(count, mixer_heads, -1),
        grad_conv_bc.reshape(count, 2, -1),
        sum_rates[0],
        sum_rates[1],
        small_parts[1].reshape(mixer_heads, -1),
        small_parts[2].reshape(mixer_heads, -1),
        grad_w_out,
    )


def solution(mesh):
    placed = (
        P(("fsdp", "tp"), None),
        P(("fsdp", "tp"), None),
        P("fsdp", None),
        P("fsdp"),
        P("fsdp", None, "tp"),
        P("fsdp", None, None),
        P("fsdp", None, "tp"),
        P("tp", "fsdp"),
        P("fsdp"),
        P("fsdp", None, "tp"),
        P("fsdp", None),
        P("fsdp", None, "tp"),
        P("tp", "fsdp"),
        P("fsdp"),
        P("fsdp", None, "tp"),
        P("fsdp", None, None),
        P("fsdp", "tp"),
        P(None, "tp", "fsdp"),
        P(None, None, "fsdp"),
        P("tp"),
        P("tp"),
        P("tp", "fsdp"),
        P("tp", "fsdp"),
        P("tp", "fsdp"),
        P(("fsdp", "tp"), None),
    )
    return jax.shard_map(
        local,
        mesh=mesh,
        in_specs=placed,
        out_specs=(
            P(("fsdp", "tp"), None),
            P(("fsdp", "tp"), None),
            P(("fsdp", "tp"), None),
            P(("fsdp", "tp")),
            P("fsdp", None, "tp"),
            P(("fsdp", "tp"), None, None),
            P("fsdp", None, "tp"),
            P("tp", "fsdp"),
            P("fsdp"),
            P("fsdp", None, "tp"),
            P("fsdp", None),
            P("fsdp", None, "tp"),
            P("tp", "fsdp"),
            P("fsdp"),
            P("fsdp", None, "tp"),
            P("fsdp", None, None),
            P("fsdp", "tp"),
            P(None, "tp", "fsdp"),
            P(None, None, "fsdp"),
            P("tp"),
            P("tp"),
            P("tp", "fsdp"),
            P("tp", "fsdp"),
            P("tp", "fsdp"),
        ),
        check_vma=False,
    )
```
